32 devices in a mesh: dp: 8 (over y, x, core), sp: 4 (over z).
Axes of the slice: x: 2, y: 2, z: 4, core: 2. Of those that a mesh axis runs over, the one named last changes fastest.
Arguments:
- tokens: bfloat16 [8192, 2048], P(('dp', 'sp')), may hold values from -6 to 6
- lengths: int32 [8], P('dp'), may hold values from 64 to 1024, as said below
- cotangent: bfloat16 [8192, 2048], P(('dp', 'sp')), may hold values from -6 to 6
- ln_gains: bfloat16 [2, 2048], replicated, may hold values from 0.099609375 to 1.8984375
- ln_shifts: bfloat16 [2, 2048], replicated, may hold values from -1.5 to 1.5
- qkv_weight: bfloat16 [2048, 6144], P(('dp', 'sp')), may hold values from -0.125 to 0.125
- qkv_bias: bfloat16 [3, 2048], replicated, may hold values from -0.25 to 0.25
- out_weight: bfloat16 [2048, 2048], P(('dp', 'sp')), may hold values from -1 to 1
- up_weight: bfloat16 [8192, 2048], P(('dp', 'sp')), may hold values from -0.125 to 0.125
- up_bias: bfloat16 [8192], replicated, may hold values from -1.5 to 1.5
- down_weight: bfloat16 [8192, 2048], P(('dp', 'sp')), may hold values from -0.0625 to 0.0625
- out_bias: bfloat16 [2048], replicated, may hold values from -1.5 to 1.5
Outputs:
- output: bfloat16 [8192, 2048], P(('dp', 'sp'))
- input_grad: bfloat16 [8192, 2048], P(('dp', 'sp'))
- ln_gains_grad: float32 [2, 2048], replicated
- ln_shifts_grad: float32 [2, 2048], replicated
- qkv_weight_grad: float32 [2048, 6144], P(('dp', 'sp'))
- qkv_bias_grad: float32 [3, 2048], replicated
- out_weight_grad: float32 [2048, 2048], P(('dp', 'sp'))
- up_weight_grad: float32 [8192, 2048], P(('dp', 'sp'))
- up_bias_grad: float32 [8192], replicated
- down_weight_grad: float32 [8192, 2048], P(('dp', 'sp'))
- out_bias_grad: float32 [2048], replicated
The draws below stay inside these ranges and needn't reach their ends.
Inputs may be any that keep to these rules, and one draw needn't show every extreme that they name: `lengths`: a sequence's valid tokens fill the front of its 1024 rows; the first sequence is always full.
All inputs are finite; a program needn't handle non-finite values.
Results may differ from the reference program's by a relative error of at most 0.011.
Values may be sent and summed in bfloat16 or wider, within the bound.
A program may use at most 768 MiB of HBM per device.

```python
import jax
import jax.numpy as jnp
from jax import lax

D = 2048
HEADS = 8
HEAD = 256
ROT = 64
FF = 8192
SEQ = 1024
TOKENS = 8192
BLOCK = 512


def draw_lengths(key, part):
    seq_count = TOKENS // SEQ
    drawn = jax.random.randint(key, (seq_count,), SEQ // 16, SEQ + 1)
    return jnp.where(jnp.arange(seq_count) == 0, SEQ, drawn).astype(jnp.int32)


def block_levels(stream_key, shape, pieces, least, top_value):
    level, own = 1.0, jax.random.fold_in(stream_key, 6)
    for dim, shards_of in pieces:
        draws = jnp.exp(jax.random.uniform(jax.random.fold_in(own, dim), (shards_of,), jnp.float32, least / len(pieces), top_value / len(pieces)))
        level = level * jnp.repeat(draws, shape[dim] // shards_of).reshape([-1 if axis == dim else 1 for axis in range(len(shape))])
    return level


def gaussian(stream_key, extent, scale, reach, shards=(), kind=jnp.bfloat16):
    values = jax.random.normal(stream_key, extent, jnp.float32) * scale
    if len(shards) > 0:
        values = block_levels(stream_key, extent, shards, -0.22, 0.18) * values
    return jnp.clip(values, min=-reach, max=reach).astype(kind)


def setup_inputs(seed: int = 0) -> dict:
    streams_of = jax.random.split(jax.random.key(seed), 13)
    return {
        "tokens": gaussian(streams_of[0], (TOKENS, D), 1.0, 6.0, ((0, 32),)),
        "lengths": draw_lengths(jax.random.fold_in(streams_of[12], 71), 0),
        "cotangent": gaussian(streams_of[2], (TOKENS, D), 1.0, 6.0, ((0, 32),)),
        "ln_gains": jnp.clip(1.0 + 0.18 * jax.random.normal(streams_of[3], (2, D), jnp.float32), 0.099609375, 1.8984375).astype(jnp.bfloat16),
        "ln_shifts": gaussian(streams_of[4], (2, D), 0.3, 1.5),
        "qkv_weight": gaussian(streams_of[5], (D, 3 * D), D ** -0.5, 0.125, ((0, 32),)),
        "qkv_bias": gaussian(streams_of[6], (3, D), 0.05, 0.25),
        "out_weight": gaussian(streams_of[7], (D, D), (D // 64) ** -0.5, 1.0, ((0, 32),)),
        "up_weight": gaussian(streams_of[8], (FF, D), D ** -0.5, 0.125, ((0, 32),)),
        "up_bias": gaussian(streams_of[9], (FF,), 0.3, 1.5),
        "down_weight": gaussian(streams_of[10], (FF, D), FF ** -0.5, 0.0625, ((0, 32),)),
        "out_bias": gaussian(streams_of[11], (D,), 0.3, 1.5),
    }


@jax.custom_vjp
def low(v):
    return lax.optimization_barrier(v.astype(jnp.bfloat16)).astype(jnp.float32)

@jax.custom_vjp
def low_back(v):
    return v

def low_keep(v):
    return (low(v), None)

def low_pass(kept, grad):
    return (grad,)

def back_keep(v):
    return (v, None)

def back_low(kept, grad):
    return (low(grad),)
low.defvjp(low_keep, low_pass)
low_back.defvjp(back_keep, back_low)
eps = 1e-05
base_freq = 10000.0
precise = lax.Precision.HIGHEST
root_half = 0.7071067811865476

def matmul(left, right):
    return jnp.dot(left, right, precision=precise, preferred_element_type=jnp.float32)

def rotary_tables(positions):
    half_rot = ROT // 2
    frequency = base_freq ** (-jnp.arange(half_rot, dtype=jnp.float32) * (2.0 / ROT))
    angles = positions.astype(jnp.float32)[:, None] * frequency[None, :]
    return (jnp.cos(angles)[:, None, :], jnp.sin(angles)[:, None, :])

def rotate(tensor_in, cosine, sine_table):
    half_rot = cosine.shape[-1]
    leading = tensor_in[..., :half_rot]
    trailing = tensor_in[..., half_rot:2 * half_rot]
    return jnp.concatenate([leading * cosine - trailing * sine_table, trailing * cosine + leading * sine_table, tensor_in[..., 2 * half_rot:]], axis=-1)

def attend(queries, key_rows, values, length):
    score_scale = HEAD ** (-0.5)
    key_pos = jnp.arange(SEQ, dtype=jnp.int32)

    def one_block(block_start):
        query_rows = lax.dynamic_slice_in_dim(queries, block_start, BLOCK, 0)
        scores = low_back(jnp.einsum('qhd,khd->hqk', query_rows, key_rows, precision=precise) * score_scale)
        query_pos = block_start + jnp.arange(BLOCK, dtype=jnp.int32)
        allowed = (key_pos[None, :] <= query_pos[:, None]) & (key_pos[None, :] < length)
        scores = jnp.where(allowed[None], scores, -1e+30)
        highest = lax.optimization_barrier(jnp.max(scores, axis=-1, keepdims=True))
        weights_raw = jnp.exp(scores - highest)
        weights_low = low(weights_raw / lax.optimization_barrier(jnp.sum(weights_raw, axis=-1, keepdims=True)))
        return jnp.einsum('hqk,khd->qhd', weights_low, values, precision=precise)
    starts = jnp.arange(SEQ // BLOCK, dtype=jnp.int32) * BLOCK
    return lax.map(jax.checkpoint(one_block), starts).reshape(SEQ, D)

def layer(inputs, params, length):
    ln_gains, ln_shifts, qkv_weight, qkv_bias, out_weight, up_weight, up_bias, down_weight, out_bias = params
    centre = lax.optimization_barrier(jnp.mean(inputs, axis=-1, keepdims=True))
    centered = inputs - centre
    normed = centered * lax.rsqrt(lax.optimization_barrier(jnp.mean(centered * centered, axis=-1, keepdims=True)) + eps)
    attn_in = low(normed * ln_gains[0] + ln_shifts[0])
    mlp_in = low(normed * ln_gains[1] + ln_shifts[1])
    bias_row = qkv_bias.reshape(3 * D)
    projected = low_back(matmul(attn_in, qkv_weight) + bias_row)
    positions = jnp.arange(SEQ, dtype=jnp.int32)
    cosine, sine_table = rotary_tables(positions)
    queries = low_back(low(rotate(projected[:, :D].reshape(SEQ, HEADS, HEAD), cosine, sine_table)))
    key_rows = low_back(low(rotate(projected[:, D:2 * D].reshape(SEQ, HEADS, HEAD), cosine, sine_table)))
    values = low_back(low(projected[:, 2 * D:].reshape(SEQ, HEADS, HEAD)))
    context = low_back(low(attend(queries, key_rows, values, length)))
    pre_act = low_back(matmul(mlp_in, up_weight.T) + up_bias)
    hidden = low(0.5 * pre_act * (1.0 + lax.erf(pre_act * root_half)))
    return inputs + matmul(context, out_weight) + matmul(hidden, down_weight) + out_bias

def reference(tokens, lengths, cotangent, ln_gains, ln_shifts, qkv_weight, qkv_bias, out_weight, up_weight, up_bias, down_weight, out_bias):
    params = tuple((entry.astype(jnp.float32) for entry in (ln_gains, ln_shifts, qkv_weight, qkv_bias, out_weight, up_weight, up_bias, down_weight, out_bias)))
    seq_count = lengths.shape[0]
    seq_tokens = tokens.astype(jnp.float32).reshape(seq_count, SEQ, D)
    seq_grads = cotangent.astype(jnp.float32).reshape(seq_count, SEQ, D)

    def one_sequence(totals, entry):
        inputs, grad_rows, length = entry

        def forward(inner_inputs, inner_params):
            return layer(inner_inputs, inner_params, length)
        result, pullback = jax.vjp(forward, inputs, params)
        row_valid = (jnp.arange(SEQ, dtype=jnp.int32) < length).astype(jnp.float32)
        grad_inputs, grad_params = pullback(grad_rows * row_valid[:, None])
        totals = jax.tree.map(jnp.add, totals, grad_params)
        return (totals, (result.astype(jnp.bfloat16), grad_inputs.astype(jnp.bfloat16)))
    start_totals = jax.tree.map(jnp.zeros_like, params)
    totals, (outputs, input_grads) = lax.scan(one_sequence, start_totals, (seq_tokens, seq_grads, lengths))
    return (outputs.reshape(seq_count * SEQ, D), input_grads.reshape(seq_count * SEQ, D), totals[0], totals[1], totals[2], totals[3], totals[4], totals[5], totals[6], totals[7], totals[8])
```

```python
import jax
import jax.numpy as jnp
from jax import lax
from jax.sharding import PartitionSpec as P

D = 2048
HEADS = 8
HEAD = 256
ROT = 64


eps = 1e-05
base_freq = 10000.0
root_half = 0.7071067811865476
inv_root_two_pi = 0.3989422804014327


def contract_rows(left, right):
    return lax.dot_general(
        left, right, (((0,), (0,)), ((), ())), preferred_element_type=jnp.float32
    )


def contract_cols(left, right):
    return lax.dot_general(
        left, right, (((1,), (1,)), ((), ())), preferred_element_type=jnp.float32
    )


def gelu_value(pre_act):
    return 0.5 * pre_act * (1.0 + lax.erf(pre_act * root_half))


def gelu_slope(pre_act):
    return 0.5 * (1.0 + lax.erf(pre_act * root_half)) + pre_act * inv_root_two_pi * jnp.exp(
        -0.5 * pre_act * pre_act
    )


def rotary_tables(positions):
    half_rot = ROT // 2
    frequency = base_freq ** (-jnp.arange(half_rot, dtype=jnp.float32) * (2.0 / ROT))
    angles = positions.astype(jnp.float32)[:, None] * frequency[None, :]
    return (jnp.cos(angles)[:, None, :], jnp.sin(angles)[:, None, :])


def rotate(tensor_in, cosine, sine_table):
    half_rot = cosine.shape[-1]
    leading = tensor_in[..., :half_rot]
    trailing = tensor_in[..., half_rot : 2 * half_rot]
    return jnp.concatenate(
        [
            leading * cosine - trailing * sine_table,
            trailing * cosine + leading * sine_table,
            tensor_in[..., 2 * half_rot :],
        ],
        axis=-1,
    )


def block_mask(block_start, block_rows, seq_len, length):
    key_pos = jnp.arange(seq_len, dtype=jnp.int32)
    query_pos = block_start + jnp.arange(block_rows, dtype=jnp.int32)
    return (key_pos[None, :] <= query_pos[:, None]) & (key_pos[None, :] < length)


def attend_forward(queries, key_rows, values, length, score_scale):
    seq_len, head_width = queries.shape
    head_count = head_width // HEAD
    block_rows = min(512, seq_len)
    key_heads = key_rows.reshape(seq_len, head_count, HEAD)
    value_heads = values.reshape(seq_len, head_count, HEAD)

    def one_block(block_start):
        query_rows = lax.dynamic_slice_in_dim(queries, block_start, block_rows, 0).reshape(
            block_rows, head_count, HEAD
        )
        scores = (
            jnp.einsum("qhd,khd->hqk", query_rows, key_heads, preferred_element_type=jnp.float32)
            * score_scale
        )
        allowed = block_mask(block_start, block_rows, seq_len, length)
        scores = jnp.where(allowed[None], scores, -1e30)
        highest = jnp.max(scores, axis=-1, keepdims=True)
        weights_raw = jnp.exp(scores - highest)
        row_totals = jnp.sum(weights_raw, axis=-1, keepdims=True)
        weights_low = (weights_raw / row_totals).astype(jnp.bfloat16)
        context = jnp.einsum(
            "hqk,khd->qhd", weights_low, value_heads, preferred_element_type=jnp.float32
        )
        return (
            context.reshape(block_rows, head_width).astype(jnp.bfloat16),
            (highest + jnp.log(row_totals))[..., 0],
        )

    starts = jnp.arange(seq_len // block_rows, dtype=jnp.int32) * block_rows
    context, log_sums = lax.map(one_block, starts)
    return (context.reshape(seq_len, head_width), log_sums)


def attend_backward(queries, key_rows, values, grad_context, log_sums, length, score_scale):
    seq_len, head_width = queries.shape
    head_count = head_width // HEAD
    block_rows = min(512, seq_len)
    key_heads = key_rows.reshape(seq_len, head_count, HEAD)
    value_heads = values.reshape(seq_len, head_count, HEAD)

    def one_block(running, entry):
        grad_keys, grad_values = running
        block_start, lse_block = entry
        query_rows = lax.dynamic_slice_in_dim(queries, block_start, block_rows, 0).reshape(
            block_rows, head_count, HEAD
        )
        grad_rows = lax.dynamic_slice_in_dim(grad_context, block_start, block_rows, 0).reshape(
            block_rows, head_count, HEAD
        )
        scores = (
            jnp.einsum("qhd,khd->hqk", query_rows, key_heads, preferred_element_type=jnp.float32)
            * score_scale
        )
        allowed = block_mask(block_start, block_rows, seq_len, length)
        weights_full = jnp.where(allowed[None], jnp.exp(scores - lse_block[..., None]), 0.0)
        grad_values = grad_values + jnp.einsum(
            "hqk,qhd->khd",
            weights_full.astype(jnp.bfloat16),
            grad_rows,
            preferred_element_type=jnp.float32,
        )
        grad_probs = jnp.einsum(
            "qhd,khd->hqk", grad_rows, value_heads, preferred_element_type=jnp.float32
        )
        inner_sum = jnp.sum(weights_full * grad_probs, axis=-1, keepdims=True)
        grad_scores = (weights_full * (grad_probs - inner_sum)).astype(jnp.bfloat16)
        grad_query = (
            jnp.einsum("hqk,khd->qhd", grad_scores, key_heads, preferred_element_type=jnp.float32)
            * score_scale
        )
        grad_keys = (
            grad_keys
            + jnp.einsum(
                "hqk,qhd->khd", grad_scores, query_rows, preferred_element_type=jnp.float32
            )
            * score_scale
        )
        return ((grad_keys, grad_values), grad_query.reshape(block_rows, head_width))

    starts = jnp.arange(seq_len // block_rows, dtype=jnp.int32) * block_rows
    zero_heads = jnp.zeros((seq_len, head_count, HEAD), jnp.float32)
    (grad_keys, grad_values), grad_queries = lax.scan(
        one_block, (zero_heads, zero_heads), (starts, log_sums)
    )
    return (
        grad_queries.reshape(seq_len, head_width),
        grad_keys.reshape(seq_len, head_width),
        grad_values.reshape(seq_len, head_width),
    )


def body(
    tokens,
    lengths,
    cotangent,
    ln_gains,
    ln_shifts,
    qkv_weight,
    qkv_bias,
    out_weight,
    up_weight,
    up_bias,
    down_weight,
    out_bias,
):
    dp_size = lax.axis_size("dp")
    sp_size = lax.axis_size("sp")
    shard = lax.axis_index("sp")
    own_rows = tokens.shape[0]
    seq_rows = own_rows * sp_size
    head_width = D // sp_size
    score_scale = HEAD ** (-0.5)
    length = lengths[0]
    low = jnp.bfloat16
    full = jnp.float32

    seq_tokens = lax.all_gather(tokens, "sp", axis=0, tiled=True)
    seq_cotangent = lax.all_gather(cotangent, "sp", axis=0, tiled=True)
    qkv_rows = qkv_weight.shape[0]
    qkv_slab = lax.all_to_all(
        qkv_weight.reshape(qkv_rows, 3, sp_size, head_width),
        "sp",
        split_axis=2,
        concat_axis=0,
        tiled=True,
    )
    qkv_own = lax.all_gather(
        qkv_slab.reshape(qkv_rows * sp_size, 3 * head_width), "dp", axis=0, tiled=True
    )
    up_own = lax.all_gather(up_weight, "dp", axis=0, tiled=True)
    down_own = lax.all_gather(down_weight, "dp", axis=0, tiled=True)
    out_blocks = lax.all_gather(out_weight, "dp", axis=0, tiled=True)
    per_shard = dp_size // sp_size
    out_own = lax.all_to_all(
        out_blocks.reshape(sp_size, per_shard, qkv_rows, D),
        "sp",
        split_axis=0,
        concat_axis=2,
        tiled=True,
    ).reshape(head_width, D)
    units = up_weight.shape[0]
    unit_bias = lax.dynamic_index_in_dim(
        up_bias.reshape(dp_size, sp_size, units), shard, 1, keepdims=False
    ).reshape(dp_size * units)
    bias_own = lax.dynamic_index_in_dim(
        qkv_bias.reshape(3, sp_size, head_width), shard, 1, keepdims=False
    ).reshape(3 * head_width)

    positions = jnp.arange(seq_rows, dtype=jnp.int32)
    cosine, sine_table = rotary_tables(positions)
    gains = ln_gains.astype(full)
    shifts = ln_shifts.astype(full)
    inputs = seq_tokens.astype(full)
    centre = jnp.mean(inputs, axis=-1, keepdims=True)
    centered = inputs - centre
    inverse = lax.rsqrt(jnp.mean(centered * centered, axis=-1, keepdims=True) + eps)
    normed = centered * inverse
    attn_in = (normed * gains[0] + shifts[0]).astype(low)
    mlp_in = (normed * gains[1] + shifts[1]).astype(low)
    row_valid = positions < length
    grad_out = jnp.where(row_valid[:, None], seq_cotangent, jnp.zeros_like(seq_cotangent))

    heads_own = head_width // HEAD
    projected = jnp.dot(attn_in, qkv_own, preferred_element_type=full) + bias_own.astype(full)
    queries = (
        rotate(projected[:, :head_width].reshape(seq_rows, heads_own, HEAD), cosine, sine_table)
        .reshape(seq_rows, head_width)
        .astype(low)
    )
    key_rows = (
        rotate(
            projected[:, head_width : 2 * head_width].reshape(seq_rows, heads_own, HEAD),
            cosine,
            sine_table,
        )
        .reshape(seq_rows, head_width)
        .astype(low)
    )
    values = projected[:, 2 * head_width :].astype(low)
    context, log_sums = attend_forward(queries, key_rows, values, length, score_scale)

    pre_act = contract_cols(mlp_in, up_own) + unit_bias.astype(full)
    hidden = gelu_value(pre_act).astype(low)
    partial_out = jnp.dot(hidden, down_own, preferred_element_type=full) + jnp.dot(
        context, out_own, preferred_element_type=full
    )
    reduced_out = lax.psum_scatter(
        partial_out.astype(low), "sp", scatter_dimension=0, tiled=True
    )
    output = (
        tokens.astype(full) + reduced_out.astype(full) + out_bias.astype(full)
    ).astype(low)

    grad_hidden = contract_cols(grad_out, down_own)
    grad_pre = (grad_hidden * gelu_slope(pre_act)).astype(low)
    grad_down = lax.psum_scatter(
        contract_rows(hidden, grad_out).astype(low), "dp", scatter_dimension=0, tiled=True
    )
    grad_up = lax.psum_scatter(
        contract_rows(grad_pre, mlp_in).astype(low), "dp", scatter_dimension=0, tiled=True
    )
    grad_mlp_in = jnp.dot(grad_pre, up_own, preferred_element_type=full)

    grad_context = contract_cols(grad_out, out_own).astype(low)
    grad_dense = contract_rows(context, grad_out).astype(low)
    grad_dense = lax.all_to_all(
        grad_dense.reshape(per_shard, sp_size, qkv_rows, D),
        "sp",
        split_axis=1,
        concat_axis=0,
        tiled=True,
    ).reshape(dp_size * qkv_rows, D)
    grad_dense = lax.psum_scatter(grad_dense, "dp", scatter_dimension=0, tiled=True)
    grad_queries, grad_keys, grad_values = attend_backward(
        queries, key_rows, values, grad_context, log_sums, length, score_scale
    )

    def turn_back(grad):
        return (
            rotate(
                grad.astype(low).astype(full).reshape(seq_rows, heads_own, HEAD),
                cosine,
                -sine_table,
            )
            .reshape(seq_rows, head_width)
            .astype(low)
        )

    grad_proj = jnp.concatenate(
        [turn_back(grad_queries), turn_back(grad_keys), grad_values.astype(low)], axis=1
    )
    grad_attn_in = contract_cols(grad_proj, qkv_own)
    grad_hat = grad_attn_in * gains[0] + grad_mlp_in * gains[1]
    reduced_hat = lax.psum_scatter(
        grad_hat.astype(low), "sp", scatter_dimension=0, tiled=True
    ).astype(full)
    grad_qkv = lax.psum_scatter(
        contract_rows(attn_in, grad_proj).astype(low), "dp", scatter_dimension=0, tiled=True
    )
    grad_qkv = lax.all_to_all(
        grad_qkv.reshape(sp_size, qkv_rows, 3, 1, head_width),
        "sp",
        split_axis=0,
        concat_axis=3,
        tiled=True,
    ).reshape(qkv_rows, 3 * D)

    own_cotangent = lax.dynamic_slice_in_dim(grad_out, shard * own_rows, own_rows, 0).astype(full)
    spread_units = lax.dynamic_update_index_in_dim(
        jnp.zeros((dp_size, sp_size, units), full),
        jnp.sum(grad_pre, axis=0, dtype=full).reshape(dp_size, units),
        shard,
        1,
    ).reshape(-1)
    spread_bias = lax.dynamic_update_index_in_dim(
        jnp.zeros((3, sp_size, head_width), full),
        jnp.sum(grad_proj, axis=0, dtype=full).reshape(3, head_width),
        shard,
        1,
    ).reshape(3, D)
    gain_grad = jnp.stack(
        [jnp.sum(grad_attn_in * normed, axis=0), jnp.sum(grad_mlp_in * normed, axis=0)]
    )
    shift_grad = jnp.stack([jnp.sum(grad_attn_in, axis=0), jnp.sum(grad_mlp_in, axis=0)])
    gain_total, shift_total, qkv_bias_total, unit_total, out_bias_total = lax.psum(
        (gain_grad, shift_grad, spread_bias, spread_units, jnp.sum(own_cotangent, axis=0)),
        ("dp", "sp"),
    )

    own_inverse = lax.dynamic_slice_in_dim(inverse, shard * own_rows, own_rows, 0)
    own_normed = lax.dynamic_slice_in_dim(normed, shard * own_rows, own_rows, 0)
    grad_input = own_inverse * (
        reduced_hat
        - jnp.mean(reduced_hat, axis=-1, keepdims=True)
        - own_normed * jnp.mean(reduced_hat * own_normed, axis=-1, keepdims=True)
    )
    input_grad = (own_cotangent + grad_input).astype(low)
    return (
        output,
        input_grad,
        gain_total,
        shift_total,
        grad_qkv.astype(full),
        qkv_bias_total,
        grad_dense.astype(full),
        grad_up.astype(full),
        unit_total,
        grad_down.astype(full),
        out_bias_total,
    )


def solution(mesh):
    return jax.shard_map(
        body,
        mesh=mesh,
        in_specs=(
            P(("dp", "sp"), None),
            P("dp"),
            P(("dp", "sp"), None),
            P(),
            P(),
            P(("dp", "sp"), None),
            P(),
            P(("dp", "sp"), None),
            P(("dp", "sp"), None),
            P(),
            P(("dp", "sp"), None),
            P(),
        ),
        out_specs=(
            P(("dp", "sp"), None),
            P(("dp", "sp"), None),
            P(),
            P(),
            P(("dp", "sp"), None),
            P(),
            P(("dp", "sp"), None),
            P(("dp", "sp"), None),
            P(),
            P(("dp", "sp"), None),
            P(),
        ),
        check_vma=False,
    )
```

```python
import functools

import jax
import jax.numpy as jnp
from jax import lax
from jax.experimental import pallas as pl
from jax.experimental.pallas import tpu as pltpu
from jax.sharding import PartitionSpec as P

D = 2048
HEADS = 8
HEAD = 256
ROT = 64


eps = 1e-05
base_freq = 10000.0
root_half = 0.7071067811865476
inv_root_two_pi = 0.3989422804014327


def contract_rows(left, right):
    return lax.dot_general(
        left, right, (((0,), (0,)), ((), ())), preferred_element_type=jnp.float32
    )


def contract_cols(left, right):
    return lax.dot_general(
        left, right, (((1,), (1,)), ((), ())), preferred_element_type=jnp.float32
    )


def gelu_value(pre_act):
    return 0.5 * pre_act * (1.0 + lax.erf(pre_act * root_half))


def gelu_slope(pre_act):
    return 0.5 * (1.0 + lax.erf(pre_act * root_half)) + pre_act * inv_root_two_pi * jnp.exp(
        -0.5 * pre_act * pre_act
    )


BAND=256
def turn(x, cos_t, sin_t):
    first = x[:, :128]
    lane = lax.broadcasted_iota(jnp.int32, first.shape, 1)
    partner = jnp.where(lane < ROT // 2, pltpu.roll(first, 128 - ROT // 2, 1), pltpu.roll(first, ROT // 2, 1))
    return jnp.concatenate([first * cos_t + partner * sin_t, x[:, 128:]], axis=1)

def weights_of(q, k, start, length, scale):
    rows, cols = q.shape[0], k.shape[0]
    s = lax.dot_general(q, k, (((1,), (1,)), ((), ())), preferred_element_type=jnp.float32) * scale
    key = lax.broadcasted_iota(jnp.int32, (rows, cols), 1)
    query = start + lax.broadcasted_iota(jnp.int32, (rows, cols), 0)
    s = jnp.where((key <= query) & (key < length), s, -1e30)
    e = jnp.exp(s - jnp.max(s, axis=-1, keepdims=True))
    return e / jnp.sum(e, axis=-1, keepdims=True)

def fwd_kernel(scale, len_ref, pq, pk, pv, bq, bk, bv, cos_ref, sin_ref, q_ref, k_ref, v_ref, ctx_ref):
    length = len_ref[0]
    seq = pq.shape[0]
    cos_t, sin_t = cos_ref[...], sin_ref[...]
    q_ref[...] = turn(pq[...] + bq[...], cos_t, sin_t).astype(jnp.bfloat16)
    k_ref[...] = turn(pk[...] + bk[...], cos_t, sin_t).astype(jnp.bfloat16)
    v_ref[...] = (pv[...] + bv[...]).astype(jnp.bfloat16)
    for start in range(0, seq, BAND):
        end = start + BAND
        p = weights_of(q_ref[start:end, :], k_ref[:end, :], start, length, scale)
        ctx_ref[start:end, :] = jnp.dot(p.astype(jnp.bfloat16), v_ref[:end, :], preferred_element_type=jnp.float32).astype(jnp.bfloat16)

def attend_fwd(projected, bias, cos_t, sin_t, lengths):
    seq, width = projected.shape
    heads = width // 3 // HEAD
    col = lambda g: pl.BlockSpec((seq, HEAD), lambda h, *_, g=g: (0, g * heads + h))
    bcol = lambda g: pl.BlockSpec((1, HEAD), lambda h, *_, g=g: (0, g * heads + h))
    tab = pl.BlockSpec((seq, 128), lambda h, *_: (0, 0))
    out = pl.BlockSpec((seq, HEAD), lambda h, *_: (0, h))
    return pl.pallas_call(
        functools.partial(fwd_kernel, HEAD ** -0.5),
        grid_spec=pltpu.PrefetchScalarGridSpec(num_scalar_prefetch=1, grid=(heads,),
            in_specs=[col(0), col(1), col(2), bcol(0), bcol(1), bcol(2), tab, tab], out_specs=[out] * 4),
        out_shape=[jax.ShapeDtypeStruct((seq, heads * HEAD), jnp.bfloat16)] * 4,
        name="attend_fwd",
        cost_estimate=pl.CostEstimate(flops=heads * seq * seq * HEAD * 4, bytes_accessed=seq * width * 8, transcendentals=heads * seq * seq),
    )(lengths, projected, projected, projected, bias, bias, bias, cos_t, sin_t)

def bwd_kernel(scale, heads, len_ref, q_ref, k_ref, v_ref, g_ref, cos_ref, sin_ref, gp_ref, sum_ref, dk, dv, dq):
    length = len_ref[0]
    h = pl.program_id(0)
    seq = q_ref.shape[0]
    dk[...] = jnp.zeros_like(dk)
    dv[...] = jnp.zeros_like(dv)
    for start in range(0, seq, BAND):
        end = start + BAND
        q, g = q_ref[start:end, :], g_ref[start:end, :]
        k, v = k_ref[:end, :], v_ref[:end, :]
        p = weights_of(q, k, start, length, scale)
        gp = lax.dot_general(g, v, (((1,), (1,)), ((), ())), preferred_element_type=jnp.float32)
        ds = (p * (gp - jnp.sum(p * gp, axis=-1, keepdims=True))).astype(jnp.bfloat16)
        dq[start:end, :] = jnp.dot(ds, k, preferred_element_type=jnp.float32) * scale
        dk[:end, :] += lax.dot_general(ds, q, (((0,), (0,)), ((), ())), preferred_element_type=jnp.float32)
        dv[:end, :] += lax.dot_general(p.astype(jnp.bfloat16), g, (((0,), (0,)), ((), ())), preferred_element_type=jnp.float32)
    cos_t, sin_t = cos_ref[...], sin_ref[...]
    def back(x):
        return turn(x.astype(jnp.bfloat16).astype(jnp.float32), cos_t, -sin_t).astype(jnp.bfloat16)
    for g, piece in enumerate((back(dq[...]), back(dk[...] * scale), dv[...].astype(jnp.bfloat16))):
        at = pl.ds(pl.multiple_of((g * heads + h) * HEAD, HEAD), HEAD)
        gp_ref[:, at] = piece
        sum_ref[:, at] = jnp.sum(piece.astype(jnp.float32), axis=0, keepdims=True)

def attend_bwd(q, k, v, gctx, cos_t, sin_t, lengths):
    seq, width = q.shape
    heads = width // HEAD
    col = pl.BlockSpec((seq, HEAD), lambda h, *_: (0, h))
    tab = pl.BlockSpec((seq, 128), lambda h, *_: (0, 0))
    return pl.pallas_call(
        functools.partial(bwd_kernel, HEAD ** -0.5, heads),
        grid_spec=pltpu.PrefetchScalarGridSpec(num_scalar_prefetch=1, grid=(heads,),
            in_specs=[col] * 4 + [tab, tab],
            out_specs=[pl.BlockSpec((seq, 3 * width), lambda h, *_: (0, 0)), pl.BlockSpec((1, 3 * width), lambda h, *_: (0, 0))],
            scratch_shapes=[pltpu.VMEM((seq, HEAD), jnp.float32)] * 3),
        out_shape=[jax.ShapeDtypeStruct((seq, 3 * width), jnp.bfloat16), jax.ShapeDtypeStruct((1, 3 * width), jnp.float32)],
        name="attend_bwd",
        cost_estimate=pl.CostEstimate(flops=heads * seq * seq * HEAD * 10, bytes_accessed=seq * width * 20, transcendentals=heads * seq * seq),
    )(lengths, q, k, v, gctx, cos_t, sin_t)

def rotary_rows(seq):
    half = ROT // 2
    freq = 10000.0 ** (-jnp.arange(half, dtype=jnp.float32) * (2.0 / ROT))
    ang = jnp.arange(seq, dtype=jnp.int32).astype(jnp.float32)[:, None] * freq[None, :]
    c, s = jnp.cos(ang), jnp.sin(ang)
    rest = 128 - ROT
    return (jnp.concatenate([c, c, jnp.ones((seq, rest), jnp.float32)], 1), jnp.concatenate([-s, s, jnp.zeros((seq, rest), jnp.float32)], 1))

MESH = pl.DeviceIdType.MESH

def square_partners(dp):
    core, x, y = dp % 2, (dp // 2) % 2, dp // 4
    across_x, across_y = dp + 2 - 4 * x, dp + 4 - 8 * y
    first = across_x * (1 - core) + across_y * core
    second = across_y * (1 - core) + across_x * core
    return first, second, across_x + across_y - dp, 1 - 2 * core

def gather_kernel(sp_size, qkv_ref, out_ref, up_ref, down_ref, qkv_all, out_all, up_all, down_all,
                  send_sem, recv_sem, slab_send, slab_recv, local_sem, turn_send, turn_recv):
    dp, sp = lax.axis_index("dp"), lax.axis_index("sp")
    first, second, diagonal, flip = square_partners(dp)
    sibling = dp + flip
    per = 2
    pair, lane = dp // per, dp % per
    rows = qkv_ref.shape[0]
    wide = up_ref.shape[1]
    head_width = wide // sp_size
    turn_dp = sp * per + lane

    barrier = pltpu.get_barrier_semaphore()
    for other in (first, second, sibling):
        pl.semaphore_signal(barrier, inc=1, device_id=(other, sp), device_id_type=MESH)
    for step in range(1, sp_size):
        pl.semaphore_signal(barrier, inc=1, device_id=(dp, lax.rem(sp + step, sp_size)), device_id_type=MESH)
    @pl.when(pair != sp)
    def _():
        pl.semaphore_signal(barrier, inc=1, device_id=(turn_dp, pair), device_id_type=MESH)

    pl.semaphore_wait(barrier, 2 + sp_size + jnp.where(pair != sp, 1, 0))

    def slab_at(owner_sp):
        return pl.ds(pl.multiple_of((dp * sp_size + owner_sp) * rows, rows), rows)

    def slab_copy(step, part):
        there = lax.rem(sp + step, sp_size)
        return pltpu.make_async_remote_copy(
            src_ref=qkv_ref.at[:, pl.ds(pl.multiple_of(part * wide + there * head_width, head_width), head_width)],
            dst_ref=qkv_all.at[slab_at(sp), pl.ds(part * head_width, head_width)],
            send_sem=slab_send.at[step - 1, part], recv_sem=slab_recv.at[step - 1, part],
            device_id=(dp, there), device_id_type=MESH)

    def slab_arrival(step, part):
        origin = lax.rem(sp + sp_size - step, sp_size)
        return pltpu.make_async_remote_copy(
            src_ref=qkv_ref.at[:, pl.ds(part * head_width, head_width)],
            dst_ref=qkv_all.at[slab_at(origin), pl.ds(part * head_width, head_width)],
            send_sem=slab_send.at[step - 1, part], recv_sem=slab_recv.at[step - 1, part],
            device_id=(dp, origin), device_id_type=MESH)

    units = up_ref.shape[0]
    slab = rows * sp_size

    def plain(height):
        return lambda owner: pl.ds(pl.multiple_of(owner * height, height), height)

    def turned(owner):
        return pl.ds(pl.multiple_of((owner % per) * slab + (owner // per) * rows, rows), rows)

    arrays = ((up_ref, up_all, plain(units)), (down_ref, down_all, plain(units)), (None, qkv_all, plain(slab)), (None, out_all, turned))

    def copy(index, message, block, target):
        source, result, place = arrays[index]
        at = result.at[place(block)]
        src = at
        if source is not None and message < 3:
            src = source
        return pltpu.make_async_remote_copy(
            src_ref=src, dst_ref=at, send_sem=send_sem.at[index, message], recv_sem=recv_sem.at[index, message],
            device_id=(target, sp), device_id_type=MESH)

    sends = ((dp, first), (dp, second), (dp, sibling), (first, second), (first, sibling), (second, sibling), (diagonal, sibling))
    arrivals = (first, second, sibling, diagonal, second + flip, first + flip, diagonal + flip)

    def start(index, message):
        copy(index, message, *sends[message]).start()

    def arrived(index, message):
        copy(index, message, arrivals[message], dp).wait_recv()

    def own(index):
        for message in (0, 1, 2):
            start(index, message)

    def keep(source, target, which):
        return pltpu.make_async_copy(source, target, local_sem.at[which])

    own(0)
    for step in range(1, sp_size):
        for part in range(3):
            slab_copy(step, part).start()

    out_place = out_all.at[turned(turn_dp)]
    my_out_place = out_all.at[turned(dp)]
    turn = pltpu.make_async_remote_copy(
        src_ref=out_ref, dst_ref=out_place, send_sem=turn_send, recv_sem=turn_recv,
        device_id=(turn_dp, pair), device_id_type=MESH)
    turn_arrival = pltpu.make_async_remote_copy(
        src_ref=out_ref, dst_ref=my_out_place, send_sem=turn_send, recv_sem=turn_recv,
        device_id=(turn_dp, pair), device_id_type=MESH)

    @pl.when(pair != sp)
    def _():
        turn.start()

    own(1)
    local = [keep(up_ref, up_all.at[plain(units)(dp)], 0), keep(down_ref, down_all.at[plain(units)(dp)], 1)]
    for part in range(3):
        local.append(keep(
            qkv_ref.at[:, pl.ds(pl.multiple_of(part * wide + sp * head_width, head_width), head_width)],
            qkv_all.at[slab_at(sp), pl.ds(part * head_width, head_width)], 2 + part))
    for c in local:
        c.start()

    def onward(index):
        arrived(index, 0)
        start(index, 3)
        start(index, 4)
        arrived(index, 1)
        start(index, 5)

    onward(0)
    for step in range(1, sp_size):
        for part in range(3):
            slab_arrival(step, part).wait_recv()
    for c in local:
        c.wait()
    own(2)

    @pl.when(pair == sp)
    def _():
        c = keep(out_ref, my_out_place, 5)
        c.start()
        c.wait()

    @pl.when(pair != sp)
    def _():
        turn_arrival.wait_recv()

    own(3)
    onward(1)
    onward(2)
    onward(3)
    for index in range(4):
        arrived(index, 3)
        start(index, 6)
    for index in range(4):
        for message in (2, 4, 5, 6):
            arrived(index, message)
    for index in range(4):
        for message in range(7):
            copy(index, message, *sends[message]).wait_send()
    for step in range(1, sp_size):
        for part in range(3):
            slab_copy(step, part).wait_send()

    @pl.when(pair != sp)
    def _():
        turn.wait_send()

def gather_weights(dp_size, sp_size, qkv_weight, out_weight, up_weight, down_weight):
    rows, wide = out_weight.shape
    units = up_weight.shape[0]
    low = jnp.bfloat16
    hbm = pl.BlockSpec(memory_space=pltpu.HBM)
    vmem = pl.BlockSpec(memory_space=pltpu.VMEM)
    dma = pltpu.SemaphoreType.DMA
    return pl.pallas_call(
        functools.partial(gather_kernel, sp_size),
        out_shape=[jax.ShapeDtypeStruct((rows * sp_size * dp_size, 3 * wide // sp_size), low),
                   jax.ShapeDtypeStruct((rows * dp_size, wide), low),
                   jax.ShapeDtypeStruct((units * dp_size, wide), low),
                   jax.ShapeDtypeStruct((units * dp_size, wide), low)],
        in_specs=[vmem] * 4, out_specs=[hbm] * 4,
        scratch_shapes=[dma((4, 7)), dma((4, 7)), dma((sp_size - 1, 3)), dma((sp_size - 1, 3)), dma((6,)), dma, dma],
        compiler_params=pltpu.CompilerParams(collective_id=0, has_side_effects=True),
        cost_estimate=pl.CostEstimate(flops=0, bytes_accessed=300 * 1000 * 1000, transcendentals=0),
        name="gather_weights",
    )(qkv_weight, out_weight, up_weight, down_weight)

def gather_plain(dp_size, sp_size, qkv_weight, out_weight, up_weight, down_weight):
    head_width = D // sp_size
    qkv_rows = qkv_weight.shape[0]
    qkv_slab = lax.all_to_all(
        qkv_weight.reshape(qkv_rows, 3, sp_size, head_width),
        "sp",
        split_axis=2,
        concat_axis=0,
        tiled=True,
    )
    qkv_own = lax.all_gather(
        qkv_slab.reshape(qkv_rows * sp_size, 3 * head_width), "dp", axis=0, tiled=True
    )
    up_own = lax.all_gather(up_weight, "dp", axis=0, tiled=True)
    down_own = lax.all_gather(down_weight, "dp", axis=0, tiled=True)
    out_blocks = lax.all_gather(out_weight, "dp", axis=0, tiled=True)
    out_own = lax.all_to_all(
        out_blocks.reshape(sp_size, dp_size // sp_size, qkv_rows, D),
        "sp",
        split_axis=0,
        concat_axis=2,
        tiled=True,
    ).reshape(head_width, D)
    return qkv_own, out_own, up_own, down_own


def body(
    tokens,
    lengths,
    cotangent,
    ln_gains,
    ln_shifts,
    qkv_weight,
    qkv_bias,
    out_weight,
    up_weight,
    up_bias,
    down_weight,
    out_bias,
):
    dp_size = lax.axis_size("dp")
    sp_size = lax.axis_size("sp")
    shard = lax.axis_index("sp")
    own_rows = tokens.shape[0]
    seq_rows = own_rows * sp_size
    head_width = D // sp_size
    length = lengths[0]
    low = jnp.bfloat16
    full = jnp.float32

    seq_tokens = lax.all_gather(tokens, "sp", axis=0, tiled=True)
    seq_cotangent = lax.all_gather(cotangent, "sp", axis=0, tiled=True)
    qkv_rows = qkv_weight.shape[0]
    per_shard = dp_size // sp_size
    square = dp_size == 8 and sp_size == 4
    gather = gather_weights if square else gather_plain
    qkv_own, out_own, up_own, down_own = gather(
        dp_size, sp_size, qkv_weight, out_weight, up_weight, down_weight
    )
    units = up_weight.shape[0]
    unit_bias = lax.dynamic_index_in_dim(
        up_bias.reshape(dp_size, sp_size, units), shard, 1, keepdims=False
    ).reshape(dp_size * units)
    bias_own = lax.dynamic_index_in_dim(
        qkv_bias.reshape(3, sp_size, head_width), shard, 1, keepdims=False
    ).reshape(3 * head_width)

    positions = jnp.arange(seq_rows, dtype=jnp.int32)
    cos_rows, sin_rows = rotary_rows(seq_rows)
    gains = ln_gains.astype(full)
    shifts = ln_shifts.astype(full)
    inputs = seq_tokens.astype(full)
    centre = jnp.mean(inputs, axis=-1, keepdims=True)
    centered = inputs - centre
    inverse = lax.rsqrt(jnp.mean(centered * centered, axis=-1, keepdims=True) + eps)
    normed = centered * inverse
    attn_in = (normed * gains[0] + shifts[0]).astype(low)
    mlp_in = (normed * gains[1] + shifts[1]).astype(low)
    row_valid = positions < length
    grad_out = jnp.where(row_valid[:, None], seq_cotangent, jnp.zeros_like(seq_cotangent))

    projected = jnp.dot(attn_in, qkv_own, preferred_element_type=full)
    queries, key_rows, values, context = attend_fwd(
        projected, bias_own.astype(full)[None], cos_rows, sin_rows, lengths
    )

    pre_act = contract_cols(mlp_in, up_own) + unit_bias.astype(full)
    hidden = gelu_value(pre_act).astype(low)
    partial_out = jnp.dot(hidden, down_own, preferred_element_type=full) + jnp.dot(
        context, out_own, preferred_element_type=full
    )
    reduced_out = lax.psum_scatter(
        partial_out.astype(low), "sp", scatter_dimension=0, tiled=True
    )
    output = (
        tokens.astype(full) + reduced_out.astype(full) + out_bias.astype(full)
    ).astype(low)

    grad_hidden = contract_cols(grad_out, down_own)
    grad_pre = (grad_hidden * gelu_slope(pre_act)).astype(low)
    grad_down = lax.psum_scatter(
        contract_rows(hidden, grad_out).astype(low), "dp", scatter_dimension=0, tiled=True
    )
    grad_up = lax.psum_scatter(
        contract_rows(grad_pre, mlp_in).astype(low), "dp", scatter_dimension=0, tiled=True
    )
    grad_mlp_in = jnp.dot(grad_pre, up_own, preferred_element_type=full)

    grad_context = contract_cols(grad_out, out_own).astype(low)
    grad_dense = contract_rows(context, grad_out).astype(low)
    grad_dense = lax.all_to_all(
        grad_dense.reshape(per_shard, sp_size, qkv_rows, D),
        "sp",
        split_axis=1,
        concat_axis=0,
        tiled=True,
    ).reshape(dp_size * qkv_rows, D)
    grad_dense = lax.psum_scatter(grad_dense, "dp", scatter_dimension=0, tiled=True)
    grad_proj, grad_proj_sum = attend_bwd(
        queries, key_rows, values, grad_context, cos_rows, sin_rows, lengths
    )
    grad_attn_in = contract_cols(grad_proj, qkv_own)
    grad_hat = grad_attn_in * gains[0] + grad_mlp_in * gains[1]
    reduced_hat = lax.psum_scatter(
        grad_hat.astype(low), "sp", scatter_dimension=0, tiled=True
    ).astype(full)
    grad_qkv = lax.psum_scatter(
        contract_rows(attn_in, grad_proj).astype(low), "dp", scatter_dimension=0, tiled=True
    )
    grad_qkv = lax.all_to_all(
        grad_qkv.reshape(sp_size, qkv_rows, 3, 1, head_width),
        "sp",
        split_axis=0,
        concat_axis=3,
        tiled=True,
    ).reshape(qkv_rows, 3 * D)

    own_cotangent = lax.dynamic_slice_in_dim(grad_out, shard * own_rows, own_rows, 0).astype(full)
    spread_units = lax.dynamic_update_index_in_dim(
        jnp.zeros((dp_size, sp_size, units), full),
        jnp.sum(grad_pre, axis=0, dtype=full).reshape(dp_size, units),
        shard,
        1,
    ).reshape(-1)
    spread_bias = lax.dynamic_update_index_in_dim(
        jnp.zeros((3, sp_size, head_width), full),
        grad_proj_sum.reshape(3, head_width),
        shard,
        1,
    ).reshape(3, D)
    gain_grad = jnp.stack(
        [jnp.sum(grad_attn_in * normed, axis=0), jnp.sum(grad_mlp_in * normed, axis=0)]
    )
    shift_grad = jnp.stack([jnp.sum(grad_attn_in, axis=0), jnp.sum(grad_mlp_in, axis=0)])
    gain_total, shift_total, qkv_bias_total, unit_total, out_bias_total = lax.psum(
        (gain_grad, shift_grad, spread_bias, spread_units, jnp.sum(own_cotangent, axis=0)),
        ("dp", "sp"),
    )

    own_inverse = lax.dynamic_slice_in_dim(inverse, shard * own_rows, own_rows, 0)
    own_normed = lax.dynamic_slice_in_dim(normed, shard * own_rows, own_rows, 0)
    grad_input = own_inverse * (
        reduced_hat
        - jnp.mean(reduced_hat, axis=-1, keepdims=True)
        - own_normed * jnp.mean(reduced_hat * own_normed, axis=-1, keepdims=True)
    )
    input_grad = (own_cotangent + grad_input).astype(low)
    return (
        output,
        input_grad,
        gain_total,
        shift_total,
        grad_qkv.astype(full),
        qkv_bias_total,
        grad_dense.astype(full),
        grad_up.astype(full),
        unit_total,
        grad_down.astype(full),
        out_bias_total,
    )


def solution(mesh):
    return jax.shard_map(
        body,
        mesh=mesh,
        in_specs=(
            P(("dp", "sp"), None),
            P("dp"),
            P(("dp", "sp"), None),
            P(),
            P(),
            P(("dp", "sp"), None),
            P(),
            P(("dp", "sp"), None),
            P(("dp", "sp"), None),
            P(),
            P(("dp", "sp"), None),
            P(),
        ),
        out_specs=(
            P(("dp", "sp"), None),
            P(("dp", "sp"), None),
            P(),
            P(),
            P(("dp", "sp"), None),
            P(),
            P(("dp", "sp"), None),
            P(("dp", "sp"), None),
            P(),
            P(("dp", "sp"), None),
            P(),
        ),
        check_vma=False,
    )
```

```python
import functools

import jax
import jax.numpy as jnp
from jax import lax
from jax.experimental import pallas as pl
from jax.experimental.pallas import tpu as pltpu
from jax.sharding import PartitionSpec as P

D = 2048
HEADS = 8
HEAD = 256
ROT = 64


eps = 1e-05
base_freq = 10000.0
root_half = 0.7071067811865476
inv_root_two_pi = 0.3989422804014327


def contract_rows(left, right):
    return lax.dot_general(
        left, right, (((0,), (0,)), ((), ())), preferred_element_type=jnp.float32
    )


def contract_cols(left, right):
    return lax.dot_general(
        left, right, (((1,), (1,)), ((), ())), preferred_element_type=jnp.float32
    )


def gelu_value(pre_act):
    return 0.5 * pre_act * (1.0 + lax.erf(pre_act * root_half))


def gelu_slope(pre_act):
    return 0.5 * (1.0 + lax.erf(pre_act * root_half)) + pre_act * inv_root_two_pi * jnp.exp(
        -0.5 * pre_act * pre_act
    )


BAND=256
def turn(x, cos_t, sin_t):
    first = x[:, :128]
    lane = lax.broadcasted_iota(jnp.int32, first.shape, 1)
    partner = jnp.where(lane < ROT // 2, pltpu.roll(first, 128 - ROT // 2, 1), pltpu.roll(first, ROT // 2, 1))
    return jnp.concatenate([first * cos_t + partner * sin_t, x[:, 128:]], axis=1)

def weights_of(q, k, start, length, scale):
    rows, cols = q.shape[0], k.shape[0]
    s = lax.dot_general(q, k, (((1,), (1,)), ((), ())), preferred_element_type=jnp.float32) * scale
    key = lax.broadcasted_iota(jnp.int32, (rows, cols), 1)
    query = start + lax.broadcasted_iota(jnp.int32, (rows, cols), 0)
    s = jnp.where((key <= query) & (key < length), s, -1e30)
    e = jnp.exp(s - jnp.max(s, axis=-1, keepdims=True))
    return e / jnp.sum(e, axis=-1, keepdims=True)

def fwd_kernel(scale, len_ref, pq, pk, pv, bq, bk, bv, cos_ref, sin_ref, q_ref, k_ref, v_ref, ctx_ref):
    length = len_ref[0]
    seq = pq.shape[0]
    cos_t, sin_t = cos_ref[...], sin_ref[...]
    q_ref[...] = turn(pq[...] + bq[...], cos_t, sin_t).astype(jnp.bfloat16)
    k_ref[...] = turn(pk[...] + bk[...], cos_t, sin_t).astype(jnp.bfloat16)
    v_ref[...] = (pv[...] + bv[...]).astype(jnp.bfloat16)
    for start in range(0, seq, BAND):
        end = start + BAND
        p = weights_of(q_ref[start:end, :], k_ref[:end, :], start, length, scale)
        ctx_ref[start:end, :] = jnp.dot(p.astype(jnp.bfloat16), v_ref[:end, :], preferred_element_type=jnp.float32).astype(jnp.bfloat16)

def attend_fwd(projected, bias, cos_t, sin_t, lengths):
    seq, width = projected.shape
    heads = width // 3 // HEAD
    col = lambda g: pl.BlockSpec((seq, HEAD), lambda h, *_, g=g: (0, g * heads + h))
    bcol = lambda g: pl.BlockSpec((1, HEAD), lambda h, *_, g=g: (0, g * heads + h))
    tab = pl.BlockSpec((seq, 128), lambda h, *_: (0, 0))
    out = pl.BlockSpec((seq, HEAD), lambda h, *_: (0, h))
    return pl.pallas_call(
        functools.partial(fwd_kernel, HEAD ** -0.5),
        grid_spec=pltpu.PrefetchScalarGridSpec(num_scalar_prefetch=1, grid=(heads,),
            in_specs=[col(0), col(1), col(2), bcol(0), bcol(1), bcol(2), tab, tab], out_specs=[out] * 4),
        out_shape=[jax.ShapeDtypeStruct((seq, heads * HEAD), jnp.bfloat16)] * 4,
        name="attend_fwd",
        cost_estimate=pl.CostEstimate(flops=heads * seq * seq * HEAD * 4, bytes_accessed=seq * width * 8, transcendentals=heads * seq * seq),
    )(lengths, projected, projected, projected, bias, bias, bias, cos_t, sin_t)

def bwd_kernel(scale, heads, len_ref, q_ref, k_ref, v_ref, g_ref, cos_ref, sin_ref, gp_ref, sum_ref, dk, dv, dq):
    length = len_ref[0]
    h = pl.program_id(0)
    seq = q_ref.shape[0]
    dk[...] = jnp.zeros_like(dk)
    dv[...] = jnp.zeros_like(dv)
    for start in range(0, seq, BAND):
        end = start + BAND
        q, g = q_ref[start:end, :], g_ref[start:end, :]
        k, v = k_ref[:end, :], v_ref[:end, :]
        p = weights_of(q, k, start, length, scale)
        gp = lax.dot_general(g, v, (((1,), (1,)), ((), ())), preferred_element_type=jnp.float32)
        ds = (p * (gp - jnp.sum(p * gp, axis=-1, keepdims=True))).astype(jnp.bfloat16)
        dq[start:end, :] = jnp.dot(ds, k, preferred_element_type=jnp.float32) * scale
        dk[:end, :] += lax.dot_general(ds, q, (((0,), (0,)), ((), ())), preferred_element_type=jnp.float32)
        dv[:end, :] += lax.dot_general(p.astype(jnp.bfloat16), g, (((0,), (0,)), ((), ())), preferred_element_type=jnp.float32)
    cos_t, sin_t = cos_ref[...], sin_ref[...]
    def back(x):
        return turn(x.astype(jnp.bfloat16).astype(jnp.float32), cos_t, -sin_t).astype(jnp.bfloat16)
    for g, piece in enumerate((back(dq[...]), back(dk[...] * scale), dv[...].astype(jnp.bfloat16))):
        at = pl.ds(pl.multiple_of((g * heads + h) * HEAD, HEAD), HEAD)
        gp_ref[:, at] = piece
        sum_ref[:, at] = jnp.sum(piece.astype(jnp.float32), axis=0, keepdims=True)

def attend_bwd(q, k, v, gctx, cos_t, sin_t, lengths):
    seq, width = q.shape
    heads = width // HEAD
    col = pl.BlockSpec((seq, HEAD), lambda h, *_: (0, h))
    tab = pl.BlockSpec((seq, 128), lambda h, *_: (0, 0))
    return pl.pallas_call(
        functools.partial(bwd_kernel, HEAD ** -0.5, heads),
        grid_spec=pltpu.PrefetchScalarGridSpec(num_scalar_prefetch=1, grid=(heads,),
            in_specs=[col] * 4 + [tab, tab],
            out_specs=[pl.BlockSpec((seq, 3 * width), lambda h, *_: (0, 0)), pl.BlockSpec((1, 3 * width), lambda h, *_: (0, 0))],
            scratch_shapes=[pltpu.VMEM((seq, HEAD), jnp.float32)] * 3),
        out_shape=[jax.ShapeDtypeStruct((seq, 3 * width), jnp.bfloat16), jax.ShapeDtypeStruct((1, 3 * width), jnp.float32)],
        name="attend_bwd",
        cost_estimate=pl.CostEstimate(flops=heads * seq * seq * HEAD * 10, bytes_accessed=seq * width * 20, transcendentals=heads * seq * seq),
    )(lengths, q, k, v, gctx, cos_t, sin_t)

def rotary_rows(seq):
    half = ROT // 2
    freq = 10000.0 ** (-jnp.arange(half, dtype=jnp.float32) * (2.0 / ROT))
    ang = jnp.arange(seq, dtype=jnp.int32).astype(jnp.float32)[:, None] * freq[None, :]
    c, s = jnp.cos(ang), jnp.sin(ang)
    rest = 128 - ROT
    return (jnp.concatenate([c, c, jnp.ones((seq, rest), jnp.float32)], 1), jnp.concatenate([-s, s, jnp.zeros((seq, rest), jnp.float32)], 1))

MESH = pl.DeviceIdType.MESH

def square_partners(dp):
    core, x, y = dp % 2, (dp // 2) % 2, dp // 4
    across_x, across_y = dp + 2 - 4 * x, dp + 4 - 8 * y
    first = across_x * (1 - core) + across_y * core
    second = across_y * (1 - core) + across_x * core
    return first, second, across_x + across_y - dp, 1 - 2 * core

def gather_kernel(sp_size, qkv_ref, out_ref, up_ref, down_ref, qkv_all, out_all, up_all, down_all,
                  send_sem, recv_sem, slab_send, slab_recv, local_sem, turn_send, turn_recv):
    dp, sp = lax.axis_index("dp"), lax.axis_index("sp")
    first, second, diagonal, flip = square_partners(dp)
    sibling = dp + flip
    per = 2
    pair, lane = dp // per, dp % per
    rows = qkv_ref.shape[0]
    wide = up_ref.shape[1]
    head_width = wide // sp_size
    turn_dp = sp * per + lane

    barrier = pltpu.get_barrier_semaphore()
    for other in (first, second, sibling):
        pl.semaphore_signal(barrier, inc=1, device_id=(other, sp), device_id_type=MESH)
    for step in range(1, sp_size):
        pl.semaphore_signal(barrier, inc=1, device_id=(dp, lax.rem(sp + step, sp_size)), device_id_type=MESH)
    @pl.when(pair != sp)
    def _():
        pl.semaphore_signal(barrier, inc=1, device_id=(turn_dp, pair), device_id_type=MESH)

    pl.semaphore_wait(barrier, 2 + sp_size + jnp.where(pair != sp, 1, 0))

    def slab_at(owner_sp):
        return pl.ds(pl.multiple_of((dp * sp_size + owner_sp) * rows, rows), rows)

    def slab_copy(step, part):
        there = lax.rem(sp + step, sp_size)
        return pltpu.make_async_remote_copy(
            src_ref=qkv_ref.at[:, pl.ds(pl.multiple_of(part * wide + there * head_width, head_width), head_width)],
            dst_ref=qkv_all.at[slab_at(sp), pl.ds(part * head_width, head_width)],
            send_sem=slab_send.at[step - 1, part], recv_sem=slab_recv.at[step - 1, part],
            device_id=(dp, there), device_id_type=MESH)

    def slab_arrival(step, part):
        origin = lax.rem(sp + sp_size - step, sp_size)
        return pltpu.make_async_remote_copy(
            src_ref=qkv_ref.at[:, pl.ds(part * head_width, head_width)],
            dst_ref=qkv_all.at[slab_at(origin), pl.ds(part * head_width, head_width)],
            send_sem=slab_send.at[step - 1, part], recv_sem=slab_recv.at[step - 1, part],
            device_id=(dp, origin), device_id_type=MESH)

    units = up_ref.shape[0]
    slab = rows * sp_size

    def plain(height):
        return lambda owner: pl.ds(pl.multiple_of(owner * height, height), height)

    def turned(owner):
        return pl.ds(pl.multiple_of((owner % per) * slab + (owner // per) * rows, rows), rows)

    arrays = ((up_ref, up_all, plain(units)), (down_ref, down_all, plain(units)), (None, qkv_all, plain(slab)), (None, out_all, turned))

    def copy(index, message, block, target):
        source, result, place = arrays[index]
        at = result.at[place(block)]
        src = at
        if source is not None and message < 3:
            src = source
        return pltpu.make_async_remote_copy(
            src_ref=src, dst_ref=at, send_sem=send_sem.at[index, message], recv_sem=recv_sem.at[index, message],
            device_id=(target, sp), device_id_type=MESH)

    sends = ((dp, first), (dp, second), (dp, sibling), (first, second), (first, sibling), (second, sibling), (diagonal, sibling))
    arrivals = (first, second, sibling, diagonal, second + flip, first + flip, diagonal + flip)

    def start(index, message):
        copy(index, message, *sends[message]).start()

    def arrived(index, message):
        copy(index, message, arrivals[message], dp).wait_recv()

    def own(index):
        for message in (0, 1, 2):
            start(index, message)

    def keep(source, target, which):
        return pltpu.make_async_copy(source, target, local_sem.at[which])

    own(0)
    for step in range(1, sp_size):
        for part in range(3):
            slab_copy(step, part).start()

    out_place = out_all.at[turned(turn_dp)]
    my_out_place = out_all.at[turned(dp)]
    turn = pltpu.make_async_remote_copy(
        src_ref=out_ref, dst_ref=out_place, send_sem=turn_send, recv_sem=turn_recv,
        device_id=(turn_dp, pair), device_id_type=MESH)
    turn_arrival = pltpu.make_async_remote_copy(
        src_ref=out_ref, dst_ref=my_out_place, send_sem=turn_send, recv_sem=turn_recv,
        device_id=(turn_dp, pair), device_id_type=MESH)

    @pl.when(pair != sp)
    def _():
        turn.start()

    own(1)
    local = [keep(up_ref, up_all.at[plain(units)(dp)], 0), keep(down_ref, down_all.at[plain(units)(dp)], 1)]
    for part in range(3):
        local.append(keep(
            qkv_ref.at[:, pl.ds(pl.multiple_of(part * wide + sp * head_width, head_width), head_width)],
            qkv_all.at[slab_at(sp), pl.ds(part * head_width, head_width)], 2 + part))
    for c in local:
        c.start()

    def onward(index):
        arrived(index, 0)
        start(index, 3)
        start(index, 4)
        arrived(index, 1)
        start(index, 5)

    onward(0)
    for step in range(1, sp_size):
        for part in range(3):
            slab_arrival(step, part).wait_recv()
    for c in local:
        c.wait()
    own(2)

    @pl.when(pair == sp)
    def _():
        c = keep(out_ref, my_out_place, 5)
        c.start()
        c.wait()

    @pl.when(pair != sp)
    def _():
        turn_arrival.wait_recv()

    own(3)
    onward(1)
    onward(2)
    onward(3)
    for index in range(4):
        arrived(index, 3)
        start(index, 6)
    for index in range(4):
        for message in (2, 4, 5, 6):
            arrived(index, message)
    for index in range(4):
        for message in range(7):
            copy(index, message, *sends[message]).wait_send()
    for step in range(1, sp_size):
        for part in range(3):
            slab_copy(step, part).wait_send()

    @pl.when(pair != sp)
    def _():
        turn.wait_send()

def gather_weights(dp_size, sp_size, qkv_weight, out_weight, up_weight, down_weight):
    rows, wide = out_weight.shape
    units = up_weight.shape[0]
    low = jnp.bfloat16
    hbm = pl.BlockSpec(memory_space=pltpu.HBM)
    vmem = pl.BlockSpec(memory_space=pltpu.VMEM)
    dma = pltpu.SemaphoreType.DMA
    return pl.pallas_call(
        functools.partial(gather_kernel, sp_size),
        out_shape=[jax.ShapeDtypeStruct((rows * sp_size * dp_size, 3 * wide // sp_size), low),
                   jax.ShapeDtypeStruct((rows * dp_size, wide), low),
                   jax.ShapeDtypeStruct((units * dp_size, wide), low),
                   jax.ShapeDtypeStruct((units * dp_size, wide), low)],
        in_specs=[vmem] * 4, out_specs=[hbm] * 4,
        scratch_shapes=[dma((4, 7)), dma((4, 7)), dma((sp_size - 1, 3)), dma((sp_size - 1, 3)), dma((6,)), dma, dma],
        compiler_params=pltpu.CompilerParams(collective_id=0, has_side_effects=True),
        cost_estimate=pl.CostEstimate(flops=0, bytes_accessed=300 * 1000 * 1000, transcendentals=0),
        name="gather_weights",
    )(qkv_weight, out_weight, up_weight, down_weight)

CHUNK = 512


def back_kernel(sp_size, hidden_hbm, cot_hbm, pre_hbm, mlp_hbm, attn_hbm, proj_hbm, ctx_hbm, small_ref,
                down_out, up_out, qkv_out, dense_out, small_out,
                left_a, right_a, left_b, right_b, ctx, lent,
                down_sum, up_sum, qkv_sum, dense_sum, down_sib, up_sib, qkv_sib, dense_sib,
                down_one, up_one, qkv_one, dense_one, down_two, up_two, qkv_two, dense_two, dense_part,
                small_acc, small_in, small_z,
                load_sem, store_sem, sib_send, sib_recv, one_send, one_recv, two_send, two_recv,
                slab_send, slab_recv, turn_send, turn_recv, small_send, small_recv, z_send, z_recv):
    dp, sp = lax.axis_index("dp"), lax.axis_index("sp")
    full, low = jnp.float32, jnp.bfloat16
    core, chip = dp % 2, dp // 2
    x, y = chip % 2, chip // 2
    per = 2
    pair, lane = dp // per, dp % per
    turn_dp = sp * per + lane
    sibling = dp + 1 - 2 * core
    across_x, across_y = dp + 2 - 4 * x, dp + 4 - 8 * y
    first = across_y * (1 - core) + across_x * core
    second = across_x * (1 - core) + across_y * core
    first_mask, second_mask = 2 - core, 1 + core
    units = down_sum.shape[1]
    slab_width = qkv_sum.shape[2]
    head_width = slab_width // 3
    rows = dense_one.shape[1]
    wide = right_a.shape[1]

    def chip_of(mask):
        return lax.rem(x + lax.rem(mask, 2), 2) + 2 * lax.rem(y + mask // 2, 2)

    def load(source, target, which):
        return pltpu.make_async_copy(source, target, load_sem.at[which])

    loads = [load(hidden_hbm, left_a, 0), load(cot_hbm, right_a, 1), load(ctx_hbm, ctx, 2),
             load(pre_hbm, left_b, 3), load(mlp_hbm, right_b, 4)]
    for c in loads:
        c.start()

    barrier = pltpu.get_barrier_semaphore()
    for other in (first, second, sibling):
        pl.semaphore_signal(barrier, inc=1, device_id=(other, sp), device_id_type=MESH)
    for step in range(1, sp_size):
        pl.semaphore_signal(barrier, inc=1, device_id=(dp, lax.rem(sp + step, sp_size)), device_id_type=MESH)

    @pl.when(pair != sp)
    def _():
        pl.semaphore_signal(barrier, inc=1, device_id=(turn_dp, pair), device_id_type=MESH)

    pl.semaphore_wait(barrier, 2 + sp_size + jnp.where(pair != sp, 1, 0))

    def remote(source, target, send, recv, device):
        return pltpu.make_async_remote_copy(
            src_ref=source, dst_ref=target, send_sem=send, recv_sem=recv,
            device_id=device, device_id_type=MESH)

    def small_copy(stage):
        return remote(small_ref if stage == 0 else small_acc.at[stage - 1], small_in.at[stage],
                      small_send.at[stage], small_recv.at[stage], ((sibling, across_x, across_y)[stage], sp))

    def small_step(stage):
        small_copy(stage).wait_recv()
        before = small_ref[...] if stage == 0 else small_acc[stage - 1]
        small_acc[stage] = before + small_in[stage]

    def z_copy(step):
        return remote(small_acc.at[2], small_z.at[sp], z_send.at[step - 1], z_recv.at[step - 1],
                      (dp, lax.rem(sp + step, sp_size)))

    def z_arrival(step):
        origin = lax.rem(sp + sp_size - step, sp_size)
        return remote(small_acc.at[2], small_z.at[origin], z_send.at[step - 1], z_recv.at[step - 1], (dp, origin))

    small_copy(0).start()

    class Wide:
        def __init__(self, index, left, right, width, sums, sib, one, two):
            self.index, self.left, self.right, self.width = index, left, right, width
            self.sums, self.sib, self.one, self.two = sums, sib, one, two

        def product(self, block, store):
            at = pl.ds(pl.multiple_of(block * units, units), units)

            def columns(part, carry):
                to = pl.ds(pl.multiple_of(part * CHUNK, CHUNK), CHUNK)
                store(to, lax.dot_general(
                    self.left[:, at], self.right[:, to], (((0,), (0,)), ((), ())),
                    preferred_element_type=full))
                return carry
            lax.fori_loop(0, self.width // CHUNK, columns, 0)

        def lend(self, slot):
            return lent.at[slot, :, :self.width]

        def sib_copy(self, slot):
            place = chip_of(3 - slot)
            return remote(self.lend(slot), self.sib.at[place], sib_send.at[self.index, slot],
                          sib_recv.at[self.index, slot], (sibling, sp))

        def for_sibling(self, previous):
            def step(slot, carry):
                if previous is not None:
                    previous.sib_copy(slot).wait_send()
                block = chip_of(3 - slot) * 2 + 1 - core

                def store(to, total):
                    lent[slot, :, to] = total.astype(low)
                self.product(block, store)
                self.sib_copy(slot).start()
                return carry
            lax.fori_loop(0, 4, step, 0)

        def own(self, mask, slot):
            place = chip_of(mask)
            self.sib_copy(slot).wait_recv()

            def store(to, total):
                self.sums[mask, :, to] = (total + self.sib[place, :, to].astype(full)).astype(low)
            self.product(place * 2 + core, store)

        def first_copy(self, slot):
            mask = 3 - slot * (1 + core)
            return remote(self.sums.at[mask], self.one.at[slot], one_send.at[self.index, slot],
                          one_recv.at[self.index, slot], (first, sp))

        def for_self(self):
            def leave(slot, carry):
                mask = 3 - slot * (1 + core)
                self.own(mask, 3 - mask)
                self.first_copy(slot).start()
                return carry
            lax.fori_loop(0, 2, leave, 0)

            def stay(slot, carry):
                mask = second_mask * (1 - slot)
                self.own(mask, 3 - mask)
                return carry
            lax.fori_loop(0, 2, stay, 0)

        def second_copy(self):
            return remote(self.sums.at[second_mask], self.two, two_send.at[self.index],
                          two_recv.at[self.index], (second, sp))

        def block(self, mask):
            return self.sums.at[mask]

    class Dense(Wide):
        def sib_copy(self, slot):
            return remote(dense_part.at[0], self.sib, sib_send.at[self.index, 0],
                          sib_recv.at[self.index, 0], (sibling, sp))

        def for_sibling(self, previous):
            def store(to, total):
                dense_part[0, :, to] = total.astype(low)
            self.product(1 - core, store)
            self.sib_copy(0).start()

        def block(self, mask):
            return self.sums.at[pl.ds(pl.multiple_of(chip_of(mask) * rows, rows), rows)]

        def first_copy(self, slot):
            mask = 3 - slot * (1 + core)
            return remote(self.block(mask), self.one.at[slot], one_send.at[self.index, slot],
                          one_recv.at[self.index, slot], (first, sp))

        def for_self(self):
            self.sib_copy(0).wait_recv()

            def store(to, total):
                self.sums[:, to] = (total + self.sib[:, to].astype(full)).astype(low)
            self.product(core, store)
            for slot in (0, 1):
                self.first_copy(slot).start()

        def second_copy(self):
            return remote(self.block(second_mask), self.two, two_send.at[self.index],
                          two_recv.at[self.index], (second, sp))

    down = Wide(0, left_a, right_a, wide, down_sum, down_sib, down_one, down_two)
    dense = Dense(1, ctx, right_a, wide, dense_sum, dense_sib, dense_one, dense_two)
    up = Wide(2, left_b, right_b, wide, up_sum, up_sib, up_one, up_two)
    qkv = Wide(3, left_a, right_a, slab_width, qkv_sum, qkv_sib, qkv_one, qkv_two)

    def add_into(target, *others):
        height = target.shape[0]
        step_rows = 32

        def step(i, carry):
            at = pl.ds(pl.multiple_of(i * step_rows, step_rows), step_rows)
            total = target[at, :].astype(full)
            for other in others:
                total = total + other[at, :].astype(full)
            target[at, :] = total.astype(low)
            return carry
        lax.fori_loop(0, height // step_rows, step, 0)

    def onward(array):
        array.first_copy(0).wait_recv()
        add_into(array.block(second_mask), array.one.at[0])
        array.second_copy().start()

    def finish(array):
        array.first_copy(1).wait_recv()
        array.second_copy().wait_recv()
        add_into(array.block(0), array.one.at[1], array.two)

    loads[0].wait()
    loads[1].wait()
    down.for_sibling(None)
    small_step(0)
    small_copy(1).start()
    down.for_self()
    loads[2].wait()
    dense.for_sibling(None)
    small_step(1)
    small_copy(2).start()
    dense.for_self()
    late = [load(attn_hbm, left_a, 0), load(proj_hbm, right_a.at[:, :slab_width], 1)]
    for c in late:
        c.start()
    loads[3].wait()
    loads[4].wait()
    up.for_sibling(down)
    onward(down)
    small_step(2)
    for step in range(1, sp_size):
        z_copy(step).start()
    small_z[sp] = small_acc[2]
    up.for_self()
    for c in late:
        c.wait()
    onward(dense)
    qkv.for_sibling(up)
    qkv.for_self()
    onward(up)
    finish(down)
    stores = [pltpu.make_async_copy(down.block(0), down_out, store_sem.at[0])]
    stores[0].start()
    finish(dense)

    def turn(target):
        return remote(dense.block(0), target, turn_send, turn_recv, (turn_dp, pair))

    @pl.when(pair != sp)
    def _():
        turn(dense_out).start()

    @pl.when(pair == sp)
    def _():
        c = pltpu.make_async_copy(dense.block(0), dense_out, store_sem.at[1])
        c.start()
        c.wait()

    onward(qkv)
    finish(up)
    stores.append(pltpu.make_async_copy(up.block(0), up_out, store_sem.at[2]))
    stores[1].start()
    for step in range(1, sp_size):
        z_arrival(step).wait_recv()
    total = small_z[0]
    for place in range(1, sp_size):
        total = total + small_z[place]
    small_out[...] = total
    finish(qkv)

    def slab_rows(owner):
        return pl.ds(pl.multiple_of(owner * rows, rows), rows)

    def slab_copy(step, part, origin, there):
        at = pl.ds(pl.multiple_of(part * wide + origin * head_width, head_width), head_width)
        return remote(qkv_sum.at[0, slab_rows(there), pl.ds(part * head_width, head_width)], qkv_out.at[:, at],
                      slab_send.at[step - 1, part], slab_recv.at[step - 1, part], (dp, there))

    for step in range(1, sp_size):
        for part in range(3):
            slab_copy(step, part, sp, lax.rem(sp + step, sp_size)).start()
    for part in range(3):
        at = pl.ds(pl.multiple_of(part * wide + sp * head_width, head_width), head_width)
        c = pltpu.make_async_copy(qkv_sum.at[0, slab_rows(sp), pl.ds(part * head_width, head_width)],
                                  qkv_out.at[:, at], store_sem.at[3 + part])
        c.start()
        stores.append(c)
    for step in range(1, sp_size):
        for part in range(3):
            slab_copy(step, part, lax.rem(sp + sp_size - step, sp_size), sp).wait_recv()

    @pl.when(pair != sp)
    def _():
        turn(dense_out).wait_recv()
        turn(dense_out).wait_send()

    for c in stores:
        c.wait()
    for slot in range(4):
        qkv.sib_copy(slot).wait_send()
    dense.sib_copy(0).wait_send()
    for array in (down, dense, up, qkv):
        for slot in (0, 1):
            array.first_copy(slot).wait_send()
        array.second_copy().wait_send()
    for stage in range(3):
        small_copy(stage).wait_send()
    for step in range(1, sp_size):
        z_copy(step).wait_send()
        for part in range(3):
            slab_copy(step, part, sp, lax.rem(sp + step, sp_size)).wait_send()

def reduce_gradients(sp_size, rows, hidden, grad_out, grad_pre, mlp_in, attn_in, grad_proj, context, small):
    seq, wide = mlp_in.shape
    slab_width = grad_proj.shape[1]
    units = 4 * rows
    full, low = jnp.float32, jnp.bfloat16
    hbm = pl.BlockSpec(memory_space=pltpu.HBM)
    vmem = pl.BlockSpec(memory_space=pltpu.VMEM)
    dma = pltpu.SemaphoreType.DMA
    def v(*shape, kind=low):
        return pltpu.VMEM(shape, kind)
    scratch = [
        v(seq, wide), v(seq, wide), v(seq, wide), v(seq, wide), v(seq, context.shape[1]), v(4, units, wide),
        v(4, units, wide), v(4, units, wide), v(4, units, slab_width), v(4 * rows, wide),
        v(4, units, wide), v(4, units, wide), v(4, units, slab_width), v(4 * rows, wide),
        v(2, units, wide), v(2, units, wide), v(2, units, slab_width), v(2, rows, wide),
        v(units, wide), v(units, wide), v(units, slab_width), v(rows, wide),
        v(1, 4 * rows, wide),
        v(3, *small.shape, kind=full), v(3, *small.shape, kind=full), v(sp_size, *small.shape, kind=full),
        dma((5,)), dma((6,)), dma((4, 4)), dma((4, 4)), dma((4, 2)), dma((4, 2)), dma((4,)), dma((4,)),
        dma((sp_size - 1, 3)), dma((sp_size - 1, 3)), dma, dma, dma((3,)), dma((3,)), dma((sp_size - 1,)), dma((sp_size - 1,)),
    ]
    return pl.pallas_call(
        functools.partial(back_kernel, sp_size),
        out_shape=[jax.ShapeDtypeStruct((units, wide), low), jax.ShapeDtypeStruct((units, wide), low),
                   jax.ShapeDtypeStruct((rows, 3 * wide), low), jax.ShapeDtypeStruct((rows, wide), low),
                   jax.ShapeDtypeStruct(small.shape, full)],
        in_specs=[hbm] * 7 + [vmem], out_specs=[hbm] * 4 + [vmem],
        scratch_shapes=scratch,
        compiler_params=pltpu.CompilerParams(collective_id=1, has_side_effects=True, vmem_limit_bytes=67043328),
        cost_estimate=pl.CostEstimate(flops=26 * 10 ** 9, bytes_accessed=300 * 1000 * 1000, transcendentals=0),
        name="reduce_gradients",
    )(hidden, grad_out, grad_pre, mlp_in, attn_in, grad_proj, context, small)

def gather_plain(dp_size, sp_size, qkv_weight, out_weight, up_weight, down_weight):
    head_width = D // sp_size
    qkv_rows = qkv_weight.shape[0]
    qkv_slab = lax.all_to_all(
        qkv_weight.reshape(qkv_rows, 3, sp_size, head_width),
        "sp",
        split_axis=2,
        concat_axis=0,
        tiled=True,
    )
    qkv_own = lax.all_gather(
        qkv_slab.reshape(qkv_rows * sp_size, 3 * head_width), "dp", axis=0, tiled=True
    )
    up_own = lax.all_gather(up_weight, "dp", axis=0, tiled=True)
    down_own = lax.all_gather(down_weight, "dp", axis=0, tiled=True)
    out_blocks = lax.all_gather(out_weight, "dp", axis=0, tiled=True)
    out_own = lax.all_to_all(
        out_blocks.reshape(sp_size, dp_size // sp_size, qkv_rows, D),
        "sp",
        split_axis=0,
        concat_axis=2,
        tiled=True,
    ).reshape(head_width, D)
    return qkv_own, out_own, up_own, down_own


def reduce_plain(
    dp_size, sp_size, rows, hidden, grad_out, grad_pre, mlp_in, attn_in, grad_proj, context
):
    def scatter(left, right):
        return lax.psum_scatter(
            contract_rows(left, right).astype(jnp.bfloat16), "dp", scatter_dimension=0, tiled=True
        )

    grad_dense = lax.all_to_all(
        contract_rows(context, grad_out)
        .astype(jnp.bfloat16)
        .reshape(dp_size // sp_size, sp_size, rows, D),
        "sp",
        split_axis=1,
        concat_axis=0,
        tiled=True,
    ).reshape(dp_size * rows, D)
    grad_dense = lax.psum_scatter(grad_dense, "dp", scatter_dimension=0, tiled=True)
    grad_qkv = lax.all_to_all(
        scatter(attn_in, grad_proj).reshape(sp_size, rows, 3, 1, D // sp_size),
        "sp",
        split_axis=0,
        concat_axis=3,
        tiled=True,
    ).reshape(rows, 3 * D)
    return scatter(hidden, grad_out), scatter(grad_pre, mlp_in), grad_qkv, grad_dense


def body(
    tokens,
    lengths,
    cotangent,
    ln_gains,
    ln_shifts,
    qkv_weight,
    qkv_bias,
    out_weight,
    up_weight,
    up_bias,
    down_weight,
    out_bias,
):
    dp_size = lax.axis_size("dp")
    sp_size = lax.axis_size("sp")
    shard = lax.axis_index("sp")
    own_rows = tokens.shape[0]
    seq_rows = own_rows * sp_size
    head_width = D // sp_size
    length = lengths[0]
    low = jnp.bfloat16
    full = jnp.float32

    seq_tokens = lax.all_gather(tokens, "sp", axis=0, tiled=True)
    seq_cotangent = lax.all_gather(cotangent, "sp", axis=0, tiled=True)
    qkv_rows = qkv_weight.shape[0]
    per_shard = dp_size // sp_size
    square = dp_size == 8 and sp_size == 4
    gather = gather_weights if square else gather_plain
    qkv_own, out_own, up_own, down_own = gather(
        dp_size, sp_size, qkv_weight, out_weight, up_weight, down_weight
    )
    units = up_weight.shape[0]
    unit_bias = lax.dynamic_index_in_dim(
        up_bias.reshape(dp_size, sp_size, units), shard, 1, keepdims=False
    ).reshape(dp_size * units)
    bias_own = lax.dynamic_index_in_dim(
        qkv_bias.reshape(3, sp_size, head_width), shard, 1, keepdims=False
    ).reshape(3 * head_width)

    positions = jnp.arange(seq_rows, dtype=jnp.int32)
    cos_rows, sin_rows = rotary_rows(seq_rows)
    gains = ln_gains.astype(full)
    shifts = ln_shifts.astype(full)
    inputs = seq_tokens.astype(full)
    centre = jnp.mean(inputs, axis=-1, keepdims=True)
    centered = inputs - centre
    inverse = lax.rsqrt(jnp.mean(centered * centered, axis=-1, keepdims=True) + eps)
    normed = centered * inverse
    attn_in = (normed * gains[0] + shifts[0]).astype(low)
    mlp_in = (normed * gains[1] + shifts[1]).astype(low)
    row_valid = positions < length

    projected = jnp.dot(attn_in, qkv_own, preferred_element_type=full)
    queries, key_rows, values, context = attend_fwd(
        projected, bias_own.astype(full)[None], cos_rows, sin_rows, lengths
    )

    pre_act = contract_cols(mlp_in, up_own) + unit_bias.astype(full)
    hidden = gelu_value(pre_act).astype(low)
    partial_out = jnp.dot(hidden, down_own, preferred_element_type=full) + jnp.dot(
        context, out_own, preferred_element_type=full
    )
    reduced_out = lax.psum_scatter(
        partial_out.astype(low), "sp", scatter_dimension=0, tiled=True
    )
    output = (
        tokens.astype(full) + reduced_out.astype(full) + out_bias.astype(full)
    ).astype(low)

    seq_cotangent, _ = lax.optimization_barrier((seq_cotangent, partial_out))
    grad_out = jnp.where(row_valid[:, None], seq_cotangent, jnp.zeros_like(seq_cotangent))
    grad_hidden = contract_cols(grad_out, down_own)
    grad_pre = (grad_hidden * gelu_slope(pre_act)).astype(low)
    grad_mlp_in = jnp.dot(grad_pre, up_own, preferred_element_type=full)

    grad_context = contract_cols(grad_out, out_own).astype(low)
    grad_proj, grad_proj_sum = attend_bwd(
        queries, key_rows, values, grad_context, cos_rows, sin_rows, lengths
    )
    grad_attn_in = contract_cols(grad_proj, qkv_own)
    grad_hat = grad_attn_in * gains[0] + grad_mlp_in * gains[1]
    reduced_hat = lax.psum_scatter(
        grad_hat.astype(low), "sp", scatter_dimension=0, tiled=True
    ).astype(full)
    own_cotangent = lax.dynamic_slice_in_dim(grad_out, shard * own_rows, own_rows, 0).astype(full)
    spread_units = lax.dynamic_update_index_in_dim(
        jnp.zeros((dp_size, sp_size, units), full),
        jnp.sum(grad_pre, axis=0, dtype=full).reshape(dp_size, units),
        shard,
        1,
    ).reshape(-1)
    spread_bias = lax.dynamic_update_index_in_dim(
        jnp.zeros((3, sp_size, head_width), full),
        grad_proj_sum.reshape(3, head_width),
        shard,
        1,
    ).reshape(3, D)
    gain_grad = jnp.stack(
        [jnp.sum(grad_attn_in * normed, axis=0), jnp.sum(grad_mlp_in * normed, axis=0)]
    )
    shift_grad = jnp.stack([jnp.sum(grad_attn_in, axis=0), jnp.sum(grad_mlp_in, axis=0)])
    out_bias_part = jnp.sum(own_cotangent, axis=0)
    if square:
        small = jnp.concatenate(
            [
                piece.reshape(-1, 128)
                for piece in (gain_grad, shift_grad, spread_bias, spread_units, out_bias_part)
            ]
        )
        grad_down, grad_up, grad_qkv, grad_dense, small = reduce_gradients(
            sp_size,
            qkv_rows,
            hidden,
            grad_out,
            grad_pre,
            mlp_in,
            attn_in,
            grad_proj,
            context,
            small,
        )
        small = small.reshape(-1)
        ends = [2 * D, 4 * D, 7 * D, 7 * D + dp_size * sp_size * units]
        gain_total, shift_total, qkv_bias_total, unit_total, out_bias_total = jnp.split(small, ends)
        gain_total = gain_total.reshape(2, D)
        shift_total = shift_total.reshape(2, D)
        qkv_bias_total = qkv_bias_total.reshape(3, D)
    else:
        grad_down, grad_up, grad_qkv, grad_dense = reduce_plain(
            dp_size,
            sp_size,
            qkv_rows,
            hidden,
            grad_out,
            grad_pre,
            mlp_in,
            attn_in,
            grad_proj,
            context,
        )
        gain_total, shift_total, qkv_bias_total, unit_total, out_bias_total = lax.psum(
            (gain_grad, shift_grad, spread_bias, spread_units, out_bias_part), ("dp", "sp")
        )

    own_inverse = lax.dynamic_slice_in_dim(inverse, shard * own_rows, own_rows, 0)
    own_normed = lax.dynamic_slice_in_dim(normed, shard * own_rows, own_rows, 0)
    grad_input = own_inverse * (
        reduced_hat
        - jnp.mean(reduced_hat, axis=-1, keepdims=True)
        - own_normed * jnp.mean(reduced_hat * own_normed, axis=-1, keepdims=True)
    )
    input_grad = (own_cotangent + grad_input).astype(low)
    return (
        output,
        input_grad,
        gain_total,
        shift_total,
        grad_qkv.astype(full),
        qkv_bias_total,
        grad_dense.astype(full),
        grad_up.astype(full),
        unit_total,
        grad_down.astype(full),
        out_bias_total,
    )


def solution(mesh):
    return jax.shard_map(
        body,
        mesh=mesh,
        in_specs=(
            P(("dp", "sp"), None),
            P("dp"),
            P(("dp", "sp"), None),
            P(),
            P(),
            P(("dp", "sp"), None),
            P(),
            P(("dp", "sp"), None),
            P(("dp", "sp"), None),
            P(),
            P(("dp", "sp"), None),
            P(),
        ),
        out_specs=(
            P(("dp", "sp"), None),
            P(("dp", "sp"), None),
            P(),
            P(),
            P(("dp", "sp"), None),
            P(),
            P(("dp", "sp"), None),
            P(("dp", "sp"), None),
            P(),
            P(("dp", "sp"), None),
            P(),
        ),
        check_vma=False,
    )
```

```python
import functools

import jax
import jax.numpy as jnp
from jax import lax
from jax.experimental import pallas as pl
from jax.experimental.pallas import tpu as pltpu
from jax.sharding import PartitionSpec as P

D = 2048
HEADS = 8
HEAD = 256
ROT = 64


eps = 1e-05
base_freq = 10000.0
root_half = 0.7071067811865476
inv_root_two_pi = 0.3989422804014327


def contract_rows(left, right):
    return lax.dot_general(
        left, right, (((0,), (0,)), ((), ())), preferred_element_type=jnp.float32
    )


def contract_cols(left, right):
    return lax.dot_general(
        left, right, (((1,), (1,)), ((), ())), preferred_element_type=jnp.float32
    )


def gelu_value(pre_act):
    return 0.5 * pre_act * (1.0 + lax.erf(pre_act * root_half))


def gelu_slope(pre_act):
    return 0.5 * (1.0 + lax.erf(pre_act * root_half)) + pre_act * inv_root_two_pi * jnp.exp(
        -0.5 * pre_act * pre_act
    )


BAND=256
def turn(x, cos_t, sin_t):
    first = x[:, :128]
    lane = lax.broadcasted_iota(jnp.int32, first.shape, 1)
    partner = jnp.where(lane < ROT // 2, pltpu.roll(first, 128 - ROT // 2, 1), pltpu.roll(first, ROT // 2, 1))
    return jnp.concatenate([first * cos_t + partner * sin_t, x[:, 128:]], axis=1)

def weights_of(q, k, start, length, scale):
    rows, cols = q.shape[0], k.shape[0]
    s = lax.dot_general(q, k, (((1,), (1,)), ((), ())), preferred_element_type=jnp.float32) * scale
    key = lax.broadcasted_iota(jnp.int32, (rows, cols), 1)
    query = start + lax.broadcasted_iota(jnp.int32, (rows, cols), 0)
    s = jnp.where((key <= query) & (key < length), s, -1e30)
    e = jnp.exp(s - jnp.max(s, axis=-1, keepdims=True))
    return e / jnp.sum(e, axis=-1, keepdims=True)

def fwd_kernel(scale, len_ref, pq, pk, pv, bq, bk, bv, cos_ref, sin_ref, q_ref, k_ref, v_ref, ctx_ref):
    length = len_ref[0]
    seq = pq.shape[0]
    cos_t, sin_t = cos_ref[...], sin_ref[...]
    q_ref[...] = turn(pq[...] + bq[...], cos_t, sin_t).astype(jnp.bfloat16)
    k_ref[...] = turn(pk[...] + bk[...], cos_t, sin_t).astype(jnp.bfloat16)
    v_ref[...] = (pv[...] + bv[...]).astype(jnp.bfloat16)
    for start in range(0, seq, BAND):
        end = start + BAND
        p = weights_of(q_ref[start:end, :], k_ref[:end, :], start, length, scale)
        ctx_ref[start:end, :] = jnp.dot(p.astype(jnp.bfloat16), v_ref[:end, :], preferred_element_type=jnp.float32).astype(jnp.bfloat16)

def attend_fwd(projected, bias, cos_t, sin_t, lengths):
    seq, width = projected.shape
    heads = width // 3 // HEAD
    col = lambda g: pl.BlockSpec((seq, HEAD), lambda h, *_, g=g: (0, g * heads + h))
    bcol = lambda g: pl.BlockSpec((1, HEAD), lambda h, *_, g=g: (0, g * heads + h))
    tab = pl.BlockSpec((seq, 128), lambda h, *_: (0, 0))
    out = pl.BlockSpec((seq, HEAD), lambda h, *_: (0, h))
    return pl.pallas_call(
        functools.partial(fwd_kernel, HEAD ** -0.5),
        grid_spec=pltpu.PrefetchScalarGridSpec(num_scalar_prefetch=1, grid=(heads,),
            in_specs=[col(0), col(1), col(2), bcol(0), bcol(1), bcol(2), tab, tab], out_specs=[out] * 4),
        out_shape=[jax.ShapeDtypeStruct((seq, heads * HEAD), jnp.bfloat16)] * 4,
        name="attend_fwd",
        cost_estimate=pl.CostEstimate(flops=heads * seq * seq * HEAD * 4, bytes_accessed=seq * width * 8, transcendentals=heads * seq * seq),
    )(lengths, projected, projected, projected, bias, bias, bias, cos_t, sin_t)

def bwd_kernel(scale, heads, len_ref, q_ref, k_ref, v_ref, g_ref, cos_ref, sin_ref, gp_ref, sum_ref, dk, dv, dq):
    length = len_ref[0]
    h = pl.program_id(0)
    seq = q_ref.shape[0]
    dk[...] = jnp.zeros_like(dk)
    dv[...] = jnp.zeros_like(dv)
    for start in range(0, seq, BAND):
        end = start + BAND
        q, g = q_ref[start:end, :], g_ref[start:end, :]
        k, v = k_ref[:end, :], v_ref[:end, :]
        p = weights_of(q, k, start, length, scale)
        gp = lax.dot_general(g, v, (((1,), (1,)), ((), ())), preferred_element_type=jnp.float32)
        ds = (p * (gp - jnp.sum(p * gp, axis=-1, keepdims=True))).astype(jnp.bfloat16)
        dq[start:end, :] = jnp.dot(ds, k, preferred_element_type=jnp.float32) * scale
        dk[:end, :] += lax.dot_general(ds, q, (((0,), (0,)), ((), ())), preferred_element_type=jnp.float32)
        dv[:end, :] += lax.dot_general(p.astype(jnp.bfloat16), g, (((0,), (0,)), ((), ())), preferred_element_type=jnp.float32)
    cos_t, sin_t = cos_ref[...], sin_ref[...]
    def back(x):
        return turn(x.astype(jnp.bfloat16).astype(jnp.float32), cos_t, -sin_t).astype(jnp.bfloat16)
    for g, piece in enumerate((back(dq[...]), back(dk[...] * scale), dv[...].astype(jnp.bfloat16))):
        at = pl.ds(pl.multiple_of((g * heads + h) * HEAD, HEAD), HEAD)
        gp_ref[:, at] = piece
        sum_ref[:, at] = jnp.sum(piece.astype(jnp.float32), axis=0, keepdims=True)

def attend_bwd(q, k, v, gctx, cos_t, sin_t, lengths):
    seq, width = q.shape
    heads = width // HEAD
    col = pl.BlockSpec((seq, HEAD), lambda h, *_: (0, h))
    tab = pl.BlockSpec((seq, 128), lambda h, *_: (0, 0))
    return pl.pallas_call(
        functools.partial(bwd_kernel, HEAD ** -0.5, heads),
        grid_spec=pltpu.PrefetchScalarGridSpec(num_scalar_prefetch=1, grid=(heads,),
            in_specs=[col] * 4 + [tab, tab],
            out_specs=[pl.BlockSpec((seq, 3 * width), lambda h, *_: (0, 0)), pl.BlockSpec((1, 3 * width), lambda h, *_: (0, 0))],
            scratch_shapes=[pltpu.VMEM((seq, HEAD), jnp.float32)] * 3),
        out_shape=[jax.ShapeDtypeStruct((seq, 3 * width), jnp.bfloat16), jax.ShapeDtypeStruct((1, 3 * width), jnp.float32)],
        name="attend_bwd",
        cost_estimate=pl.CostEstimate(flops=heads * seq * seq * HEAD * 10, bytes_accessed=seq * width * 20, transcendentals=heads * seq * seq),
    )(lengths, q, k, v, gctx, cos_t, sin_t)

def rotary_rows(seq):
    half = ROT // 2
    freq = 10000.0 ** (-jnp.arange(half, dtype=jnp.float32) * (2.0 / ROT))
    ang = jnp.arange(seq, dtype=jnp.int32).astype(jnp.float32)[:, None] * freq[None, :]
    c, s = jnp.cos(ang), jnp.sin(ang)
    rest = 128 - ROT
    return (jnp.concatenate([c, c, jnp.ones((seq, rest), jnp.float32)], 1), jnp.concatenate([-s, s, jnp.zeros((seq, rest), jnp.float32)], 1))

MESH = pl.DeviceIdType.MESH

def square_partners(dp):
    core, x, y = dp % 2, (dp // 2) % 2, dp // 4
    across_x, across_y = dp + 2 - 4 * x, dp + 4 - 8 * y
    first = across_x * (1 - core) + across_y * core
    second = across_y * (1 - core) + across_x * core
    return first, second, across_x + across_y - dp, 1 - 2 * core

def gather_kernel(sp_size, qkv_ref, out_ref, up_ref, down_ref, qkv_all, out_all, up_all, down_all,
                  send_sem, recv_sem, slab_send, slab_recv, local_sem, turn_send, turn_recv):
    dp, sp = lax.axis_index("dp"), lax.axis_index("sp")
    first, second, diagonal, flip = square_partners(dp)
    sibling = dp + flip
    per = 2
    pair, lane = dp // per, dp % per
    rows = qkv_ref.shape[0]
    wide = up_ref.shape[1]
    head_width = wide // sp_size
    turn_dp = sp * per + lane

    barrier = pltpu.get_barrier_semaphore()
    for other in (first, second, sibling):
        pl.semaphore_signal(barrier, inc=1, device_id=(other, sp), device_id_type=MESH)
    for step in range(1, sp_size):
        pl.semaphore_signal(barrier, inc=1, device_id=(dp, lax.rem(sp + step, sp_size)), device_id_type=MESH)
    @pl.when(pair != sp)
    def _():
        pl.semaphore_signal(barrier, inc=1, device_id=(turn_dp, pair), device_id_type=MESH)

    pl.semaphore_wait(barrier, 2 + sp_size + jnp.where(pair != sp, 1, 0))

    def slab_at(owner_sp):
        return pl.ds(pl.multiple_of((dp * sp_size + owner_sp) * rows, rows), rows)

    def slab_copy(step, part):
        there = lax.rem(sp + step, sp_size)
        return pltpu.make_async_remote_copy(
            src_ref=qkv_ref.at[:, pl.ds(pl.multiple_of(part * wide + there * head_width, head_width), head_width)],
            dst_ref=qkv_all.at[slab_at(sp), pl.ds(part * head_width, head_width)],
            send_sem=slab_send.at[step - 1, part], recv_sem=slab_recv.at[step - 1, part],
            device_id=(dp, there), device_id_type=MESH)

    def slab_arrival(step, part):
        origin = lax.rem(sp + sp_size - step, sp_size)
        return pltpu.make_async_remote_copy(
            src_ref=qkv_ref.at[:, pl.ds(part * head_width, head_width)],
            dst_ref=qkv_all.at[slab_at(origin), pl.ds(part * head_width, head_width)],
            send_sem=slab_send.at[step - 1, part], recv_sem=slab_recv.at[step - 1, part],
            device_id=(dp, origin), device_id_type=MESH)

    units = up_ref.shape[0]
    slab = rows * sp_size

    def plain(height):
        return lambda owner: pl.ds(pl.multiple_of(owner * height, height), height)

    def turned(owner):
        return pl.ds(pl.multiple_of((owner % per) * slab + (owner // per) * rows, rows), rows)

    arrays = ((up_ref, up_all, plain(units)), (down_ref, down_all, plain(units)), (None, qkv_all, plain(slab)), (None, out_all, turned))

    def copy(index, message, block, target):
        source, result, place = arrays[index]
        at = result.at[place(block)]
        src = at
        if source is not None and message < 3:
            src = source
        return pltpu.make_async_remote_copy(
            src_ref=src, dst_ref=at, send_sem=send_sem.at[index, message], recv_sem=recv_sem.at[index, message],
            device_id=(target, sp), device_id_type=MESH)

    sends = ((dp, first), (dp, second), (dp, sibling), (first, second), (first, sibling), (second, sibling), (diagonal, sibling))
    arrivals = (first, second, sibling, diagonal, second + flip, first + flip, diagonal + flip)

    def start(index, message):
        copy(index, message, *sends[message]).start()

    def arrived(index, message):
        copy(index, message, arrivals[message], dp).wait_recv()

    def own(index):
        for message in (0, 1, 2):
            start(index, message)

    def keep(source, target, which):
        return pltpu.make_async_copy(source, target, local_sem.at[which])

    own(0)
    for step in range(1, sp_size):
        for part in range(3):
            slab_copy(step, part).start()

    out_place = out_all.at[turned(turn_dp)]
    my_out_place = out_all.at[turned(dp)]
    turn = pltpu.make_async_remote_copy(
        src_ref=out_ref, dst_ref=out_place, send_sem=turn_send, recv_sem=turn_recv,
        device_id=(turn_dp, pair), device_id_type=MESH)
    turn_arrival = pltpu.make_async_remote_copy(
        src_ref=out_ref, dst_ref=my_out_place, send_sem=turn_send, recv_sem=turn_recv,
        device_id=(turn_dp, pair), device_id_type=MESH)

    @pl.when(pair != sp)
    def _():
        turn.start()

    own(1)
    local = [keep(up_ref, up_all.at[plain(units)(dp)], 0), keep(down_ref, down_all.at[plain(units)(dp)], 1)]
    for part in range(3):
        local.append(keep(
            qkv_ref.at[:, pl.ds(pl.multiple_of(part * wide + sp * head_width, head_width), head_width)],
            qkv_all.at[slab_at(sp), pl.ds(part * head_width, head_width)], 2 + part))
    for c in local:
        c.start()

    def onward(index):
        arrived(index, 0)
        start(index, 3)
        start(index, 4)
        arrived(index, 1)
        start(index, 5)

    onward(0)
    for step in range(1, sp_size):
        for part in range(3):
            slab_arrival(step, part).wait_recv()
    for c in local:
        c.wait()
    own(2)

    @pl.when(pair == sp)
    def _():
        c = keep(out_ref, my_out_place, 5)
        c.start()
        c.wait()

    @pl.when(pair != sp)
    def _():
        turn_arrival.wait_recv()

    own(3)
    onward(1)
    onward(2)
    onward(3)
    for index in range(4):
        arrived(index, 3)
        start(index, 6)
    for index in range(4):
        for message in (2, 4, 5, 6):
            arrived(index, message)
    for index in range(4):
        for message in range(7):
            copy(index, message, *sends[message]).wait_send()
    for step in range(1, sp_size):
        for part in range(3):
            slab_copy(step, part).wait_send()

    @pl.when(pair != sp)
    def _():
        turn.wait_send()

def gather_weights(dp_size, sp_size, qkv_weight, out_weight, up_weight, down_weight):
    rows, wide = out_weight.shape
    units = up_weight.shape[0]
    low = jnp.bfloat16
    hbm = pl.BlockSpec(memory_space=pltpu.HBM)
    vmem = pl.BlockSpec(memory_space=pltpu.VMEM)
    dma = pltpu.SemaphoreType.DMA
    return pl.pallas_call(
        functools.partial(gather_kernel, sp_size),
        out_shape=[jax.ShapeDtypeStruct((rows * sp_size * dp_size, 3 * wide // sp_size), low),
                   jax.ShapeDtypeStruct((rows * dp_size, wide), low),
                   jax.ShapeDtypeStruct((units * dp_size, wide), low),
                   jax.ShapeDtypeStruct((units * dp_size, wide), low)],
        in_specs=[vmem] * 4, out_specs=[hbm] * 4,
        scratch_shapes=[dma((4, 7)), dma((4, 7)), dma((sp_size - 1, 3)), dma((sp_size - 1, 3)), dma((6,)), dma, dma],
        compiler_params=pltpu.CompilerParams(collective_id=0, has_side_effects=True),
        cost_estimate=pl.CostEstimate(flops=0, bytes_accessed=300 * 1000 * 1000, transcendentals=0),
        name="gather_weights",
    )(qkv_weight, out_weight, up_weight, down_weight)

CHUNK = 512


def back_kernel(sp_size, hidden_hbm, cot_hbm, pre_hbm, mlp_hbm, attn_hbm, proj_hbm, ctx_hbm, small_ref,
                down_out, up_out, qkv_out, dense_out, small_out,
                left_a, right_a, left_b, right_b, ctx, lent,
                down_sum, up_sum, qkv_sum, dense_sum, down_sib, up_sib, qkv_sib, dense_sib,
                down_one, up_one, qkv_one, dense_one, down_two, up_two, qkv_two, dense_two, dense_part,
                small_acc, small_in, small_z,
                load_sem, store_sem, sib_send, sib_recv, one_send, one_recv, two_send, two_recv,
                slab_send, slab_recv, turn_send, turn_recv, small_send, small_recv, z_send, z_recv):
    dp, sp = lax.axis_index("dp"), lax.axis_index("sp")
    full, low = jnp.float32, jnp.bfloat16
    core, chip = dp % 2, dp // 2
    x, y = chip % 2, chip // 2
    per = 2
    pair, lane = dp // per, dp % per
    turn_dp = sp * per + lane
    sibling = dp + 1 - 2 * core
    across_x, across_y = dp + 2 - 4 * x, dp + 4 - 8 * y
    first = across_y * (1 - core) + across_x * core
    second = across_x * (1 - core) + across_y * core
    first_mask, second_mask = 2 - core, 1 + core
    units = down_sum.shape[1]
    slab_width = qkv_sum.shape[2]
    head_width = slab_width // 3
    rows = dense_one.shape[1]
    wide = right_a.shape[1]

    def chip_of(mask):
        return lax.rem(x + lax.rem(mask, 2), 2) + 2 * lax.rem(y + mask // 2, 2)

    def load(source, target, which):
        return pltpu.make_async_copy(source, target, load_sem.at[which])

    loads = [load(hidden_hbm, left_a, 0), load(cot_hbm, right_a, 1), load(ctx_hbm, ctx, 2),
             load(pre_hbm, left_b, 3), load(mlp_hbm, right_b, 4)]
    for c in loads:
        c.start()

    barrier = pltpu.get_barrier_semaphore()
    for other in (first, second, sibling):
        pl.semaphore_signal(barrier, inc=1, device_id=(other, sp), device_id_type=MESH)
    for step in range(1, sp_size):
        pl.semaphore_signal(barrier, inc=1, device_id=(dp, lax.rem(sp + step, sp_size)), device_id_type=MESH)

    @pl.when(pair != sp)
    def _():
        pl.semaphore_signal(barrier, inc=1, device_id=(turn_dp, pair), device_id_type=MESH)

    pl.semaphore_wait(barrier, 2 + sp_size + jnp.where(pair != sp, 1, 0))

    def remote(source, target, send, recv, device):
        return pltpu.make_async_remote_copy(
            src_ref=source, dst_ref=target, send_sem=send, recv_sem=recv,
            device_id=device, device_id_type=MESH)

    def small_copy(stage):
        return remote(small_ref if stage == 0 else small_acc.at[stage - 1], small_in.at[stage],
                      small_send.at[stage], small_recv.at[stage], ((sibling, across_x, across_y)[stage], sp))

    def small_step(stage):
        small_copy(stage).wait_recv()
        before = small_ref[...] if stage == 0 else small_acc[stage - 1]
        small_acc[stage] = before + small_in[stage]

    def z_copy(step):
        return remote(small_acc.at[2], small_z.at[sp], z_send.at[step - 1], z_recv.at[step - 1],
                      (dp, lax.rem(sp + step, sp_size)))

    def z_arrival(step):
        origin = lax.rem(sp + sp_size - step, sp_size)
        return remote(small_acc.at[2], small_z.at[origin], z_send.at[step - 1], z_recv.at[step - 1], (dp, origin))

    small_copy(0).start()

    class Wide:
        def __init__(self, index, left, right, width, sums, sib, one, two):
            self.index, self.left, self.right, self.width = index, left, right, width
            self.sums, self.sib, self.one, self.two = sums, sib, one, two

        def product(self, block, store):
            at = pl.ds(pl.multiple_of(block * units, units), units)

            def columns(part, carry):
                to = pl.ds(pl.multiple_of(part * CHUNK, CHUNK), CHUNK)
                store(to, lax.dot_general(
                    self.left[:, at], self.right[:, to], (((0,), (0,)), ((), ())),
                    preferred_element_type=full))
                return carry
            lax.fori_loop(0, self.width // CHUNK, columns, 0)

        def lend(self, slot):
            return lent.at[slot, :, :self.width]

        def sib_copy(self, slot):
            place = chip_of(3 - slot)
            return remote(self.lend(slot), self.sib.at[place], sib_send.at[self.index, slot],
                          sib_recv.at[self.index, slot], (sibling, sp))

        def for_sibling(self, previous):
            def step(slot, carry):
                if previous is not None:
                    previous.sib_copy(slot).wait_send()
                block = chip_of(3 - slot) * 2 + 1 - core

                def store(to, total):
                    lent[slot, :, to] = total.astype(low)
                self.product(block, store)
                self.sib_copy(slot).start()
                return carry
            lax.fori_loop(0, 4, step, 0)

        def own(self, mask, slot):
            place = chip_of(mask)
            self.sib_copy(slot).wait_recv()

            def store(to, total):
                self.sums[mask, :, to] = (total + self.sib[place, :, to].astype(full)).astype(low)
            self.product(place * 2 + core, store)

        def first_copy(self, slot):
            mask = 3 - slot * (1 + core)
            return remote(self.sums.at[mask], self.one.at[slot], one_send.at[self.index, slot],
                          one_recv.at[self.index, slot], (first, sp))

        def for_self(self):
            def leave(slot, carry):
                mask = 3 - slot * (1 + core)
                self.own(mask, 3 - mask)
                self.first_copy(slot).start()
                return carry
            lax.fori_loop(0, 2, leave, 0)

            def stay(slot, carry):
                mask = second_mask * (1 - slot)
                self.own(mask, 3 - mask)
                return carry
            lax.fori_loop(0, 2, stay, 0)

        def second_copy(self):
            return remote(self.sums.at[second_mask], self.two, two_send.at[self.index],
                          two_recv.at[self.index], (second, sp))

        def block(self, mask):
            return self.sums.at[mask]

    class Dense(Wide):
        def sib_copy(self, slot):
            return remote(dense_part.at[0], self.sib, sib_send.at[self.index, 0],
                          sib_recv.at[self.index, 0], (sibling, sp))

        def for_sibling(self, previous):
            def store(to, total):
                dense_part[0, :, to] = total.astype(low)
            self.product(1 - core, store)
            self.sib_copy(0).start()

        def block(self, mask):
            return self.sums.at[pl.ds(pl.multiple_of(chip_of(mask) * rows, rows), rows)]

        def first_copy(self, slot):
            mask = 3 - slot * (1 + core)
            return remote(self.block(mask), self.one.at[slot], one_send.at[self.index, slot],
                          one_recv.at[self.index, slot], (first, sp))

        def for_self(self):
            self.sib_copy(0).wait_recv()

            def store(to, total):
                self.sums[:, to] = (total + self.sib[:, to].astype(full)).astype(low)
            self.product(core, store)
            for slot in (0, 1):
                self.first_copy(slot).start()

        def second_copy(self):
            return remote(self.block(second_mask), self.two, two_send.at[self.index],
                          two_recv.at[self.index], (second, sp))

    down = Wide(0, left_a, right_a, wide, down_sum, down_sib, down_one, down_two)
    dense = Dense(1, ctx, right_a, wide, dense_sum, dense_sib, dense_one, dense_two)
    up = Wide(2, left_b, right_b, wide, up_sum, up_sib, up_one, up_two)
    qkv = Wide(3, left_a, right_a, slab_width, qkv_sum, qkv_sib, qkv_one, qkv_two)

    def add_into(target, *others):
        height = target.shape[0]
        step_rows = 32

        def step(i, carry):
            at = pl.ds(pl.multiple_of(i * step_rows, step_rows), step_rows)
            total = target[at, :].astype(full)
            for other in others:
                total = total + other[at, :].astype(full)
            target[at, :] = total.astype(low)
            return carry
        lax.fori_loop(0, height // step_rows, step, 0)

    def onward(array):
        array.first_copy(0).wait_recv()
        add_into(array.block(second_mask), array.one.at[0])
        array.second_copy().start()

    def finish(array):
        array.first_copy(1).wait_recv()
        array.second_copy().wait_recv()
        add_into(array.block(0), array.one.at[1], array.two)

    loads[0].wait()
    loads[1].wait()
    down.for_sibling(None)
    small_step(0)
    small_copy(1).start()
    down.for_self()
    loads[2].wait()
    dense.for_sibling(None)
    small_step(1)
    small_copy(2).start()
    dense.for_self()
    late = [load(attn_hbm, left_a, 0), load(proj_hbm, right_a.at[:, :slab_width], 1)]
    for c in late:
        c.start()
    loads[3].wait()
    loads[4].wait()
    up.for_sibling(down)
    onward(down)
    small_step(2)
    for step in range(1, sp_size):
        z_copy(step).start()
    small_z[sp] = small_acc[2]
    up.for_self()
    for c in late:
        c.wait()
    onward(dense)
    qkv.for_sibling(up)
    qkv.for_self()
    onward(up)
    finish(down)
    stores = [pltpu.make_async_copy(down.block(0), down_out, store_sem.at[0])]
    stores[0].start()
    finish(dense)

    def turn(target):
        return remote(dense.block(0), target, turn_send, turn_recv, (turn_dp, pair))

    @pl.when(pair != sp)
    def _():
        turn(dense_out).start()

    @pl.when(pair == sp)
    def _():
        c = pltpu.make_async_copy(dense.block(0), dense_out, store_sem.at[1])
        c.start()
        c.wait()

    onward(qkv)
    finish(up)
    stores.append(pltpu.make_async_copy(up.block(0), up_out, store_sem.at[2]))
    stores[1].start()
    for step in range(1, sp_size):
        z_arrival(step).wait_recv()
    total = small_z[0]
    for place in range(1, sp_size):
        total = total + small_z[place]
    small_out[...] = total
    finish(qkv)

    def slab_rows(owner):
        return pl.ds(pl.multiple_of(owner * rows, rows), rows)

    def slab_copy(step, part, origin, there):
        at = pl.ds(pl.multiple_of(part * wide + origin * head_width, head_width), head_width)
        return remote(qkv_sum.at[0, slab_rows(there), pl.ds(part * head_width, head_width)], qkv_out.at[:, at],
                      slab_send.at[step - 1, part], slab_recv.at[step - 1, part], (dp, there))

    for step in range(1, sp_size):
        for part in range(3):
            slab_copy(step, part, sp, lax.rem(sp + step, sp_size)).start()
    for part in range(3):
        at = pl.ds(pl.multiple_of(part * wide + sp * head_width, head_width), head_width)
        c = pltpu.make_async_copy(qkv_sum.at[0, slab_rows(sp), pl.ds(part * head_width, head_width)],
                                  qkv_out.at[:, at], store_sem.at[3 + part])
        c.start()
        stores.append(c)
    for step in range(1, sp_size):
        for part in range(3):
            slab_copy(step, part, lax.rem(sp + sp_size - step, sp_size), sp).wait_recv()

    @pl.when(pair != sp)
    def _():
        turn(dense_out).wait_recv()
        turn(dense_out).wait_send()

    for c in stores:
        c.wait()
    for slot in range(4):
        qkv.sib_copy(slot).wait_send()
    dense.sib_copy(0).wait_send()
    for array in (down, dense, up, qkv):
        for slot in (0, 1):
            array.first_copy(slot).wait_send()
        array.second_copy().wait_send()
    for stage in range(3):
        small_copy(stage).wait_send()
    for step in range(1, sp_size):
        z_copy(step).wait_send()
        for part in range(3):
            slab_copy(step, part, sp, lax.rem(sp + step, sp_size)).wait_send()

def reduce_gradients(sp_size, rows, hidden, grad_out, grad_pre, mlp_in, attn_in, grad_proj, context, small):
    seq, wide = mlp_in.shape
    slab_width = grad_proj.shape[1]
    units = 4 * rows
    full, low = jnp.float32, jnp.bfloat16
    hbm = pl.BlockSpec(memory_space=pltpu.HBM)
    vmem = pl.BlockSpec(memory_space=pltpu.VMEM)
    dma = pltpu.SemaphoreType.DMA
    def v(*shape, kind=low):
        return pltpu.VMEM(shape, kind)
    scratch = [
        v(seq, wide), v(seq, wide), v(seq, wide), v(seq, wide), v(seq, context.shape[1]), v(4, units, wide),
        v(4, units, wide), v(4, units, wide), v(4, units, slab_width), v(4 * rows, wide),
        v(4, units, wide), v(4, units, wide), v(4, units, slab_width), v(4 * rows, wide),
        v(2, units, wide), v(2, units, wide), v(2, units, slab_width), v(2, rows, wide),
        v(units, wide), v(units, wide), v(units, slab_width), v(rows, wide),
        v(1, 4 * rows, wide),
        v(3, *small.shape, kind=full), v(3, *small.shape, kind=full), v(sp_size, *small.shape, kind=full),
        dma((5,)), dma((6,)), dma((4, 4)), dma((4, 4)), dma((4, 2)), dma((4, 2)), dma((4,)), dma((4,)),
        dma((sp_size - 1, 3)), dma((sp_size - 1, 3)), dma, dma, dma((3,)), dma((3,)), dma((sp_size - 1,)), dma((sp_size - 1,)),
    ]
    return pl.pallas_call(
        functools.partial(back_kernel, sp_size),
        out_shape=[jax.ShapeDtypeStruct((units, wide), low), jax.ShapeDtypeStruct((units, wide), low),
                   jax.ShapeDtypeStruct((rows, 3 * wide), low), jax.ShapeDtypeStruct((rows, wide), low),
                   jax.ShapeDtypeStruct(small.shape, full)],
        in_specs=[hbm] * 7 + [vmem], out_specs=[hbm] * 4 + [vmem],
        scratch_shapes=scratch,
        compiler_params=pltpu.CompilerParams(collective_id=1, has_side_effects=True, vmem_limit_bytes=67043328),
        cost_estimate=pl.CostEstimate(flops=26 * 10 ** 9, bytes_accessed=300 * 1000 * 1000, transcendentals=0),
        name="reduce_gradients",
    )(hidden, grad_out, grad_pre, mlp_in, attn_in, grad_proj, context, small)

def gather_plain(dp_size, sp_size, qkv_weight, out_weight, up_weight, down_weight):
    head_width = D // sp_size
    qkv_rows = qkv_weight.shape[0]
    qkv_slab = lax.all_to_all(
        qkv_weight.reshape(qkv_rows, 3, sp_size, head_width),
        "sp",
        split_axis=2,
        concat_axis=0,
        tiled=True,
    )
    qkv_own = lax.all_gather(
        qkv_slab.reshape(qkv_rows * sp_size, 3 * head_width), "dp", axis=0, tiled=True
    )
    up_own = lax.all_gather(up_weight, "dp", axis=0, tiled=True)
    down_own = lax.all_gather(down_weight, "dp", axis=0, tiled=True)
    out_blocks = lax.all_gather(out_weight, "dp", axis=0, tiled=True)
    out_own = lax.all_to_all(
        out_blocks.reshape(sp_size, dp_size // sp_size, qkv_rows, D),
        "sp",
        split_axis=0,
        concat_axis=2,
        tiled=True,
    ).reshape(head_width, D)
    return qkv_own, out_own, up_own, down_own


def reduce_plain(
    dp_size, sp_size, rows, hidden, grad_out, grad_pre, mlp_in, attn_in, grad_proj, context
):
    def scatter(left, right):
        return lax.psum_scatter(
            contract_rows(left, right).astype(jnp.bfloat16), "dp", scatter_dimension=0, tiled=True
        )

    grad_dense = lax.all_to_all(
        contract_rows(context, grad_out)
        .astype(jnp.bfloat16)
        .reshape(dp_size // sp_size, sp_size, rows, D),
        "sp",
        split_axis=1,
        concat_axis=0,
        tiled=True,
    ).reshape(dp_size * rows, D)
    grad_dense = lax.psum_scatter(grad_dense, "dp", scatter_dimension=0, tiled=True)
    grad_qkv = lax.all_to_all(
        scatter(attn_in, grad_proj).reshape(sp_size, rows, 3, 1, D // sp_size),
        "sp",
        split_axis=0,
        concat_axis=3,
        tiled=True,
    ).reshape(rows, 3 * D)
    return scatter(hidden, grad_out), scatter(grad_pre, mlp_in), grad_qkv, grad_dense


def body(
    tokens,
    lengths,
    cotangent,
    ln_gains,
    ln_shifts,
    qkv_weight,
    qkv_bias,
    out_weight,
    up_weight,
    up_bias,
    down_weight,
    out_bias,
):
    dp_size = lax.axis_size("dp")
    sp_size = lax.axis_size("sp")
    shard = lax.axis_index("sp")
    own_rows = tokens.shape[0]
    seq_rows = own_rows * sp_size
    head_width = D // sp_size
    length = lengths[0]
    low = jnp.bfloat16
    full = jnp.float32

    seq_tokens = lax.all_gather(tokens, "sp", axis=0, tiled=True)
    seq_cotangent = lax.all_gather(cotangent, "sp", axis=0, tiled=True)
    qkv_rows = qkv_weight.shape[0]
    per_shard = dp_size // sp_size
    square = dp_size == 8 and sp_size == 4
    gather = gather_weights if square else gather_plain
    qkv_own, out_own, up_own, down_own = gather(
        dp_size, sp_size, qkv_weight, out_weight, up_weight, down_weight
    )
    units = up_weight.shape[0]
    unit_bias = lax.dynamic_index_in_dim(
        up_bias.reshape(dp_size, sp_size, units), shard, 1, keepdims=False
    ).reshape(dp_size * units)
    bias_own = lax.dynamic_index_in_dim(
        qkv_bias.reshape(3, sp_size, head_width), shard, 1, keepdims=False
    ).reshape(3 * head_width)

    positions = jnp.arange(seq_rows, dtype=jnp.int32)
    cos_rows, sin_rows = rotary_rows(seq_rows)
    gains = ln_gains.astype(full)
    shifts = ln_shifts.astype(full)
    inputs = seq_tokens.astype(full)
    centre = jnp.mean(inputs, axis=-1, keepdims=True)
    centered = inputs - centre
    inverse = lax.rsqrt(jnp.mean(centered * centered, axis=-1, keepdims=True) + eps)
    normed = centered * inverse
    attn_in = (normed * gains[0] + shifts[0]).astype(low)
    mlp_in = (normed * gains[1] + shifts[1]).astype(low)
    row_valid = positions < length

    projected = jnp.dot(attn_in, qkv_own, preferred_element_type=full)
    queries, key_rows, values, context = attend_fwd(
        projected, bias_own.astype(full)[None], cos_rows, sin_rows, lengths
    )

    pre_act = contract_cols(mlp_in, up_own) + unit_bias.astype(full)
    hidden = gelu_value(pre_act).astype(low)
    partial_out = jnp.dot(hidden, down_own, preferred_element_type=full) + jnp.dot(
        context, out_own, preferred_element_type=full
    )
    reduced_out = lax.psum_scatter(
        partial_out.astype(low), "sp", scatter_dimension=0, tiled=True
    )
    seq_cotangent, _ = lax.optimization_barrier((seq_cotangent, partial_out))
    grad_out = jnp.where(row_valid[:, None], seq_cotangent, jnp.zeros_like(seq_cotangent))
    grad_hidden = contract_cols(grad_out, down_own)
    grad_pre = (grad_hidden * gelu_slope(pre_act)).astype(low)
    grad_mlp_in = jnp.dot(grad_pre, up_own, preferred_element_type=full)

    grad_context = contract_cols(grad_out, out_own).astype(low)
    grad_proj, grad_proj_sum = attend_bwd(
        queries, key_rows, values, grad_context, cos_rows, sin_rows, lengths
    )
    grad_attn_in = contract_cols(grad_proj, qkv_own)
    grad_hat = grad_attn_in * gains[0] + grad_mlp_in * gains[1]
    reduced_hat = lax.psum_scatter(
        grad_hat.astype(low), "sp", scatter_dimension=0, tiled=True
    )
    own_cotangent = lax.dynamic_slice_in_dim(grad_out, shard * own_rows, own_rows, 0).astype(full)
    spread_units = lax.dynamic_update_index_in_dim(
        jnp.zeros((dp_size, sp_size, units), full),
        jnp.sum(grad_pre, axis=0, dtype=full).reshape(dp_size, units),
        shard,
        1,
    ).reshape(-1)
    spread_bias = lax.dynamic_update_index_in_dim(
        jnp.zeros((3, sp_size, head_width), full),
        grad_proj_sum.reshape(3, head_width),
        shard,
        1,
    ).reshape(3, D)
    gain_grad = jnp.stack(
        [jnp.sum(grad_attn_in * normed, axis=0), jnp.sum(grad_mlp_in * normed, axis=0)]
    )
    shift_grad = jnp.stack([jnp.sum(grad_attn_in, axis=0), jnp.sum(grad_mlp_in, axis=0)])
    out_bias_part = jnp.sum(own_cotangent, axis=0)
    if square:
        small = jnp.concatenate(
            [
                piece.reshape(-1, 128)
                for piece in (gain_grad, shift_grad, spread_bias, spread_units, out_bias_part)
            ]
        )
        small, reduced_out = lax.optimization_barrier((small, reduced_out))
        grad_down, grad_up, grad_qkv, grad_dense, small = reduce_gradients(
            sp_size,
            qkv_rows,
            hidden,
            grad_out,
            grad_pre,
            mlp_in,
            attn_in,
            grad_proj,
            context,
            small,
        )
        reduced_hat, small = lax.optimization_barrier((reduced_hat, small))
        small = small.reshape(-1)
        ends = [2 * D, 4 * D, 7 * D, 7 * D + dp_size * sp_size * units]
        gain_total, shift_total, qkv_bias_total, unit_total, out_bias_total = jnp.split(small, ends)
        gain_total = gain_total.reshape(2, D)
        shift_total = shift_total.reshape(2, D)
        qkv_bias_total = qkv_bias_total.reshape(3, D)
    else:
        grad_down, grad_up, grad_qkv, grad_dense = reduce_plain(
            dp_size,
            sp_size,
            qkv_rows,
            hidden,
            grad_out,
            grad_pre,
            mlp_in,
            attn_in,
            grad_proj,
            context,
        )
        gain_total, shift_total, qkv_bias_total, unit_total, out_bias_total = lax.psum(
            (gain_grad, shift_grad, spread_bias, spread_units, out_bias_part), ("dp", "sp")
        )

    output = (
        tokens.astype(full) + reduced_out.astype(full) + out_bias.astype(full)
    ).astype(low)

    reduced_hat = reduced_hat.astype(full)
    own_inverse = lax.dynamic_slice_in_dim(inverse, shard * own_rows, own_rows, 0)
    own_normed = lax.dynamic_slice_in_dim(normed, shard * own_rows, own_rows, 0)
    grad_input = own_inverse * (
        reduced_hat
        - jnp.mean(reduced_hat, axis=-1, keepdims=True)
        - own_normed * jnp.mean(reduced_hat * own_normed, axis=-1, keepdims=True)
    )
    input_grad = (own_cotangent + grad_input).astype(low)
    return (
        output,
        input_grad,
        gain_total,
        shift_total,
        grad_qkv.astype(full),
        qkv_bias_total,
        grad_dense.astype(full),
        grad_up.astype(full),
        unit_total,
        grad_down.astype(full),
        out_bias_total,
    )


def solution(mesh):
    return jax.shard_map(
        body,
        mesh=mesh,
        in_specs=(
            P(("dp", "sp"), None),
            P("dp"),
            P(("dp", "sp"), None),
            P(),
            P(),
            P(("dp", "sp"), None),
            P(),
            P(("dp", "sp"), None),
            P(("dp", "sp"), None),
            P(),
            P(("dp", "sp"), None),
            P(),
        ),
        out_specs=(
            P(("dp", "sp"), None),
            P(("dp", "sp"), None),
            P(),
            P(),
            P(("dp", "sp"), None),
            P(),
            P(("dp", "sp"), None),
            P(("dp", "sp"), None),
            P(),
            P(("dp", "sp"), None),
            P(),
        ),
        check_vma=False,
    )
```

```python
import functools

import jax
import jax.numpy as jnp
from jax import lax
from jax.experimental import pallas as pl
from jax.experimental.pallas import tpu as pltpu
from jax.sharding import PartitionSpec as P

D = 2048
HEADS = 8
HEAD = 256
ROT = 64


eps = 1e-05
base_freq = 10000.0
root_half = 0.7071067811865476
inv_root_two_pi = 0.3989422804014327


def contract_rows(left, right):
    return lax.dot_general(
        left, right, (((0,), (0,)), ((), ())), preferred_element_type=jnp.float32
    )


def contract_cols(left, right):
    return lax.dot_general(
        left, right, (((1,), (1,)), ((), ())), preferred_element_type=jnp.float32
    )


def gelu_value(pre_act):
    return 0.5 * pre_act * (1.0 + lax.erf(pre_act * root_half))


def gelu_slope(pre_act):
    return 0.5 * (1.0 + lax.erf(pre_act * root_half)) + pre_act * inv_root_two_pi * jnp.exp(
        -0.5 * pre_act * pre_act
    )


BAND=256
def turn(x, cos_t, sin_t):
    first = x[:, :128]
    lane = lax.broadcasted_iota(jnp.int32, first.shape, 1)
    partner = jnp.where(lane < ROT // 2, pltpu.roll(first, 128 - ROT // 2, 1), pltpu.roll(first, ROT // 2, 1))
    return jnp.concatenate([first * cos_t + partner * sin_t, x[:, 128:]], axis=1)

def weights_of(q, k, start, length, scale):
    rows, cols = q.shape[0], k.shape[0]
    s = lax.dot_general(q, k, (((1,), (1,)), ((), ())), preferred_element_type=jnp.float32) * scale
    key = lax.broadcasted_iota(jnp.int32, (rows, cols), 1)
    query = start + lax.broadcasted_iota(jnp.int32, (rows, cols), 0)
    s = jnp.where((key <= query) & (key < length), s, -1e30)
    e = jnp.exp(s - jnp.max(s, axis=-1, keepdims=True))
    return e / jnp.sum(e, axis=-1, keepdims=True)

def fwd_kernel(scale, len_ref, pq, pk, pv, bq, bk, bv, cos_ref, sin_ref, q_ref, k_ref, v_ref, ctx_ref):
    length = len_ref[0]
    seq = pq.shape[0]
    cos_t, sin_t = cos_ref[...], sin_ref[...]
    q_ref[...] = turn(pq[...] + bq[...], cos_t, sin_t).astype(jnp.bfloat16)
    k_ref[...] = turn(pk[...] + bk[...], cos_t, sin_t).astype(jnp.bfloat16)
    v_ref[...] = (pv[...] + bv[...]).astype(jnp.bfloat16)
    for start in range(0, seq, BAND):
        end = start + BAND
        p = weights_of(q_ref[start:end, :], k_ref[:end, :], start, length, scale)
        ctx_ref[start:end, :] = jnp.dot(p.astype(jnp.bfloat16), v_ref[:end, :], preferred_element_type=jnp.float32).astype(jnp.bfloat16)

def attend_fwd(projected, bias, cos_t, sin_t, lengths):
    seq, width = projected.shape
    heads = width // 3 // HEAD
    col = lambda g: pl.BlockSpec((seq, HEAD), lambda h, *_, g=g: (0, g * heads + h))
    bcol = lambda g: pl.BlockSpec((1, HEAD), lambda h, *_, g=g: (0, g * heads + h))
    tab = pl.BlockSpec((seq, 128), lambda h, *_: (0, 0))
    out = pl.BlockSpec((seq, HEAD), lambda h, *_: (0, h))
    return pl.pallas_call(
        functools.partial(fwd_kernel, HEAD ** -0.5),
        grid_spec=pltpu.PrefetchScalarGridSpec(num_scalar_prefetch=1, grid=(heads,),
            in_specs=[col(0), col(1), col(2), bcol(0), bcol(1), bcol(2), tab, tab], out_specs=[out] * 4),
        out_shape=[jax.ShapeDtypeStruct((seq, heads * HEAD), jnp.bfloat16)] * 4,
        name="attend_fwd",
        cost_estimate=pl.CostEstimate(flops=heads * seq * seq * HEAD * 4, bytes_accessed=seq * width * 8, transcendentals=heads * seq * seq),
    )(lengths, projected, projected, projected, bias, bias, bias, cos_t, sin_t)

def bwd_kernel(scale, heads, len_ref, q_ref, k_ref, v_ref, g_ref, cos_ref, sin_ref, gp_ref, sum_ref, dk, dv, dq):
    length = len_ref[0]
    h = pl.program_id(0)
    seq = q_ref.shape[0]
    dk[...] = jnp.zeros_like(dk)
    dv[...] = jnp.zeros_like(dv)
    for start in range(0, seq, BAND):
        end = start + BAND
        q, g = q_ref[start:end, :], g_ref[start:end, :]
        k, v = k_ref[:end, :], v_ref[:end, :]
        p = weights_of(q, k, start, length, scale)
        gp = lax.dot_general(g, v, (((1,), (1,)), ((), ())), preferred_element_type=jnp.float32)
        ds = (p * (gp - jnp.sum(p * gp, axis=-1, keepdims=True))).astype(jnp.bfloat16)
        dq[start:end, :] = jnp.dot(ds, k, preferred_element_type=jnp.float32) * scale
        dk[:end, :] += lax.dot_general(ds, q, (((0,), (0,)), ((), ())), preferred_element_type=jnp.float32)
        dv[:end, :] += lax.dot_general(p.astype(jnp.bfloat16), g, (((0,), (0,)), ((), ())), preferred_element_type=jnp.float32)
    cos_t, sin_t = cos_ref[...], sin_ref[...]
    def back(x):
        return turn(x.astype(jnp.bfloat16).astype(jnp.float32), cos_t, -sin_t).astype(jnp.bfloat16)
    for g, piece in enumerate((back(dq[...]), back(dk[...] * scale), dv[...].astype(jnp.bfloat16))):
        at = pl.ds(pl.multiple_of((g * heads + h) * HEAD, HEAD), HEAD)
        gp_ref[:, at] = piece
        sum_ref[:, at] = jnp.sum(piece.astype(jnp.float32), axis=0, keepdims=True)

def attend_bwd(q, k, v, gctx, cos_t, sin_t, lengths):
    seq, width = q.shape
    heads = width // HEAD
    col = pl.BlockSpec((seq, HEAD), lambda h, *_: (0, h))
    tab = pl.BlockSpec((seq, 128), lambda h, *_: (0, 0))
    return pl.pallas_call(
        functools.partial(bwd_kernel, HEAD ** -0.5, heads),
        grid_spec=pltpu.PrefetchScalarGridSpec(num_scalar_prefetch=1, grid=(heads,),
            in_specs=[col] * 4 + [tab, tab],
            out_specs=[pl.BlockSpec((seq, 3 * width), lambda h, *_: (0, 0)), pl.BlockSpec((1, 3 * width), lambda h, *_: (0, 0))],
            scratch_shapes=[pltpu.VMEM((seq, HEAD), jnp.float32)] * 3),
        out_shape=[jax.ShapeDtypeStruct((seq, 3 * width), jnp.bfloat16), jax.ShapeDtypeStruct((1, 3 * width), jnp.float32)],
        name="attend_bwd",
        cost_estimate=pl.CostEstimate(flops=heads * seq * seq * HEAD * 10, bytes_accessed=seq * width * 20, transcendentals=heads * seq * seq),
    )(lengths, q, k, v, gctx, cos_t, sin_t)

def rotary_rows(seq):
    half = ROT // 2
    freq = 10000.0 ** (-jnp.arange(half, dtype=jnp.float32) * (2.0 / ROT))
    ang = jnp.arange(seq, dtype=jnp.int32).astype(jnp.float32)[:, None] * freq[None, :]
    c, s = jnp.cos(ang), jnp.sin(ang)
    rest = 128 - ROT
    return (jnp.concatenate([c, c, jnp.ones((seq, rest), jnp.float32)], 1), jnp.concatenate([-s, s, jnp.zeros((seq, rest), jnp.float32)], 1))

MESH = pl.DeviceIdType.MESH

def square_partners(dp):
    core, x, y = dp % 2, (dp // 2) % 2, dp // 4
    across_x, across_y = dp + 2 - 4 * x, dp + 4 - 8 * y
    first = across_x * (1 - core) + across_y * core
    second = across_y * (1 - core) + across_x * core
    return first, second, across_x + across_y - dp, 1 - 2 * core

class Hops:
    def __init__(self, count, dp, sp, source, result, send, recv):
        self.count, self.dp, self.sp, self.source, self.result = count, dp, sp, source, result
        self.send, self.recv, self.rows = send, recv, source.shape[0]

    def place(self, owner):
        return pl.ds(pl.multiple_of(owner * self.rows, self.rows), self.rows)

    def copy(self, way, step, owner, own):
        to = lax.rem(self.sp + (1 if way == 0 else self.count - 1), self.count)
        at = self.result.at[self.place(owner)]
        return pltpu.make_async_remote_copy(
            src_ref=self.source if own else at, dst_ref=at, send_sem=self.send.at[way, step],
            recv_sem=self.recv.at[way, step], device_id=(self.dp, to), device_id_type=MESH)

    def sends(self, way, step):
        if way == 0:
            return (self.sp >= step) & (self.sp < self.count - 1)
        return (self.sp < self.count - step) & (self.sp > 0)

    def receives(self, way, step):
        return self.sp >= step + 1 if way == 0 else self.sp < self.count - step - 1

    def owner(self, way, step):
        return self.sp - step if way == 0 else self.sp + step

    def start(self, way, step):
        @pl.when(self.sends(way, step))
        def _():
            self.copy(way, step, self.owner(way, step), step == 0).start()

    def begin(self):
        for way in (0, 1):
            self.start(way, 0)

    def forward(self, step):
        for way in (0, 1):
            @pl.when(self.receives(way, step - 1))
            def _():
                self.copy(way, step - 1, self.owner(way, step), False).wait_recv()
            if step < self.count - 1:
                self.start(way, step)

    def finish(self):
        for step in range(self.count - 1):
            for way in (0, 1):
                @pl.when(self.sends(way, step))
                def _():
                    self.copy(way, step, self.owner(way, step), step == 0).wait_send()


def gather_kernel(sp_size, qkv_ref, out_ref, up_ref, tok_ref, qkv_all, out_all, up_all, tok_all,
                  send_sem, recv_sem, slab_send, slab_recv, local_sem, turn_send, turn_recv, hop_send, hop_recv):
    dp, sp = lax.axis_index("dp"), lax.axis_index("sp")
    first, second, diagonal, flip = square_partners(dp)
    sibling = dp + flip
    per = 2
    pair, lane = dp // per, dp % per
    rows = qkv_ref.shape[0]
    wide = up_ref.shape[1]
    head_width = wide // sp_size
    turn_dp = sp * per + lane

    barrier = pltpu.get_barrier_semaphore()
    for other in (first, second, sibling):
        pl.semaphore_signal(barrier, inc=1, device_id=(other, sp), device_id_type=MESH)
    for step in range(1, sp_size):
        pl.semaphore_signal(barrier, inc=1, device_id=(dp, lax.rem(sp + step, sp_size)), device_id_type=MESH)
    @pl.when(pair != sp)
    def _():
        pl.semaphore_signal(barrier, inc=1, device_id=(turn_dp, pair), device_id_type=MESH)

    pl.semaphore_wait(barrier, 2 + sp_size + jnp.where(pair != sp, 1, 0))

    def slab_at(owner_sp):
        return pl.ds(pl.multiple_of((dp * sp_size + owner_sp) * rows, rows), rows)

    def slab_copy(step, part):
        there = lax.rem(sp + step, sp_size)
        return pltpu.make_async_remote_copy(
            src_ref=qkv_ref.at[:, pl.ds(pl.multiple_of(part * wide + there * head_width, head_width), head_width)],
            dst_ref=qkv_all.at[slab_at(sp), pl.ds(part * head_width, head_width)],
            send_sem=slab_send.at[step - 1, part], recv_sem=slab_recv.at[step - 1, part],
            device_id=(dp, there), device_id_type=MESH)

    def slab_arrival(step, part):
        origin = lax.rem(sp + sp_size - step, sp_size)
        return pltpu.make_async_remote_copy(
            src_ref=qkv_ref.at[:, pl.ds(part * head_width, head_width)],
            dst_ref=qkv_all.at[slab_at(origin), pl.ds(part * head_width, head_width)],
            send_sem=slab_send.at[step - 1, part], recv_sem=slab_recv.at[step - 1, part],
            device_id=(dp, origin), device_id_type=MESH)

    units = up_ref.shape[0]
    slab = rows * sp_size

    def plain(height):
        return lambda owner: pl.ds(pl.multiple_of(owner * height, height), height)

    def turned(owner):
        return pl.ds(pl.multiple_of((owner % per) * slab + (owner // per) * rows, rows), rows)

    arrays = ((up_ref, up_all, plain(units)), (None, qkv_all, plain(slab)), (None, out_all, turned))
    hops = Hops(sp_size, dp, sp, tok_ref, tok_all, hop_send, hop_recv)

    def copy(index, message, block, target):
        source, result, place = arrays[index]
        at = result.at[place(block)]
        src = at
        if source is not None and message < 3:
            src = source
        return pltpu.make_async_remote_copy(
            src_ref=src, dst_ref=at, send_sem=send_sem.at[index, message], recv_sem=recv_sem.at[index, message],
            device_id=(target, sp), device_id_type=MESH)

    sends = ((dp, first), (dp, second), (dp, sibling), (first, second), (first, sibling), (second, sibling), (diagonal, sibling))
    arrivals = (first, second, sibling, diagonal, second + flip, first + flip, diagonal + flip)

    def start(index, message):
        copy(index, message, *sends[message]).start()

    def arrived(index, message):
        copy(index, message, arrivals[message], dp).wait_recv()

    def own(index):
        for message in (0, 1, 2):
            start(index, message)

    def keep(source, target, which):
        return pltpu.make_async_copy(source, target, local_sem.at[which])

    hops.begin()
    own(0)
    for step in range(1, sp_size):
        for part in range(3):
            slab_copy(step, part).start()

    out_place = out_all.at[turned(turn_dp)]
    my_out_place = out_all.at[turned(dp)]
    turn = pltpu.make_async_remote_copy(
        src_ref=out_ref, dst_ref=out_place, send_sem=turn_send, recv_sem=turn_recv,
        device_id=(turn_dp, pair), device_id_type=MESH)
    turn_arrival = pltpu.make_async_remote_copy(
        src_ref=out_ref, dst_ref=my_out_place, send_sem=turn_send, recv_sem=turn_recv,
        device_id=(turn_dp, pair), device_id_type=MESH)

    @pl.when(pair != sp)
    def _():
        turn.start()

    local = [keep(tok_ref, tok_all.at[hops.place(sp)], 0), keep(up_ref, up_all.at[plain(units)(dp)], 1)]
    for part in range(3):
        local.append(keep(
            qkv_ref.at[:, pl.ds(pl.multiple_of(part * wide + sp * head_width, head_width), head_width)],
            qkv_all.at[slab_at(sp), pl.ds(part * head_width, head_width)], 2 + part))
    for c in local:
        c.start()

    def onward(index):
        arrived(index, 0)
        start(index, 3)
        start(index, 4)
        arrived(index, 1)
        start(index, 5)

    onward(0)
    hops.forward(1)

    @pl.when(pair == sp)
    def _():
        c = keep(out_ref, my_out_place, 5)
        c.start()
        c.wait()

    @pl.when(pair != sp)
    def _():
        turn_arrival.wait_recv()

    own(2)
    for step in range(1, sp_size):
        for part in range(3):
            slab_arrival(step, part).wait_recv()
    for c in local:
        c.wait()
    own(1)
    arrived(0, 3)
    start(0, 6)
    onward(2)
    hops.forward(2)
    onward(1)
    for index in (2, 1):
        arrived(index, 3)
        start(index, 6)
    hops.forward(3)
    for index in range(3):
        for message in (2, 4, 5, 6):
            arrived(index, message)
    for index in range(3):
        for message in range(7):
            copy(index, message, *sends[message]).wait_send()
    for step in range(1, sp_size):
        for part in range(3):
            slab_copy(step, part).wait_send()

    @pl.when(pair != sp)
    def _():
        turn.wait_send()

    hops.finish()

def gather_weights(dp_size, sp_size, qkv_weight, out_weight, up_weight, tokens):
    rows, wide = out_weight.shape
    units = up_weight.shape[0]
    low = jnp.bfloat16
    hbm = pl.BlockSpec(memory_space=pltpu.HBM)
    vmem = pl.BlockSpec(memory_space=pltpu.VMEM)
    dma = pltpu.SemaphoreType.DMA
    return pl.pallas_call(
        functools.partial(gather_kernel, sp_size),
        out_shape=[jax.ShapeDtypeStruct((rows * sp_size * dp_size, 3 * wide // sp_size), low),
                   jax.ShapeDtypeStruct((rows * dp_size, wide), low),
                   jax.ShapeDtypeStruct((units * dp_size, wide), low),
                   jax.ShapeDtypeStruct((tokens.shape[0] * sp_size, wide), low)],
        in_specs=[vmem] * 4, out_specs=[hbm] * 4,
        scratch_shapes=[dma((3, 7)), dma((3, 7)), dma((sp_size - 1, 3)), dma((sp_size - 1, 3)), dma((6,)), dma, dma,
                        dma((2, sp_size)), dma((2, sp_size))],
        compiler_params=pltpu.CompilerParams(collective_id=0, has_side_effects=True),
        cost_estimate=pl.CostEstimate(flops=0, bytes_accessed=250 * 1000 * 1000, transcendentals=0),
        name="gather_weights",
    )(qkv_weight, out_weight, up_weight, tokens)

def front_kernel(len_ref, tok_hbm, qkv_hbm, up_hbm, down_ref, gain_ref, shift_ref, qkv_bias_ref, unit_bias_ref,
                 cos_ref, sin_ref,
                 down_all, attn_out, mlp_out, hidden_out, pre_out, q_ref, k_ref, v_ref, ctx_ref,
                 tok, attn, mlp, qkv_w, up_w, hidden, pre,
                 send_sem, recv_sem, load_sem, store_sem, hidden_sem, pre_sem, keep_sem):
    full, low = jnp.float32, jnp.bfloat16
    dp, sp = lax.axis_index("dp"), lax.axis_index("sp")
    first, second, diagonal, flip = square_partners(dp)
    sibling = dp + flip
    seq, wide = tok.shape
    units = down_ref.shape[0]
    width = q_ref.shape[1]
    scale = HEAD ** -0.5
    band = 256

    def load(source, target, which):
        return pltpu.make_async_copy(source, target, load_sem.at[which])

    token_loads = [load(tok_hbm.at[pl.ds(r, band)], tok.at[pl.ds(r, band)], r // band) for r in range(0, seq, band)]
    loads = token_loads + [load(qkv_hbm, qkv_w, seq // band), load(up_hbm, up_w, seq // band + 1)]
    for c in loads:
        c.start()

    barrier = pltpu.get_barrier_semaphore()
    for other in (first, second, sibling):
        pl.semaphore_signal(barrier, inc=1, device_id=(other, sp), device_id_type=MESH)
    pl.semaphore_wait(barrier, 3)

    sends = ((dp, first), (dp, second), (dp, sibling), (first, second), (first, sibling), (second, sibling), (diagonal, sibling))
    arrivals = (first, second, sibling, diagonal, second + flip, first + flip, diagonal + flip)

    def copy(message, block, target):
        at = down_all.at[pl.ds(pl.multiple_of(block * units, units), units)]
        return pltpu.make_async_remote_copy(
            src_ref=down_ref if message < 3 else at, dst_ref=at,
            send_sem=send_sem.at[message], recv_sem=recv_sem.at[message],
            device_id=(target, sp), device_id_type=MESH)

    def start(message):
        copy(message, *sends[message]).start()

    def arrived(message):
        copy(message, arrivals[message], sibling).wait_recv()

    for message in (0, 1, 2):
        start(message)
    keep = pltpu.make_async_copy(down_ref, down_all.at[pl.ds(pl.multiple_of(dp * units, units), units)], keep_sem)
    keep.start()

    def normalize(i, carry):
        at = pl.ds(pl.multiple_of(i * 32, 32), 32)
        rows = tok[at, :].astype(full)
        centered = rows - jnp.mean(rows, axis=-1, keepdims=True)
        normed = centered * lax.rsqrt(jnp.mean(centered * centered, axis=-1, keepdims=True) + eps)
        attn[at, :] = (normed * gain_ref[0:1, :] + shift_ref[0:1, :]).astype(low)
        mlp[at, :] = (normed * gain_ref[1:2, :] + shift_ref[1:2, :]).astype(low)
        return carry

    for part, c in enumerate(token_loads):
        c.wait()
        lax.fori_loop(part * band // 32, (part + 1) * band // 32, normalize, 0)
    stores = [pltpu.make_async_copy(attn, attn_out, store_sem.at[0]), pltpu.make_async_copy(mlp, mlp_out, store_sem.at[1])]
    for c in stores:
        c.start()
    loads[-2].wait()

    def head(h, carry):
        lanes = pl.ds(pl.multiple_of(h * HEAD, HEAD), HEAD)

        def project(r, carry):
            at = pl.ds(pl.multiple_of(r * band, band), band)
            cos_t, sin_t = cos_ref[at, :], sin_ref[at, :]
            for part, target in enumerate((q_ref, k_ref, v_ref)):
                cols = pl.ds(pl.multiple_of(part * width + h * HEAD, HEAD), HEAD)
                value = jnp.dot(attn[at, :], qkv_w[:, cols], preferred_element_type=full) + qkv_bias_ref[:, cols]
                if part < 2:
                    value = turn(value, cos_t, sin_t)
                target[at, lanes] = value.astype(low)
            return carry
        lax.fori_loop(0, seq // band, project, 0)
        for begin in range(0, seq, band):
            end = begin + band
            p = weights_of(q_ref[begin:end, lanes], k_ref[:end, lanes], begin, len_ref[0], scale)
            ctx_ref[begin:end, lanes] = jnp.dot(p.astype(low), v_ref[:end, lanes], preferred_element_type=full).astype(low)
        return carry

    lax.fori_loop(0, width // HEAD, head, 0)
    arrived(0)
    start(3)
    start(4)
    arrived(1)
    start(5)
    loads[-1].wait()

    def hidden_store(block, slot):
        return pltpu.make_async_copy(hidden.at[slot], hidden_out.at[:, pl.ds(pl.multiple_of(block * units, units), units)],
                                     hidden_sem.at[slot])

    def pre_store(block, slot):
        return pltpu.make_async_copy(pre.at[slot], pre_out.at[:, pl.ds(pl.multiple_of(block * units, units), units)],
                                     pre_sem.at[slot])

    def unit_block(block, carry):
        slot = lax.rem(block, 2)

        @pl.when(block >= 2)
        def _():
            hidden_store(block - 2, slot).wait()
            pre_store(block - 2, slot).wait()

        of = pl.ds(pl.multiple_of(block * units, units), units)

        def row_band(r, carry):
            at = pl.ds(pl.multiple_of(r * band, band), band)
            value = lax.dot_general(mlp[at, :], up_w[of, :], (((1,), (1,)), ((), ())), preferred_element_type=full)
            value = value + unit_bias_ref[:, of]
            pre[slot, at, :] = value
            hidden[slot, at, :] = gelu_value(value).astype(low)
            return carry
        lax.fori_loop(0, seq // band, row_band, 0)
        hidden_store(block, slot).start()
        pre_store(block, slot).start()
        return carry

    blocks = up_w.shape[0] // units
    lax.fori_loop(0, blocks // 2, unit_block, 0)
    arrived(3)
    start(6)
    lax.fori_loop(blocks // 2, blocks, unit_block, 0)
    for block in (blocks - 2, blocks - 1):
        hidden_store(block, block % 2).wait()
        pre_store(block, block % 2).wait()
    for c in stores:
        c.wait()
    keep.wait()
    for message in (2, 4, 5, 6):
        arrived(message)
    for message in range(7):
        copy(message, *sends[message]).wait_send()

def front(tokens, qkv_own, up_own, down_weight, gains, shifts, qkv_bias, unit_bias, cos_t, sin_t, lengths, dp_size):
    seq, wide = tokens.shape
    units = down_weight.shape[0]
    width = qkv_own.shape[1] // 3
    all_units = up_own.shape[0]
    full, low = jnp.float32, jnp.bfloat16
    hbm = pl.BlockSpec(memory_space=pltpu.HBM)
    vmem = pl.BlockSpec(memory_space=pltpu.VMEM)
    dma = pltpu.SemaphoreType.DMA
    shape = jax.ShapeDtypeStruct
    return pl.pallas_call(
        front_kernel,
        out_shape=[shape((units * dp_size, wide), low), shape((seq, wide), low), shape((seq, wide), low),
                   shape((seq, all_units), low), shape((seq, all_units), full)] + [shape((seq, width), low)] * 4,
        in_specs=[pl.BlockSpec(memory_space=pltpu.SMEM), hbm, hbm, hbm] + [vmem] * 7,
        out_specs=[hbm] * 5 + [vmem] * 4,
        scratch_shapes=[pltpu.VMEM((seq, wide), low)] * 3 + [
            pltpu.VMEM(qkv_own.shape, low), pltpu.VMEM(up_own.shape, low),
            pltpu.VMEM((2, seq, units), low), pltpu.VMEM((2, seq, units), full),
            dma((7,)), dma((7,)), dma((seq // 256 + 2,)), dma((2,)), dma((2,)), dma((2,)), dma],
        compiler_params=pltpu.CompilerParams(collective_id=2, has_side_effects=True, vmem_limit_bytes=60 << 20),
        cost_estimate=pl.CostEstimate(flops=16 * 10 ** 9, bytes_accessed=60 * 1000 * 1000, transcendentals=0),
        name="front",
    )(lengths, tokens, qkv_own, up_own, down_weight, gains, shifts, qkv_bias, unit_bias, cos_t, sin_t)

CHUNK = 512


def back_kernel(sp_size, hidden_hbm, cot_hbm, pre_hbm, mlp_hbm, attn_hbm, proj_hbm, ctx_hbm, small_ref,
                down_out, up_out, qkv_out, dense_out, small_out,
                left_a, right_a, left_b, right_b, ctx, lent,
                down_sum, up_sum, qkv_sum, dense_sum, down_sib, up_sib, qkv_sib, dense_sib,
                down_one, up_one, qkv_one, dense_one, down_two, up_two, qkv_two, dense_two, dense_part,
                small_acc, small_in, small_z,
                load_sem, store_sem, sib_send, sib_recv, one_send, one_recv, two_send, two_recv,
                slab_send, slab_recv, turn_send, turn_recv, small_send, small_recv, z_send, z_recv):
    dp, sp = lax.axis_index("dp"), lax.axis_index("sp")
    full, low = jnp.float32, jnp.bfloat16
    core, chip = dp % 2, dp // 2
    x, y = chip % 2, chip // 2
    per = 2
    pair, lane = dp // per, dp % per
    turn_dp = sp * per + lane
    sibling = dp + 1 - 2 * core
    across_x, across_y = dp + 2 - 4 * x, dp + 4 - 8 * y
    first = across_y * (1 - core) + across_x * core
    second = across_x * (1 - core) + across_y * core
    first_mask, second_mask = 2 - core, 1 + core
    units = down_sum.shape[1]
    slab_width = qkv_sum.shape[2]
    head_width = slab_width // 3
    rows = dense_one.shape[1]
    wide = right_a.shape[1]

    def chip_of(mask):
        return lax.rem(x + lax.rem(mask, 2), 2) + 2 * lax.rem(y + mask // 2, 2)

    def load(source, target, which):
        return pltpu.make_async_copy(source, target, load_sem.at[which])

    loads = [load(attn_hbm, left_a, 0), load(proj_hbm, right_a.at[:, :slab_width], 1), load(cot_hbm, right_b, 2),
             load(ctx_hbm, ctx, 3), load(hidden_hbm, left_b, 4)]
    for c in loads:
        c.start()

    barrier = pltpu.get_barrier_semaphore()
    for other in (first, second, sibling):
        pl.semaphore_signal(barrier, inc=1, device_id=(other, sp), device_id_type=MESH)
    for step in range(1, sp_size):
        pl.semaphore_signal(barrier, inc=1, device_id=(dp, lax.rem(sp + step, sp_size)), device_id_type=MESH)

    @pl.when(pair != sp)
    def _():
        pl.semaphore_signal(barrier, inc=1, device_id=(turn_dp, pair), device_id_type=MESH)

    pl.semaphore_wait(barrier, 2 + sp_size + jnp.where(pair != sp, 1, 0))

    def remote(source, target, send, recv, device):
        return pltpu.make_async_remote_copy(
            src_ref=source, dst_ref=target, send_sem=send, recv_sem=recv,
            device_id=device, device_id_type=MESH)

    def small_copy(stage):
        return remote(small_ref if stage == 0 else small_acc.at[stage - 1], small_in.at[stage],
                      small_send.at[stage], small_recv.at[stage], ((sibling, across_x, across_y)[stage], sp))

    def small_step(stage):
        small_copy(stage).wait_recv()
        before = small_ref[...] if stage == 0 else small_acc[stage - 1]
        small_acc[stage] = before + small_in[stage]

    def z_copy(step):
        return remote(small_acc.at[2], small_z.at[sp], z_send.at[step - 1], z_recv.at[step - 1],
                      (dp, lax.rem(sp + step, sp_size)))

    def z_arrival(step):
        origin = lax.rem(sp + sp_size - step, sp_size)
        return remote(small_acc.at[2], small_z.at[origin], z_send.at[step - 1], z_recv.at[step - 1], (dp, origin))

    small_copy(0).start()

    class Wide:
        def __init__(self, index, left, right, width, sums, sib, one, two):
            self.index, self.left, self.right, self.width = index, left, right, width
            self.sums, self.sib, self.one, self.two = sums, sib, one, two

        def product(self, block, store):
            at = pl.ds(pl.multiple_of(block * units, units), units)

            def columns(part, carry):
                to = pl.ds(pl.multiple_of(part * CHUNK, CHUNK), CHUNK)
                store(to, lax.dot_general(
                    self.left[:, at], self.right[:, to], (((0,), (0,)), ((), ())),
                    preferred_element_type=full))
                return carry
            lax.fori_loop(0, self.width // CHUNK, columns, 0)

        def lend(self, slot):
            return lent.at[slot, :, :self.width]

        def sib_copy(self, slot):
            place = chip_of(3 - slot)
            return remote(self.lend(slot), self.sib.at[place], sib_send.at[self.index, slot],
                          sib_recv.at[self.index, slot], (sibling, sp))

        def for_sibling(self, previous):
            def step(slot, carry):
                if previous is not None:
                    previous.sib_copy(slot).wait_send()
                block = chip_of(3 - slot) * 2 + 1 - core

                def store(to, total):
                    lent[slot, :, to] = total.astype(low)
                self.product(block, store)
                self.sib_copy(slot).start()
                return carry
            lax.fori_loop(0, 4, step, 0)

        def own(self, mask, slot):
            place = chip_of(mask)
            self.sib_copy(slot).wait_recv()

            def store(to, total):
                self.sums[mask, :, to] = (total + self.sib[place, :, to].astype(full)).astype(low)
            self.product(place * 2 + core, store)

        def first_copy(self, slot):
            mask = 3 - slot * (1 + core)
            return remote(self.sums.at[mask], self.one.at[slot], one_send.at[self.index, slot],
                          one_recv.at[self.index, slot], (first, sp))

        def for_self(self):
            def leave(slot, carry):
                mask = 3 - slot * (1 + core)
                self.own(mask, 3 - mask)
                self.first_copy(slot).start()
                return carry
            lax.fori_loop(0, 2, leave, 0)

            def stay(slot, carry):
                mask = second_mask * (1 - slot)
                self.own(mask, 3 - mask)
                return carry
            lax.fori_loop(0, 2, stay, 0)

        def second_copy(self):
            return remote(self.sums.at[second_mask], self.two, two_send.at[self.index],
                          two_recv.at[self.index], (second, sp))

        def block(self, mask):
            return self.sums.at[mask]

    class Dense(Wide):
        def sib_copy(self, slot):
            return remote(dense_part.at[0], self.sib, sib_send.at[self.index, 0],
                          sib_recv.at[self.index, 0], (sibling, sp))

        def for_sibling(self, previous):
            def store(to, total):
                dense_part[0, :, to] = total.astype(low)
            self.product(1 - core, store)
            self.sib_copy(0).start()

        def block(self, mask):
            return self.sums.at[pl.ds(pl.multiple_of(chip_of(mask) * rows, rows), rows)]

        def first_copy(self, slot):
            mask = 3 - slot * (1 + core)
            return remote(self.block(mask), self.one.at[slot], one_send.at[self.index, slot],
                          one_recv.at[self.index, slot], (first, sp))

        def for_self(self):
            self.sib_copy(0).wait_recv()

            def store(to, total):
                self.sums[:, to] = (total + self.sib[:, to].astype(full)).astype(low)
            self.product(core, store)
            for slot in (0, 1):
                self.first_copy(slot).start()

        def second_copy(self):
            return remote(self.block(second_mask), self.two, two_send.at[self.index],
                          two_recv.at[self.index], (second, sp))

    qkv = Wide(0, left_a, right_a, slab_width, qkv_sum, qkv_sib, qkv_one, qkv_two)
    dense = Dense(1, ctx, right_b, wide, dense_sum, dense_sib, dense_one, dense_two)
    down = Wide(2, left_b, right_b, wide, down_sum, down_sib, down_one, down_two)
    up = Wide(3, left_a, right_a, wide, up_sum, up_sib, up_one, up_two)

    def add_into(target, *others):
        height = target.shape[0]
        step_rows = 32

        def step(i, carry):
            at = pl.ds(pl.multiple_of(i * step_rows, step_rows), step_rows)
            total = target[at, :].astype(full)
            for other in others:
                total = total + other[at, :].astype(full)
            target[at, :] = total.astype(low)
            return carry
        lax.fori_loop(0, height // step_rows, step, 0)

    def onward(array):
        array.first_copy(0).wait_recv()
        add_into(array.block(second_mask), array.one.at[0])
        array.second_copy().start()

    def finish(array):
        array.first_copy(1).wait_recv()
        array.second_copy().wait_recv()
        add_into(array.block(0), array.one.at[1], array.two)

    def turn(target):
        return remote(dense.block(0), target, turn_send, turn_recv, (turn_dp, pair))

    def slab_rows(owner):
        return pl.ds(pl.multiple_of(owner * rows, rows), rows)

    def slab_columns(part, owner):
        return pl.ds(pl.multiple_of(part * wide + owner * head_width, head_width), head_width)

    def slab_copy(step, part, origin, there):
        return remote(qkv_sum.at[0, slab_rows(there), pl.ds(part * head_width, head_width)],
                      qkv_out.at[:, slab_columns(part, origin)],
                      slab_send.at[step - 1, part], slab_recv.at[step - 1, part], (dp, there))

    stores = []

    def store(source, target):
        c = pltpu.make_async_copy(source, target, store_sem.at[len(stores)])
        c.start()
        stores.append(c)

    loads[0].wait()
    loads[1].wait()
    qkv.for_sibling(None)
    small_step(0)
    small_copy(1).start()
    qkv.for_self()
    late = [load(pre_hbm, left_a, 0), load(mlp_hbm, right_a, 1)]
    for c in late:
        c.start()
    loads[2].wait()
    loads[3].wait()
    dense.for_sibling(None)
    small_step(1)
    small_copy(2).start()
    dense.for_self()
    loads[4].wait()
    down.for_sibling(qkv)
    onward(qkv)
    small_step(2)
    for step in range(1, sp_size):
        z_copy(step).start()
    small_z[sp] = small_acc[2]
    down.for_self()
    onward(dense)
    for c in late:
        c.wait()
    up.for_sibling(down)
    finish(qkv)
    for step in range(1, sp_size):
        for part in range(3):
            slab_copy(step, part, sp, lax.rem(sp + step, sp_size)).start()
    for part in range(3):
        store(qkv_sum.at[0, slab_rows(sp), pl.ds(part * head_width, head_width)], qkv_out.at[:, slab_columns(part, sp)])
    up.for_self()
    onward(down)
    finish(dense)

    @pl.when(pair != sp)
    def _():
        turn(dense_out).start()

    @pl.when(pair == sp)
    def _():
        c = pltpu.make_async_copy(dense.block(0), dense_out, store_sem.at[5])
        c.start()
        c.wait()

    for step in range(1, sp_size):
        z_arrival(step).wait_recv()
    total = small_z[0]
    for place in range(1, sp_size):
        total = total + small_z[place]
    small_out[...] = total
    onward(up)
    finish(down)
    store(down.block(0), down_out)
    for step in range(1, sp_size):
        for part in range(3):
            slab_copy(step, part, lax.rem(sp + sp_size - step, sp_size), sp).wait_recv()

    @pl.when(pair != sp)
    def _():
        turn(dense_out).wait_recv()
        turn(dense_out).wait_send()

    for slot in range(4):
        up.sib_copy(slot).wait_send()
    dense.sib_copy(0).wait_send()
    for array in (qkv, dense, down, up):
        for slot in (0, 1):
            array.first_copy(slot).wait_send()
        array.second_copy().wait_send()
    for stage in range(3):
        small_copy(stage).wait_send()
    for step in range(1, sp_size):
        z_copy(step).wait_send()
        for part in range(3):
            slab_copy(step, part, sp, lax.rem(sp + step, sp_size)).wait_send()
    finish(up)
    store(up.block(0), up_out)
    for c in stores:
        c.wait()

def reduce_gradients(sp_size, rows, hidden, grad_out, grad_pre, mlp_in, attn_in, grad_proj, context, small):
    seq, wide = mlp_in.shape
    slab_width = grad_proj.shape[1]
    units = 4 * rows
    full, low = jnp.float32, jnp.bfloat16
    hbm = pl.BlockSpec(memory_space=pltpu.HBM)
    vmem = pl.BlockSpec(memory_space=pltpu.VMEM)
    dma = pltpu.SemaphoreType.DMA
    def v(*shape, kind=low):
        return pltpu.VMEM(shape, kind)
    scratch = [
        v(seq, wide), v(seq, wide), v(seq, wide), v(seq, wide), v(seq, context.shape[1]), v(4, units, wide),
        v(4, units, wide), v(4, units, wide), v(4, units, slab_width), v(4 * rows, wide),
        v(4, units, wide), v(4, units, wide), v(4, units, slab_width), v(4 * rows, wide),
        v(2, units, wide), v(2, units, wide), v(2, units, slab_width), v(2, rows, wide),
        v(units, wide), v(units, wide), v(units, slab_width), v(rows, wide),
        v(1, 4 * rows, wide),
        v(3, *small.shape, kind=full), v(3, *small.shape, kind=full), v(sp_size, *small.shape, kind=full),
        dma((5,)), dma((6,)), dma((4, 4)), dma((4, 4)), dma((4, 2)), dma((4, 2)), dma((4,)), dma((4,)),
        dma((sp_size - 1, 3)), dma((sp_size - 1, 3)), dma, dma, dma((3,)), dma((3,)), dma((sp_size - 1,)), dma((sp_size - 1,)),
    ]
    return pl.pallas_call(
        functools.partial(back_kernel, sp_size),
        out_shape=[jax.ShapeDtypeStruct((units, wide), low), jax.ShapeDtypeStruct((units, wide), low),
                   jax.ShapeDtypeStruct((rows, 3 * wide), low), jax.ShapeDtypeStruct((rows, wide), low),
                   jax.ShapeDtypeStruct(small.shape, full)],
        in_specs=[hbm] * 7 + [vmem], out_specs=[hbm] * 4 + [vmem],
        scratch_shapes=scratch,
        compiler_params=pltpu.CompilerParams(collective_id=1, has_side_effects=True, vmem_limit_bytes=67043328),
        cost_estimate=pl.CostEstimate(flops=26 * 10 ** 9, bytes_accessed=300 * 1000 * 1000, transcendentals=0),
        name="reduce_gradients",
    )(hidden, grad_out, grad_pre, mlp_in, attn_in, grad_proj, context, small)

def gather_plain(dp_size, sp_size, qkv_weight, out_weight, up_weight, down_weight):
    head_width = D // sp_size
    qkv_rows = qkv_weight.shape[0]
    qkv_slab = lax.all_to_all(
        qkv_weight.reshape(qkv_rows, 3, sp_size, head_width),
        "sp",
        split_axis=2,
        concat_axis=0,
        tiled=True,
    )
    qkv_own = lax.all_gather(
        qkv_slab.reshape(qkv_rows * sp_size, 3 * head_width), "dp", axis=0, tiled=True
    )
    up_own = lax.all_gather(up_weight, "dp", axis=0, tiled=True)
    down_own = lax.all_gather(down_weight, "dp", axis=0, tiled=True)
    out_blocks = lax.all_gather(out_weight, "dp", axis=0, tiled=True)
    out_own = lax.all_to_all(
        out_blocks.reshape(sp_size, dp_size // sp_size, qkv_rows, D),
        "sp",
        split_axis=0,
        concat_axis=2,
        tiled=True,
    ).reshape(head_width, D)
    return qkv_own, out_own, up_own, down_own


def reduce_plain(
    dp_size, sp_size, rows, hidden, grad_out, grad_pre, mlp_in, attn_in, grad_proj, context
):
    def scatter(left, right):
        return lax.psum_scatter(
            contract_rows(left, right).astype(jnp.bfloat16), "dp", scatter_dimension=0, tiled=True
        )

    grad_dense = lax.all_to_all(
        contract_rows(context, grad_out)
        .astype(jnp.bfloat16)
        .reshape(dp_size // sp_size, sp_size, rows, D),
        "sp",
        split_axis=1,
        concat_axis=0,
        tiled=True,
    ).reshape(dp_size * rows, D)
    grad_dense = lax.psum_scatter(grad_dense, "dp", scatter_dimension=0, tiled=True)
    grad_qkv = lax.all_to_all(
        scatter(attn_in, grad_proj).reshape(sp_size, rows, 3, 1, D // sp_size),
        "sp",
        split_axis=0,
        concat_axis=3,
        tiled=True,
    ).reshape(rows, 3 * D)
    return scatter(hidden, grad_out), scatter(grad_pre, mlp_in), grad_qkv, grad_dense


def body(
    tokens,
    lengths,
    cotangent,
    ln_gains,
    ln_shifts,
    qkv_weight,
    qkv_bias,
    out_weight,
    up_weight,
    up_bias,
    down_weight,
    out_bias,
):
    dp_size = lax.axis_size("dp")
    sp_size = lax.axis_size("sp")
    shard = lax.axis_index("sp")
    own_rows = tokens.shape[0]
    seq_rows = own_rows * sp_size
    head_width = D // sp_size
    length = lengths[0]
    low = jnp.bfloat16
    full = jnp.float32

    qkv_rows = qkv_weight.shape[0]
    units = up_weight.shape[0]
    square = dp_size == 8 and sp_size == 4
    unit_bias = (
        lax.dynamic_index_in_dim(
            up_bias.reshape(dp_size, sp_size, units), shard, 1, keepdims=False
        )
        .reshape(dp_size * units)
        .astype(full)
    )
    bias_own = (
        lax.dynamic_index_in_dim(
            qkv_bias.reshape(3, sp_size, head_width), shard, 1, keepdims=False
        )
        .reshape(1, 3 * head_width)
        .astype(full)
    )
    positions = jnp.arange(seq_rows, dtype=jnp.int32)
    cos_rows, sin_rows = rotary_rows(seq_rows)
    gains = ln_gains.astype(full)
    shifts = ln_shifts.astype(full)
    row_valid = positions < length
    if square:
        qkv_own, out_own, up_own, seq_tokens = gather_weights(
            dp_size, sp_size, qkv_weight, out_weight, up_weight, tokens
        )
        cotangent, qkv_own = lax.optimization_barrier((cotangent, qkv_own))
    else:
        seq_tokens = lax.all_gather(tokens, "sp", axis=0, tiled=True)
        qkv_own, out_own, up_own, down_own = gather_plain(
            dp_size, sp_size, qkv_weight, out_weight, up_weight, down_weight
        )
    seq_cotangent = lax.all_gather(cotangent, "sp", axis=0, tiled=True)
    inputs = seq_tokens.astype(full)
    centre = jnp.mean(inputs, axis=-1, keepdims=True)
    centered = inputs - centre
    inverse = lax.rsqrt(jnp.mean(centered * centered, axis=-1, keepdims=True) + eps)
    normed = centered * inverse
    if square:
        down_own, attn_in, mlp_in, hidden, pre_act, queries, key_rows, values, context = front(
            seq_tokens,
            qkv_own,
            up_own,
            down_weight,
            gains,
            shifts,
            bias_own,
            unit_bias[None],
            cos_rows,
            sin_rows,
            lengths,
            dp_size,
        )
    else:
        attn_in = (normed * gains[0] + shifts[0]).astype(low)
        mlp_in = (normed * gains[1] + shifts[1]).astype(low)
        projected = jnp.dot(attn_in, qkv_own, preferred_element_type=full)
        queries, key_rows, values, context = attend_fwd(
            projected, bias_own, cos_rows, sin_rows, lengths
        )
        pre_act = contract_cols(mlp_in, up_own) + unit_bias
        hidden = gelu_value(pre_act).astype(low)
    partial_out = jnp.dot(hidden, down_own, preferred_element_type=full) + jnp.dot(
        context, out_own, preferred_element_type=full
    )
    reduced_out = lax.psum_scatter(
        partial_out.astype(low), "sp", scatter_dimension=0, tiled=True
    )
    seq_cotangent, _ = lax.optimization_barrier((seq_cotangent, partial_out))
    grad_out = jnp.where(row_valid[:, None], seq_cotangent, jnp.zeros_like(seq_cotangent))
    grad_hidden = contract_cols(grad_out, down_own)
    grad_pre = (grad_hidden * gelu_slope(pre_act)).astype(low)
    grad_mlp_in = jnp.dot(grad_pre, up_own, preferred_element_type=full)

    grad_context = contract_cols(grad_out, out_own).astype(low)
    grad_proj, grad_proj_sum = attend_bwd(
        queries, key_rows, values, grad_context, cos_rows, sin_rows, lengths
    )
    grad_attn_in = contract_cols(grad_proj, qkv_own)
    grad_hat = grad_attn_in * gains[0] + grad_mlp_in * gains[1]
    reduced_hat = lax.psum_scatter(
        grad_hat.astype(low), "sp", scatter_dimension=0, tiled=True
    )
    own_cotangent = lax.dynamic_slice_in_dim(grad_out, shard * own_rows, own_rows, 0).astype(full)
    spread_units = lax.dynamic_update_index_in_dim(
        jnp.zeros((dp_size, sp_size, units), full),
        jnp.sum(grad_pre, axis=0, dtype=full).reshape(dp_size, units),
        shard,
        1,
    ).reshape(-1)
    spread_bias = lax.dynamic_update_index_in_dim(
        jnp.zeros((3, sp_size, head_width), full),
        grad_proj_sum.reshape(3, head_width),
        shard,
        1,
    ).reshape(3, D)
    gain_grad = jnp.stack(
        [jnp.sum(grad_attn_in * normed, axis=0), jnp.sum(grad_mlp_in * normed, axis=0)]
    )
    shift_grad = jnp.stack([jnp.sum(grad_attn_in, axis=0), jnp.sum(grad_mlp_in, axis=0)])
    out_bias_part = jnp.sum(own_cotangent, axis=0)
    if square:
        small = jnp.concatenate(
            [
                piece.reshape(-1, 128)
                for piece in (gain_grad, shift_grad, spread_bias, spread_units, out_bias_part)
            ]
        )
        small, reduced_out = lax.optimization_barrier((small, reduced_out))
        grad_down, grad_up, grad_qkv, grad_dense, small = reduce_gradients(
            sp_size,
            qkv_rows,
            hidden,
            grad_out,
            grad_pre,
            mlp_in,
            attn_in,
            grad_proj,
            context,
            small,
        )
        reduced_hat, small = lax.optimization_barrier((reduced_hat, small))
        small = small.reshape(-1)
        ends = [2 * D, 4 * D, 7 * D, 7 * D + dp_size * sp_size * units]
        gain_total, shift_total, qkv_bias_total, unit_total, out_bias_total = jnp.split(small, ends)
        gain_total = gain_total.reshape(2, D)
        shift_total = shift_total.reshape(2, D)
        qkv_bias_total = qkv_bias_total.reshape(3, D)
    else:
        grad_down, grad_up, grad_qkv, grad_dense = reduce_plain(
            dp_size,
            sp_size,
            qkv_rows,
            hidden,
            grad_out,
            grad_pre,
            mlp_in,
            attn_in,
            grad_proj,
            context,
        )
        gain_total, shift_total, qkv_bias_total, unit_total, out_bias_total = lax.psum(
            (gain_grad, shift_grad, spread_bias, spread_units, out_bias_part), ("dp", "sp")
        )

    output = (
        tokens.astype(full) + reduced_out.astype(full) + out_bias.astype(full)
    ).astype(low)

    reduced_hat = reduced_hat.astype(full)
    own_inverse = lax.dynamic_slice_in_dim(inverse, shard * own_rows, own_rows, 0)
    own_normed = lax.dynamic_slice_in_dim(normed, shard * own_rows, own_rows, 0)
    grad_input = own_inverse * (
        reduced_hat
        - jnp.mean(reduced_hat, axis=-1, keepdims=True)
        - own_normed * jnp.mean(reduced_hat * own_normed, axis=-1, keepdims=True)
    )
    input_grad = (own_cotangent + grad_input).astype(low)
    return (
        output,
        input_grad,
        gain_total,
        shift_total,
        grad_qkv.astype(full),
        qkv_bias_total,
        grad_dense.astype(full),
        grad_up.astype(full),
        unit_total,
        grad_down.astype(full),
        out_bias_total,
    )


def solution(mesh):
    return jax.shard_map(
        body,
        mesh=mesh,
        in_specs=(
            P(("dp", "sp"), None),
            P("dp"),
            P(("dp", "sp"), None),
            P(),
            P(),
            P(("dp", "sp"), None),
            P(),
            P(("dp", "sp"), None),
            P(("dp", "sp"), None),
            P(),
            P(("dp", "sp"), None),
            P(),
        ),
        out_specs=(
            P(("dp", "sp"), None),
            P(("dp", "sp"), None),
            P(),
            P(),
            P(("dp", "sp"), None),
            P(),
            P(("dp", "sp"), None),
            P(("dp", "sp"), None),
            P(),
            P(("dp", "sp"), None),
            P(),
        ),
        check_vma=False,
    )
```

```python
import functools

import jax
import jax.numpy as jnp
from jax import lax
from jax.experimental import pallas as pl
from jax.experimental.pallas import tpu as pltpu
from jax.sharding import PartitionSpec as P

D = 2048
HEADS = 8
HEAD = 256
ROT = 64


eps = 1e-05
base_freq = 10000.0
root_half = 0.7071067811865476
inv_root_two_pi = 0.3989422804014327


def contract_rows(left, right):
    return lax.dot_general(
        left, right, (((0,), (0,)), ((), ())), preferred_element_type=jnp.float32
    )


def contract_cols(left, right):
    return lax.dot_general(
        left, right, (((1,), (1,)), ((), ())), preferred_element_type=jnp.float32
    )


def gelu_value(pre_act):
    return 0.5 * pre_act * (1.0 + lax.erf(pre_act * root_half))


def gelu_slope(pre_act):
    return 0.5 * (1.0 + lax.erf(pre_act * root_half)) + pre_act * inv_root_two_pi * jnp.exp(
        -0.5 * pre_act * pre_act
    )


BAND=256
def turn(x, cos_t, sin_t):
    first = x[:, :128]
    lane = lax.broadcasted_iota(jnp.int32, first.shape, 1)
    partner = jnp.where(lane < ROT // 2, pltpu.roll(first, 128 - ROT // 2, 1), pltpu.roll(first, ROT // 2, 1))
    return jnp.concatenate([first * cos_t + partner * sin_t, x[:, 128:]], axis=1)

def weights_of(q, k, start, length, scale):
    rows, cols = q.shape[0], k.shape[0]
    s = lax.dot_general(q, k, (((1,), (1,)), ((), ())), preferred_element_type=jnp.float32) * scale
    key = lax.broadcasted_iota(jnp.int32, (rows, cols), 1)
    query = start + lax.broadcasted_iota(jnp.int32, (rows, cols), 0)
    s = jnp.where((key <= query) & (key < length), s, -1e30)
    e = jnp.exp(s - jnp.max(s, axis=-1, keepdims=True))
    return e / jnp.sum(e, axis=-1, keepdims=True)

def fwd_kernel(scale, len_ref, pq, pk, pv, bq, bk, bv, cos_ref, sin_ref, q_ref, k_ref, v_ref, ctx_ref):
    length = len_ref[0]
    seq = pq.shape[0]
    cos_t, sin_t = cos_ref[...], sin_ref[...]
    q_ref[...] = turn(pq[...] + bq[...], cos_t, sin_t).astype(jnp.bfloat16)
    k_ref[...] = turn(pk[...] + bk[...], cos_t, sin_t).astype(jnp.bfloat16)
    v_ref[...] = (pv[...] + bv[...]).astype(jnp.bfloat16)
    for start in range(0, seq, BAND):
        end = start + BAND
        p = weights_of(q_ref[start:end, :], k_ref[:end, :], start, length, scale)
        ctx_ref[start:end, :] = jnp.dot(p.astype(jnp.bfloat16), v_ref[:end, :], preferred_element_type=jnp.float32).astype(jnp.bfloat16)

def attend_fwd(projected, bias, cos_t, sin_t, lengths):
    seq, width = projected.shape
    heads = width // 3 // HEAD
    col = lambda g: pl.BlockSpec((seq, HEAD), lambda h, *_, g=g: (0, g * heads + h))
    bcol = lambda g: pl.BlockSpec((1, HEAD), lambda h, *_, g=g: (0, g * heads + h))
    tab = pl.BlockSpec((seq, 128), lambda h, *_: (0, 0))
    out = pl.BlockSpec((seq, HEAD), lambda h, *_: (0, h))
    return pl.pallas_call(
        functools.partial(fwd_kernel, HEAD ** -0.5),
        grid_spec=pltpu.PrefetchScalarGridSpec(num_scalar_prefetch=1, grid=(heads,),
            in_specs=[col(0), col(1), col(2), bcol(0), bcol(1), bcol(2), tab, tab], out_specs=[out] * 4),
        out_shape=[jax.ShapeDtypeStruct((seq, heads * HEAD), jnp.bfloat16)] * 4,
        name="attend_fwd",
        cost_estimate=pl.CostEstimate(flops=heads * seq * seq * HEAD * 4, bytes_accessed=seq * width * 8, transcendentals=heads * seq * seq),
    )(lengths, projected, projected, projected, bias, bias, bias, cos_t, sin_t)

def bwd_kernel(scale, heads, len_ref, q_ref, k_ref, v_ref, g_ref, cos_ref, sin_ref, gp_ref, sum_ref, dk, dv, dq):
    length = len_ref[0]
    h = pl.program_id(0)
    seq = q_ref.shape[0]
    dk[...] = jnp.zeros_like(dk)
    dv[...] = jnp.zeros_like(dv)
    for start in range(0, seq, BAND):
        end = start + BAND
        q, g = q_ref[start:end, :], g_ref[start:end, :]
        k, v = k_ref[:end, :], v_ref[:end, :]
        p = weights_of(q, k, start, length, scale)
        gp = lax.dot_general(g, v, (((1,), (1,)), ((), ())), preferred_element_type=jnp.float32)
        ds = (p * (gp - jnp.sum(p * gp, axis=-1, keepdims=True))).astype(jnp.bfloat16)
        dq[start:end, :] = jnp.dot(ds, k, preferred_element_type=jnp.float32) * scale
        dk[:end, :] += lax.dot_general(ds, q, (((0,), (0,)), ((), ())), preferred_element_type=jnp.float32)
        dv[:end, :] += lax.dot_general(p.astype(jnp.bfloat16), g, (((0,), (0,)), ((), ())), preferred_element_type=jnp.float32)
    cos_t, sin_t = cos_ref[...], sin_ref[...]
    def back(x):
        return turn(x.astype(jnp.bfloat16).astype(jnp.float32), cos_t, -sin_t).astype(jnp.bfloat16)
    for g, piece in enumerate((back(dq[...]), back(dk[...] * scale), dv[...].astype(jnp.bfloat16))):
        at = pl.ds(pl.multiple_of((g * heads + h) * HEAD, HEAD), HEAD)
        gp_ref[:, at] = piece
        sum_ref[:, at] = jnp.sum(piece.astype(jnp.float32), axis=0, keepdims=True)

def attend_bwd(q, k, v, gctx, cos_t, sin_t, lengths):
    seq, width = q.shape
    heads = width // HEAD
    col = pl.BlockSpec((seq, HEAD), lambda h, *_: (0, h))
    tab = pl.BlockSpec((seq, 128), lambda h, *_: (0, 0))
    return pl.pallas_call(
        functools.partial(bwd_kernel, HEAD ** -0.5, heads),
        grid_spec=pltpu.PrefetchScalarGridSpec(num_scalar_prefetch=1, grid=(heads,),
            in_specs=[col] * 4 + [tab, tab],
            out_specs=[pl.BlockSpec((seq, 3 * width), lambda h, *_: (0, 0)), pl.BlockSpec((1, 3 * width), lambda h, *_: (0, 0))],
            scratch_shapes=[pltpu.VMEM((seq, HEAD), jnp.float32)] * 3),
        out_shape=[jax.ShapeDtypeStruct((seq, 3 * width), jnp.bfloat16), jax.ShapeDtypeStruct((1, 3 * width), jnp.float32)],
        name="attend_bwd",
        cost_estimate=pl.CostEstimate(flops=heads * seq * seq * HEAD * 10, bytes_accessed=seq * width * 20, transcendentals=heads * seq * seq),
    )(lengths, q, k, v, gctx, cos_t, sin_t)

def rotary_rows(seq):
    half = ROT // 2
    freq = 10000.0 ** (-jnp.arange(half, dtype=jnp.float32) * (2.0 / ROT))
    ang = jnp.arange(seq, dtype=jnp.int32).astype(jnp.float32)[:, None] * freq[None, :]
    c, s = jnp.cos(ang), jnp.sin(ang)
    rest = 128 - ROT
    return (jnp.concatenate([c, c, jnp.ones((seq, rest), jnp.float32)], 1), jnp.concatenate([-s, s, jnp.zeros((seq, rest), jnp.float32)], 1))

MESH = pl.DeviceIdType.MESH

def square_partners(dp):
    core, x, y = dp % 2, (dp // 2) % 2, dp // 4
    across_x, across_y = dp + 2 - 4 * x, dp + 4 - 8 * y
    first = across_x * (1 - core) + across_y * core
    second = across_y * (1 - core) + across_x * core
    return first, second, across_x + across_y - dp, 1 - 2 * core

class Hops:
    def __init__(self, count, dp, sp, source, result, send, recv):
        self.count, self.dp, self.sp, self.source, self.result = count, dp, sp, source, result
        self.send, self.recv, self.rows = send, recv, source.shape[0]

    def place(self, owner):
        return pl.ds(pl.multiple_of(owner * self.rows, self.rows), self.rows)

    def copy(self, way, step, owner, own):
        to = lax.rem(self.sp + (1 if way == 0 else self.count - 1), self.count)
        at = self.result.at[self.place(owner)]
        return pltpu.make_async_remote_copy(
            src_ref=self.source if own else at, dst_ref=at, send_sem=self.send.at[way, step],
            recv_sem=self.recv.at[way, step], device_id=(self.dp, to), device_id_type=MESH)

    def sends(self, way, step):
        if way == 0:
            return (self.sp >= step) & (self.sp < self.count - 1)
        return (self.sp < self.count - step) & (self.sp > 0)

    def receives(self, way, step):
        return self.sp >= step + 1 if way == 0 else self.sp < self.count - step - 1

    def owner(self, way, step):
        return self.sp - step if way == 0 else self.sp + step

    def start(self, way, step):
        @pl.when(self.sends(way, step))
        def _():
            self.copy(way, step, self.owner(way, step), step == 0).start()

    def begin(self):
        for way in (0, 1):
            self.start(way, 0)

    def forward(self, step):
        for way in (0, 1):
            @pl.when(self.receives(way, step - 1))
            def _():
                self.copy(way, step - 1, self.owner(way, step), False).wait_recv()
            if step < self.count - 1:
                self.start(way, step)

    def finish(self):
        for step in range(self.count - 1):
            for way in (0, 1):
                @pl.when(self.sends(way, step))
                def _():
                    self.copy(way, step, self.owner(way, step), step == 0).wait_send()


def gather_kernel(sp_size, qkv_ref, out_ref, up_ref, tok_ref, freq_ref, qkv_all, out_all, up_all, tok_all,
                  cos_ref, sin_ref,
                  send_sem, recv_sem, slab_send, slab_recv, local_sem, turn_send, turn_recv, hop_send, hop_recv):
    dp, sp = lax.axis_index("dp"), lax.axis_index("sp")
    first, second, diagonal, flip = square_partners(dp)
    sibling = dp + flip
    per = 2
    pair, lane = dp // per, dp % per
    rows = qkv_ref.shape[0]
    wide = up_ref.shape[1]
    head_width = wide // sp_size
    turn_dp = sp * per + lane

    barrier = pltpu.get_barrier_semaphore()
    for other in (first, second, sibling):
        pl.semaphore_signal(barrier, inc=1, device_id=(other, sp), device_id_type=MESH)
    for step in range(1, sp_size):
        pl.semaphore_signal(barrier, inc=1, device_id=(dp, lax.rem(sp + step, sp_size)), device_id_type=MESH)
    @pl.when(pair != sp)
    def _():
        pl.semaphore_signal(barrier, inc=1, device_id=(turn_dp, pair), device_id_type=MESH)

    pl.semaphore_wait(barrier, 2 + sp_size + jnp.where(pair != sp, 1, 0))

    def slab_at(owner_sp):
        return pl.ds(pl.multiple_of((dp * sp_size + owner_sp) * rows, rows), rows)

    def slab_copy(step, part):
        there = lax.rem(sp + step, sp_size)
        return pltpu.make_async_remote_copy(
            src_ref=qkv_ref.at[:, pl.ds(pl.multiple_of(part * wide + there * head_width, head_width), head_width)],
            dst_ref=qkv_all.at[slab_at(sp), pl.ds(part * head_width, head_width)],
            send_sem=slab_send.at[step - 1, part], recv_sem=slab_recv.at[step - 1, part],
            device_id=(dp, there), device_id_type=MESH)

    def slab_arrival(step, part):
        origin = lax.rem(sp + sp_size - step, sp_size)
        return pltpu.make_async_remote_copy(
            src_ref=qkv_ref.at[:, pl.ds(part * head_width, head_width)],
            dst_ref=qkv_all.at[slab_at(origin), pl.ds(part * head_width, head_width)],
            send_sem=slab_send.at[step - 1, part], recv_sem=slab_recv.at[step - 1, part],
            device_id=(dp, origin), device_id_type=MESH)

    units = up_ref.shape[0]
    slab = rows * sp_size

    def plain(height):
        return lambda owner: pl.ds(pl.multiple_of(owner * height, height), height)

    def turned(owner):
        return pl.ds(pl.multiple_of((owner % per) * slab + (owner // per) * rows, rows), rows)

    arrays = ((up_ref, up_all, plain(units)), (None, qkv_all, plain(slab)), (None, out_all, turned))
    hops = Hops(sp_size, dp, sp, tok_ref, tok_all, hop_send, hop_recv)

    def copy(index, message, block, target):
        source, result, place = arrays[index]
        at = result.at[place(block)]
        src = at
        if source is not None and message < 3:
            src = source
        return pltpu.make_async_remote_copy(
            src_ref=src, dst_ref=at, send_sem=send_sem.at[index, message], recv_sem=recv_sem.at[index, message],
            device_id=(target, sp), device_id_type=MESH)

    sends = ((dp, first), (dp, second), (dp, sibling), (first, second), (first, sibling), (second, sibling), (diagonal, sibling))
    arrivals = (first, second, sibling, diagonal, second + flip, first + flip, diagonal + flip)

    def start(index, message):
        copy(index, message, *sends[message]).start()

    def arrived(index, message):
        copy(index, message, arrivals[message], dp).wait_recv()

    def own(index):
        for message in (0, 1, 2):
            start(index, message)

    def keep(source, target, which):
        return pltpu.make_async_copy(source, target, local_sem.at[which])

    hops.begin()
    own(0)
    for step in range(1, sp_size):
        for part in range(3):
            slab_copy(step, part).start()

    out_place = out_all.at[turned(turn_dp)]
    my_out_place = out_all.at[turned(dp)]
    turn = pltpu.make_async_remote_copy(
        src_ref=out_ref, dst_ref=out_place, send_sem=turn_send, recv_sem=turn_recv,
        device_id=(turn_dp, pair), device_id_type=MESH)
    turn_arrival = pltpu.make_async_remote_copy(
        src_ref=out_ref, dst_ref=my_out_place, send_sem=turn_send, recv_sem=turn_recv,
        device_id=(turn_dp, pair), device_id_type=MESH)

    @pl.when(pair != sp)
    def _():
        turn.start()

    local = [keep(tok_ref, tok_all.at[hops.place(sp)], 0), keep(up_ref, up_all.at[plain(units)(dp)], 1)]
    for part in range(3):
        local.append(keep(
            qkv_ref.at[:, pl.ds(pl.multiple_of(part * wide + sp * head_width, head_width), head_width)],
            qkv_all.at[slab_at(sp), pl.ds(part * head_width, head_width)], 2 + part))
    for c in local:
        c.start()

    def onward(index):
        arrived(index, 0)
        start(index, 3)
        start(index, 4)
        arrived(index, 1)
        start(index, 5)

    def table(i, carry):
        at = pl.ds(pl.multiple_of(i * 64, 64), 64)
        lane = lax.broadcasted_iota(jnp.int32, (64, 128), 1)
        position = i * 64 + lax.broadcasted_iota(jnp.int32, (64, 128), 0)
        angle = position.astype(jnp.float32) * freq_ref[...]
        turned_lane = lane < ROT
        cos_ref[at, :] = jnp.where(turned_lane, jnp.cos(angle), 1.0)
        sine = jnp.sin(angle)
        sin_ref[at, :] = jnp.where(turned_lane, jnp.where(lane < ROT // 2, -sine, sine), 0.0)
        return carry

    onward(0)
    hops.forward(1)
    lax.fori_loop(0, cos_ref.shape[0] // 64, table, 0)

    @pl.when(pair == sp)
    def _():
        c = keep(out_ref, my_out_place, 5)
        c.start()
        c.wait()

    @pl.when(pair != sp)
    def _():
        turn_arrival.wait_recv()

    own(2)
    for step in range(1, sp_size):
        for part in range(3):
            slab_arrival(step, part).wait_recv()
    for c in local:
        c.wait()
    own(1)
    arrived(0, 3)
    start(0, 6)
    onward(2)
    hops.forward(2)
    onward(1)
    for index in (2, 1):
        arrived(index, 3)
        start(index, 6)
    hops.forward(3)
    for index in range(3):
        for message in (2, 4, 5, 6):
            arrived(index, message)
    for index in range(3):
        for message in range(7):
            copy(index, message, *sends[message]).wait_send()
    for step in range(1, sp_size):
        for part in range(3):
            slab_copy(step, part).wait_send()

    @pl.when(pair != sp)
    def _():
        turn.wait_send()

    hops.finish()

def gather_weights(dp_size, sp_size, qkv_weight, out_weight, up_weight, tokens):
    rows, wide = out_weight.shape
    units = up_weight.shape[0]
    seq = tokens.shape[0] * sp_size
    low = jnp.bfloat16
    half = ROT // 2
    freq = base_freq ** (-jnp.arange(half, dtype=jnp.float32) * (2.0 / ROT))
    freq = jnp.concatenate([freq, freq, jnp.zeros((128 - ROT,), jnp.float32)])[None]
    hbm = pl.BlockSpec(memory_space=pltpu.HBM)
    vmem = pl.BlockSpec(memory_space=pltpu.VMEM)
    dma = pltpu.SemaphoreType.DMA
    shape = jax.ShapeDtypeStruct
    return pl.pallas_call(
        functools.partial(gather_kernel, sp_size),
        out_shape=[shape((rows * sp_size * dp_size, 3 * wide // sp_size), low),
                   shape((rows * dp_size, wide), low),
                   shape((units * dp_size, wide), low),
                   shape((seq, wide), low),
                   shape((seq, 128), jnp.float32), shape((seq, 128), jnp.float32)],
        in_specs=[vmem] * 5, out_specs=[hbm] * 4 + [vmem] * 2,
        scratch_shapes=[dma((3, 7)), dma((3, 7)), dma((sp_size - 1, 3)), dma((sp_size - 1, 3)), dma((6,)), dma, dma,
                        dma((2, sp_size)), dma((2, sp_size))],
        compiler_params=pltpu.CompilerParams(collective_id=0, has_side_effects=True),
        cost_estimate=pl.CostEstimate(flops=0, bytes_accessed=250 * 1000 * 1000, transcendentals=0),
        name="gather_weights",
    )(qkv_weight, out_weight, up_weight, tokens, freq)

def front_kernel(sp_size, len_ref, tok_hbm, qkv_hbm, up_hbm, out_hbm, down_ref, cot_ref, gain_ref, shift_ref, qkv_bias_ref, unit_bias_ref,
                 cos_ref, sin_ref,
                 down_all, cot_all, attn_out, mlp_out, hidden_out, pre_out, part_out, q_ref, k_ref, v_ref, ctx_ref,
                 tok, attn, mlp, qkv_w, up_w, hidden, pre,
                 send_sem, recv_sem, load_sem, store_sem, pre_sem, keep_sem, part_sem, hop_send, hop_recv):
    full, low = jnp.float32, jnp.bfloat16
    dp, sp = lax.axis_index("dp"), lax.axis_index("sp")
    first, second, diagonal, flip = square_partners(dp)
    sibling = dp + flip
    seq, wide = tok.shape
    units = down_ref.shape[0]
    width = q_ref.shape[1]
    scale = HEAD ** -0.5
    band = 256

    def load(source, target, which):
        return pltpu.make_async_copy(source, target, load_sem.at[which])

    token_loads = [load(tok_hbm.at[pl.ds(r, band)], tok.at[pl.ds(r, band)], r // band) for r in range(0, seq, band)]
    loads = token_loads + [load(qkv_hbm, qkv_w, seq // band), load(up_hbm, up_w, seq // band + 1)]
    for c in loads:
        c.start()

    barrier = pltpu.get_barrier_semaphore()
    for other in (first, second, sibling):
        pl.semaphore_signal(barrier, inc=1, device_id=(other, sp), device_id_type=MESH)
    for step in range(1, sp_size):
        pl.semaphore_signal(barrier, inc=1, device_id=(dp, lax.rem(sp + step, sp_size)), device_id_type=MESH)
    pl.semaphore_wait(barrier, 2 + sp_size)

    sends = ((dp, first), (dp, second), (dp, sibling), (first, second), (first, sibling), (second, sibling), (diagonal, sibling))
    arrivals = (first, second, sibling, diagonal, second + flip, first + flip, diagonal + flip)

    def copy(message, block, target):
        at = down_all.at[pl.ds(pl.multiple_of(block * units, units), units)]
        return pltpu.make_async_remote_copy(
            src_ref=down_ref if message < 3 else at, dst_ref=at,
            send_sem=send_sem.at[message], recv_sem=recv_sem.at[message],
            device_id=(target, sp), device_id_type=MESH)

    def start(message):
        copy(message, *sends[message]).start()

    def arrived(message):
        copy(message, arrivals[message], sibling).wait_recv()

    hops = Hops(sp_size, dp, sp, cot_ref, cot_all, hop_send, hop_recv)
    hops.begin()
    for message in (0, 1, 2):
        start(message)
    keeps = [pltpu.make_async_copy(down_ref, down_all.at[pl.ds(pl.multiple_of(dp * units, units), units)], keep_sem.at[0]),
             pltpu.make_async_copy(cot_ref, cot_all.at[hops.place(sp)], keep_sem.at[1])]
    for c in keeps:
        c.start()

    def normalize(i, carry):
        at = pl.ds(pl.multiple_of(i * 32, 32), 32)
        rows = tok[at, :].astype(full)
        centered = rows - jnp.mean(rows, axis=-1, keepdims=True)
        normed = centered * lax.rsqrt(jnp.mean(centered * centered, axis=-1, keepdims=True) + eps)
        attn[at, :] = (normed * gain_ref[0:1, :] + shift_ref[0:1, :]).astype(low)
        mlp[at, :] = (normed * gain_ref[1:2, :] + shift_ref[1:2, :]).astype(low)
        return carry

    for part, c in enumerate(token_loads):
        c.wait()
        lax.fori_loop(part * band // 32, (part + 1) * band // 32, normalize, 0)
    stores = [pltpu.make_async_copy(attn, attn_out, store_sem.at[0]), pltpu.make_async_copy(mlp, mlp_out, store_sem.at[1])]
    for c in stores:
        c.start()
    loads[-2].wait()

    def head(h, carry):
        lanes = pl.ds(pl.multiple_of(h * HEAD, HEAD), HEAD)

        def project(r, carry):
            at = pl.ds(pl.multiple_of(r * band, band), band)
            cos_t, sin_t = cos_ref[at, :], sin_ref[at, :]
            for part, target in enumerate((q_ref, k_ref, v_ref)):
                cols = pl.ds(pl.multiple_of(part * width + h * HEAD, HEAD), HEAD)
                value = jnp.dot(attn[at, :], qkv_w[:, cols], preferred_element_type=full) + qkv_bias_ref[:, cols]
                if part < 2:
                    value = turn(value, cos_t, sin_t)
                target[at, lanes] = value.astype(low)
            return carry
        lax.fori_loop(0, seq // band, project, 0)
        for begin in range(0, seq, band):
            end = begin + band
            p = weights_of(q_ref[begin:end, lanes], k_ref[:end, lanes], begin, len_ref[0], scale)
            ctx_ref[begin:end, lanes] = jnp.dot(p.astype(low), v_ref[:end, lanes], preferred_element_type=full).astype(low)
        return carry

    lax.fori_loop(0, width // HEAD, head, 0)
    arrived(0)
    start(3)
    start(4)
    arrived(1)
    start(5)
    hops.forward(1)
    loads[-1].wait()

    def pre_store(block, slot):
        return pltpu.make_async_copy(pre.at[slot], pre_out.at[:, pl.ds(pl.multiple_of(block * units, units), units)],
                                     pre_sem.at[slot])

    def unit_block(block, carry):
        slot = lax.rem(block, 2)

        @pl.when(block >= 2)
        def _():
            pre_store(block - 2, slot).wait()

        of = pl.ds(pl.multiple_of(block * units, units), units)

        def row_band(r, carry):
            at = pl.ds(pl.multiple_of(r * band, band), band)
            value = lax.dot_general(mlp[at, :], up_w[of, :], (((1,), (1,)), ((), ())), preferred_element_type=full)
            value = value + unit_bias_ref[:, of]
            pre[slot, at, :] = value
            hidden[at, of] = gelu_value(value).astype(low)
            return carry
        lax.fori_loop(0, seq // band, row_band, 0)
        pre_store(block, slot).start()
        return carry

    blocks = up_w.shape[0] // units
    lax.fori_loop(0, blocks // 2, unit_block, 0)
    arrived(3)
    start(6)
    lax.fori_loop(blocks // 2, blocks, unit_block, 0)
    for block in (blocks - 2, blocks - 1):
        pre_store(block, block % 2).wait()
    for c in stores + keeps:
        c.wait()
    hidden_store = pltpu.make_async_copy(hidden, hidden_out, store_sem.at[0])
    hidden_store.start()
    for message in (2, 4, 5, 6):
        arrived(message)
    half = up_w.shape[0] // 2
    out_rows = out_hbm.shape[0]
    late = [load(down_all.at[pl.ds(0, half)], tok, 0), load(down_all.at[pl.ds(half, half)], attn, 1),
            load(out_hbm, up_w.at[pl.ds(0, out_rows)], 2)]
    for c in late:
        c.start()
    hops.forward(2)
    for c in late:
        c.wait()

    def part_store(r):
        at = pl.ds(pl.multiple_of(r * band, band), band)
        return pltpu.make_async_copy(mlp.at[at], part_out.at[at], part_sem.at[r])

    def out_band(r, carry):
        at = pl.ds(pl.multiple_of(r * band, band), band)

        def out_columns(c, carry):
            to = pl.ds(pl.multiple_of(c * band, band), band)
            total = jnp.dot(hidden[at, :half], tok[:, to], preferred_element_type=full)
            total = total + jnp.dot(hidden[at, half:], attn[:, to], preferred_element_type=full)
            total = total + jnp.dot(ctx_ref[at, :], up_w[:out_rows, to], preferred_element_type=full)
            mlp[at, to] = total.astype(low)
            return carry
        lax.fori_loop(0, wide // band, out_columns, 0)
        part_store(r).start()
        return carry
    lax.fori_loop(0, seq // band, out_band, 0)
    hops.forward(3)
    for r in range(seq // band):
        part_store(r).wait()
    hidden_store.wait()
    for message in range(7):
        copy(message, *sends[message]).wait_send()
    hops.finish()

def front(sp_size, tokens, qkv_own, up_own, out_own, down_weight, cotangent, gains, shifts, qkv_bias, unit_bias, cos_t, sin_t,
          lengths, dp_size):
    seq, wide = tokens.shape
    units = down_weight.shape[0]
    width = qkv_own.shape[1] // 3
    all_units = up_own.shape[0]
    full, low = jnp.float32, jnp.bfloat16
    hbm = pl.BlockSpec(memory_space=pltpu.HBM)
    vmem = pl.BlockSpec(memory_space=pltpu.VMEM)
    dma = pltpu.SemaphoreType.DMA
    shape = jax.ShapeDtypeStruct
    return pl.pallas_call(
        functools.partial(front_kernel, sp_size),
        out_shape=[shape((units * dp_size, wide), low), shape((seq, wide), low), shape((seq, wide), low), shape((seq, wide), low),
                   shape((seq, all_units), low), shape((seq, all_units), full), shape((seq, wide), low)]
        + [shape((seq, width), low)] * 4,
        in_specs=[pl.BlockSpec(memory_space=pltpu.SMEM), hbm, hbm, hbm, hbm] + [vmem] * 8,
        out_specs=[hbm] * 7 + [vmem] * 4,
        scratch_shapes=[pltpu.VMEM((seq, wide), low)] * 3 + [
            pltpu.VMEM(qkv_own.shape, low), pltpu.VMEM(up_own.shape, low),
            pltpu.VMEM((seq, all_units), low), pltpu.VMEM((2, seq, units), full),
            dma((7,)), dma((7,)), dma((seq // 256 + 2,)), dma((2,)), dma((2,)), dma((2,)), dma((seq // 256,)),
            dma((2, sp_size)), dma((2, sp_size))],
        compiler_params=pltpu.CompilerParams(collective_id=2, has_side_effects=True, vmem_limit_bytes=60 << 20),
        cost_estimate=pl.CostEstimate(flops=26 * 10 ** 9, bytes_accessed=80 * 1000 * 1000, transcendentals=0),
        name="front",
    )(lengths, tokens, qkv_own, up_own, out_own, down_weight, cotangent, gains, shifts, qkv_bias, unit_bias, cos_t, sin_t)

CHUNK = 512


def add_into(target, *others):
    step_rows = 32

    def step(i, carry):
        at = pl.ds(pl.multiple_of(i * step_rows, step_rows), step_rows)
        total = target[at, :].astype(jnp.float32)
        for other in others:
            total = total + other[at, :].astype(jnp.float32)
        target[at, :] = total.astype(jnp.bfloat16)
        return carry

    lax.fori_loop(0, target.shape[0] // step_rows, step, 0)


class Square:
    def __init__(self, sp_size, lent, sib_send, sib_recv, one_send, one_recv, two_send, two_recv):
        self.dp, self.sp, self.sp_size = lax.axis_index("dp"), lax.axis_index("sp"), sp_size
        self.core, self.chip = self.dp % 2, self.dp // 2
        self.x, self.y = self.chip % 2, self.chip // 2
        self.sibling = self.dp + 1 - 2 * self.core
        self.across_x, self.across_y = self.dp + 2 - 4 * self.x, self.dp + 4 - 8 * self.y
        self.first = self.across_y * (1 - self.core) + self.across_x * self.core
        self.second = self.across_x * (1 - self.core) + self.across_y * self.core
        self.second_mask = 1 + self.core
        self.lent = lent
        self.sib_send, self.sib_recv, self.one_send, self.one_recv, self.two_send, self.two_recv = (
            sib_send, sib_recv, one_send, one_recv, two_send, two_recv)

    def chip_of(self, mask):
        return lax.rem(self.x + lax.rem(mask, 2), 2) + 2 * lax.rem(self.y + mask // 2, 2)

    def greet(self, barrier):
        for other in (self.first, self.second, self.sibling):
            pl.semaphore_signal(barrier, inc=1, device_id=(other, self.sp), device_id_type=MESH)
        for step in range(1, self.sp_size):
            pl.semaphore_signal(
                barrier, inc=1, device_id=(self.dp, lax.rem(self.sp + step, self.sp_size)), device_id_type=MESH)


def remote(source, target, send, recv, device):
    return pltpu.make_async_remote_copy(
        src_ref=source, dst_ref=target, send_sem=send, recv_sem=recv, device_id=device, device_id_type=MESH)


class Wide:
    def __init__(self, place, index, left, right, width, sums, sib, one, two):
        self.place, self.index, self.left, self.right, self.width = place, index, left, right, width
        self.sums, self.sib, self.one, self.two = sums, sib, one, two
        self.units = sums.shape[1]

    def product(self, block, store):
        at = pl.ds(pl.multiple_of(block * self.units, self.units), self.units)

        def columns(part, carry):
            to = pl.ds(pl.multiple_of(part * CHUNK, CHUNK), CHUNK)
            store(to, lax.dot_general(
                self.left[:, at], self.right[:, to], (((0,), (0,)), ((), ())),
                preferred_element_type=jnp.float32))
            return carry
        lax.fori_loop(0, self.width // CHUNK, columns, 0)

    def sib_copy(self, slot):
        p = self.place
        return remote(p.lent.at[slot, :, :self.width], self.sib.at[p.chip_of(3 - slot)],
                      p.sib_send.at[self.index, slot], p.sib_recv.at[self.index, slot], (p.sibling, p.sp))

    def for_sibling(self, previous):
        p = self.place

        def step(slot, carry):
            if previous is not None:
                previous.sib_copy(slot).wait_send()

            def store(to, total):
                p.lent[slot, :, to] = total.astype(jnp.bfloat16)
            self.product(p.chip_of(3 - slot) * 2 + 1 - p.core, store)
            self.sib_copy(slot).start()
            return carry
        lax.fori_loop(0, 4, step, 0)

    def own(self, mask, slot):
        at = self.place.chip_of(mask)
        self.sib_copy(slot).wait_recv()

        def store(to, total):
            self.sums[mask, :, to] = (total + self.sib[at, :, to].astype(jnp.float32)).astype(jnp.bfloat16)
        self.product(at * 2 + self.place.core, store)

    def for_self(self):
        core = self.place.core

        def leave(slot, carry):
            mask = 3 - slot * (1 + core)
            self.own(mask, 3 - mask)
            self.first_copy(slot).start()
            return carry
        lax.fori_loop(0, 2, leave, 0)

        def stay(slot, carry):
            mask = self.place.second_mask * (1 - slot)
            self.own(mask, 3 - mask)
            return carry
        lax.fori_loop(0, 2, stay, 0)

    def block(self, mask):
        return self.sums.at[mask]

    def first_copy(self, slot):
        p = self.place
        return remote(self.block(3 - slot * (1 + p.core)), self.one.at[slot], p.one_send.at[self.index, slot],
                      p.one_recv.at[self.index, slot], (p.first, p.sp))

    def second_copy(self):
        p = self.place
        return remote(self.block(p.second_mask), self.two, p.two_send.at[self.index],
                      p.two_recv.at[self.index], (p.second, p.sp))

    def onward(self):
        self.first_copy(0).wait_recv()
        add_into(self.block(self.place.second_mask), self.one.at[0])
        self.second_copy().start()

    def finish(self):
        self.first_copy(1).wait_recv()
        self.second_copy().wait_recv()
        add_into(self.block(0), self.one.at[1], self.two)

    def drain(self):
        for slot in (0, 1):
            self.first_copy(slot).wait_send()
        self.second_copy().wait_send()


class Dense(Wide):
    def __init__(self, place, index, left, right, width, sums, sib, one, two, part):
        self.place, self.index, self.left, self.right, self.width = place, index, left, right, width
        self.sums, self.sib, self.one, self.two, self.part = sums, sib, one, two, part
        self.units, self.rows = sums.shape[0], one.shape[1]

    def sib_copy(self, slot):
        p = self.place
        return remote(self.part, self.sib, p.sib_send.at[self.index, 0], p.sib_recv.at[self.index, 0], (p.sibling, p.sp))

    def for_sibling(self, previous):
        def store(to, total):
            self.part[:, to] = total.astype(jnp.bfloat16)
        self.product(1 - self.place.core, store)
        self.sib_copy(0).start()

    def for_self(self):
        self.sib_copy(0).wait_recv()

        def store(to, total):
            self.sums[:, to] = (total + self.sib[:, to].astype(jnp.float32)).astype(jnp.bfloat16)
        self.product(self.place.core, store)
        for slot in (0, 1):
            self.first_copy(slot).start()

    def block(self, mask):
        return self.sums.at[pl.ds(pl.multiple_of(self.place.chip_of(mask) * self.rows, self.rows), self.rows)]


class Fold:
    def __init__(self, place, source, inbox, stage, stage_sem, send, recv):
        self.place, self.source, self.inbox, self.stage = place, source, inbox, stage
        self.stage_sem, self.send, self.recv = stage_sem, send, recv
        self.rows = stage.shape[0]

    def along(self, way):
        last = self.place.sp_size - 1
        return self.place.sp if way == 0 else last - self.place.sp

    def rows_of(self, way, step):
        count = self.place.sp_size
        owner = self.along(way) + count - step
        owner = owner if way == 0 else count - 1 - owner
        return self.source.at[pl.ds(pl.multiple_of(owner * self.rows, self.rows), self.rows)]

    def copy(self, way, step, own):
        p = self.place
        to = lax.rem(p.sp + (1 if way == 0 else p.sp_size - 1), p.sp_size)
        source = self.rows_of(way, step) if own else self.inbox.at[way, max(step - 2, 0)]
        return remote(source, self.inbox.at[way, step - 1], self.send.at[way, step - 1],
                      self.recv.at[way, step - 1], (p.dp, to))

    def take(self, rows):
        c = pltpu.make_async_copy(rows, self.stage, self.stage_sem)
        c.start()
        c.wait()

    def step(self, step):
        last = self.place.sp_size - 1
        for way in (0, 1):
            if step == 1:
                @pl.when(self.along(way) == 0)
                def _():
                    for early in range(1, last + 1):
                        self.copy(way, early, True).start()
            else:
                @pl.when((self.along(way) > 0) & (self.along(way) < step) & (self.along(way) < last))
                def _():
                    self.take(self.rows_of(way, step))
                    self.copy(way, step - 1, False).wait_recv()
                    add_into(self.inbox.at[way, step - 2], self.stage)
                    self.copy(way, step, False).start()

    def finish(self):
        last = self.place.sp_size - 1
        self.take(self.source.at[pl.ds(pl.multiple_of(self.place.sp * self.rows, self.rows), self.rows)])
        for way in (0, 1):
            @pl.when(self.along(way) > 0)
            def _():
                self.copy(way, last, False).wait_recv()
                add_into(self.stage, self.inbox.at[way, last - 1])

    def drain(self):
        last = self.place.sp_size - 1
        for way in (0, 1):
            for step in range(1, last + 1):
                @pl.when(self.along(way) == 0)
                def _():
                    self.copy(way, step, True).wait_send()

                if step > 1:
                    @pl.when((self.along(way) > 0) & (self.along(way) < step) & (self.along(way) < last))
                    def _():
                        self.copy(way, step, False).wait_send()


def middle_kernel(sp_size, len_ref, cot_hbm, out_hbm, q_hbm, k_hbm, v_hbm, pre_hbm, hidden_hbm, down_hbm, up_hbm, qkv_hbm,
                  tok_hbm, part_hbm, gain_ref, cos_ref, sin_ref,
                  down_out, hat_out, proj_out, gpre_out, gout_out, red_out, small_ref,
                  cot, left, gpre, up_w, qkv_w, pre, gctx, gproj, dq, dk, dv, mean_s, inv_s,
                  lent, down_sum, down_sib, down_one, down_two, inbox, stage,
                  load_sem, stream_sem, store_sem, stage_sem, sib_send, sib_recv, one_send, one_recv, two_send, two_recv,
                  fold_send, fold_recv):
    full, low = jnp.float32, jnp.bfloat16
    place = Square(sp_size, lent, sib_send, sib_recv, one_send, one_recv, two_send, two_recv)
    seq, wide = cot.shape
    width = gctx.shape[1]
    heads = width // HEAD
    units = down_sum.shape[1]
    blocks = up_w.shape[0] // units
    out_rows = out_hbm.shape[0]
    band = 256
    bands = seq // band
    scale = HEAD ** -0.5

    def load(source, target, which):
        c = pltpu.make_async_copy(source, target, load_sem.at[which])
        c.start()
        return c

    early = [load(cot_hbm, cot, 0), load(hidden_hbm, left, 1), load(out_hbm, up_w.at[pl.ds(0, out_rows)], 2)]
    for i, source in enumerate((q_hbm, k_hbm, v_hbm)):
        early.append(load(source, qkv_w.at[pl.ds(0, seq), pl.ds(i * width, width)], 3 + i))

    def down_load(block, slot):
        return pltpu.make_async_copy(
            down_hbm.at[pl.ds(pl.multiple_of(block * units, units), units)],
            up_w.at[pl.ds(pl.multiple_of(out_rows + slot * units, units), units)], stream_sem.at[0, slot])

    def pre_load(block, slot):
        return pltpu.make_async_copy(
            pre_hbm.at[:, pl.ds(pl.multiple_of(block * units, units), units)], pre.at[slot], stream_sem.at[1, slot])

    for slot in (0, 1):
        down_load(slot, slot).start()
        pre_load(slot, slot).start()

    barrier = pltpu.get_barrier_semaphore()
    place.greet(barrier)
    pl.semaphore_wait(barrier, 2 + sp_size)
    fold = Fold(place, part_hbm, inbox, stage, stage_sem, fold_send, fold_recv)
    fold.step(1)
    small_ref[...] = jnp.zeros_like(small_ref)
    gain_row, shift_row, bias_row, unit_row = 0, 2, 4, 7
    per_row = wide // (sp_size * units)
    last_row = unit_row + blocks // per_row

    early[0].wait()

    def mask_rows(i, carry):
        at = pl.ds(pl.multiple_of(i * 32, 32), 32)
        row = i * 32 + lax.broadcasted_iota(jnp.int32, (32, wide), 0)
        cot[at, :] = jnp.where(row < len_ref[0], cot[at, :].astype(full), 0.0).astype(low)
        return carry
    lax.fori_loop(0, seq // 32, mask_rows, 0)
    stores = [pltpu.make_async_copy(cot, gout_out, store_sem.at[0])]
    stores[0].start()

    def own_rows(i, carry):
        at = pl.ds(pl.multiple_of(place.sp * (seq // sp_size) + i * 32, 32), 32)
        return carry + jnp.sum(cot[at, :].astype(full), axis=0, keepdims=True)
    small_ref[last_row:last_row + 1, :] = lax.fori_loop(0, seq // sp_size // 32, own_rows, jnp.zeros((1, wide), full))

    down = Wide(place, 0, left, cot, wide, down_sum, down_sib, down_one, down_two)
    early[1].wait()
    down.for_sibling(None)
    early[2].wait()

    def context_band(r, carry):
        at = pl.ds(pl.multiple_of(r * band, band), band)
        gctx[at, :] = lax.dot_general(
            cot[at, :], up_w[:out_rows, :], (((1,), (1,)), ((), ())), preferred_element_type=full).astype(low)
        return carry
    lax.fori_loop(0, bands, context_band, 0)
    down.for_self()
    fold.step(2)
    for c in early[3:]:
        c.wait()

    def head(h, carry):
        lanes = pl.ds(pl.multiple_of(h * HEAD, HEAD), HEAD)
        k_lanes = pl.ds(pl.multiple_of(width + h * HEAD, HEAD), HEAD)
        v_lanes = pl.ds(pl.multiple_of(2 * width + h * HEAD, HEAD), HEAD)
        dk[...] = jnp.zeros_like(dk)
        dv[...] = jnp.zeros_like(dv)
        for begin in range(0, seq, band):
            end = begin + band
            q, g = qkv_w[begin:end, lanes], gctx[begin:end, lanes]
            k, v = qkv_w[:end, k_lanes], qkv_w[:end, v_lanes]
            p = weights_of(q, k, begin, len_ref[0], scale)
            gp = lax.dot_general(g, v, (((1,), (1,)), ((), ())), preferred_element_type=full)
            ds = (p * (gp - jnp.sum(p * gp, axis=-1, keepdims=True))).astype(low)
            dq[begin:end, :] = jnp.dot(ds, k, preferred_element_type=full) * scale
            dk[:end, :] += lax.dot_general(ds, q, (((0,), (0,)), ((), ())), preferred_element_type=full)
            dv[:end, :] += lax.dot_general(p.astype(low), g, (((0,), (0,)), ((), ())), preferred_element_type=full)

        def back(r, sums):
            at = pl.ds(pl.multiple_of(r * band, band), band)
            cos_t, sin_t = cos_ref[at, :], -sin_ref[at, :]
            pieces = (turn(dq[at, :].astype(low).astype(full), cos_t, sin_t).astype(low),
                      turn((dk[at, :] * scale).astype(low).astype(full), cos_t, sin_t).astype(low),
                      dv[at, :].astype(low))
            out = []
            for part, (piece, total) in enumerate(zip(pieces, sums)):
                gproj[at, pl.ds(pl.multiple_of(part * width + h * HEAD, HEAD), HEAD)] = piece
                out.append(total + jnp.sum(piece.astype(full), axis=0, keepdims=True))
            return tuple(out)
        sums = lax.fori_loop(0, bands, back, (jnp.zeros((1, HEAD), full),) * 3)
        for part, total in enumerate(sums):
            small_ref[bias_row + part:bias_row + part + 1,
                      pl.ds(pl.multiple_of(place.sp * width + h * HEAD, HEAD), HEAD)] = total
        return carry
    lax.fori_loop(0, heads, head, 0)
    stores.append(pltpu.make_async_copy(gproj, proj_out, store_sem.at[1]))
    stores[1].start()
    qkv_load = load(qkv_hbm, qkv_w, 3)

    def unit_block(block, carry):
        slot = lax.rem(block, 2)
        down_load(block, slot).wait()
        pre_load(block, slot).wait()
        of = pl.ds(pl.multiple_of(block * units, units), units)
        room = pl.ds(pl.multiple_of(out_rows + slot * units, units), units)

        def row_band(r, total):
            at = pl.ds(pl.multiple_of(r * band, band), band)
            value = lax.dot_general(cot[at, :], up_w[room, :], (((1,), (1,)), ((), ())), preferred_element_type=full)
            value = (value * gelu_slope(pre[slot, at, :])).astype(low)
            gpre[at, of] = value
            return total + jnp.sum(value.astype(full), axis=0, keepdims=True)
        total = lax.fori_loop(0, bands, row_band, jnp.zeros((1, units), full))
        small_ref[pl.ds(unit_row + block // per_row, 1),
                  pl.ds(pl.multiple_of((lax.rem(block, per_row) * sp_size + place.sp) * units, units), units)] = total

        @pl.when(block + 2 < blocks)
        def _():
            down_load(block + 2, slot).start()
            pre_load(block + 2, slot).start()
        return carry

    lax.fori_loop(0, blocks // 2, unit_block, 0)
    fold.step(3)
    down.onward()
    tok_load = load(tok_hbm, left, 1)
    lax.fori_loop(blocks // 2, blocks, unit_block, 0)
    up_load = load(up_hbm, up_w, 0)
    stores.append(pltpu.make_async_copy(gpre, gpre_out, store_sem.at[2]))
    stores[2].start()
    tok_load.wait()

    def statistics(i, carry):
        at = pl.ds(pl.multiple_of(i * 32, 32), 32)
        rows = left[at, :].astype(full)
        mean = jnp.mean(rows, axis=-1, keepdims=True)
        centered = rows - mean
        inverse = lax.rsqrt(jnp.mean(centered * centered, axis=-1, keepdims=True) + eps)
        mean_s[at, :] = jnp.broadcast_to(mean, (32, 128))
        inv_s[at, :] = jnp.broadcast_to(inverse, (32, 128))
        return carry
    lax.fori_loop(0, seq // 32, statistics, 0)
    stores[0].wait()
    qkv_load.wait()
    up_load.wait()

    def hat_store(r):
        at = pl.ds(pl.multiple_of(r * band, band), band)
        return pltpu.make_async_copy(cot.at[at], hat_out.at[at], store_sem.at[3 + r])

    def hat_band(r):
        at = pl.ds(r * band, band)

        def columns(c, carry):
            to = pl.ds(pl.multiple_of(c * band, band), band)
            from_mlp = jnp.dot(gpre[at, :], up_w[:, to], preferred_element_type=full)
            from_attn = lax.dot_general(gproj[at, :], qkv_w[to, :], (((1,), (1,)), ((), ())), preferred_element_type=full)
            normed = (left[at, to].astype(full) - mean_s[at, 0:1]) * inv_s[at, 0:1]
            small_ref[gain_row:gain_row + 1, to] += jnp.sum(from_attn * normed, axis=0, keepdims=True)
            small_ref[gain_row + 1:gain_row + 2, to] += jnp.sum(from_mlp * normed, axis=0, keepdims=True)
            small_ref[shift_row:shift_row + 1, to] += jnp.sum(from_attn, axis=0, keepdims=True)
            small_ref[shift_row + 1:shift_row + 2, to] += jnp.sum(from_mlp, axis=0, keepdims=True)
            cot[at, to] = (from_attn * gain_ref[0:1, to] + from_mlp * gain_ref[1:2, to]).astype(low)
            return carry
        lax.fori_loop(0, wide // band, columns, 0)
        hat_store(r).start()

    for r in range(bands):
        hat_band(r)
    fold.finish()
    stores.append(pltpu.make_async_copy(stage, red_out, store_sem.at[3 + bands]))
    stores[-1].start()
    down.finish()
    stores.append(pltpu.make_async_copy(down.block(0), down_out, store_sem.at[4 + bands]))
    stores[-1].start()
    for r in range(bands):
        hat_store(r).wait()
    for c in stores[1:]:
        c.wait()
    for slot in range(4):
        down.sib_copy(slot).wait_send()
    down.drain()
    fold.drain()


def middle(sp_size, dp_size, lengths, cotangent, out_own, queries, key_rows, values, pre_act, hidden, down_own, up_own, qkv_own,
           tokens, partial_out, gains, cos_t, sin_t):
    seq, wide = tokens.shape
    width = queries.shape[1]
    units = up_own.shape[0] // dp_size
    own = seq // sp_size
    full, low = jnp.float32, jnp.bfloat16
    hbm = pl.BlockSpec(memory_space=pltpu.HBM)
    vmem = pl.BlockSpec(memory_space=pltpu.VMEM)
    dma = pltpu.SemaphoreType.DMA
    shape = jax.ShapeDtypeStruct

    def v(*dims, kind=low):
        return pltpu.VMEM(dims, kind)
    bands = seq // 256
    return pl.pallas_call(
        functools.partial(middle_kernel, sp_size),
        out_shape=[shape((units, wide), low), shape((seq, wide), low), shape((seq, 3 * width), low), shape(hidden.shape, low),
                   shape((seq, wide), low), shape((own, wide), low), shape((16, wide), full)],
        in_specs=[pl.BlockSpec(memory_space=pltpu.SMEM)] + [hbm] * 12 + [vmem] * 3,
        out_specs=[hbm] * 6 + [vmem],
        scratch_shapes=[
            v(seq, wide), v(seq, wide), v(*hidden.shape), v(*up_own.shape), v(*qkv_own.shape), v(2, seq, units, kind=full),
            v(seq, width), v(seq, 3 * width), v(seq, HEAD, kind=full), v(seq, HEAD, kind=full), v(seq, HEAD, kind=full),
            v(seq, 128, kind=full), v(seq, 128, kind=full),
            v(4, units, wide), v(4, units, wide), v(4, units, wide), v(2, units, wide), v(units, wide),
            v(2, sp_size - 1, own, wide), v(own, wide),
            dma((6,)), dma((2, 2)), dma((5 + bands,)), dma, dma((1, 4)), dma((1, 4)), dma((1, 2)), dma((1, 2)), dma((1,)), dma((1,)),
            dma((2, sp_size - 1)), dma((2, sp_size - 1))],
        compiler_params=pltpu.CompilerParams(collective_id=3, has_side_effects=True, vmem_limit_bytes=67043328),
        cost_estimate=pl.CostEstimate(flops=40 * 10 ** 9, bytes_accessed=90 * 1000 * 1000, transcendentals=0),
        name="middle",
    )(lengths, cotangent, out_own, queries, key_rows, values, pre_act, hidden, down_own, up_own, qkv_own, tokens, partial_out,
      gains, cos_t, sin_t)


def back_kernel(sp_size, cot_hbm, pre_hbm, mlp_hbm, attn_hbm, proj_hbm, ctx_hbm, hat_hbm, small_ref,
                up_out, qkv_out, dense_out, red_out, small_out,
                left_a, right_a, left_b, right_b, ctx, lent,
                up_sum, qkv_sum, dense_sum, up_sib, qkv_sib, dense_sib, up_one, qkv_one, dense_one, up_two, qkv_two, dense_two,
                dense_part, small_acc, small_in, small_z, inbox, stage,
                load_sem, store_sem, stage_sem, sib_send, sib_recv, one_send, one_recv, two_send, two_recv,
                slab_send, slab_recv, turn_send, turn_recv, small_send, small_recv, z_send, z_recv, fold_send, fold_recv):
    place = Square(sp_size, lent, sib_send, sib_recv, one_send, one_recv, two_send, two_recv)
    dp, sp = place.dp, place.sp
    per = 2
    pair, lane = dp // per, dp % per
    turn_dp = sp * per + lane
    slab_width = qkv_sum.shape[2]
    head_width = slab_width // 3
    rows = dense_one.shape[1]
    wide = left_b.shape[1]

    def load(source, target, which):
        c = pltpu.make_async_copy(source, target, load_sem.at[which])
        c.start()
        return c

    loads = [load(attn_hbm, left_a, 0), load(proj_hbm, right_a, 1), load(cot_hbm, right_b, 2), load(ctx_hbm, ctx, 3),
             load(pre_hbm, left_b, 4)]

    barrier = pltpu.get_barrier_semaphore()
    place.greet(barrier)

    @pl.when(pair != sp)
    def _():
        pl.semaphore_signal(barrier, inc=1, device_id=(turn_dp, pair), device_id_type=MESH)

    pl.semaphore_wait(barrier, 2 + sp_size + jnp.where(pair != sp, 1, 0))
    fold = Fold(place, hat_hbm, inbox, stage, stage_sem, fold_send, fold_recv)
    fold.step(1)

    def small_copy(stage_of):
        partner = (place.sibling, place.across_x, place.across_y)[stage_of]
        return remote(small_ref if stage_of == 0 else small_acc.at[stage_of - 1], small_in.at[stage_of],
                      small_send.at[stage_of], small_recv.at[stage_of], (partner, sp))

    def small_step(stage_of):
        small_copy(stage_of).wait_recv()
        before = small_ref[...] if stage_of == 0 else small_acc[stage_of - 1]
        small_acc[stage_of] = before + small_in[stage_of]

    def z_copy(step):
        return remote(small_acc.at[2], small_z.at[sp], z_send.at[step - 1], z_recv.at[step - 1],
                      (dp, lax.rem(sp + step, sp_size)))

    def z_arrival(step):
        origin = lax.rem(sp + sp_size - step, sp_size)
        return remote(small_acc.at[2], small_z.at[origin], z_send.at[step - 1], z_recv.at[step - 1], (dp, origin))

    small_copy(0).start()
    qkv = Wide(place, 0, left_a, right_a, slab_width, qkv_sum, qkv_sib, qkv_one, qkv_two)
    dense = Dense(place, 1, ctx, right_b, wide, dense_sum, dense_sib, dense_one, dense_two, dense_part)
    up = Wide(place, 2, left_b, right_b, wide, up_sum, up_sib, up_one, up_two)

    def turn_copy():
        return remote(dense.block(0), dense_out, turn_send, turn_recv, (turn_dp, pair))

    def slab_rows(owner):
        return pl.ds(pl.multiple_of(owner * rows, rows), rows)

    def slab_columns(part, owner):
        return pl.ds(pl.multiple_of(part * wide + owner * head_width, head_width), head_width)

    def slab_copy(step, part, origin, there):
        return remote(qkv_sum.at[0, slab_rows(there), pl.ds(part * head_width, head_width)],
                      qkv_out.at[:, slab_columns(part, origin)],
                      slab_send.at[step - 1, part], slab_recv.at[step - 1, part], (dp, there))

    stores = []

    def store(source, target):
        c = pltpu.make_async_copy(source, target, store_sem.at[len(stores)])
        c.start()
        stores.append(c)

    loads[0].wait()
    loads[1].wait()
    qkv.for_sibling(None)
    small_step(0)
    small_copy(1).start()
    qkv.for_self()
    loads[2].wait()
    loads[3].wait()
    dense.for_sibling(None)
    small_step(1)
    small_copy(2).start()
    dense.for_self()
    late = load(mlp_hbm, right_b, 2)
    fold.step(2)
    loads[4].wait()
    late.wait()
    up.for_sibling(qkv)
    qkv.onward()
    small_step(2)
    for step in range(1, sp_size):
        z_copy(step).start()
    small_z[sp] = small_acc[2]
    up.for_self()
    dense.onward()
    qkv.finish()
    for step in range(1, sp_size):
        for part in range(3):
            slab_copy(step, part, sp, lax.rem(sp + step, sp_size)).start()
    for part in range(3):
        store(qkv_sum.at[0, slab_rows(sp), pl.ds(part * head_width, head_width)], qkv_out.at[:, slab_columns(part, sp)])
    fold.step(3)
    dense.finish()

    @pl.when(pair != sp)
    def _():
        turn_copy().start()

    @pl.when(pair == sp)
    def _():
        c = pltpu.make_async_copy(dense.block(0), dense_out, store_sem.at[5])
        c.start()
        c.wait()

    for step in range(1, sp_size):
        z_arrival(step).wait_recv()
    total = small_z[0]
    for origin in range(1, sp_size):
        total = total + small_z[origin]
    small_out[...] = total
    up.onward()
    for step in range(1, sp_size):
        for part in range(3):
            slab_copy(step, part, lax.rem(sp + sp_size - step, sp_size), sp).wait_recv()

    @pl.when(pair != sp)
    def _():
        turn_copy().wait_recv()
        turn_copy().wait_send()

    for slot in range(4):
        up.sib_copy(slot).wait_send()
    dense.sib_copy(0).wait_send()
    fold.finish()
    store(stage, red_out)
    for array in (qkv, dense, up):
        array.drain()
    for stage_of in range(3):
        small_copy(stage_of).wait_send()
    for step in range(1, sp_size):
        z_copy(step).wait_send()
        for part in range(3):
            slab_copy(step, part, sp, lax.rem(sp + step, sp_size)).wait_send()
    fold.drain()
    up.finish()
    store(up.block(0), up_out)
    for c in stores:
        c.wait()


def reduce_gradients(sp_size, rows, grad_out, grad_pre, mlp_in, attn_in, grad_proj, context, grad_hat, small):
    seq, wide = mlp_in.shape
    slab_width = grad_proj.shape[1]
    units = 4 * rows
    own = seq // sp_size
    full, low = jnp.float32, jnp.bfloat16
    hbm = pl.BlockSpec(memory_space=pltpu.HBM)
    vmem = pl.BlockSpec(memory_space=pltpu.VMEM)
    dma = pltpu.SemaphoreType.DMA
    shape = jax.ShapeDtypeStruct

    def v(*dims, kind=low):
        return pltpu.VMEM(dims, kind)
    scratch = [
        v(seq, wide), v(seq, slab_width), v(seq, wide), v(seq, wide), v(seq, context.shape[1]), v(4, units, wide),
        v(4, units, wide), v(4, units, slab_width), v(4 * rows, wide),
        v(4, units, wide), v(4, units, slab_width), v(4 * rows, wide),
        v(2, units, wide), v(2, units, slab_width), v(2, rows, wide),
        v(units, wide), v(units, slab_width), v(rows, wide),
        v(4 * rows, wide),
        v(3, *small.shape, kind=full), v(3, *small.shape, kind=full), v(sp_size, *small.shape, kind=full),
        v(2, sp_size - 1, own, wide), v(own, wide),
        dma((5,)), dma((6,)), dma, dma((3, 4)), dma((3, 4)), dma((3, 2)), dma((3, 2)), dma((3,)), dma((3,)),
        dma((sp_size - 1, 3)), dma((sp_size - 1, 3)), dma, dma, dma((3,)), dma((3,)), dma((sp_size - 1,)), dma((sp_size - 1,)),
        dma((2, sp_size - 1)), dma((2, sp_size - 1)),
    ]
    return pl.pallas_call(
        functools.partial(back_kernel, sp_size),
        out_shape=[shape((units, wide), low), shape((rows, 3 * wide), low), shape((rows, wide), low), shape((own, wide), low),
                   shape(small.shape, full)],
        in_specs=[hbm] * 7 + [vmem], out_specs=[hbm] * 4 + [vmem],
        scratch_shapes=scratch,
        compiler_params=pltpu.CompilerParams(collective_id=1, has_side_effects=True, vmem_limit_bytes=67043328),
        cost_estimate=pl.CostEstimate(flops=17 * 10 ** 9, bytes_accessed=200 * 1000 * 1000, transcendentals=0),
        name="reduce_gradients",
    )(grad_out, grad_pre, mlp_in, attn_in, grad_proj, context, grad_hat, small)

def gather_plain(dp_size, sp_size, qkv_weight, out_weight, up_weight, down_weight):
    head_width = D // sp_size
    qkv_rows = qkv_weight.shape[0]
    qkv_slab = lax.all_to_all(
        qkv_weight.reshape(qkv_rows, 3, sp_size, head_width),
        "sp",
        split_axis=2,
        concat_axis=0,
        tiled=True,
    )
    qkv_own = lax.all_gather(
        qkv_slab.reshape(qkv_rows * sp_size, 3 * head_width), "dp", axis=0, tiled=True
    )
    up_own = lax.all_gather(up_weight, "dp", axis=0, tiled=True)
    down_own = lax.all_gather(down_weight, "dp", axis=0, tiled=True)
    out_blocks = lax.all_gather(out_weight, "dp", axis=0, tiled=True)
    out_own = lax.all_to_all(
        out_blocks.reshape(sp_size, dp_size // sp_size, qkv_rows, D),
        "sp",
        split_axis=0,
        concat_axis=2,
        tiled=True,
    ).reshape(head_width, D)
    return qkv_own, out_own, up_own, down_own


def reduce_plain(
    dp_size, sp_size, rows, hidden, grad_out, grad_pre, mlp_in, attn_in, grad_proj, context
):
    def scatter(left, right):
        return lax.psum_scatter(
            contract_rows(left, right).astype(jnp.bfloat16), "dp", scatter_dimension=0, tiled=True
        )

    grad_dense = lax.all_to_all(
        contract_rows(context, grad_out)
        .astype(jnp.bfloat16)
        .reshape(dp_size // sp_size, sp_size, rows, D),
        "sp",
        split_axis=1,
        concat_axis=0,
        tiled=True,
    ).reshape(dp_size * rows, D)
    grad_dense = lax.psum_scatter(grad_dense, "dp", scatter_dimension=0, tiled=True)
    grad_qkv = lax.all_to_all(
        scatter(attn_in, grad_proj).reshape(sp_size, rows, 3, 1, D // sp_size),
        "sp",
        split_axis=0,
        concat_axis=3,
        tiled=True,
    ).reshape(rows, 3 * D)
    return scatter(hidden, grad_out), scatter(grad_pre, mlp_in), grad_qkv, grad_dense


def body(
    tokens,
    lengths,
    cotangent,
    ln_gains,
    ln_shifts,
    qkv_weight,
    qkv_bias,
    out_weight,
    up_weight,
    up_bias,
    down_weight,
    out_bias,
):
    dp_size = lax.axis_size("dp")
    sp_size = lax.axis_size("sp")
    shard = lax.axis_index("sp")
    own_rows = tokens.shape[0]
    seq_rows = own_rows * sp_size
    head_width = D // sp_size
    length = lengths[0]
    low = jnp.bfloat16
    full = jnp.float32

    qkv_rows = qkv_weight.shape[0]
    units = up_weight.shape[0]
    square = dp_size == 8 and sp_size == 4
    unit_bias = (
        lax.dynamic_index_in_dim(
            up_bias.reshape(dp_size, sp_size, units), shard, 1, keepdims=False
        )
        .reshape(dp_size * units)
        .astype(full)
    )
    bias_own = (
        lax.dynamic_index_in_dim(
            qkv_bias.reshape(3, sp_size, head_width), shard, 1, keepdims=False
        )
        .reshape(1, 3 * head_width)
        .astype(full)
    )
    positions = jnp.arange(seq_rows, dtype=jnp.int32)
    gains = ln_gains.astype(full)
    shifts = ln_shifts.astype(full)
    row_valid = positions < length
    if square:
        qkv_own, out_own, up_own, seq_tokens, cos_rows, sin_rows = gather_weights(
            dp_size, sp_size, qkv_weight, out_weight, up_weight, tokens
        )
    else:
        cos_rows, sin_rows = rotary_rows(seq_rows)
        seq_tokens = lax.all_gather(tokens, "sp", axis=0, tiled=True)
        qkv_own, out_own, up_own, down_own = gather_plain(
            dp_size, sp_size, qkv_weight, out_weight, up_weight, down_weight
        )
        seq_cotangent = lax.all_gather(cotangent, "sp", axis=0, tiled=True)
    own_valid = shard * own_rows + jnp.arange(own_rows, dtype=jnp.int32) < length
    own_cotangent = jnp.where(own_valid[:, None], cotangent.astype(full), 0.0)
    if square:
        (
            down_own,
            seq_cotangent,
            attn_in,
            mlp_in,
            hidden,
            pre_act,
            partial_out,
            queries,
            key_rows,
            values,
            context,
        ) = front(
            sp_size,
            seq_tokens,
            qkv_own,
            up_own,
            out_own,
            down_weight,
            cotangent,
            gains,
            shifts,
            bias_own,
            unit_bias[None],
            cos_rows,
            sin_rows,
            lengths,
            dp_size,
        )
        grad_down, grad_hat, grad_proj, grad_pre, grad_out, reduced_out, small = middle(
            sp_size,
            dp_size,
            lengths,
            seq_cotangent,
            out_own,
            queries,
            key_rows,
            values,
            pre_act,
            hidden,
            down_own,
            up_own,
            qkv_own,
            seq_tokens,
            partial_out,
            gains,
            cos_rows,
            sin_rows,
        )
        grad_up, grad_qkv, grad_dense, reduced_hat, small = reduce_gradients(
            sp_size,
            qkv_rows,
            grad_out,
            grad_pre,
            mlp_in,
            attn_in,
            grad_proj,
            context,
            grad_hat,
            small,
        )
        gain_total, shift_total, qkv_bias_total = small[:2], small[2:4], small[4:7]
        unit_rows = up_bias.shape[0] // D
        unit_total = small[7 : 7 + unit_rows].reshape(-1)
        out_bias_total = small[7 + unit_rows]
    else:
        inputs = seq_tokens.astype(full)
        centre = jnp.mean(inputs, axis=-1, keepdims=True)
        centered = inputs - centre
        inverse = lax.rsqrt(jnp.mean(centered * centered, axis=-1, keepdims=True) + eps)
        normed = centered * inverse
        attn_in = (normed * gains[0] + shifts[0]).astype(low)
        mlp_in = (normed * gains[1] + shifts[1]).astype(low)
        projected = jnp.dot(attn_in, qkv_own, preferred_element_type=full)
        queries, key_rows, values, context = attend_fwd(
            projected, bias_own, cos_rows, sin_rows, lengths
        )
        pre_act = contract_cols(mlp_in, up_own) + unit_bias
        hidden = gelu_value(pre_act).astype(low)
        partial_out = (
            jnp.dot(hidden, down_own, preferred_element_type=full)
            + jnp.dot(context, out_own, preferred_element_type=full)
        ).astype(low)
        reduced_out = lax.psum_scatter(
            partial_out, "sp", scatter_dimension=0, tiled=True
        )
        grad_out = jnp.where(row_valid[:, None], seq_cotangent, jnp.zeros_like(seq_cotangent))
        grad_hidden = contract_cols(grad_out, down_own)
        grad_pre = (grad_hidden * gelu_slope(pre_act)).astype(low)
        grad_mlp_in = jnp.dot(grad_pre, up_own, preferred_element_type=full)

        grad_context = contract_cols(grad_out, out_own).astype(low)
        grad_proj, grad_proj_sum = attend_bwd(
            queries, key_rows, values, grad_context, cos_rows, sin_rows, lengths
        )
        grad_attn_in = contract_cols(grad_proj, qkv_own)
        grad_hat = grad_attn_in * gains[0] + grad_mlp_in * gains[1]
        reduced_hat = lax.psum_scatter(
            grad_hat.astype(low), "sp", scatter_dimension=0, tiled=True
        )
        spread_units = lax.dynamic_update_index_in_dim(
            jnp.zeros((dp_size, sp_size, units), full),
            jnp.sum(grad_pre, axis=0, dtype=full).reshape(dp_size, units),
            shard,
            1,
        ).reshape(-1)
        spread_bias = lax.dynamic_update_index_in_dim(
            jnp.zeros((3, sp_size, head_width), full),
            grad_proj_sum.reshape(3, head_width),
            shard,
            1,
        ).reshape(3, D)
        gain_grad = jnp.stack(
            [jnp.sum(grad_attn_in * normed, axis=0), jnp.sum(grad_mlp_in * normed, axis=0)]
        )
        shift_grad = jnp.stack([jnp.sum(grad_attn_in, axis=0), jnp.sum(grad_mlp_in, axis=0)])
        out_bias_part = jnp.sum(own_cotangent, axis=0)
        grad_down, grad_up, grad_qkv, grad_dense = reduce_plain(
            dp_size,
            sp_size,
            qkv_rows,
            hidden,
            grad_out,
            grad_pre,
            mlp_in,
            attn_in,
            grad_proj,
            context,
        )
        gain_total, shift_total, qkv_bias_total, unit_total, out_bias_total = lax.psum(
            (gain_grad, shift_grad, spread_bias, spread_units, out_bias_part), ("dp", "sp")
        )


    output = (
        tokens.astype(full) + reduced_out.astype(full) + out_bias.astype(full)
    ).astype(low)

    reduced_hat = reduced_hat.astype(full)
    own_centered = tokens.astype(full) - jnp.mean(tokens.astype(full), axis=-1, keepdims=True)
    own_inverse = lax.rsqrt(jnp.mean(own_centered * own_centered, axis=-1, keepdims=True) + eps)
    own_normed = own_centered * own_inverse
    grad_input = own_inverse * (
        reduced_hat
        - jnp.mean(reduced_hat, axis=-1, keepdims=True)
        - own_normed * jnp.mean(reduced_hat * own_normed, axis=-1, keepdims=True)
    )
    input_grad = (own_cotangent + grad_input).astype(low)
    return (
        output,
        input_grad,
        gain_total,
        shift_total,
        grad_qkv.astype(full),
        qkv_bias_total,
        grad_dense.astype(full),
        grad_up.astype(full),
        unit_total,
        grad_down.astype(full),
        out_bias_total,
    )


def solution(mesh):
    return jax.shard_map(
        body,
        mesh=mesh,
        in_specs=(
            P(("dp", "sp"), None),
            P("dp"),
            P(("dp", "sp"), None),
            P(),
            P(),
            P(("dp", "sp"), None),
            P(),
            P(("dp", "sp"), None),
            P(("dp", "sp"), None),
            P(),
            P(("dp", "sp"), None),
            P(),
        ),
        out_specs=(
            P(("dp", "sp"), None),
            P(("dp", "sp"), None),
            P(),
            P(),
            P(("dp", "sp"), None),
            P(),
            P(("dp", "sp"), None),
            P(("dp", "sp"), None),
            P(),
            P(("dp", "sp"), None),
            P(),
        ),
        check_vma=False,
    )
```

```python
import functools

import jax
import jax.numpy as jnp
from jax import lax
from jax.experimental import pallas as pl
from jax.experimental.pallas import tpu as pltpu
from jax.sharding import PartitionSpec as P

D = 2048
HEADS = 8
HEAD = 256
ROT = 64


eps = 1e-05
base_freq = 10000.0
root_half = 0.7071067811865476
inv_root_two_pi = 0.3989422804014327


def contract_rows(left, right):
    return lax.dot_general(
        left, right, (((0,), (0,)), ((), ())), preferred_element_type=jnp.float32
    )


def contract_cols(left, right):
    return lax.dot_general(
        left, right, (((1,), (1,)), ((), ())), preferred_element_type=jnp.float32
    )


def gelu_value(pre_act):
    return 0.5 * pre_act * (1.0 + lax.erf(pre_act * root_half))


def gelu_slope(pre_act):
    return 0.5 * (1.0 + lax.erf(pre_act * root_half)) + pre_act * inv_root_two_pi * jnp.exp(
        -0.5 * pre_act * pre_act
    )


BAND=256
def turn(x, cos_t, sin_t):
    first = x[:, :128]
    lane = lax.broadcasted_iota(jnp.int32, first.shape, 1)
    partner = jnp.where(lane < ROT // 2, pltpu.roll(first, 128 - ROT // 2, 1), pltpu.roll(first, ROT // 2, 1))
    return jnp.concatenate([first * cos_t + partner * sin_t, x[:, 128:]], axis=1)

def weights_of(q, k, start, length, scale):
    rows, cols = q.shape[0], k.shape[0]
    s = lax.dot_general(q, k, (((1,), (1,)), ((), ())), preferred_element_type=jnp.float32) * scale
    key = lax.broadcasted_iota(jnp.int32, (rows, cols), 1)
    query = start + lax.broadcasted_iota(jnp.int32, (rows, cols), 0)
    s = jnp.where((key <= query) & (key < length), s, -1e30)
    e = jnp.exp(s - jnp.max(s, axis=-1, keepdims=True))
    return e / jnp.sum(e, axis=-1, keepdims=True)

def fwd_kernel(scale, len_ref, pq, pk, pv, bq, bk, bv, cos_ref, sin_ref, q_ref, k_ref, v_ref, ctx_ref):
    length = len_ref[0]
    seq = pq.shape[0]
    cos_t, sin_t = cos_ref[...], sin_ref[...]
    q_ref[...] = turn(pq[...] + bq[...], cos_t, sin_t).astype(jnp.bfloat16)
    k_ref[...] = turn(pk[...] + bk[...], cos_t, sin_t).astype(jnp.bfloat16)
    v_ref[...] = (pv[...] + bv[...]).astype(jnp.bfloat16)
    for start in range(0, seq, BAND):
        end = start + BAND
        p = weights_of(q_ref[start:end, :], k_ref[:end, :], start, length, scale)
        ctx_ref[start:end, :] = jnp.dot(p.astype(jnp.bfloat16), v_ref[:end, :], preferred_element_type=jnp.float32).astype(jnp.bfloat16)

def attend_fwd(projected, bias, cos_t, sin_t, lengths):
    seq, width = projected.shape
    heads = width // 3 // HEAD
    col = lambda g: pl.BlockSpec((seq, HEAD), lambda h, *_, g=g: (0, g * heads + h))
    bcol = lambda g: pl.BlockSpec((1, HEAD), lambda h, *_, g=g: (0, g * heads + h))
    tab = pl.BlockSpec((seq, 128), lambda h, *_: (0, 0))
    out = pl.BlockSpec((seq, HEAD), lambda h, *_: (0, h))
    return pl.pallas_call(
        functools.partial(fwd_kernel, HEAD ** -0.5),
        grid_spec=pltpu.PrefetchScalarGridSpec(num_scalar_prefetch=1, grid=(heads,),
            in_specs=[col(0), col(1), col(2), bcol(0), bcol(1), bcol(2), tab, tab], out_specs=[out] * 4),
        out_shape=[jax.ShapeDtypeStruct((seq, heads * HEAD), jnp.bfloat16)] * 4,
        name="attend_fwd",
        cost_estimate=pl.CostEstimate(flops=heads * seq * seq * HEAD * 4, bytes_accessed=seq * width * 8, transcendentals=heads * seq * seq),
    )(lengths, projected, projected, projected, bias, bias, bias, cos_t, sin_t)

def bwd_kernel(scale, heads, len_ref, q_ref, k_ref, v_ref, g_ref, cos_ref, sin_ref, gp_ref, sum_ref, dk, dv, dq):
    length = len_ref[0]
    h = pl.program_id(0)
    seq = q_ref.shape[0]
    dk[...] = jnp.zeros_like(dk)
    dv[...] = jnp.zeros_like(dv)
    for start in range(0, seq, BAND):
        end = start + BAND
        q, g = q_ref[start:end, :], g_ref[start:end, :]
        k, v = k_ref[:end, :], v_ref[:end, :]
        p = weights_of(q, k, start, length, scale)
        gp = lax.dot_general(g, v, (((1,), (1,)), ((), ())), preferred_element_type=jnp.float32)
        ds = (p * (gp - jnp.sum(p * gp, axis=-1, keepdims=True))).astype(jnp.bfloat16)
        dq[start:end, :] = jnp.dot(ds, k, preferred_element_type=jnp.float32) * scale
        dk[:end, :] += lax.dot_general(ds, q, (((0,), (0,)), ((), ())), preferred_element_type=jnp.float32)
        dv[:end, :] += lax.dot_general(p.astype(jnp.bfloat16), g, (((0,), (0,)), ((), ())), preferred_element_type=jnp.float32)
    cos_t, sin_t = cos_ref[...], sin_ref[...]
    def back(x):
        return turn(x.astype(jnp.bfloat16).astype(jnp.float32), cos_t, -sin_t).astype(jnp.bfloat16)
    for g, piece in enumerate((back(dq[...]), back(dk[...] * scale), dv[...].astype(jnp.bfloat16))):
        at = pl.ds(pl.multiple_of((g * heads + h) * HEAD, HEAD), HEAD)
        gp_ref[:, at] = piece
        sum_ref[:, at] = jnp.sum(piece.astype(jnp.float32), axis=0, keepdims=True)

def attend_bwd(q, k, v, gctx, cos_t, sin_t, lengths):
    seq, width = q.shape
    heads = width // HEAD
    col = pl.BlockSpec((seq, HEAD), lambda h, *_: (0, h))
    tab = pl.BlockSpec((seq, 128), lambda h, *_: (0, 0))
    return pl.pallas_call(
        functools.partial(bwd_kernel, HEAD ** -0.5, heads),
        grid_spec=pltpu.PrefetchScalarGridSpec(num_scalar_prefetch=1, grid=(heads,),
            in_specs=[col] * 4 + [tab, tab],
            out_specs=[pl.BlockSpec((seq, 3 * width), lambda h, *_: (0, 0)), pl.BlockSpec((1, 3 * width), lambda h, *_: (0, 0))],
            scratch_shapes=[pltpu.VMEM((seq, HEAD), jnp.float32)] * 3),
        out_shape=[jax.ShapeDtypeStruct((seq, 3 * width), jnp.bfloat16), jax.ShapeDtypeStruct((1, 3 * width), jnp.float32)],
        name="attend_bwd",
        cost_estimate=pl.CostEstimate(flops=heads * seq * seq * HEAD * 10, bytes_accessed=seq * width * 20, transcendentals=heads * seq * seq),
    )(lengths, q, k, v, gctx, cos_t, sin_t)

def rotary_rows(seq):
    half = ROT // 2
    freq = 10000.0 ** (-jnp.arange(half, dtype=jnp.float32) * (2.0 / ROT))
    ang = jnp.arange(seq, dtype=jnp.int32).astype(jnp.float32)[:, None] * freq[None, :]
    c, s = jnp.cos(ang), jnp.sin(ang)
    rest = 128 - ROT
    return (jnp.concatenate([c, c, jnp.ones((seq, rest), jnp.float32)], 1), jnp.concatenate([-s, s, jnp.zeros((seq, rest), jnp.float32)], 1))

MESH = pl.DeviceIdType.MESH

def square_partners(dp):
    core, x, y = dp % 2, (dp // 2) % 2, dp // 4
    across_x, across_y = dp + 2 - 4 * x, dp + 4 - 8 * y
    first = across_x * (1 - core) + across_y * core
    second = across_y * (1 - core) + across_x * core
    return first, second, across_x + across_y - dp, 1 - 2 * core

class Hops:
    def __init__(self, count, dp, sp, source, result, send, recv):
        self.count, self.dp, self.sp, self.source, self.result = count, dp, sp, source, result
        self.send, self.recv, self.rows = send, recv, source.shape[0]

    def place(self, owner):
        return pl.ds(pl.multiple_of(owner * self.rows, self.rows), self.rows)

    def copy(self, way, step, owner, own):
        to = lax.rem(self.sp + (1 if way == 0 else self.count - 1), self.count)
        at = self.result.at[self.place(owner)]
        return pltpu.make_async_remote_copy(
            src_ref=self.source if own else at, dst_ref=at, send_sem=self.send.at[way, step],
            recv_sem=self.recv.at[way, step], device_id=(self.dp, to), device_id_type=MESH)

    def sends(self, way, step):
        if way == 0:
            return (self.sp >= step) & (self.sp < self.count - 1)
        return (self.sp < self.count - step) & (self.sp > 0)

    def receives(self, way, step):
        return self.sp >= step + 1 if way == 0 else self.sp < self.count - step - 1

    def owner(self, way, step):
        return self.sp - step if way == 0 else self.sp + step

    def start(self, way, step):
        @pl.when(self.sends(way, step))
        def _():
            self.copy(way, step, self.owner(way, step), step == 0).start()

    def begin(self):
        for way in (0, 1):
            self.start(way, 0)

    def relay(self, step):
        for way in (0, 1):
            @pl.when(self.receives(way, step - 1) & self.sends(way, step))
            def _():
                self.copy(way, step - 1, self.owner(way, step), False).wait_recv()
                self.copy(way, step, self.owner(way, step), False).start()

    def settle(self, step):
        for way in (0, 1):
            @pl.when(self.receives(way, step - 1) & jnp.logical_not(self.sends(way, step)))
            def _():
                self.copy(way, step - 1, self.owner(way, step), False).wait_recv()

    def finish(self):
        for step in range(self.count - 1):
            for way in (0, 1):
                @pl.when(self.sends(way, step))
                def _():
                    self.copy(way, step, self.owner(way, step), step == 0).wait_send()


def front_kernel(sp_size, len_ref, qkv_ref, out_ref, up_ref, down_ref, tok_ref, cot_ref, freq_ref, gain_ref, shift_ref,
                 qkv_bias_ref, unit_bias_ref,
                 qkv_all, out_all, up_all, down_all, tok_all, cot_all, attn_out, mlp_out, hidden_out, pre_out, part_out,
                 cos_ref, sin_ref, mean_ref, inv_ref, q_ref, k_ref, v_ref, ctx_ref,
                 tok, attn, mlp, qkv_w, up_w, hidden, pre,
                 send_sem, recv_sem, slab_send, slab_recv, keep_sem, turn_send, turn_recv, tok_send, tok_recv, cot_send, cot_recv,
                 load_sem, store_sem, pre_sem, part_sem):
    full, low = jnp.float32, jnp.bfloat16
    dp, sp = lax.axis_index("dp"), lax.axis_index("sp")
    first, second, diagonal, flip = square_partners(dp)
    sibling = dp + flip
    per = 2
    pair, lane = dp // per, dp % per
    rows = qkv_ref.shape[0]
    seq, wide = tok.shape
    own_rows = tok_ref.shape[0]
    head_width = wide // sp_size
    units = down_ref.shape[0]
    slab = rows * sp_size
    width = q_ref.shape[1]
    turn_dp = sp * per + lane
    scale = HEAD ** -0.5
    band = 256

    barrier = pltpu.get_barrier_semaphore()
    for other in (first, second, sibling):
        pl.semaphore_signal(barrier, inc=1, device_id=(other, sp), device_id_type=MESH)
    for step in range(1, sp_size):
        pl.semaphore_signal(barrier, inc=1, device_id=(dp, lax.rem(sp + step, sp_size)), device_id_type=MESH)

    @pl.when(pair != sp)
    def _():
        pl.semaphore_signal(barrier, inc=1, device_id=(turn_dp, pair), device_id_type=MESH)

    pl.semaphore_wait(barrier, 2 + sp_size + jnp.where(pair != sp, 1, 0))

    def remote_copy(source, target, send, recv, device):
        return pltpu.make_async_remote_copy(
            src_ref=source, dst_ref=target, send_sem=send, recv_sem=recv, device_id=device, device_id_type=MESH)

    def slab_at(owner):
        return pl.ds(pl.multiple_of((dp * sp_size + owner) * rows, rows), rows)

    def slab_columns(part, there):
        return pl.ds(pl.multiple_of(part * wide + there * head_width, head_width), head_width)

    def slab_copy(step, part, there, origin):
        return remote_copy(
            qkv_ref.at[:, slab_columns(part, there)],
            qkv_all.at[slab_at(origin), pl.ds(part * head_width, head_width)],
            slab_send.at[step - 1, part], slab_recv.at[step - 1, part], (dp, there))

    def plain(height):
        return lambda owner: pl.ds(pl.multiple_of(owner * height, height), height)

    def turned(owner):
        return pl.ds(pl.multiple_of((owner % per) * slab + (owner // per) * rows, rows), rows)

    def turn_copy(landing):
        return remote_copy(out_ref, out_all.at[turned(landing)], turn_send, turn_recv, (turn_dp, pair))

    arrays = ((up_ref, up_all, plain(units)), (None, qkv_all, plain(slab)), (None, out_all, turned), (down_ref, down_all, plain(units)))
    UP, QKV, OUT, DOWN = 0, 1, 2, 3

    def copy(index, message, block, target):
        source, result, place = arrays[index]
        at = result.at[place(block)]
        return remote_copy(at if source is None or message > 2 else source, at,
                           send_sem.at[index, message], recv_sem.at[index, message], (target, sp))

    sends = ((dp, first), (dp, second), (dp, sibling), (first, second), (first, sibling), (second, sibling), (diagonal, sibling))
    arrivals = (first, second, sibling, diagonal, second + flip, first + flip, diagonal + flip)

    def start(index, message):
        copy(index, message, *sends[message]).start()

    def arrived(index, message):
        copy(index, message, arrivals[message], sibling).wait_recv()

    def own(index):
        for message in (0, 1, 2):
            start(index, message)

    def onward(index):
        arrived(index, 0)
        start(index, 3)
        start(index, 4)
        arrived(index, 1)
        start(index, 5)

    def corner(index):
        arrived(index, 3)
        start(index, 6)

    def complete(index):
        for message in (2, 4, 5, 6):
            arrived(index, message)

    def load(source, target, which):
        c = pltpu.make_async_copy(source, target, load_sem.at[which])
        c.start()
        return c

    for step in range(1, sp_size):
        for part in range(3):
            slab_copy(step, part, lax.rem(sp + step, sp_size), sp).start()

    @pl.when(pair != sp)
    def _():
        turn_copy(turn_dp).start()

    own(UP)
    tokens = Hops(sp_size, dp, sp, tok_ref, tok_all, tok_send, tok_recv)
    cotangents = Hops(sp_size, dp, sp, cot_ref, cot_all, cot_send, cot_recv)
    tokens.begin()
    keeps = []

    def keep(source, target):
        c = pltpu.make_async_copy(source, target, keep_sem.at[len(keeps)])
        c.start()
        keeps.append(c)

    for part in range(3):
        keep(qkv_ref.at[:, slab_columns(part, sp)], qkv_all.at[slab_at(sp), pl.ds(part * head_width, head_width)])
    keep(up_ref, up_all.at[plain(units)(dp)])
    keep(down_ref, down_all.at[plain(units)(dp)])
    keep(tok_ref, tok_all.at[tokens.place(sp)])
    keep(cot_ref, cot_all.at[cotangents.place(sp)])

    def normalize(source, source_start, target_start):
        def chunk(i, carry):
            at = pl.ds(pl.multiple_of(target_start + i * 32, 32), 32)
            values = source[pl.ds(pl.multiple_of(source_start + i * 32, 32), 32), :].astype(full)
            mean = jnp.mean(values, axis=-1, keepdims=True)
            centered = values - mean
            inverse = lax.rsqrt(jnp.mean(centered * centered, axis=-1, keepdims=True) + eps)
            normed = centered * inverse
            mean_ref[at, :] = jnp.broadcast_to(mean, (32, 128))
            inv_ref[at, :] = jnp.broadcast_to(inverse, (32, 128))
            attn[at, :] = (normed * gain_ref[0:1, :].astype(full) + shift_ref[0:1, :].astype(full)).astype(low)
            mlp[at, :] = (normed * gain_ref[1:2, :].astype(full) + shift_ref[1:2, :].astype(full)).astype(low)
            return carry
        lax.fori_loop(0, own_rows // 32, chunk, 0)

    def absorb(step):
        for way in (0, 1):
            @pl.when(tokens.receives(way, step - 1))
            def _():
                at = tokens.place(tokens.owner(way, step))
                c = load(tok_all.at[at], tok.at[at], way)
                c.wait()
                begin = tokens.owner(way, step) * own_rows
                normalize(tok, begin, begin)

    def table(i, carry):
        at = pl.ds(pl.multiple_of(i * 64, 64), 64)
        lanes = lax.broadcasted_iota(jnp.int32, (64, 128), 1)
        position = i * 64 + lax.broadcasted_iota(jnp.int32, (64, 128), 0)
        angle = position.astype(full) * freq_ref[...]
        cos_ref[at, :] = jnp.where(lanes < ROT, jnp.cos(angle), 1.0)
        sine = jnp.sin(angle)
        sin_ref[at, :] = jnp.where(lanes < ROT, jnp.where(lanes < ROT // 2, -sine, sine), 0.0)
        return carry

    normalize(tok_ref, 0, sp * own_rows)
    lax.fori_loop(0, seq // 64, table, 0)
    for step in range(1, sp_size):
        for part in range(3):
            slab_copy(step, part, sp, lax.rem(sp + sp_size - step, sp_size)).wait_recv()
    for c in keeps[:3]:
        c.wait()
    own(QKV)

    @pl.when(pair == sp)
    def _():
        c = pltpu.make_async_copy(out_ref, out_all.at[turned(dp)], keep_sem.at[7])
        c.start()
        c.wait()

    @pl.when(pair != sp)
    def _():
        turn_copy(dp).wait_recv()

    own(OUT)
    onward(UP)
    tokens.relay(1)
    onward(QKV)
    onward(OUT)
    own(DOWN)
    tokens.settle(1)
    absorb(1)
    tokens.relay(2)
    cotangents.begin()
    corner(UP)
    complete(UP)
    for c in keeps[3:]:
        c.wait()
    up_load = load(up_all, up_w, 2)
    tokens.settle(2)
    absorb(2)
    corner(QKV)
    corner(OUT)
    complete(QKV)
    qkv_load = load(qkv_all, qkv_w, 3)
    complete(OUT)
    onward(DOWN)
    tokens.settle(3)
    absorb(3)
    stores = [pltpu.make_async_copy(attn, attn_out, store_sem.at[0]), pltpu.make_async_copy(mlp, mlp_out, store_sem.at[1])]
    for c in stores:
        c.start()
    qkv_load.wait()

    def head(h, carry):
        lanes = pl.ds(pl.multiple_of(h * HEAD, HEAD), HEAD)

        def project(r, carry):
            at = pl.ds(pl.multiple_of(r * band, band), band)
            cos_t, sin_t = cos_ref[at, :], sin_ref[at, :]
            for part, target in enumerate((q_ref, k_ref, v_ref)):
                cols = pl.ds(pl.multiple_of(part * width + h * HEAD, HEAD), HEAD)
                value = jnp.dot(attn[at, :], qkv_w[:, cols], preferred_element_type=full) + qkv_bias_ref[:, cols]
                if part < 2:
                    value = turn(value, cos_t, sin_t)
                target[at, lanes] = value.astype(low)
            return carry
        lax.fori_loop(0, seq // band, project, 0)
        for begin in range(0, seq, band):
            end = begin + band
            p = weights_of(q_ref[begin:end, lanes], k_ref[:end, lanes], begin, len_ref[0], scale)
            ctx_ref[begin:end, lanes] = jnp.dot(p.astype(low), v_ref[:end, lanes], preferred_element_type=full).astype(low)
        return carry

    lax.fori_loop(0, width // HEAD, head, 0)
    corner(DOWN)
    cotangents.relay(1)
    up_load.wait()

    def pre_store(block, slot):
        return pltpu.make_async_copy(pre.at[slot], pre_out.at[:, pl.ds(pl.multiple_of(block * units, units), units)],
                                     pre_sem.at[slot])

    def unit_block(block, carry):
        slot = lax.rem(block, 2)

        @pl.when(block >= 2)
        def _():
            pre_store(block - 2, slot).wait()

        of = pl.ds(pl.multiple_of(block * units, units), units)

        def row_band(r, carry):
            at = pl.ds(pl.multiple_of(r * band, band), band)
            value = lax.dot_general(mlp[at, :], up_w[of, :], (((1,), (1,)), ((), ())), preferred_element_type=full)
            value = value + unit_bias_ref[:, of]
            pre[slot, at, :] = value
            hidden[at, of] = gelu_value(value).astype(low)
            return carry
        lax.fori_loop(0, seq // band, row_band, 0)
        pre_store(block, slot).start()
        return carry

    blocks = up_w.shape[0] // units
    lax.fori_loop(0, blocks // 2, unit_block, 0)
    complete(DOWN)
    half = up_w.shape[0] // 2
    stores[0].wait()
    late = [load(down_all.at[pl.ds(0, half)], tok, 0), load(down_all.at[pl.ds(half, half)], attn, 1)]
    lax.fori_loop(blocks // 2, blocks, unit_block, 0)
    out_rows = out_all.shape[0]
    late.append(load(out_all, up_w.at[pl.ds(0, out_rows)], 2))
    cotangents.relay(2)
    for block in (blocks - 2, blocks - 1):
        pre_store(block, block % 2).wait()
    stores[1].wait()
    hidden_store = pltpu.make_async_copy(hidden, hidden_out, store_sem.at[0])
    hidden_store.start()
    for c in late:
        c.wait()

    def part_store(r):
        at = pl.ds(pl.multiple_of(r * band, band), band)
        return pltpu.make_async_copy(mlp.at[at], part_out.at[at], part_sem.at[r])

    def out_band(r, carry):
        at = pl.ds(pl.multiple_of(r * band, band), band)

        def out_columns(c, carry):
            to = pl.ds(pl.multiple_of(c * band, band), band)
            total = jnp.dot(hidden[at, :half], tok[:, to], preferred_element_type=full)
            total = total + jnp.dot(hidden[at, half:], attn[:, to], preferred_element_type=full)
            total = total + jnp.dot(ctx_ref[at, :], up_w[:out_rows, to], preferred_element_type=full)
            mlp[at, to] = total.astype(low)
            return carry
        lax.fori_loop(0, wide // band, out_columns, 0)
        part_store(r).start()
        return carry
    lax.fori_loop(0, seq // band, out_band, 0)
    for r in range(seq // band):
        part_store(r).wait()
    hidden_store.wait()
    for index in range(4):
        for message in range(7):
            copy(index, message, *sends[message]).wait_send()
    for step in range(1, sp_size):
        for part in range(3):
            slab_copy(step, part, lax.rem(sp + step, sp_size), sp).wait_send()

    @pl.when(pair != sp)
    def _():
        turn_copy(turn_dp).wait_send()

    tokens.finish()
    for step in (1, 2, 3):
        cotangents.settle(step)
    cotangents.finish()


def front(sp_size, dp_size, lengths, qkv_weight, out_weight, up_weight, down_weight, tokens, cotangent, gains, shifts, qkv_bias,
          unit_bias):
    rows, wide = out_weight.shape
    units = up_weight.shape[0]
    seq = tokens.shape[0] * sp_size
    width = wide // sp_size
    all_units = units * dp_size
    full, low = jnp.float32, jnp.bfloat16
    half = ROT // 2
    freq = base_freq ** (-jnp.arange(half, dtype=full) * (2.0 / ROT))
    freq = jnp.concatenate([freq, freq, jnp.zeros((128 - ROT,), full)])[None]
    hbm = pl.BlockSpec(memory_space=pltpu.HBM)
    vmem = pl.BlockSpec(memory_space=pltpu.VMEM)
    dma = pltpu.SemaphoreType.DMA
    shape = jax.ShapeDtypeStruct
    qkv_shape = (rows * sp_size * dp_size, 3 * width)
    return pl.pallas_call(
        functools.partial(front_kernel, sp_size),
        out_shape=[shape(qkv_shape, low), shape((rows * dp_size, wide), low), shape((all_units, wide), low),
                   shape((all_units, wide), low), shape((seq, wide), low), shape((seq, wide), low),
                   shape((seq, wide), low), shape((seq, wide), low), shape((seq, all_units), low), shape((seq, all_units), full),
                   shape((seq, wide), low)]
        + [shape((seq, 128), full)] * 4 + [shape((seq, width), low)] * 4,
        in_specs=[pl.BlockSpec(memory_space=pltpu.SMEM)] + [vmem] * 11,
        out_specs=[hbm] * 11 + [vmem] * 8,
        scratch_shapes=[pltpu.VMEM((seq, wide), low)] * 3 + [
            pltpu.VMEM(qkv_shape, low), pltpu.VMEM((all_units, wide), low),
            pltpu.VMEM((seq, all_units), low), pltpu.VMEM((2, seq, units), full),
            dma((4, 7)), dma((4, 7)), dma((sp_size - 1, 3)), dma((sp_size - 1, 3)), dma((8,)), dma, dma,
            dma((2, sp_size)), dma((2, sp_size)), dma((2, sp_size)), dma((2, sp_size)),
            dma((4,)), dma((2,)), dma((2,)), dma((seq // 256,))],
        compiler_params=pltpu.CompilerParams(collective_id=0, has_side_effects=True, vmem_limit_bytes=62 << 20),
        cost_estimate=pl.CostEstimate(flops=26 * 10 ** 9, bytes_accessed=300 * 1000 * 1000, transcendentals=0),
        name="front",
    )(lengths, qkv_weight, out_weight, up_weight, down_weight, tokens, cotangent, freq, gains, shifts, qkv_bias, unit_bias)

CHUNK = 512


def add_into(target, *others):
    step_rows = 32

    def step(i, carry):
        at = pl.ds(pl.multiple_of(i * step_rows, step_rows), step_rows)
        total = target[at, :].astype(jnp.float32)
        for other in others:
            total = total + other[at, :].astype(jnp.float32)
        target[at, :] = total.astype(jnp.bfloat16)
        return carry

    lax.fori_loop(0, target.shape[0] // step_rows, step, 0)


class Square:
    def __init__(self, sp_size, lent, sib_send, sib_recv, one_send, one_recv, two_send, two_recv):
        self.dp, self.sp, self.sp_size = lax.axis_index("dp"), lax.axis_index("sp"), sp_size
        self.core, self.chip = self.dp % 2, self.dp // 2
        self.x, self.y = self.chip % 2, self.chip // 2
        self.sibling = self.dp + 1 - 2 * self.core
        self.across_x, self.across_y = self.dp + 2 - 4 * self.x, self.dp + 4 - 8 * self.y
        self.first = self.across_y * (1 - self.core) + self.across_x * self.core
        self.second = self.across_x * (1 - self.core) + self.across_y * self.core
        self.second_mask = 1 + self.core
        self.lent = lent
        self.sib_send, self.sib_recv, self.one_send, self.one_recv, self.two_send, self.two_recv = (
            sib_send, sib_recv, one_send, one_recv, two_send, two_recv)

    def chip_of(self, mask):
        return lax.rem(self.x + lax.rem(mask, 2), 2) + 2 * lax.rem(self.y + mask // 2, 2)

    def greet(self, barrier):
        for other in (self.first, self.second, self.sibling):
            pl.semaphore_signal(barrier, inc=1, device_id=(other, self.sp), device_id_type=MESH)
        for step in range(1, self.sp_size):
            pl.semaphore_signal(
                barrier, inc=1, device_id=(self.dp, lax.rem(self.sp + step, self.sp_size)), device_id_type=MESH)


def remote(source, target, send, recv, device):
    return pltpu.make_async_remote_copy(
        src_ref=source, dst_ref=target, send_sem=send, recv_sem=recv, device_id=device, device_id_type=MESH)


class Wide:
    def __init__(self, place, index, left, right, width, sums, sib, one, two):
        self.place, self.index, self.left, self.right, self.width = place, index, left, right, width
        self.sums, self.sib, self.one, self.two = sums, sib, one, two
        self.units = sums.shape[1]

    def product(self, block, store):
        at = pl.ds(pl.multiple_of(block * self.units, self.units), self.units)

        def columns(part, carry):
            to = pl.ds(pl.multiple_of(part * CHUNK, CHUNK), CHUNK)
            store(to, lax.dot_general(
                self.left[:, at], self.right[:, to], (((0,), (0,)), ((), ())),
                preferred_element_type=jnp.float32))
            return carry
        lax.fori_loop(0, self.width // CHUNK, columns, 0)

    def sib_copy(self, slot):
        p = self.place
        return remote(p.lent.at[slot, :, :self.width], self.sib.at[p.chip_of(3 - slot)],
                      p.sib_send.at[self.index, slot], p.sib_recv.at[self.index, slot], (p.sibling, p.sp))

    def for_sibling(self, previous):
        p = self.place

        def step(slot, carry):
            if previous is not None:
                previous.sib_copy(slot).wait_send()

            def store(to, total):
                p.lent[slot, :, to] = total.astype(jnp.bfloat16)
            self.product(p.chip_of(3 - slot) * 2 + 1 - p.core, store)
            self.sib_copy(slot).start()
            return carry
        lax.fori_loop(0, 4, step, 0)

    def own(self, mask, slot):
        at = self.place.chip_of(mask)
        self.sib_copy(slot).wait_recv()

        def store(to, total):
            self.sums[mask, :, to] = (total + self.sib[at, :, to].astype(jnp.float32)).astype(jnp.bfloat16)
        self.product(at * 2 + self.place.core, store)

    def for_self(self):
        core = self.place.core

        def leave(slot, carry):
            mask = 3 - slot * (1 + core)
            self.own(mask, 3 - mask)
            self.first_copy(slot).start()
            return carry
        lax.fori_loop(0, 2, leave, 0)

        def stay(slot, carry):
            mask = self.place.second_mask * (1 - slot)
            self.own(mask, 3 - mask)
            return carry
        lax.fori_loop(0, 2, stay, 0)

    def block(self, mask):
        return self.sums.at[mask]

    def first_copy(self, slot):
        p = self.place
        return remote(self.block(3 - slot * (1 + p.core)), self.one.at[slot], p.one_send.at[self.index, slot],
                      p.one_recv.at[self.index, slot], (p.first, p.sp))

    def second_copy(self):
        p = self.place
        return remote(self.block(p.second_mask), self.two, p.two_send.at[self.index],
                      p.two_recv.at[self.index], (p.second, p.sp))

    def onward(self):
        self.first_copy(0).wait_recv()
        add_into(self.block(self.place.second_mask), self.one.at[0])
        self.second_copy().start()

    def finish(self):
        self.first_copy(1).wait_recv()
        self.second_copy().wait_recv()
        add_into(self.block(0), self.one.at[1], self.two)

    def drain(self):
        for slot in (0, 1):
            self.first_copy(slot).wait_send()
        self.second_copy().wait_send()


class Dense(Wide):
    def __init__(self, place, index, left, right, width, sums, sib, one, two, part):
        self.place, self.index, self.left, self.right, self.width = place, index, left, right, width
        self.sums, self.sib, self.one, self.two, self.part = sums, sib, one, two, part
        self.units, self.rows = sums.shape[0], one.shape[1]

    def sib_copy(self, slot):
        p = self.place
        return remote(self.part, self.sib, p.sib_send.at[self.index, 0], p.sib_recv.at[self.index, 0], (p.sibling, p.sp))

    def for_sibling(self, previous):
        def store(to, total):
            self.part[:, to] = total.astype(jnp.bfloat16)
        self.product(1 - self.place.core, store)
        self.sib_copy(0).start()

    def for_self(self):
        self.sib_copy(0).wait_recv()

        def store(to, total):
            self.sums[:, to] = (total + self.sib[:, to].astype(jnp.float32)).astype(jnp.bfloat16)
        self.product(self.place.core, store)
        for slot in (0, 1):
            self.first_copy(slot).start()

    def block(self, mask):
        return self.sums.at[pl.ds(pl.multiple_of(self.place.chip_of(mask) * self.rows, self.rows), self.rows)]


class Fold:
    def __init__(self, place, source, inbox, stage, stage_sem, send, recv, begun=1):
        self.begun = begun
        self.place, self.source, self.inbox, self.stage = place, source, inbox, stage
        self.stage_sem, self.send, self.recv = stage_sem, send, recv
        self.rows = stage.shape[0]

    def along(self, way):
        last = self.place.sp_size - 1
        return self.place.sp if way == 0 else last - self.place.sp

    def rows_of(self, way, step):
        count = self.place.sp_size
        owner = self.along(way) + count - step
        owner = owner if way == 0 else count - 1 - owner
        return self.source.at[pl.ds(pl.multiple_of(owner * self.rows, self.rows), self.rows)]

    def copy(self, way, step, own):
        p = self.place
        to = lax.rem(p.sp + (1 if way == 0 else p.sp_size - 1), p.sp_size)
        source = self.rows_of(way, step) if own else self.inbox.at[way, max(step - 2, 0)]
        return remote(source, self.inbox.at[way, step - 1], self.send.at[way, step - 1],
                      self.recv.at[way, step - 1], (p.dp, to))

    def take(self, rows):
        c = pltpu.make_async_copy(rows, self.stage, self.stage_sem)
        c.start()
        c.wait()

    def step(self, step):
        last = self.place.sp_size - 1
        for way in (0, 1):
            if step >= self.begun:
                @pl.when(self.along(way) == 0)
                def _():
                    self.copy(way, step, True).start()

            if step > 1:
                @pl.when((self.along(way) > 0) & (self.along(way) < step) & (self.along(way) < last))
                def _():
                    self.take(self.rows_of(way, step))
                    if step > self.begun:
                        self.copy(way, step - 1, False).wait_recv()
                    add_into(self.inbox.at[way, step - 2], self.stage)
                    self.copy(way, step, False).start()

    def finish(self):
        last = self.place.sp_size - 1
        self.take(self.source.at[pl.ds(pl.multiple_of(self.place.sp * self.rows, self.rows), self.rows)])
        for way in (0, 1):
            @pl.when(self.along(way) > 0)
            def _():
                self.copy(way, last, False).wait_recv()
                add_into(self.stage, self.inbox.at[way, last - 1])

    def drain(self):
        last = self.place.sp_size - 1
        for way in (0, 1):
            for step in range(1, last + 1):
                if step >= self.begun:
                    @pl.when(self.along(way) == 0)
                    def _():
                        self.copy(way, step, True).wait_send()

                if step > 1:
                    @pl.when((self.along(way) > 0) & (self.along(way) < step) & (self.along(way) < last))
                    def _():
                        self.copy(way, step, False).wait_send()


def middle_kernel(sp_size, len_ref, cot_hbm, out_hbm, q_hbm, k_hbm, v_hbm, pre_hbm, hidden_hbm, down_hbm, up_hbm, qkv_hbm,
                  tok_hbm, part_hbm, mlp_hbm, gain_ref, cos_ref, sin_ref, mean_s, inv_s,
                  down_out, up_out, hat_out, hat_in, proj_out, gout_out, red_out, small_ref,
                  cot, left, gpre, up_w, qkv_w, pre, gctx, gproj, dq, dk, dv,
                  lent, down_sum, down_sib, down_one, down_two, inbox, stage,
                  load_sem, stream_sem, store_sem, stage_sem, sib_send, sib_recv, one_send, one_recv, two_send, two_recv,
                  fold_send, fold_recv, hat_send, hat_recv, sib_free, one_free):
    full, low = jnp.float32, jnp.bfloat16
    place = Square(sp_size, lent, sib_send, sib_recv, one_send, one_recv, two_send, two_recv)
    seq, wide = cot.shape
    width = gctx.shape[1]
    heads = width // HEAD
    units = down_sum.shape[1]
    blocks = up_w.shape[0] // units
    out_rows = out_hbm.shape[0]
    band = 256
    bands = seq // band
    scale = HEAD ** -0.5

    def load(source, target, which):
        c = pltpu.make_async_copy(source, target, load_sem.at[which])
        c.start()
        return c

    early = [load(cot_hbm, cot, 0), load(hidden_hbm, left, 1), load(out_hbm, up_w.at[pl.ds(0, out_rows)], 2)]
    for i, source in enumerate((q_hbm, k_hbm, v_hbm)):
        early.append(load(source, qkv_w.at[pl.ds(0, seq), pl.ds(i * width, width)], 3 + i))

    def down_load(block, slot):
        return pltpu.make_async_copy(
            down_hbm.at[pl.ds(pl.multiple_of(block * units, units), units)],
            up_w.at[pl.ds(pl.multiple_of(out_rows + slot * units, units), units)], stream_sem.at[0, slot])

    def pre_load(block, slot):
        return pltpu.make_async_copy(
            pre_hbm.at[:, pl.ds(pl.multiple_of(block * units, units), units)], pre.at[slot], stream_sem.at[1, slot])

    for slot in (0, 1):
        down_load(slot, slot).start()
        pre_load(slot, slot).start()

    barrier = pltpu.get_barrier_semaphore()
    place.greet(barrier)
    pl.semaphore_wait(barrier, 2 + sp_size)
    fold = Fold(place, part_hbm, inbox, stage, stage_sem, fold_send, fold_recv)
    fold.step(1)
    small_ref[...] = jnp.zeros_like(small_ref)
    gain_row, shift_row, bias_row, unit_row = 0, 2, 4, 7
    per_row = wide // (sp_size * units)
    last_row = unit_row + blocks // per_row

    early[0].wait()

    def mask_rows(i, carry):
        at = pl.ds(pl.multiple_of(i * 32, 32), 32)
        row = i * 32 + lax.broadcasted_iota(jnp.int32, (32, wide), 0)
        cot[at, :] = jnp.where(row < len_ref[0], cot[at, :].astype(full), 0.0).astype(low)
        return carry
    lax.fori_loop(0, seq // 32, mask_rows, 0)
    stores = [pltpu.make_async_copy(cot, gout_out, store_sem.at[0])]
    stores[0].start()

    def own_rows(i, carry):
        at = pl.ds(pl.multiple_of(place.sp * (seq // sp_size) + i * 32, 32), 32)
        return carry + jnp.sum(cot[at, :].astype(full), axis=0, keepdims=True)
    small_ref[last_row:last_row + 1, :] = lax.fori_loop(0, seq // sp_size // 32, own_rows, jnp.zeros((1, wide), full))

    down = Wide(place, 0, left, cot, wide, down_sum, down_sib, down_one, down_two)
    early[1].wait()
    down.for_sibling(None)
    early[2].wait()

    def context_band(r, carry):
        at = pl.ds(pl.multiple_of(r * band, band), band)
        gctx[at, :] = lax.dot_general(
            cot[at, :], up_w[:out_rows, :], (((1,), (1,)), ((), ())), preferred_element_type=full).astype(low)
        return carry
    lax.fori_loop(0, bands, context_band, 0)
    down.for_self()
    mlp_load = load(mlp_hbm, left, 1)
    pl.semaphore_signal(sib_free, inc=1, device_id=(place.sibling, place.sp), device_id_type=MESH)
    fold.step(2)
    for c in early[3:]:
        c.wait()

    def head(h, carry):
        lanes = pl.ds(pl.multiple_of(h * HEAD, HEAD), HEAD)
        k_lanes = pl.ds(pl.multiple_of(width + h * HEAD, HEAD), HEAD)
        v_lanes = pl.ds(pl.multiple_of(2 * width + h * HEAD, HEAD), HEAD)
        dk[...] = jnp.zeros_like(dk)
        dv[...] = jnp.zeros_like(dv)
        for begin in range(0, seq, band):
            end = begin + band
            q, g = qkv_w[begin:end, lanes], gctx[begin:end, lanes]
            k, v = qkv_w[:end, k_lanes], qkv_w[:end, v_lanes]
            p = weights_of(q, k, begin, len_ref[0], scale)
            gp = lax.dot_general(g, v, (((1,), (1,)), ((), ())), preferred_element_type=full)
            ds = (p * (gp - jnp.sum(p * gp, axis=-1, keepdims=True))).astype(low)
            dq[begin:end, :] = jnp.dot(ds, k, preferred_element_type=full) * scale
            dk[:end, :] += lax.dot_general(ds, q, (((0,), (0,)), ((), ())), preferred_element_type=full)
            dv[:end, :] += lax.dot_general(p.astype(low), g, (((0,), (0,)), ((), ())), preferred_element_type=full)

        def back(r, sums):
            at = pl.ds(pl.multiple_of(r * band, band), band)
            cos_t, sin_t = cos_ref[at, :], -sin_ref[at, :]
            pieces = (turn(dq[at, :].astype(low).astype(full), cos_t, sin_t).astype(low),
                      turn((dk[at, :] * scale).astype(low).astype(full), cos_t, sin_t).astype(low),
                      dv[at, :].astype(low))
            out = []
            for part, (piece, total) in enumerate(zip(pieces, sums)):
                gproj[at, pl.ds(pl.multiple_of(part * width + h * HEAD, HEAD), HEAD)] = piece
                out.append(total + jnp.sum(piece.astype(full), axis=0, keepdims=True))
            return tuple(out)
        sums = lax.fori_loop(0, bands, back, (jnp.zeros((1, HEAD), full),) * 3)
        for part, total in enumerate(sums):
            small_ref[bias_row + part:bias_row + part + 1,
                      pl.ds(pl.multiple_of(place.sp * width + h * HEAD, HEAD), HEAD)] = total
        return carry
    lax.fori_loop(0, heads, head, 0)
    stores.append(pltpu.make_async_copy(gproj, proj_out, store_sem.at[1]))
    stores[1].start()
    qkv_load = load(qkv_hbm, qkv_w, 3)

    def unit_block(block, carry):
        slot = lax.rem(block, 2)
        down_load(block, slot).wait()
        pre_load(block, slot).wait()
        of = pl.ds(pl.multiple_of(block * units, units), units)
        room = pl.ds(pl.multiple_of(out_rows + slot * units, units), units)

        def row_band(r, total):
            at = pl.ds(pl.multiple_of(r * band, band), band)
            value = lax.dot_general(cot[at, :], up_w[room, :], (((1,), (1,)), ((), ())), preferred_element_type=full)
            value = (value * gelu_slope(pre[slot, at, :])).astype(low)
            gpre[at, of] = value
            return total + jnp.sum(value.astype(full), axis=0, keepdims=True)
        total = lax.fori_loop(0, bands, row_band, jnp.zeros((1, units), full))
        small_ref[pl.ds(unit_row + block // per_row, 1),
                  pl.ds(pl.multiple_of((lax.rem(block, per_row) * sp_size + place.sp) * units, units), units)] = total

        @pl.when(block + 2 < blocks)
        def _():
            down_load(block + 2, slot).start()
            pre_load(block + 2, slot).start()
        return carry

    down.onward()
    lax.fori_loop(0, 3 * blocks // 4, unit_block, 0)
    fold.step(3)
    lax.fori_loop(3 * blocks // 4, blocks, unit_block, 0)
    up_load = load(up_hbm, up_w, 0)
    down.finish()
    stores.append(pltpu.make_async_copy(down.block(0), down_out, store_sem.at[3 + bands]))
    stores[2].start()
    pl.semaphore_signal(one_free, inc=1, device_id=(place.first, place.sp), device_id_type=MESH)
    up = Wide(place, 1, gpre, left, wide, down_sum, down_sib, down_one, down_two)
    mlp_load.wait()
    pl.semaphore_wait(sib_free, 1)
    up.for_sibling(down)
    down.drain()
    stores[2].wait()
    pl.semaphore_wait(one_free, 1)
    up.for_self()
    tok_load = load(tok_hbm, left, 1)
    tok_load.wait()
    stores[0].wait()
    qkv_load.wait()
    up_load.wait()

    upper = 2 * place.sp // sp_size

    def hat_rows(r):
        return pl.ds(pl.multiple_of(((1 - upper) * (bands - 1 - r) + upper * r) * band, band), band)

    def hat_store(r):
        return pltpu.make_async_copy(cot.at[hat_rows(r)], hat_out.at[hat_rows(r)], store_sem.at[3 + r])

    def hat_hop(way):
        to = lax.rem(place.sp + (1 if way == 0 else sp_size - 1), sp_size)
        return remote(cot.at[hat_rows(0)], hat_in.at[way], hat_send.at[way], hat_recv.at[way], (place.dp, to))

    def hat_band(r, carry):
        at = hat_rows(r)

        def columns(c, carry):
            to = pl.ds(pl.multiple_of(c * band, band), band)
            from_mlp = jnp.dot(gpre[at, :], up_w[:, to], preferred_element_type=full)
            from_attn = lax.dot_general(gproj[at, :], qkv_w[to, :], (((1,), (1,)), ((), ())), preferred_element_type=full)
            normed = (left[at, to].astype(full) - mean_s[at, 0:1]) * inv_s[at, 0:1]
            small_ref[gain_row:gain_row + 1, to] += jnp.sum(from_attn * normed, axis=0, keepdims=True)
            small_ref[gain_row + 1:gain_row + 2, to] += jnp.sum(from_mlp * normed, axis=0, keepdims=True)
            small_ref[shift_row:shift_row + 1, to] += jnp.sum(from_attn, axis=0, keepdims=True)
            small_ref[shift_row + 1:shift_row + 2, to] += jnp.sum(from_mlp, axis=0, keepdims=True)
            cot[at, to] = (from_attn * gain_ref[0:1, to].astype(full) + from_mlp * gain_ref[1:2, to].astype(full)).astype(low)
            return carry
        lax.fori_loop(0, wide // band, columns, 0)
        hat_store(r).start()
        return carry

    hat_band(0, 0)
    for way in (0, 1):
        @pl.when(fold.along(way) == 0)
        def _():
            hat_hop(way).start()
    lax.fori_loop(1, bands, hat_band, 0)
    fold.finish()
    stores.append(pltpu.make_async_copy(stage, red_out, store_sem.at[4 + bands]))
    stores[-1].start()
    for slot, mask in enumerate((place.second_mask, 0)):
        up.first_copy(slot).wait_recv()
        add_into(up.block(mask), up.one.at[slot])
        stores.append(pltpu.make_async_copy(up.block(mask), up_out.at[slot], store_sem.at[5 + bands + slot]))
        stores[-1].start()
    for r in range(bands):
        hat_store(r).wait()
    for which in (1, 3, 4, 5):
        stores[which].wait()
    for slot in range(4):
        up.sib_copy(slot).wait_send()
    for slot in (0, 1):
        up.first_copy(slot).wait_send()
    fold.drain()
    for way in (0, 1):
        @pl.when(fold.along(way) == 0)
        def _():
            hat_hop(way).wait_send()

        @pl.when(fold.along(way) == 1)
        def _():
            hat_hop(way).wait_recv()


def middle(sp_size, dp_size, lengths, cotangent, out_own, queries, key_rows, values, pre_act, hidden, down_own, up_own, qkv_own,
           tokens, partial_out, mlp_in, gains, cos_t, sin_t, means, inverses):
    seq, wide = tokens.shape
    width = queries.shape[1]
    units = up_own.shape[0] // dp_size
    own = seq // sp_size
    full, low = jnp.float32, jnp.bfloat16
    hbm = pl.BlockSpec(memory_space=pltpu.HBM)
    vmem = pl.BlockSpec(memory_space=pltpu.VMEM)
    dma = pltpu.SemaphoreType.DMA
    shape = jax.ShapeDtypeStruct

    def v(*dims, kind=low):
        return pltpu.VMEM(dims, kind)
    bands = seq // 256
    return pl.pallas_call(
        functools.partial(middle_kernel, sp_size),
        out_shape=[shape((units, wide), low), shape((2, units, wide), low), shape((seq, wide), low), shape((2, own, wide), low),
                   shape((seq, 3 * width), low),
                   shape((seq, wide), low), shape((own, wide), low), shape((16, wide), full)],
        in_specs=[pl.BlockSpec(memory_space=pltpu.SMEM)] + [hbm] * 13 + [vmem] * 5,
        out_specs=[hbm] * 7 + [vmem],
        scratch_shapes=[
            v(seq, wide), v(seq, wide), v(*hidden.shape), v(*up_own.shape), v(*qkv_own.shape), v(2, seq, units, kind=full),
            v(seq, width), v(seq, 3 * width), v(seq, HEAD, kind=full), v(seq, HEAD, kind=full), v(seq, HEAD, kind=full),
            v(4, units, wide), v(4, units, wide), v(4, units, wide), v(2, units, wide), v(units, wide),
            v(2, sp_size - 1, own, wide), v(own, wide),
            dma((6,)), dma((2, 2)), dma((7 + bands,)), dma, dma((2, 4)), dma((2, 4)), dma((2, 2)), dma((2, 2)), dma((2,)), dma((2,)),
            dma((2, sp_size - 1)), dma((2, sp_size - 1)), dma((2,)), dma((2,)),
            pltpu.SemaphoreType.REGULAR, pltpu.SemaphoreType.REGULAR],
        compiler_params=pltpu.CompilerParams(collective_id=3, has_side_effects=True, vmem_limit_bytes=67043328),
        cost_estimate=pl.CostEstimate(flops=40 * 10 ** 9, bytes_accessed=90 * 1000 * 1000, transcendentals=0),
        name="middle",
    )(lengths, cotangent, out_own, queries, key_rows, values, pre_act, hidden, down_own, up_own, qkv_own, tokens, partial_out,
      mlp_in, gains, cos_t, sin_t, means, inverses)


def back_kernel(sp_size, cot_hbm, attn_hbm, proj_hbm, ctx_hbm, hat_hbm, hop_hbm, up_hbm, small_ref,
                up_out, qkv_out, dense_out, red_out, small_out,
                left, right, cot, ctx, lent,
                qkv_sum, dense_sum, qkv_sib, dense_sib, qkv_one, dense_one, qkv_two, dense_two,
                dense_part, up_room, up_two, small_acc, small_in, small_z, inbox, stage,
                load_sem, store_sem, stage_sem, sib_send, sib_recv, one_send, one_recv, two_send, two_recv,
                slab_send, slab_recv, turn_send, turn_recv, up_send, up_recv, small_send, small_recv, z_send, z_recv,
                fold_send, fold_recv):
    place = Square(sp_size, lent, sib_send, sib_recv, one_send, one_recv, two_send, two_recv)
    dp, sp = place.dp, place.sp
    per = 2
    pair, lane = dp // per, dp % per
    turn_dp = sp * per + lane
    slab_width = qkv_sum.shape[2]
    head_width = slab_width // 3
    rows = dense_one.shape[1]
    wide = left.shape[1]

    def load(source, target, which):
        c = pltpu.make_async_copy(source, target, load_sem.at[which])
        c.start()
        return c

    up_load = load(up_hbm, up_room, 0)
    hops = [load(hop_hbm.at[way], inbox.at[way, 0], 1 + way) for way in (0, 1)]
    loads = [load(ctx_hbm, ctx, 3), load(cot_hbm, cot, 4), load(attn_hbm, left, 5), load(proj_hbm, right, 6)]

    barrier = pltpu.get_barrier_semaphore()
    place.greet(barrier)

    @pl.when(pair != sp)
    def _():
        pl.semaphore_signal(barrier, inc=1, device_id=(turn_dp, pair), device_id_type=MESH)

    pl.semaphore_wait(barrier, 2 + sp_size + jnp.where(pair != sp, 1, 0))
    fold = Fold(place, hat_hbm, inbox, stage, stage_sem, fold_send, fold_recv, begun=2)

    def small_copy(stage_of):
        partner = (place.sibling, place.across_x, place.across_y)[stage_of]
        return remote(small_ref if stage_of == 0 else small_acc.at[stage_of - 1], small_in.at[stage_of],
                      small_send.at[stage_of], small_recv.at[stage_of], (partner, sp))

    def small_step(stage_of):
        small_copy(stage_of).wait_recv()
        before = small_ref[...] if stage_of == 0 else small_acc[stage_of - 1]
        small_acc[stage_of] = before + small_in[stage_of]

    def z_copy(step):
        return remote(small_acc.at[2], small_z.at[sp], z_send.at[step - 1], z_recv.at[step - 1],
                      (dp, lax.rem(sp + step, sp_size)))

    def z_arrival(step):
        origin = lax.rem(sp + sp_size - step, sp_size)
        return remote(small_acc.at[2], small_z.at[origin], z_send.at[step - 1], z_recv.at[step - 1], (dp, origin))

    def up_copy():
        return remote(up_room.at[0], up_two, up_send, up_recv, (place.second, sp))

    def turn_copy():
        return remote(dense.block(0), dense_out, turn_send, turn_recv, (turn_dp, pair))

    def slab_rows(owner):
        return pl.ds(pl.multiple_of(owner * rows, rows), rows)

    def slab_columns(part, owner):
        return pl.ds(pl.multiple_of(part * wide + owner * head_width, head_width), head_width)

    def slab_copy(step, part, origin, there):
        return remote(qkv_sum.at[0, slab_rows(there), pl.ds(part * head_width, head_width)],
                      qkv_out.at[:, slab_columns(part, origin)],
                      slab_send.at[step - 1, part], slab_recv.at[step - 1, part], (dp, there))

    stores = []

    def store(source, target):
        c = pltpu.make_async_copy(source, target, store_sem.at[len(stores)])
        c.start()
        stores.append(c)

    small_copy(0).start()
    up_load.wait()
    up_copy().start()
    dense = Dense(place, 0, ctx, cot, wide, dense_sum, dense_sib, dense_one, dense_two, dense_part)
    qkv = Wide(place, 1, left, right, slab_width, qkv_sum, qkv_sib, qkv_one, qkv_two)
    for way in (0, 1):
        hops[way].wait()
    fold.step(2)
    small_step(0)
    small_copy(1).start()
    loads[0].wait()
    loads[1].wait()
    dense.for_sibling(None)
    loads[2].wait()
    loads[3].wait()
    qkv.for_sibling(None)
    small_step(1)
    small_copy(2).start()
    dense.for_self()
    qkv.for_self()
    small_step(2)
    for step in range(1, sp_size):
        z_copy(step).start()
    small_z[sp] = small_acc[2]
    fold.step(3)
    dense.onward()
    qkv.onward()
    dense.finish()

    @pl.when(pair != sp)
    def _():
        turn_copy().start()

    @pl.when(pair == sp)
    def _():
        c = pltpu.make_async_copy(dense.block(0), dense_out, store_sem.at[5])
        c.start()
        c.wait()

    qkv.finish()
    for step in range(1, sp_size):
        for part in range(3):
            slab_copy(step, part, sp, lax.rem(sp + step, sp_size)).start()
    for part in range(3):
        store(qkv_sum.at[0, slab_rows(sp), pl.ds(part * head_width, head_width)], qkv_out.at[:, slab_columns(part, sp)])
    up_copy().wait_recv()
    add_into(up_room.at[1], up_two)
    store(up_room.at[1], up_out)
    for step in range(1, sp_size):
        z_arrival(step).wait_recv()
    total = small_z[0]
    for origin in range(1, sp_size):
        total = total + small_z[origin]
    small_out[...] = total
    fold.finish()
    store(stage, red_out)
    for slot in range(4):
        qkv.sib_copy(slot).wait_send()
    dense.sib_copy(0).wait_send()
    for array in (dense, qkv):
        array.drain()
    up_copy().wait_send()
    for stage_of in range(3):
        small_copy(stage_of).wait_send()
    fold.drain()
    for step in range(1, sp_size):
        z_copy(step).wait_send()
        for part in range(3):
            slab_copy(step, part, lax.rem(sp + sp_size - step, sp_size), sp).wait_recv()
            slab_copy(step, part, sp, lax.rem(sp + step, sp_size)).wait_send()

    @pl.when(pair != sp)
    def _():
        turn_copy().wait_recv()
        turn_copy().wait_send()

    for c in stores:
        c.wait()


def reduce_gradients(sp_size, rows, grad_out, attn_in, grad_proj, context, grad_hat, hat_hop, up_sums, small):
    seq, wide = attn_in.shape
    slab_width = grad_proj.shape[1]
    units = up_sums.shape[1]
    slab = 4 * rows
    own = seq // sp_size
    full, low = jnp.float32, jnp.bfloat16
    hbm = pl.BlockSpec(memory_space=pltpu.HBM)
    vmem = pl.BlockSpec(memory_space=pltpu.VMEM)
    dma = pltpu.SemaphoreType.DMA
    shape = jax.ShapeDtypeStruct

    def v(*dims, kind=low):
        return pltpu.VMEM(dims, kind)
    scratch = [
        v(seq, wide), v(seq, slab_width), v(seq, wide), v(seq, context.shape[1]), v(4, slab, slab_width),
        v(4, slab, slab_width), v(slab, wide), v(4, slab, slab_width), v(slab, wide),
        v(2, slab, slab_width), v(2, rows, wide), v(slab, slab_width), v(rows, wide),
        v(slab, wide), v(2, units, wide), v(units, wide),
        v(3, *small.shape, kind=full), v(3, *small.shape, kind=full), v(sp_size, *small.shape, kind=full),
        v(2, sp_size - 1, own, wide), v(own, wide),
        dma((7,)), dma((6,)), dma, dma((2, 4)), dma((2, 4)), dma((2, 2)), dma((2, 2)), dma((2,)), dma((2,)),
        dma((sp_size - 1, 3)), dma((sp_size - 1, 3)), dma, dma, dma, dma, dma((3,)), dma((3,)),
        dma((sp_size - 1,)), dma((sp_size - 1,)), dma((2, sp_size - 1)), dma((2, sp_size - 1)),
    ]
    return pl.pallas_call(
        functools.partial(back_kernel, sp_size),
        out_shape=[shape((units, wide), low), shape((rows, 3 * wide), low), shape((rows, wide), low), shape((own, wide), low),
                   shape(small.shape, full)],
        in_specs=[hbm] * 7 + [vmem], out_specs=[hbm] * 4 + [vmem],
        scratch_shapes=scratch,
        compiler_params=pltpu.CompilerParams(collective_id=1, has_side_effects=True, vmem_limit_bytes=62 << 20),
        cost_estimate=pl.CostEstimate(flops=9 * 10 ** 9, bytes_accessed=200 * 1000 * 1000, transcendentals=0),
        name="reduce_gradients",
    )(grad_out, attn_in, grad_proj, context, grad_hat, hat_hop, up_sums, small)

def gather_plain(dp_size, sp_size, qkv_weight, out_weight, up_weight, down_weight):
    head_width = D // sp_size
    qkv_rows = qkv_weight.shape[0]
    qkv_slab = lax.all_to_all(
        qkv_weight.reshape(qkv_rows, 3, sp_size, head_width),
        "sp",
        split_axis=2,
        concat_axis=0,
        tiled=True,
    )
    qkv_own = lax.all_gather(
        qkv_slab.reshape(qkv_rows * sp_size, 3 * head_width), "dp", axis=0, tiled=True
    )
    up_own = lax.all_gather(up_weight, "dp", axis=0, tiled=True)
    down_own = lax.all_gather(down_weight, "dp", axis=0, tiled=True)
    out_blocks = lax.all_gather(out_weight, "dp", axis=0, tiled=True)
    out_own = lax.all_to_all(
        out_blocks.reshape(sp_size, dp_size // sp_size, qkv_rows, D),
        "sp",
        split_axis=0,
        concat_axis=2,
        tiled=True,
    ).reshape(head_width, D)
    return qkv_own, out_own, up_own, down_own


def reduce_plain(
    dp_size, sp_size, rows, hidden, grad_out, grad_pre, mlp_in, attn_in, grad_proj, context
):
    def scatter(left, right):
        return lax.psum_scatter(
            contract_rows(left, right).astype(jnp.bfloat16), "dp", scatter_dimension=0, tiled=True
        )

    grad_dense = lax.all_to_all(
        contract_rows(context, grad_out)
        .astype(jnp.bfloat16)
        .reshape(dp_size // sp_size, sp_size, rows, D),
        "sp",
        split_axis=1,
        concat_axis=0,
        tiled=True,
    ).reshape(dp_size * rows, D)
    grad_dense = lax.psum_scatter(grad_dense, "dp", scatter_dimension=0, tiled=True)
    grad_qkv = lax.all_to_all(
        scatter(attn_in, grad_proj).reshape(sp_size, rows, 3, 1, D // sp_size),
        "sp",
        split_axis=0,
        concat_axis=3,
        tiled=True,
    ).reshape(rows, 3 * D)
    return scatter(hidden, grad_out), scatter(grad_pre, mlp_in), grad_qkv, grad_dense


def body(
    tokens,
    lengths,
    cotangent,
    ln_gains,
    ln_shifts,
    qkv_weight,
    qkv_bias,
    out_weight,
    up_weight,
    up_bias,
    down_weight,
    out_bias,
):
    dp_size = lax.axis_size("dp")
    sp_size = lax.axis_size("sp")
    shard = lax.axis_index("sp")
    own_rows = tokens.shape[0]
    seq_rows = own_rows * sp_size
    head_width = D // sp_size
    length = lengths[0]
    low = jnp.bfloat16
    full = jnp.float32

    qkv_rows = qkv_weight.shape[0]
    units = up_weight.shape[0]
    square = dp_size == 8 and sp_size == 4
    unit_bias = (
        lax.dynamic_index_in_dim(
            up_bias.reshape(dp_size, sp_size, units), shard, 1, keepdims=False
        )
        .reshape(dp_size * units)
        .astype(full)
    )
    bias_own = (
        lax.dynamic_index_in_dim(
            qkv_bias.reshape(3, sp_size, head_width), shard, 1, keepdims=False
        )
        .reshape(1, 3 * head_width)
        .astype(full)
    )
    positions = jnp.arange(seq_rows, dtype=jnp.int32)
    gains = ln_gains.astype(full)
    shifts = ln_shifts.astype(full)
    row_valid = positions < length
    if not square:
        cos_rows, sin_rows = rotary_rows(seq_rows)
        seq_tokens = lax.all_gather(tokens, "sp", axis=0, tiled=True)
        qkv_own, out_own, up_own, down_own = gather_plain(
            dp_size, sp_size, qkv_weight, out_weight, up_weight, down_weight
        )
        seq_cotangent = lax.all_gather(cotangent, "sp", axis=0, tiled=True)
    own_valid = shard * own_rows + jnp.arange(own_rows, dtype=jnp.int32) < length
    own_cotangent = jnp.where(own_valid[:, None], cotangent.astype(full), 0.0)
    if square:
        (
            qkv_own,
            out_own,
            up_own,
            down_own,
            seq_tokens,
            seq_cotangent,
            attn_in,
            mlp_in,
            hidden,
            pre_act,
            partial_out,
            cos_rows,
            sin_rows,
            means,
            inverses,
            queries,
            key_rows,
            values,
            context,
        ) = front(
            sp_size,
            dp_size,
            lengths,
            qkv_weight,
            out_weight,
            up_weight,
            down_weight,
            tokens,
            cotangent,
            ln_gains,
            ln_shifts,
            bias_own,
            unit_bias[None],
        )
        grad_down, up_sums, grad_hat, hat_hop, grad_proj, grad_out, reduced_out, small = middle(
            sp_size,
            dp_size,
            lengths,
            seq_cotangent,
            out_own,
            queries,
            key_rows,
            values,
            pre_act,
            hidden,
            down_own,
            up_own,
            qkv_own,
            seq_tokens,
            partial_out,
            mlp_in,
            ln_gains,
            cos_rows,
            sin_rows,
            means,
            inverses,
        )
        grad_up, grad_qkv, grad_dense, reduced_hat, small = reduce_gradients(
            sp_size,
            qkv_rows,
            grad_out,
            attn_in,
            grad_proj,
            context,
            grad_hat,
            hat_hop,
            up_sums,
            small,
        )
        gain_total, shift_total, qkv_bias_total = small[:2], small[2:4], small[4:7]
        unit_rows = up_bias.shape[0] // D
        unit_total = small[7 : 7 + unit_rows].reshape(-1)
        out_bias_total = small[7 + unit_rows]
    else:
        inputs = seq_tokens.astype(full)
        centre = jnp.mean(inputs, axis=-1, keepdims=True)
        centered = inputs - centre
        inverse = lax.rsqrt(jnp.mean(centered * centered, axis=-1, keepdims=True) + eps)
        normed = centered * inverse
        attn_in = (normed * gains[0] + shifts[0]).astype(low)
        mlp_in = (normed * gains[1] + shifts[1]).astype(low)
        projected = jnp.dot(attn_in, qkv_own, preferred_element_type=full)
        queries, key_rows, values, context = attend_fwd(
            projected, bias_own, cos_rows, sin_rows, lengths
        )
        pre_act = contract_cols(mlp_in, up_own) + unit_bias
        hidden = gelu_value(pre_act).astype(low)
        partial_out = (
            jnp.dot(hidden, down_own, preferred_element_type=full)
            + jnp.dot(context, out_own, preferred_element_type=full)
        ).astype(low)
        reduced_out = lax.psum_scatter(
            partial_out, "sp", scatter_dimension=0, tiled=True
        )
        grad_out = jnp.where(row_valid[:, None], seq_cotangent, jnp.zeros_like(seq_cotangent))
        grad_hidden = contract_cols(grad_out, down_own)
        grad_pre = (grad_hidden * gelu_slope(pre_act)).astype(low)
        grad_mlp_in = jnp.dot(grad_pre, up_own, preferred_element_type=full)

        grad_context = contract_cols(grad_out, out_own).astype(low)
        grad_proj, grad_proj_sum = attend_bwd(
            queries, key_rows, values, grad_context, cos_rows, sin_rows, lengths
        )
        grad_attn_in = contract_cols(grad_proj, qkv_own)
        grad_hat = grad_attn_in * gains[0] + grad_mlp_in * gains[1]
        reduced_hat = lax.psum_scatter(
            grad_hat.astype(low), "sp", scatter_dimension=0, tiled=True
        )
        spread_units = lax.dynamic_update_index_in_dim(
            jnp.zeros((dp_size, sp_size, units), full),
            jnp.sum(grad_pre, axis=0, dtype=full).reshape(dp_size, units),
            shard,
            1,
        ).reshape(-1)
        spread_bias = lax.dynamic_update_index_in_dim(
            jnp.zeros((3, sp_size, head_width), full),
            grad_proj_sum.reshape(3, head_width),
            shard,
            1,
        ).reshape(3, D)
        gain_grad = jnp.stack(
            [jnp.sum(grad_attn_in * normed, axis=0), jnp.sum(grad_mlp_in * normed, axis=0)]
        )
        shift_grad = jnp.stack([jnp.sum(grad_attn_in, axis=0), jnp.sum(grad_mlp_in, axis=0)])
        out_bias_part = jnp.sum(own_cotangent, axis=0)
        grad_down, grad_up, grad_qkv, grad_dense = reduce_plain(
            dp_size,
            sp_size,
            qkv_rows,
            hidden,
            grad_out,
            grad_pre,
            mlp_in,
            attn_in,
            grad_proj,
            context,
        )
        gain_total, shift_total, qkv_bias_total, unit_total, out_bias_total = lax.psum(
            (gain_grad, shift_grad, spread_bias, spread_units, out_bias_part), ("dp", "sp")
        )


    output = (
        tokens.astype(full) + reduced_out.astype(full) + out_bias.astype(full)
    ).astype(low)

    reduced_hat = reduced_hat.astype(full)
    own_centered = tokens.astype(full) - jnp.mean(tokens.astype(full), axis=-1, keepdims=True)
    own_inverse = lax.rsqrt(jnp.mean(own_centered * own_centered, axis=-1, keepdims=True) + eps)
    own_normed = own_centered * own_inverse
    grad_input = own_inverse * (
        reduced_hat
        - jnp.mean(reduced_hat, axis=-1, keepdims=True)
        - own_normed * jnp.mean(reduced_hat * own_normed, axis=-1, keepdims=True)
    )
    input_grad = (own_cotangent + grad_input).astype(low)
    return (
        output,
        input_grad,
        gain_total,
        shift_total,
        grad_qkv.astype(full),
        qkv_bias_total,
        grad_dense.astype(full),
        grad_up.astype(full),
        unit_total,
        grad_down.astype(full),
        out_bias_total,
    )


def solution(mesh):
    return jax.shard_map(
        body,
        mesh=mesh,
        in_specs=(
            P(("dp", "sp"), None),
            P("dp"),
            P(("dp", "sp"), None),
            P(),
            P(),
            P(("dp", "sp"), None),
            P(),
            P(("dp", "sp"), None),
            P(("dp", "sp"), None),
            P(),
            P(("dp", "sp"), None),
            P(),
        ),
        out_specs=(
            P(("dp", "sp"), None),
            P(("dp", "sp"), None),
            P(),
            P(),
            P(("dp", "sp"), None),
            P(),
            P(("dp", "sp"), None),
            P(("dp", "sp"), None),
            P(),
            P(("dp", "sp"), None),
            P(),
        ),
        check_vma=False,
    )
```

```python
import functools

import jax
import jax.numpy as jnp
from jax import lax
from jax.experimental import pallas as pl
from jax.experimental.pallas import tpu as pltpu
from jax.sharding import PartitionSpec as P

D = 2048
HEADS = 8
HEAD = 256
ROT = 64


eps = 1e-05
base_freq = 10000.0
root_half = 0.7071067811865476
inv_root_two_pi = 0.3989422804014327


def contract_rows(left, right):
    return lax.dot_general(
        left, right, (((0,), (0,)), ((), ())), preferred_element_type=jnp.float32
    )


def contract_cols(left, right):
    return lax.dot_general(
        left, right, (((1,), (1,)), ((), ())), preferred_element_type=jnp.float32
    )


def gelu_value(pre_act):
    return 0.5 * pre_act * (1.0 + lax.erf(pre_act * root_half))


def gelu_slope(pre_act):
    return 0.5 * (1.0 + lax.erf(pre_act * root_half)) + pre_act * inv_root_two_pi * jnp.exp(
        -0.5 * pre_act * pre_act
    )


BAND=256
def turn(x, cos_t, sin_t):
    first = x[:, :128]
    lane = lax.broadcasted_iota(jnp.int32, first.shape, 1)
    partner = jnp.where(lane < ROT // 2, pltpu.roll(first, 128 - ROT // 2, 1), pltpu.roll(first, ROT // 2, 1))
    return jnp.concatenate([first * cos_t + partner * sin_t, x[:, 128:]], axis=1)

def weights_of(q, k, start, length, scale):
    rows, cols = q.shape[0], k.shape[0]
    s = lax.dot_general(q, k, (((1,), (1,)), ((), ())), preferred_element_type=jnp.float32) * scale
    key = lax.broadcasted_iota(jnp.int32, (rows, cols), 1)
    query = start + lax.broadcasted_iota(jnp.int32, (rows, cols), 0)
    s = jnp.where((key <= query) & (key < length), s, -1e30)
    e = jnp.exp(s - jnp.max(s, axis=-1, keepdims=True))
    return e / jnp.sum(e, axis=-1, keepdims=True)

def fwd_kernel(scale, len_ref, pq, pk, pv, bq, bk, bv, cos_ref, sin_ref, q_ref, k_ref, v_ref, ctx_ref):
    length = len_ref[0]
    seq = pq.shape[0]
    cos_t, sin_t = cos_ref[...], sin_ref[...]
    q_ref[...] = turn(pq[...] + bq[...], cos_t, sin_t).astype(jnp.bfloat16)
    k_ref[...] = turn(pk[...] + bk[...], cos_t, sin_t).astype(jnp.bfloat16)
    v_ref[...] = (pv[...] + bv[...]).astype(jnp.bfloat16)
    for start in range(0, seq, BAND):
        end = start + BAND
        p = weights_of(q_ref[start:end, :], k_ref[:end, :], start, length, scale)
        ctx_ref[start:end, :] = jnp.dot(p.astype(jnp.bfloat16), v_ref[:end, :], preferred_element_type=jnp.float32).astype(jnp.bfloat16)

def attend_fwd(projected, bias, cos_t, sin_t, lengths):
    seq, width = projected.shape
    heads = width // 3 // HEAD
    col = lambda g: pl.BlockSpec((seq, HEAD), lambda h, *_, g=g: (0, g * heads + h))
    bcol = lambda g: pl.BlockSpec((1, HEAD), lambda h, *_, g=g: (0, g * heads + h))
    tab = pl.BlockSpec((seq, 128), lambda h, *_: (0, 0))
    out = pl.BlockSpec((seq, HEAD), lambda h, *_: (0, h))
    return pl.pallas_call(
        functools.partial(fwd_kernel, HEAD ** -0.5),
        grid_spec=pltpu.PrefetchScalarGridSpec(num_scalar_prefetch=1, grid=(heads,),
            in_specs=[col(0), col(1), col(2), bcol(0), bcol(1), bcol(2), tab, tab], out_specs=[out] * 4),
        out_shape=[jax.ShapeDtypeStruct((seq, heads * HEAD), jnp.bfloat16)] * 4,
        name="attend_fwd",
        cost_estimate=pl.CostEstimate(flops=heads * seq * seq * HEAD * 4, bytes_accessed=seq * width * 8, transcendentals=heads * seq * seq),
    )(lengths, projected, projected, projected, bias, bias, bias, cos_t, sin_t)

def bwd_kernel(scale, heads, len_ref, q_ref, k_ref, v_ref, g_ref, cos_ref, sin_ref, gp_ref, sum_ref, dk, dv, dq):
    length = len_ref[0]
    h = pl.program_id(0)
    seq = q_ref.shape[0]
    dk[...] = jnp.zeros_like(dk)
    dv[...] = jnp.zeros_like(dv)
    for start in range(0, seq, BAND):
        end = start + BAND
        q, g = q_ref[start:end, :], g_ref[start:end, :]
        k, v = k_ref[:end, :], v_ref[:end, :]
        p = weights_of(q, k, start, length, scale)
        gp = lax.dot_general(g, v, (((1,), (1,)), ((), ())), preferred_element_type=jnp.float32)
        ds = (p * (gp - jnp.sum(p * gp, axis=-1, keepdims=True))).astype(jnp.bfloat16)
        dq[start:end, :] = jnp.dot(ds, k, preferred_element_type=jnp.float32) * scale
        dk[:end, :] += lax.dot_general(ds, q, (((0,), (0,)), ((), ())), preferred_element_type=jnp.float32)
        dv[:end, :] += lax.dot_general(p.astype(jnp.bfloat16), g, (((0,), (0,)), ((), ())), preferred_element_type=jnp.float32)
    cos_t, sin_t = cos_ref[...], sin_ref[...]
    def back(x):
        return turn(x.astype(jnp.bfloat16).astype(jnp.float32), cos_t, -sin_t).astype(jnp.bfloat16)
    for g, piece in enumerate((back(dq[...]), back(dk[...] * scale), dv[...].astype(jnp.bfloat16))):
        at = pl.ds(pl.multiple_of((g * heads + h) * HEAD, HEAD), HEAD)
        gp_ref[:, at] = piece
        sum_ref[:, at] = jnp.sum(piece.astype(jnp.float32), axis=0, keepdims=True)

def attend_bwd(q, k, v, gctx, cos_t, sin_t, lengths):
    seq, width = q.shape
    heads = width // HEAD
    col = pl.BlockSpec((seq, HEAD), lambda h, *_: (0, h))
    tab = pl.BlockSpec((seq, 128), lambda h, *_: (0, 0))
    return pl.pallas_call(
        functools.partial(bwd_kernel, HEAD ** -0.5, heads),
        grid_spec=pltpu.PrefetchScalarGridSpec(num_scalar_prefetch=1, grid=(heads,),
            in_specs=[col] * 4 + [tab, tab],
            out_specs=[pl.BlockSpec((seq, 3 * width), lambda h, *_: (0, 0)), pl.BlockSpec((1, 3 * width), lambda h, *_: (0, 0))],
            scratch_shapes=[pltpu.VMEM((seq, HEAD), jnp.float32)] * 3),
        out_shape=[jax.ShapeDtypeStruct((seq, 3 * width), jnp.bfloat16), jax.ShapeDtypeStruct((1, 3 * width), jnp.float32)],
        name="attend_bwd",
        cost_estimate=pl.CostEstimate(flops=heads * seq * seq * HEAD * 10, bytes_accessed=seq * width * 20, transcendentals=heads * seq * seq),
    )(lengths, q, k, v, gctx, cos_t, sin_t)

def rotary_rows(seq):
    half = ROT // 2
    freq = 10000.0 ** (-jnp.arange(half, dtype=jnp.float32) * (2.0 / ROT))
    ang = jnp.arange(seq, dtype=jnp.int32).astype(jnp.float32)[:, None] * freq[None, :]
    c, s = jnp.cos(ang), jnp.sin(ang)
    rest = 128 - ROT
    return (jnp.concatenate([c, c, jnp.ones((seq, rest), jnp.float32)], 1), jnp.concatenate([-s, s, jnp.zeros((seq, rest), jnp.float32)], 1))

MESH = pl.DeviceIdType.MESH

def square_partners(dp):
    core, x, y = dp % 2, (dp // 2) % 2, dp // 4
    across_x, across_y = dp + 2 - 4 * x, dp + 4 - 8 * y
    first = across_x * (1 - core) + across_y * core
    second = across_y * (1 - core) + across_x * core
    return first, second, across_x + across_y - dp, 1 - 2 * core

class Hops:
    def __init__(self, count, dp, sp, source, result, send, recv):
        self.count, self.dp, self.sp, self.source, self.result = count, dp, sp, source, result
        self.send, self.recv, self.rows = send, recv, source.shape[0]

    def place(self, owner):
        return pl.ds(pl.multiple_of(owner * self.rows, self.rows), self.rows)

    def copy(self, way, step, owner, own):
        to = lax.rem(self.sp + (1 if way == 0 else self.count - 1), self.count)
        at = self.result.at[self.place(owner)]
        return pltpu.make_async_remote_copy(
            src_ref=self.source if own else at, dst_ref=at, send_sem=self.send.at[way, step],
            recv_sem=self.recv.at[way, step], device_id=(self.dp, to), device_id_type=MESH)

    def sends(self, way, step):
        if way == 0:
            return (self.sp >= step) & (self.sp < self.count - 1)
        return (self.sp < self.count - step) & (self.sp > 0)

    def receives(self, way, step):
        return self.sp >= step + 1 if way == 0 else self.sp < self.count - step - 1

    def owner(self, way, step):
        return self.sp - step if way == 0 else self.sp + step

    def start(self, way, step):
        @pl.when(self.sends(way, step))
        def _():
            self.copy(way, step, self.owner(way, step), step == 0).start()

    def begin(self):
        for way in (0, 1):
            self.start(way, 0)

    def relay(self, step):
        for way in (0, 1):
            @pl.when(self.receives(way, step - 1) & self.sends(way, step))
            def _():
                self.copy(way, step - 1, self.owner(way, step), False).wait_recv()
                self.copy(way, step, self.owner(way, step), False).start()

    def settle(self, step):
        for way in (0, 1):
            @pl.when(self.receives(way, step - 1) & jnp.logical_not(self.sends(way, step)))
            def _():
                self.copy(way, step - 1, self.owner(way, step), False).wait_recv()

    def finish(self):
        for step in range(self.count - 1):
            for way in (0, 1):
                @pl.when(self.sends(way, step))
                def _():
                    self.copy(way, step, self.owner(way, step), step == 0).wait_send()


NEAR = 2


def front_kernel(sp_size, len_ref, qkv_ref, out_ref, up_ref, down_ref, tok_ref, cot_ref, freq_ref, gain_ref, shift_ref,
                 qkv_bias_ref, unit_bias_ref,
                 qkv_all, out_all, up_all, down_all, tok_all, cot_all, attn_out, mlp_out, hidden_out, pre_out, part_out, part_in, gpre_out,
                 cos_ref, sin_ref, mean_ref, inv_ref, unit_ref, q_ref, k_ref, v_ref, ctx_ref,
                 tok, attn, mlp, qkv_w, up_w, hidden, pre, cot, gpre,
                 send_sem, recv_sem, slab_send, slab_recv, keep_sem, turn_send, turn_recv, tok_send, tok_recv, cot_send, cot_recv,
                 load_sem, store_sem, pre_sem, part_sem, hop_send, hop_recv, slope_sem, gpre_sem):
    full, low = jnp.float32, jnp.bfloat16
    dp, sp = lax.axis_index("dp"), lax.axis_index("sp")
    first, second, diagonal, flip = square_partners(dp)
    sibling = dp + flip
    per = 2
    pair, lane = dp // per, dp % per
    rows = qkv_ref.shape[0]
    seq, wide = tok.shape
    own_rows = tok_ref.shape[0]
    head_width = wide // sp_size
    units = down_ref.shape[0]
    slab = rows * sp_size
    width = q_ref.shape[1]
    turn_dp = sp * per + lane
    scale = HEAD ** -0.5
    band = 256

    barrier = pltpu.get_barrier_semaphore()
    for other in (first, second, sibling):
        pl.semaphore_signal(barrier, inc=1, device_id=(other, sp), device_id_type=MESH)
    for step in range(1, sp_size):
        pl.semaphore_signal(barrier, inc=1, device_id=(dp, lax.rem(sp + step, sp_size)), device_id_type=MESH)

    @pl.when(pair != sp)
    def _():
        pl.semaphore_signal(barrier, inc=1, device_id=(turn_dp, pair), device_id_type=MESH)

    pl.semaphore_wait(barrier, 2 + sp_size + jnp.where(pair != sp, 1, 0))

    def remote_copy(source, target, send, recv, device):
        return pltpu.make_async_remote_copy(
            src_ref=source, dst_ref=target, send_sem=send, recv_sem=recv, device_id=device, device_id_type=MESH)

    def slab_at(owner):
        return pl.ds(pl.multiple_of((dp * sp_size + owner) * rows, rows), rows)

    def slab_columns(part, there):
        return pl.ds(pl.multiple_of(part * wide + there * head_width, head_width), head_width)

    def slab_copy(step, part, there, origin):
        return remote_copy(
            qkv_ref.at[:, slab_columns(part, there)],
            qkv_all.at[slab_at(origin), pl.ds(part * head_width, head_width)],
            slab_send.at[step - 1, part], slab_recv.at[step - 1, part], (dp, there))

    def plain(height):
        return lambda owner: pl.ds(pl.multiple_of(owner * height, height), height)

    def turned(owner):
        return pl.ds(pl.multiple_of((owner % per) * slab + (owner // per) * rows, rows), rows)

    def turn_copy(landing):
        return remote_copy(out_ref, out_all.at[turned(landing)], turn_send, turn_recv, (turn_dp, pair))

    arrays = ((up_ref, up_all, plain(units)), (None, qkv_all, plain(slab)), (None, out_all, turned), (down_ref, down_all, plain(units)))
    UP, QKV, OUT, DOWN = 0, 1, 2, 3

    def copy(index, message, block, target):
        source, result, place = arrays[index]
        at = result.at[place(block)]
        return remote_copy(at if source is None or message > 2 else source, at,
                           send_sem.at[index, message], recv_sem.at[index, message], (target, sp))

    sends = ((dp, first), (dp, second), (dp, sibling), (first, second), (first, sibling), (second, sibling), (diagonal, sibling))
    arrivals = (first, second, sibling, diagonal, second + flip, first + flip, diagonal + flip)

    def start(index, message):
        copy(index, message, *sends[message]).start()

    def arrived(index, message):
        copy(index, message, arrivals[message], sibling).wait_recv()

    def own(index):
        for message in (0, 1, 2):
            start(index, message)

    def onward(index):
        arrived(index, 0)
        start(index, 3)
        start(index, 4)
        arrived(index, 1)
        start(index, 5)

    def corner(index):
        arrived(index, 3)
        start(index, 6)

    def complete(index):
        for message in (2, 4, 5, 6):
            arrived(index, message)

    def load(source, target, which):
        c = pltpu.make_async_copy(source, target, load_sem.at[which])
        c.start()
        return c

    for step in range(1, sp_size):
        for part in range(3):
            slab_copy(step, part, lax.rem(sp + step, sp_size), sp).start()

    @pl.when(pair != sp)
    def _():
        turn_copy(turn_dp).start()

    own(UP)
    tokens = Hops(sp_size, dp, sp, tok_ref, tok_all, tok_send, tok_recv)
    cotangents = Hops(sp_size, dp, sp, cot_ref, cot_all, cot_send, cot_recv)
    tokens.begin()
    keeps = []

    def keep(source, target):
        c = pltpu.make_async_copy(source, target, keep_sem.at[len(keeps)])
        c.start()
        keeps.append(c)

    for part in range(3):
        keep(qkv_ref.at[:, slab_columns(part, sp)], qkv_all.at[slab_at(sp), pl.ds(part * head_width, head_width)])
    keep(up_ref, up_all.at[plain(units)(dp)])
    keep(down_ref, down_all.at[plain(units)(dp)])
    keep(tok_ref, tok_all.at[tokens.place(sp)])
    keep(cot_ref, cot_all.at[cotangents.place(sp)])

    def normalize(source, source_start, target_start):
        def chunk(i, carry):
            at = pl.ds(pl.multiple_of(target_start + i * 32, 32), 32)
            values = source[pl.ds(pl.multiple_of(source_start + i * 32, 32), 32), :].astype(full)
            mean = jnp.mean(values, axis=-1, keepdims=True)
            centered = values - mean
            inverse = lax.rsqrt(jnp.mean(centered * centered, axis=-1, keepdims=True) + eps)
            normed = centered * inverse
            mean_ref[at, :] = jnp.broadcast_to(mean, (32, 128))
            inv_ref[at, :] = jnp.broadcast_to(inverse, (32, 128))
            attn[at, :] = (normed * gain_ref[0:1, :].astype(full) + shift_ref[0:1, :].astype(full)).astype(low)
            mlp[at, :] = (normed * gain_ref[1:2, :].astype(full) + shift_ref[1:2, :].astype(full)).astype(low)
            return carry
        lax.fori_loop(0, own_rows // 32, chunk, 0)

    def absorb(step):
        for way in (0, 1):
            @pl.when(tokens.receives(way, step - 1))
            def _():
                at = tokens.place(tokens.owner(way, step))
                c = load(tok_all.at[at], tok.at[at], way)
                c.wait()
                begin = tokens.owner(way, step) * own_rows
                normalize(tok, begin, begin)

    def table(i, carry):
        at = pl.ds(pl.multiple_of(i * 64, 64), 64)
        lanes = lax.broadcasted_iota(jnp.int32, (64, 128), 1)
        position = i * 64 + lax.broadcasted_iota(jnp.int32, (64, 128), 0)
        angle = position.astype(full) * freq_ref[...]
        cos_ref[at, :] = jnp.where(lanes < ROT, jnp.cos(angle), 1.0)
        sine = jnp.sin(angle)
        sin_ref[at, :] = jnp.where(lanes < ROT, jnp.where(lanes < ROT // 2, -sine, sine), 0.0)
        return carry

    normalize(tok_ref, 0, sp * own_rows)
    lax.fori_loop(0, seq // 64, table, 0)
    for step in range(1, sp_size):
        for part in range(3):
            slab_copy(step, part, sp, lax.rem(sp + sp_size - step, sp_size)).wait_recv()
    for c in keeps[:3]:
        c.wait()
    own(QKV)

    @pl.when(pair == sp)
    def _():
        c = pltpu.make_async_copy(out_ref, out_all.at[turned(dp)], keep_sem.at[7])
        c.start()
        c.wait()

    @pl.when(pair != sp)
    def _():
        turn_copy(dp).wait_recv()

    own(OUT)
    onward(UP)
    tokens.relay(1)
    onward(QKV)
    onward(OUT)
    own(DOWN)
    tokens.settle(1)
    absorb(1)
    tokens.relay(2)
    cotangents.begin()
    corner(UP)
    complete(UP)
    for c in keeps[3:]:
        c.wait()
    up_load = load(up_all, up_w, 2)
    tokens.settle(2)
    absorb(2)
    corner(QKV)
    corner(OUT)
    complete(QKV)
    qkv_load = load(qkv_all, qkv_w, 3)
    complete(OUT)
    onward(DOWN)
    tokens.settle(3)
    absorb(3)
    stores = [pltpu.make_async_copy(attn, attn_out, store_sem.at[0]), pltpu.make_async_copy(mlp, mlp_out, store_sem.at[1])]
    for c in stores:
        c.start()
    qkv_load.wait()

    def head(h, carry):
        lanes = pl.ds(pl.multiple_of(h * HEAD, HEAD), HEAD)

        def project(r, carry):
            at = pl.ds(pl.multiple_of(r * band, band), band)
            cos_t, sin_t = cos_ref[at, :], sin_ref[at, :]
            for part, target in enumerate((q_ref, k_ref, v_ref)):
                cols = pl.ds(pl.multiple_of(part * width + h * HEAD, HEAD), HEAD)
                value = jnp.dot(attn[at, :], qkv_w[:, cols], preferred_element_type=full) + qkv_bias_ref[:, cols]
                if part < 2:
                    value = turn(value, cos_t, sin_t)
                target[at, lanes] = value.astype(low)
            return carry
        lax.fori_loop(0, seq // band, project, 0)
        for begin in range(0, seq, band):
            end = begin + band
            p = weights_of(q_ref[begin:end, lanes], k_ref[:end, lanes], begin, len_ref[0], scale)
            ctx_ref[begin:end, lanes] = jnp.dot(p.astype(low), v_ref[:end, lanes], preferred_element_type=full).astype(low)
        return carry

    lax.fori_loop(0, width // HEAD, head, 0)
    corner(DOWN)
    cotangents.relay(1)
    up_load.wait()

    def pre_store(block, slot):
        return pltpu.make_async_copy(pre.at[slot], pre_out.at[:, pl.ds(pl.multiple_of(block * units, units), units)],
                                     pre_sem.at[slot])

    def unit_block(block, carry):
        slot = lax.rem(block, 2)

        @pl.when(block >= 2)
        def _():
            pre_store(block - 2, slot).wait()

        of = pl.ds(pl.multiple_of(block * units, units), units)

        def row_band(r, carry):
            at = pl.ds(pl.multiple_of(r * band, band), band)
            value = lax.dot_general(mlp[at, :], up_w[of, :], (((1,), (1,)), ((), ())), preferred_element_type=full)
            value = value + unit_bias_ref[:, of]
            pre[slot, at, :] = value
            hidden[at, of] = gelu_value(value).astype(low)
            return carry
        lax.fori_loop(0, seq // band, row_band, 0)
        pre_store(block, slot).start()
        return carry

    blocks = up_w.shape[0] // units
    lax.fori_loop(0, blocks // 2, unit_block, 0)
    complete(DOWN)
    half = up_w.shape[0] // 2
    stores[0].wait()
    late = [load(down_all.at[pl.ds(0, half)], tok, 0), load(down_all.at[pl.ds(half, half)], attn, 1)]
    lax.fori_loop(blocks // 2, blocks, unit_block, 0)
    out_rows = out_all.shape[0]
    late.append(load(out_all, up_w.at[pl.ds(0, out_rows)], 2))
    cotangents.relay(2)
    for block in (blocks - 2, blocks - 1):
        pre_store(block, block % 2).wait()
    stores[1].wait()
    hidden_store = pltpu.make_async_copy(hidden, hidden_out, store_sem.at[0])
    hidden_store.start()
    for c in late:
        c.wait()

    bands = seq // band
    upper = 2 * sp // sp_size

    def band_rows(r):
        return pl.ds(pl.multiple_of(((1 - upper) * (bands - 1 - r) + upper * r) * band, band), band)

    def part_store(r):
        return pltpu.make_async_copy(mlp.at[band_rows(r)], part_out.at[band_rows(r)], part_sem.at[r])

    def part_hop(way):
        to = lax.rem(sp + (1 if way == 0 else sp_size - 1), sp_size)
        return remote_copy(mlp.at[band_rows(0)], part_in.at[way], hop_send.at[way], hop_recv.at[way], (dp, to))

    def along(way):
        return sp if way == 0 else sp_size - 1 - sp

    def out_band(r, carry):
        at = band_rows(r)

        def out_columns(c, carry):
            to = pl.ds(pl.multiple_of(c * band, band), band)
            total = jnp.dot(hidden[at, :half], tok[:, to], preferred_element_type=full)
            total = total + jnp.dot(hidden[at, half:], attn[:, to], preferred_element_type=full)
            total = total + jnp.dot(ctx_ref[at, :], up_w[:out_rows, to], preferred_element_type=full)
            mlp[at, to] = total.astype(low)
            return carry
        lax.fori_loop(0, wide // band, out_columns, 0)
        part_store(r).start()
        return carry
    out_band(0, 0)
    for way in (0, 1):
        @pl.when(along(way) == 0)
        def _():
            part_hop(way).start()
    lax.fori_loop(1, bands, out_band, 0)

    for step in (1, 2):
        cotangents.settle(step)
    unit_ref[...] = jnp.zeros_like(unit_ref)
    early = NEAR

    def near_rows(n):
        return pl.ds(pl.multiple_of((upper * (bands - NEAR) + n) * band, band), band)

    def slope_room(block):
        return pre.at[block // 4, pl.ds(pl.multiple_of(lax.rem(block, 4) * band, band), band)]

    def slope_load(n, block):
        return pltpu.make_async_copy(
            pre_out.at[near_rows(n), pl.ds(pl.multiple_of(block * units, units), units)], slope_room(block), slope_sem.at[block])

    def cot_load(n):
        return pltpu.make_async_copy(cot_all.at[near_rows(n)], cot.at[lax.rem(n, 2)], gpre_sem.at[2 + lax.rem(n, 2)])

    def gpre_store(n):
        return pltpu.make_async_copy(gpre.at[lax.rem(n, 2)], gpre_out.at[near_rows(n)], gpre_sem.at[lax.rem(n, 2)])

    def first_loads(block, carry):
        slope_load(0, block).start()
        return carry
    lax.fori_loop(0, blocks, first_loads, 0)
    cot_load(0).start()

    def near_band(n, carry):
        slot = lax.rem(n, 2)
        cot_load(n).wait()

        @pl.when(n + 1 < early)
        def _():
            cot_load(n + 1).start()

        def mask(i, carry):
            at = pl.ds(pl.multiple_of(i * 32, 32), 32)
            row = (upper * (bands - NEAR) + n) * band + i * 32 + lax.broadcasted_iota(jnp.int32, (32, wide), 0)
            cot[slot, at, :] = jnp.where(row < len_ref[0], cot[slot, at, :].astype(full), 0.0).astype(low)
            return carry
        lax.fori_loop(0, band // 32, mask, 0)

        @pl.when(n >= 2)
        def _():
            gpre_store(n - 2).wait()

        for side, room in enumerate((tok, attn)):
            def unit_part(k, carry):
                block = side * (blocks // 2) + k
                slope_load(n, block).wait()
                of = pl.ds(pl.multiple_of(block * units, units), units)
                value = lax.dot_general(cot[slot], room[pl.ds(pl.multiple_of(k * units, units), units), :],
                                        (((1,), (1,)), ((), ())), preferred_element_type=full)
                value = (value * gelu_slope(slope_room(block)[...])).astype(low)
                gpre[slot, :, of] = value
                unit_ref[:, of] += jnp.sum(value.astype(full), axis=0, keepdims=True)

                @pl.when(n + 1 < early)
                def _():
                    slope_load(n + 1, block).start()
                return carry
            lax.fori_loop(0, blocks // 2, unit_part, 0)
        gpre_store(n).start()
        return carry
    lax.fori_loop(0, early, near_band, 0)
    for n in range(max(early - 2, 0), early):
        gpre_store(n).wait()
    for r in range(seq // band):
        part_store(r).wait()
    hidden_store.wait()
    for index in range(4):
        for message in range(7):
            copy(index, message, *sends[message]).wait_send()
    for step in range(1, sp_size):
        for part in range(3):
            slab_copy(step, part, lax.rem(sp + step, sp_size), sp).wait_send()

    @pl.when(pair != sp)
    def _():
        turn_copy(turn_dp).wait_send()

    tokens.finish()
    cotangents.settle(3)
    cotangents.finish()
    for way in (0, 1):
        @pl.when(along(way) == 0)
        def _():
            part_hop(way).wait_send()

        @pl.when(along(way) == 1)
        def _():
            part_hop(way).wait_recv()


def front(sp_size, dp_size, lengths, qkv_weight, out_weight, up_weight, down_weight, tokens, cotangent, gains, shifts, qkv_bias,
          unit_bias):
    rows, wide = out_weight.shape
    units = up_weight.shape[0]
    seq = tokens.shape[0] * sp_size
    width = wide // sp_size
    all_units = units * dp_size
    full, low = jnp.float32, jnp.bfloat16
    half = ROT // 2
    freq = base_freq ** (-jnp.arange(half, dtype=full) * (2.0 / ROT))
    freq = jnp.concatenate([freq, freq, jnp.zeros((128 - ROT,), full)])[None]
    hbm = pl.BlockSpec(memory_space=pltpu.HBM)
    vmem = pl.BlockSpec(memory_space=pltpu.VMEM)
    dma = pltpu.SemaphoreType.DMA
    shape = jax.ShapeDtypeStruct
    qkv_shape = (rows * sp_size * dp_size, 3 * width)
    return pl.pallas_call(
        functools.partial(front_kernel, sp_size),
        out_shape=[shape(qkv_shape, low), shape((rows * dp_size, wide), low), shape((all_units, wide), low),
                   shape((all_units, wide), low), shape((seq, wide), low), shape((seq, wide), low),
                   shape((seq, wide), low), shape((seq, wide), low), shape((seq, all_units), low), shape((seq, all_units), full),
                   shape((seq, wide), low), shape((2, seq // sp_size, wide), low), shape((seq, all_units), low)]
        + [shape((seq, 128), full)] * 4 + [shape((1, all_units), full)] + [shape((seq, width), low)] * 4,
        in_specs=[pl.BlockSpec(memory_space=pltpu.SMEM)] + [vmem] * 11,
        out_specs=[hbm] * 13 + [vmem] * 9,
        scratch_shapes=[pltpu.VMEM((seq, wide), low)] * 3 + [
            pltpu.VMEM(qkv_shape, low), pltpu.VMEM((all_units, wide), low),
            pltpu.VMEM((seq, all_units), low), pltpu.VMEM((2, seq, units), full),
            pltpu.VMEM((2, 256, wide), low), pltpu.VMEM((2, 256, all_units), low),
            dma((4, 7)), dma((4, 7)), dma((sp_size - 1, 3)), dma((sp_size - 1, 3)), dma((8,)), dma, dma,
            dma((2, sp_size)), dma((2, sp_size)), dma((2, sp_size)), dma((2, sp_size)),
            dma((4,)), dma((2,)), dma((2,)), dma((seq // 256,)), dma((2,)), dma((2,)), dma((all_units // units,)), dma((4,))],
        compiler_params=pltpu.CompilerParams(collective_id=0, has_side_effects=True, vmem_limit_bytes=62 << 20),
        cost_estimate=pl.CostEstimate(flops=26 * 10 ** 9, bytes_accessed=300 * 1000 * 1000, transcendentals=0),
        name="front",
    )(lengths, qkv_weight, out_weight, up_weight, down_weight, tokens, cotangent, freq, gains, shifts, qkv_bias, unit_bias)

CHUNK = 512


def add_into(target, *others):
    step_rows = 32

    def step(i, carry):
        at = pl.ds(pl.multiple_of(i * step_rows, step_rows), step_rows)
        total = target[at, :].astype(jnp.float32)
        for other in others:
            total = total + other[at, :].astype(jnp.float32)
        target[at, :] = total.astype(jnp.bfloat16)
        return carry

    lax.fori_loop(0, target.shape[0] // step_rows, step, 0)


class Square:
    def __init__(self, sp_size, lent, sib_send, sib_recv, one_send, one_recv, two_send, two_recv):
        self.dp, self.sp, self.sp_size = lax.axis_index("dp"), lax.axis_index("sp"), sp_size
        self.core, self.chip = self.dp % 2, self.dp // 2
        self.x, self.y = self.chip % 2, self.chip // 2
        self.sibling = self.dp + 1 - 2 * self.core
        self.across_x, self.across_y = self.dp + 2 - 4 * self.x, self.dp + 4 - 8 * self.y
        self.first = self.across_y * (1 - self.core) + self.across_x * self.core
        self.second = self.across_x * (1 - self.core) + self.across_y * self.core
        self.second_mask = 1 + self.core
        self.lent = lent
        self.sib_send, self.sib_recv, self.one_send, self.one_recv, self.two_send, self.two_recv = (
            sib_send, sib_recv, one_send, one_recv, two_send, two_recv)

    def chip_of(self, mask):
        return lax.rem(self.x + lax.rem(mask, 2), 2) + 2 * lax.rem(self.y + mask // 2, 2)

    def greet(self, barrier):
        for other in (self.first, self.second, self.sibling):
            pl.semaphore_signal(barrier, inc=1, device_id=(other, self.sp), device_id_type=MESH)
        for step in range(1, self.sp_size):
            pl.semaphore_signal(
                barrier, inc=1, device_id=(self.dp, lax.rem(self.sp + step, self.sp_size)), device_id_type=MESH)


def remote(source, target, send, recv, device):
    return pltpu.make_async_remote_copy(
        src_ref=source, dst_ref=target, send_sem=send, recv_sem=recv, device_id=device, device_id_type=MESH)


class Wide:
    def __init__(self, place, index, left, right, width, sums, sib, one, two):
        self.place, self.index, self.left, self.right, self.width = place, index, left, right, width
        self.sums, self.sib, self.one, self.two = sums, sib, one, two
        self.units = sums.shape[1]

    def product(self, block, store):
        at = pl.ds(pl.multiple_of(block * self.units, self.units), self.units)

        def columns(part, carry):
            to = pl.ds(pl.multiple_of(part * CHUNK, CHUNK), CHUNK)
            store(to, lax.dot_general(
                self.left[:, at], self.right[:, to], (((0,), (0,)), ((), ())),
                preferred_element_type=jnp.float32))
            return carry
        lax.fori_loop(0, self.width // CHUNK, columns, 0)

    def sib_copy(self, slot):
        p = self.place
        return remote(p.lent.at[slot, :, :self.width], self.sib.at[p.chip_of(3 - slot), :, :self.width],
                      p.sib_send.at[self.index, slot], p.sib_recv.at[self.index, slot], (p.sibling, p.sp))

    def for_sibling(self, previous):
        p = self.place

        def step(slot, carry):
            if previous is not None:
                previous.sib_copy(slot).wait_send()

            def store(to, total):
                p.lent[slot, :, to] = total.astype(jnp.bfloat16)
            self.product(p.chip_of(3 - slot) * 2 + 1 - p.core, store)
            self.sib_copy(slot).start()
            return carry
        lax.fori_loop(0, 4, step, 0)

    def own(self, mask, slot):
        at = self.place.chip_of(mask)
        self.sib_copy(slot).wait_recv()

        def store(to, total):
            self.sums[mask, :, to] = (total + self.sib[at, :, to].astype(jnp.float32)).astype(jnp.bfloat16)
        self.product(at * 2 + self.place.core, store)

    def for_self(self):
        core = self.place.core

        def leave(slot, carry):
            mask = 3 - slot * (1 + core)
            self.own(mask, 3 - mask)
            self.first_copy(slot).start()
            return carry
        lax.fori_loop(0, 2, leave, 0)

        def stay(slot, carry):
            mask = self.place.second_mask * (1 - slot)
            self.own(mask, 3 - mask)
            return carry
        lax.fori_loop(0, 2, stay, 0)

    def block(self, mask):
        return self.sums.at[mask, :, :self.width]

    def from_first(self, slot):
        return self.one.at[slot, :, :self.width]

    def from_second(self):
        return self.two.at[:, :self.width]

    def first_copy(self, slot):
        p = self.place
        return remote(self.block(3 - slot * (1 + p.core)), self.from_first(slot), p.one_send.at[self.index, slot],
                      p.one_recv.at[self.index, slot], (p.first, p.sp))

    def second_copy(self):
        p = self.place
        return remote(self.block(p.second_mask), self.from_second(), p.two_send.at[self.index],
                      p.two_recv.at[self.index], (p.second, p.sp))

    def onward(self):
        self.first_copy(0).wait_recv()
        add_into(self.block(self.place.second_mask), self.from_first(0))
        self.second_copy().start()

    def finish(self):
        self.first_copy(1).wait_recv()
        self.second_copy().wait_recv()
        add_into(self.block(0), self.from_first(1), self.from_second())

    def drain(self):
        for slot in (0, 1):
            self.first_copy(slot).wait_send()
        self.second_copy().wait_send()


class Dense(Wide):
    def __init__(self, place, index, left, right, width, sums, sib, one, two, part):
        self.place, self.index, self.left, self.right, self.width = place, index, left, right, width
        self.sums, self.sib, self.one, self.two, self.part = sums, sib, one, two, part
        self.units, self.rows = sums.shape[0], one.shape[1]

    def sib_copy(self, slot):
        p = self.place
        return remote(self.part, self.sib, p.sib_send.at[self.index, 0], p.sib_recv.at[self.index, 0], (p.sibling, p.sp))

    def for_sibling(self, previous):
        def store(to, total):
            self.part[:, to] = total.astype(jnp.bfloat16)
        self.product(1 - self.place.core, store)
        self.sib_copy(0).start()

    def for_self(self):
        self.sib_copy(0).wait_recv()

        def store(to, total):
            self.sums[:, to] = (total + self.sib[:, to].astype(jnp.float32)).astype(jnp.bfloat16)
        self.product(self.place.core, store)
        for slot in (0, 1):
            self.first_copy(slot).start()

    def block(self, mask):
        return self.sums.at[pl.ds(pl.multiple_of(self.place.chip_of(mask) * self.rows, self.rows), self.rows)]


class Fold:
    def __init__(self, place, source, inbox, stage, stage_sem, send, recv, begun=1):
        self.begun = begun
        self.place, self.source, self.inbox, self.stage = place, source, inbox, stage
        self.stage_sem, self.send, self.recv = stage_sem, send, recv
        self.rows = stage.shape[0]

    def along(self, way):
        last = self.place.sp_size - 1
        return self.place.sp if way == 0 else last - self.place.sp

    def rows_of(self, way, step):
        count = self.place.sp_size
        owner = self.along(way) + count - step
        owner = owner if way == 0 else count - 1 - owner
        return self.source.at[pl.ds(pl.multiple_of(owner * self.rows, self.rows), self.rows)]

    def copy(self, way, step, own):
        p = self.place
        to = lax.rem(p.sp + (1 if way == 0 else p.sp_size - 1), p.sp_size)
        source = self.rows_of(way, step) if own else self.inbox.at[way, max(step - 2, 0)]
        return remote(source, self.inbox.at[way, step - 1], self.send.at[way, step - 1],
                      self.recv.at[way, step - 1], (p.dp, to))

    def take(self, rows):
        c = pltpu.make_async_copy(rows, self.stage, self.stage_sem)
        c.start()
        c.wait()

    def step(self, step):
        last = self.place.sp_size - 1
        for way in (0, 1):
            if step >= self.begun:
                @pl.when(self.along(way) == 0)
                def _():
                    self.copy(way, step, True).start()

            if step > 1:
                @pl.when((self.along(way) > 0) & (self.along(way) < step) & (self.along(way) < last))
                def _():
                    self.take(self.rows_of(way, step))
                    if step > self.begun:
                        self.copy(way, step - 1, False).wait_recv()
                    add_into(self.inbox.at[way, step - 2], self.stage)
                    self.copy(way, step, False).start()

    def finish(self):
        last = self.place.sp_size - 1
        self.take(self.source.at[pl.ds(pl.multiple_of(self.place.sp * self.rows, self.rows), self.rows)])
        for way in (0, 1):
            @pl.when(self.along(way) > 0)
            def _():
                self.copy(way, last, False).wait_recv()
                add_into(self.stage, self.inbox.at[way, last - 1])

    def drain(self):
        last = self.place.sp_size - 1
        for way in (0, 1):
            for step in range(1, last + 1):
                if step >= self.begun:
                    @pl.when(self.along(way) == 0)
                    def _():
                        self.copy(way, step, True).wait_send()

                if step > 1:
                    @pl.when((self.along(way) > 0) & (self.along(way) < step) & (self.along(way) < last))
                    def _():
                        self.copy(way, step, False).wait_send()


def middle_kernel(sp_size, len_ref, cot_hbm, out_hbm, q_hbm, k_hbm, v_hbm, pre_hbm, hidden_hbm, down_hbm, up_hbm, qkv_hbm,
                  tok_hbm, part_hbm, hop_hbm, near_hbm, attn_hbm, unit_ref, gain_ref, cos_ref, sin_ref, mean_s, inv_s,
                  down_out, slab_out, gpre_out, hat_out, hat_in, proj_out, gout_out, red_out, small_ref,
                  cot, left, tok, gpre, up_w, qkv_w, pre, gctx, gproj, dq, dk, dv,
                  lent, down_sum, down_sib, down_one, down_two, inbox, stage,
                  load_sem, stream_sem, store_sem, stage_sem, sib_send, sib_recv, one_send, one_recv, two_send, two_recv,
                  fold_send, fold_recv, hat_send, hat_recv, sib_free, one_free, two_free, near_sem, tok_sem):
    full, low = jnp.float32, jnp.bfloat16
    place = Square(sp_size, lent, sib_send, sib_recv, one_send, one_recv, two_send, two_recv)
    seq, wide = cot.shape
    width = gctx.shape[1]
    heads = width // HEAD
    units = down_sum.shape[1]
    blocks = up_w.shape[0] // units
    out_rows = out_hbm.shape[0]
    band = 256
    bands = seq // band
    scale = HEAD ** -0.5

    def load(source, target, which):
        c = pltpu.make_async_copy(source, target, load_sem.at[which])
        c.start()
        return c

    early = [load(cot_hbm, cot, 0), load(hidden_hbm, left, 1)]

    def down_load(block, slot):
        return pltpu.make_async_copy(
            down_hbm.at[pl.ds(pl.multiple_of(block * units, units), units)],
            up_w.at[pl.ds(pl.multiple_of(out_rows + slot * units, units), units)], stream_sem.at[0, slot])

    upper = 2 * place.sp // sp_size

    def hat_rows(r):
        return pl.ds(pl.multiple_of(((1 - upper) * (bands - 1 - r) + upper * r) * band, band), band)

    far = bands - NEAR
    near = pl.ds(pl.multiple_of(upper * far * band, band), NEAR * band)
    far_rows = pl.ds(pl.multiple_of((1 - upper) * NEAR * band, band), far * band)
    near_load = pltpu.make_async_copy(near_hbm.at[near], gpre.at[near], near_sem)

    def pre_load(block, slot):
        return pltpu.make_async_copy(
            pre_hbm.at[far_rows, pl.ds(pl.multiple_of(block * units, units), units)], pre.at[slot], stream_sem.at[1, slot])

    hops = []
    for way in (0, 1):
        hops.append(load(hop_hbm.at[way], inbox.at[way, 0], 6 + way))

    barrier = pltpu.get_barrier_semaphore()
    place.greet(barrier)
    pl.semaphore_wait(barrier, 2 + sp_size)
    fold = Fold(place, part_hbm, inbox, stage, stage_sem, fold_send, fold_recv, begun=2)
    for way in (0, 1):
        hops[way].wait()
    fold.step(2)
    early.append(load(out_hbm, up_w.at[pl.ds(0, out_rows)], 2))
    for i, source in enumerate((q_hbm, k_hbm, v_hbm)):
        early.append(load(source, qkv_w.at[pl.ds(0, seq), pl.ds(i * width, width)], 3 + i))
    for slot in (0, 1):
        down_load(slot, slot).start()
        pre_load(slot, slot).start()
    small_ref[...] = jnp.zeros_like(small_ref)
    gain_row, shift_row, bias_row, unit_row = 0, 2, 4, 7
    per_row = wide // (sp_size * units)
    last_row = unit_row + blocks // per_row

    early[0].wait()

    def mask_rows(i, carry):
        at = pl.ds(pl.multiple_of(i * 32, 32), 32)
        row = i * 32 + lax.broadcasted_iota(jnp.int32, (32, wide), 0)
        cot[at, :] = jnp.where(row < len_ref[0], cot[at, :].astype(full), 0.0).astype(low)
        return carry
    lax.fori_loop(0, seq // 32, mask_rows, 0)
    stores = [pltpu.make_async_copy(cot, gout_out, store_sem.at[0])]
    stores[0].start()

    def own_rows(i, carry):
        at = pl.ds(pl.multiple_of(place.sp * (seq // sp_size) + i * 32, 32), 32)
        return carry + jnp.sum(cot[at, :].astype(full), axis=0, keepdims=True)
    small_ref[last_row:last_row + 1, :] = lax.fori_loop(0, seq // sp_size // 32, own_rows, jnp.zeros((1, wide), full))

    down = Wide(place, 0, left, cot, wide, down_sum, down_sib, down_one, down_two)
    early[1].wait()
    down.for_sibling(None)
    down.for_self()
    early[2].wait()

    def context_band(r, carry):
        at = pl.ds(pl.multiple_of(r * band, band), band)
        gctx[at, :] = lax.dot_general(
            cot[at, :], up_w[:out_rows, :], (((1,), (1,)), ((), ())), preferred_element_type=full).astype(low)
        return carry
    lax.fori_loop(0, bands, context_band, 0)
    attn_load = load(attn_hbm, left, 1)
    near_load.start()
    late_rows = pl.ds(out_rows + 2 * units, up_w.shape[0] - out_rows - 2 * units)
    up_load = load(up_hbm.at[late_rows], up_w.at[late_rows], 8)
    pl.semaphore_signal(sib_free, inc=1, device_id=(place.sibling, place.sp), device_id_type=MESH)
    for c in early[3:]:
        c.wait()

    def head(h, carry):
        lanes = pl.ds(pl.multiple_of(h * HEAD, HEAD), HEAD)
        k_lanes = pl.ds(pl.multiple_of(width + h * HEAD, HEAD), HEAD)
        v_lanes = pl.ds(pl.multiple_of(2 * width + h * HEAD, HEAD), HEAD)
        dk[...] = jnp.zeros_like(dk)
        dv[...] = jnp.zeros_like(dv)
        for begin in range(0, seq, band):
            end = begin + band
            q, g = qkv_w[begin:end, lanes], gctx[begin:end, lanes]
            k, v = qkv_w[:end, k_lanes], qkv_w[:end, v_lanes]
            p = weights_of(q, k, begin, len_ref[0], scale)
            gp = lax.dot_general(g, v, (((1,), (1,)), ((), ())), preferred_element_type=full)
            ds = (p * (gp - jnp.sum(p * gp, axis=-1, keepdims=True))).astype(low)
            dq[begin:end, :] = jnp.dot(ds, k, preferred_element_type=full) * scale
            dk[:end, :] += lax.dot_general(ds, q, (((0,), (0,)), ((), ())), preferred_element_type=full)
            dv[:end, :] += lax.dot_general(p.astype(low), g, (((0,), (0,)), ((), ())), preferred_element_type=full)

        def back(r, sums):
            at = pl.ds(pl.multiple_of(r * band, band), band)
            cos_t, sin_t = cos_ref[at, :], -sin_ref[at, :]
            pieces = (turn(dq[at, :].astype(low).astype(full), cos_t, sin_t).astype(low),
                      turn((dk[at, :] * scale).astype(low).astype(full), cos_t, sin_t).astype(low),
                      dv[at, :].astype(low))
            out = []
            for part, (piece, total) in enumerate(zip(pieces, sums)):
                gproj[at, pl.ds(pl.multiple_of(part * width + h * HEAD, HEAD), HEAD)] = piece
                out.append(total + jnp.sum(piece.astype(full), axis=0, keepdims=True))
            return tuple(out)
        sums = lax.fori_loop(0, bands, back, (jnp.zeros((1, HEAD), full),) * 3)
        for part, total in enumerate(sums):
            small_ref[bias_row + part:bias_row + part + 1,
                      pl.ds(pl.multiple_of(place.sp * width + h * HEAD, HEAD), HEAD)] = total
        return carry
    lax.fori_loop(0, heads, head, 0)
    stores.append(pltpu.make_async_copy(gproj, proj_out, store_sem.at[1]))
    stores[1].start()
    qkv_load = load(qkv_hbm, qkv_w, 3)

    def unit_block(block, carry):
        slot = lax.rem(block, 2)
        down_load(block, slot).wait()
        pre_load(block, slot).wait()
        of = pl.ds(pl.multiple_of(block * units, units), units)
        room = pl.ds(pl.multiple_of(out_rows + slot * units, units), units)

        def far_band(r, total):
            at = pl.ds(pl.multiple_of(((1 - upper) * NEAR + r) * band, band), band)
            value = lax.dot_general(cot[at, :], up_w[room, :], (((1,), (1,)), ((), ())), preferred_element_type=full)
            value = (value * gelu_slope(pre[slot, pl.ds(pl.multiple_of(r * band, band), band), :])).astype(low)
            gpre[at, of] = value
            return total + jnp.sum(value.astype(full), axis=0, keepdims=True)
        small_ref[pl.ds(unit_row + block // per_row, 1),
                  pl.ds(pl.multiple_of((lax.rem(block, per_row) * sp_size + place.sp) * units, units), units)] = (
            lax.fori_loop(0, far, far_band, unit_ref[:, of]))

        @pl.when(block + 2 < blocks)
        def _():
            down_load(block + 2, slot).start()
            pre_load(block + 2, slot).start()
        return carry

    down.onward()
    fold.step(3)
    lax.fori_loop(0, blocks, unit_block, 0)
    used = out_rows + 2 * units
    up_loads = [load(up_hbm.at[pl.ds(0, used)], up_w.at[pl.ds(0, used)], 0), up_load]

    def tok_load(r):
        return pltpu.make_async_copy(tok_hbm.at[hat_rows(r)], tok.at[r % 2], tok_sem.at[r % 2])
    tok_load(0).start()
    tok_load(1).start()
    near_load.wait()
    gpre_store = pltpu.make_async_copy(gpre, gpre_out, store_sem.at[2])
    gpre_store.start()
    stores[0].wait()
    def hat_store(r):
        return pltpu.make_async_copy(cot.at[hat_rows(r)], hat_out.at[hat_rows(r)], store_sem.at[3 + r])

    def hat_hop(way):
        to = lax.rem(place.sp + (1 if way == 0 else sp_size - 1), sp_size)
        return remote(cot.at[hat_rows(0)], hat_in.at[way], hat_send.at[way], hat_recv.at[way], (place.dp, to))

    def hat_band(r):
        at = hat_rows(r)
        tok_load(r).wait()

        def columns(c, carry):
            to = pl.ds(pl.multiple_of(c * band, band), band)
            from_mlp = jnp.dot(gpre[at, :], up_w[:, to], preferred_element_type=full)
            from_attn = lax.dot_general(gproj[at, :], qkv_w[to, :], (((1,), (1,)), ((), ())), preferred_element_type=full)
            normed = (tok[r % 2, :, to].astype(full) - mean_s[at, 0:1]) * inv_s[at, 0:1]
            small_ref[gain_row:gain_row + 1, to] += jnp.sum(from_attn * normed, axis=0, keepdims=True)
            small_ref[gain_row + 1:gain_row + 2, to] += jnp.sum(from_mlp * normed, axis=0, keepdims=True)
            small_ref[shift_row:shift_row + 1, to] += jnp.sum(from_attn, axis=0, keepdims=True)
            small_ref[shift_row + 1:shift_row + 2, to] += jnp.sum(from_mlp, axis=0, keepdims=True)
            cot[at, to] = (from_attn * gain_ref[0:1, to].astype(full) + from_mlp * gain_ref[1:2, to].astype(full)).astype(low)
            return carry
        lax.fori_loop(0, wide // band, columns, 0)
        hat_store(r).start()
        if r + 2 < bands:
            tok_load(r + 2).start()

    qkv = Wide(place, 1, left, gproj, 3 * width, down_sum, down_sib, down_one, down_two)
    attn_load.wait()
    pl.semaphore_wait(sib_free, 1)
    qkv.for_sibling(down)
    qkv_load.wait()
    for c in up_loads:
        c.wait()
    hat_band(0)
    for way in (0, 1):
        @pl.when(fold.along(way) == 0)
        def _():
            hat_hop(way).start()
    down.finish()
    stores.append(pltpu.make_async_copy(down.block(0), down_out, store_sem.at[3 + bands]))
    stores[2].start()
    pl.semaphore_signal(one_free, inc=1, device_id=(place.first, place.sp), device_id_type=MESH)
    pl.semaphore_signal(two_free, inc=1, device_id=(place.second, place.sp), device_id_type=MESH)
    down.drain()
    stores[2].wait()
    pl.semaphore_wait(one_free, 1)
    qkv.for_self()
    for r in range(1, bands - 1):
        hat_band(r)
    pl.semaphore_wait(two_free, 1)
    qkv.onward()
    hat_band(bands - 1)
    fold.finish()
    stores.append(pltpu.make_async_copy(stage, red_out, store_sem.at[4 + bands]))
    stores[-1].start()
    qkv.finish()
    stores.append(pltpu.make_async_copy(qkv.block(0), slab_out, store_sem.at[5 + bands]))
    stores[-1].start()
    for r in range(bands):
        hat_store(r).wait()
    for which in (1, 3, 4):
        stores[which].wait()
    gpre_store.wait()
    for slot in range(4):
        qkv.sib_copy(slot).wait_send()
    qkv.drain()
    fold.drain()
    for way in (0, 1):
        @pl.when(fold.along(way) == 0)
        def _():
            hat_hop(way).wait_send()

        @pl.when(fold.along(way) == 1)
        def _():
            hat_hop(way).wait_recv()


def middle(sp_size, dp_size, lengths, cotangent, out_own, queries, key_rows, values, pre_act, hidden, down_own, up_own, qkv_own,
           tokens, partial_out, part_hop, near_pre, attn_in, unit_sums, gains, cos_t, sin_t, means, inverses):
    seq, wide = tokens.shape
    width = queries.shape[1]
    units = up_own.shape[0] // dp_size
    own = seq // sp_size
    full, low = jnp.float32, jnp.bfloat16
    hbm = pl.BlockSpec(memory_space=pltpu.HBM)
    vmem = pl.BlockSpec(memory_space=pltpu.VMEM)
    dma = pltpu.SemaphoreType.DMA
    shape = jax.ShapeDtypeStruct

    def v(*dims, kind=low):
        return pltpu.VMEM(dims, kind)
    bands = seq // 256
    return pl.pallas_call(
        functools.partial(middle_kernel, sp_size),
        out_shape=[shape((units, wide), low), shape((units, 3 * width), low), shape(hidden.shape, low), shape((seq, wide), low),
                   shape((2, own, wide), low),
                   shape((seq, 3 * width), low),
                   shape((seq, wide), low), shape((own, wide), low), shape((16, wide), full)],
        in_specs=[pl.BlockSpec(memory_space=pltpu.SMEM)] + [hbm] * 15 + [vmem] * 6,
        out_specs=[hbm] * 8 + [vmem],
        scratch_shapes=[
            v(seq, wide), v(seq, wide), v(2, 256, wide), v(*hidden.shape), v(*up_own.shape), v(*qkv_own.shape),
            v(2, (seq // 256 - NEAR) * 256, units, kind=full),
            v(seq, width), v(seq, 3 * width), v(seq, HEAD, kind=full), v(seq, HEAD, kind=full), v(seq, HEAD, kind=full),
            v(4, units, wide), v(4, units, wide), v(4, units, wide), v(2, units, wide), v(units, wide),
            v(2, sp_size - 1, own, wide), v(own, wide),
            dma((9,)), dma((2, 2)), dma((7 + bands,)), dma, dma((2, 4)), dma((2, 4)), dma((2, 2)), dma((2, 2)), dma((2,)), dma((2,)),
            dma((2, sp_size - 1)), dma((2, sp_size - 1)), dma((2,)), dma((2,)),
            pltpu.SemaphoreType.REGULAR, pltpu.SemaphoreType.REGULAR, pltpu.SemaphoreType.REGULAR, dma, dma((2,))],
        compiler_params=pltpu.CompilerParams(collective_id=3, has_side_effects=True, vmem_limit_bytes=67043328),
        cost_estimate=pl.CostEstimate(flops=40 * 10 ** 9, bytes_accessed=90 * 1000 * 1000, transcendentals=0),
        name="middle",
    )(lengths, cotangent, out_own, queries, key_rows, values, pre_act, hidden, down_own, up_own, qkv_own, tokens, partial_out,
      part_hop, near_pre, attn_in, unit_sums, gains, cos_t, sin_t, means, inverses)


def back_kernel(sp_size, cot_hbm, pre_hbm, mlp_hbm, ctx_hbm, hat_hbm, hop_hbm, slab_hbm, small_ref,
                up_out, qkv_out, dense_out, red_out, small_out,
                left, right, cot, ctx, lent,
                up_sum, dense_sum, up_sib, dense_sib, up_one, dense_one, up_two, dense_two,
                dense_part, slab, small_acc, small_in, small_z, small_fin, inbox, stage,
                load_sem, store_sem, stage_sem, sib_send, sib_recv, one_send, one_recv, two_send, two_recv,
                slab_send, slab_recv, turn_send, turn_recv, small_send, small_recv, z_send, z_recv,
                fold_send, fold_recv, plane_send, plane_recv):
    place = Square(sp_size, lent, sib_send, sib_recv, one_send, one_recv, two_send, two_recv)
    dp, sp = place.dp, place.sp
    per = 2
    pair, lane = dp // per, dp % per
    turn_dp = sp * per + lane
    slab_width = slab.shape[1]
    head_width = slab_width // 3
    rows = dense_one.shape[1]
    wide = left.shape[1]

    def load(source, target, which):
        c = pltpu.make_async_copy(source, target, load_sem.at[which])
        c.start()
        return c

    slab_load = load(slab_hbm, slab, 0)
    hops = [load(hop_hbm.at[way], inbox.at[way, 0], 1 + way) for way in (0, 1)]
    loads = [load(ctx_hbm, ctx, 3), load(cot_hbm, cot, 4)]

    barrier = pltpu.get_barrier_semaphore()
    for step in range(1, 8):
        pl.semaphore_signal(barrier, inc=1, device_id=(lax.rem(dp + step, 8), sp), device_id_type=MESH)
    for step in range(1, sp_size):
        pl.semaphore_signal(barrier, inc=1, device_id=(dp, lax.rem(sp + step, sp_size)), device_id_type=MESH)

    @pl.when(pair != sp)
    def _():
        pl.semaphore_signal(barrier, inc=1, device_id=(turn_dp, pair), device_id_type=MESH)

    pl.semaphore_wait(barrier, 6 + sp_size + jnp.where(pair != sp, 1, 0))
    fold = Fold(place, hat_hbm, inbox, stage, stage_sem, fold_send, fold_recv, begun=2)

    def small_copy(stage_of):
        partner = (place.sibling, place.across_x, place.across_y)[stage_of]
        return remote(small_ref if stage_of == 0 else small_acc.at[stage_of - 1], small_in.at[stage_of],
                      small_send.at[stage_of], small_recv.at[stage_of], (partner, sp))

    def small_step(stage_of):
        small_copy(stage_of).wait_recv()
        before = small_ref[...] if stage_of == 0 else small_acc[stage_of - 1]
        small_acc[stage_of] = before + small_in[stage_of]

    share = small_ref.shape[1] // 8

    def columns_of(owner):
        return pl.ds(pl.multiple_of(owner * share, share), share)

    def z_copy(step):
        return remote(small_acc.at[2, :, columns_of(dp)], small_z.at[sp], z_send.at[step - 1], z_recv.at[step - 1],
                      (dp, lax.rem(sp + step, sp_size)))

    def z_arrival(step):
        origin = lax.rem(sp + sp_size - step, sp_size)
        return remote(small_acc.at[2, :, columns_of(dp)], small_z.at[origin], z_send.at[step - 1], z_recv.at[step - 1],
                      (dp, origin))

    def plane_copy(step, owner, target):
        at = small_fin.at[:, columns_of(owner)]
        return remote(at, at, plane_send.at[step - 1], plane_recv.at[step - 1], (target, sp))

    def turn_copy():
        return remote(dense.block(0), dense_out, turn_send, turn_recv, (turn_dp, pair))

    def slab_rows(owner):
        return pl.ds(pl.multiple_of(owner * rows, rows), rows)

    def slab_columns(part, owner):
        return pl.ds(pl.multiple_of(part * wide + owner * head_width, head_width), head_width)

    def slab_copy(step, part, origin, there):
        return remote(slab.at[slab_rows(there), pl.ds(part * head_width, head_width)],
                      qkv_out.at[:, slab_columns(part, origin)],
                      slab_send.at[step - 1, part], slab_recv.at[step - 1, part], (dp, there))

    stores = []

    def store(source, target):
        c = pltpu.make_async_copy(source, target, store_sem.at[len(stores)])
        c.start()
        stores.append(c)

    small_copy(0).start()
    dense = Dense(place, 0, ctx, cot, wide, dense_sum, dense_sib, dense_one, dense_two, dense_part)
    up = Wide(place, 1, left, right, wide, up_sum, up_sib, up_one, up_two)
    for way in (0, 1):
        hops[way].wait()
    fold.step(2)
    slab_load.wait()
    for step in range(1, sp_size):
        for part in range(3):
            slab_copy(step, part, sp, lax.rem(sp + step, sp_size)).start()
    for part in range(3):
        store(slab.at[slab_rows(sp), pl.ds(part * head_width, head_width)], qkv_out.at[:, slab_columns(part, sp)])
    loads += [load(pre_hbm, left, 5), load(mlp_hbm, right, 6)]
    small_step(0)
    small_copy(1).start()
    loads[0].wait()
    loads[1].wait()
    dense.for_sibling(None)
    loads[2].wait()
    loads[3].wait()
    up.for_sibling(None)
    small_step(1)
    small_copy(2).start()
    dense.for_self()
    up.for_self()
    small_step(2)
    for step in range(1, sp_size):
        z_copy(step).start()
    small_z[sp] = small_acc[2, :, columns_of(dp)]
    dense.onward()
    fold.step(3)
    up.onward()
    dense.finish()

    @pl.when(pair != sp)
    def _():
        turn_copy().start()

    @pl.when(pair == sp)
    def _():
        c = pltpu.make_async_copy(dense.block(0), dense_out, store_sem.at[5])
        c.start()
        c.wait()

    for step in range(1, sp_size):
        z_arrival(step).wait_recv()
    total = small_z[0]
    for origin in range(1, sp_size):
        total = total + small_z[origin]
    small_fin[:, columns_of(dp)] = total
    for step in range(1, 8):
        plane_copy(step, dp, lax.rem(dp + step, 8)).start()
    up.finish()
    store(up.block(0), up_out)
    fold.finish()
    store(stage, red_out)
    for slot in range(4):
        up.sib_copy(slot).wait_send()
    dense.sib_copy(0).wait_send()
    for array in (dense, up):
        array.drain()
    for stage_of in range(3):
        small_copy(stage_of).wait_send()
    fold.drain()
    for step in range(1, sp_size):
        z_copy(step).wait_send()
        for part in range(3):
            slab_copy(step, part, lax.rem(sp + sp_size - step, sp_size), sp).wait_recv()
            slab_copy(step, part, sp, lax.rem(sp + step, sp_size)).wait_send()

    @pl.when(pair != sp)
    def _():
        turn_copy().wait_recv()
        turn_copy().wait_send()

    for step in range(1, 8):
        origin = lax.rem(dp + 8 - step, 8)
        plane_copy(step, origin, origin).wait_recv()
        plane_copy(step, dp, origin).wait_send()
    small_out[...] = small_fin[...]
    for c in stores:
        c.wait()


def reduce_gradients(sp_size, rows, grad_out, grad_pre, mlp_in, context, grad_hat, hat_hop, slab_sum, small):
    seq, wide = mlp_in.shape
    slab, slab_width = slab_sum.shape
    units = slab
    own = seq // sp_size
    full, low = jnp.float32, jnp.bfloat16
    hbm = pl.BlockSpec(memory_space=pltpu.HBM)
    vmem = pl.BlockSpec(memory_space=pltpu.VMEM)
    dma = pltpu.SemaphoreType.DMA
    shape = jax.ShapeDtypeStruct

    def v(*dims, kind=low):
        return pltpu.VMEM(dims, kind)
    scratch = [
        v(seq, wide), v(seq, wide), v(seq, wide), v(seq, context.shape[1]), v(4, units, wide),
        v(4, units, wide), v(slab, wide), v(4, units, wide), v(slab, wide),
        v(2, units, wide), v(2, rows, wide), v(units, wide), v(rows, wide),
        v(slab, wide), v(slab, slab_width),
        v(3, *small.shape, kind=full), v(3, *small.shape, kind=full), v(sp_size, small.shape[0], small.shape[1] // 8, kind=full), v(*small.shape, kind=full),
        v(2, sp_size - 1, own, wide), v(own, wide),
        dma((7,)), dma((6,)), dma, dma((2, 4)), dma((2, 4)), dma((2, 2)), dma((2, 2)), dma((2,)), dma((2,)),
        dma((sp_size - 1, 3)), dma((sp_size - 1, 3)), dma, dma, dma((3,)), dma((3,)),
        dma((sp_size - 1,)), dma((sp_size - 1,)), dma((2, sp_size - 1)), dma((2, sp_size - 1)), dma((7,)), dma((7,)),
    ]
    return pl.pallas_call(
        functools.partial(back_kernel, sp_size),
        out_shape=[shape((units, wide), low), shape((rows, 3 * wide), low), shape((rows, wide), low), shape((own, wide), low),
                   shape(small.shape, full)],
        in_specs=[hbm] * 7 + [vmem], out_specs=[hbm] * 4 + [vmem],
        scratch_shapes=scratch,
        compiler_params=pltpu.CompilerParams(collective_id=1, has_side_effects=True, vmem_limit_bytes=62 << 20),
        cost_estimate=pl.CostEstimate(flops=9 * 10 ** 9, bytes_accessed=200 * 1000 * 1000, transcendentals=0),
        name="reduce_gradients",
    )(grad_out, grad_pre, mlp_in, context, grad_hat, hat_hop, slab_sum, small)

def finish_kernel(len_ref, tok_ref, cot_ref, sum_ref, hat_ref, down_ref, up_ref, qkv_ref, dense_ref, bias_ref, small_ref,
                  out_ref, input_ref, gain_out, shift_out, qkv_out, qkv_bias_out, dense_out, up_out, unit_out, down_out, bias_out):
    full = jnp.float32
    part = pl.program_id(0)
    rows, wide = tok_ref.shape
    tokens = tok_ref[...].astype(full)
    out_ref[...] = (tokens + sum_ref[...].astype(full) + bias_ref[...].astype(full)).astype(out_ref.dtype)
    centered = tokens - jnp.mean(tokens, axis=-1, keepdims=True)
    inverse = lax.rsqrt(jnp.mean(centered * centered, axis=-1, keepdims=True) + eps)
    normed = centered * inverse
    hat = hat_ref[...].astype(full)
    grad = inverse * (
        hat - jnp.mean(hat, axis=-1, keepdims=True) - normed * jnp.mean(hat * normed, axis=-1, keepdims=True))
    position = (lax.axis_index("sp") * pl.num_programs(0) + part) * rows + lax.broadcasted_iota(jnp.int32, (rows, wide), 0)
    own = jnp.where(position < len_ref[0], cot_ref[...].astype(full), 0.0)
    input_ref[...] = (own + grad).astype(input_ref.dtype)
    down_out[...] = down_ref[...].astype(full)
    up_out[...] = up_ref[...].astype(full)
    qkv_out[...] = qkv_ref[...].astype(full)
    dense_out[...] = dense_ref[...].astype(full)

    @pl.when(part == 0)
    def _():
        gain_out[...] = small_ref[0:2, :]
        shift_out[...] = small_ref[2:4, :]
        qkv_bias_out[...] = small_ref[4:7, :]
        unit_rows = unit_out.shape[1] // wide
        for row in range(unit_rows):
            unit_out[:, row * wide:(row + 1) * wide] = small_ref[7 + row:8 + row, :]
        bias_out[...] = small_ref[7 + unit_rows:8 + unit_rows, :]


def finish(lengths, tokens, cotangent, reduced_out, reduced_hat, grad_down, grad_up, grad_qkv, grad_dense, out_bias, small, all_units):
    own, wide = tokens.shape
    steps = 4
    full = jnp.float32
    shape = jax.ShapeDtypeStruct

    def rows(x):
        return pl.BlockSpec((x.shape[0] // steps, x.shape[1]), lambda i: (i, 0))

    def whole(*dims):
        return pl.BlockSpec(dims, lambda i: (0, 0))
    out_row = out_bias[None]
    return pl.pallas_call(
        finish_kernel,
        grid=(steps,),
        out_shape=[shape(tokens.shape, tokens.dtype), shape(tokens.shape, tokens.dtype), shape((2, wide), full),
                   shape((2, wide), full), shape(grad_qkv.shape, full), shape((3, wide), full), shape(grad_dense.shape, full),
                   shape(grad_up.shape, full), shape((1, all_units), full), shape(grad_down.shape, full), shape((1, wide), full)],
        in_specs=[pl.BlockSpec(memory_space=pltpu.SMEM)]
        + [rows(x) for x in (tokens, cotangent, reduced_out, reduced_hat, grad_down, grad_up, grad_qkv, grad_dense)]
        + [whole(1, wide), whole(*small.shape)],
        out_specs=[rows(tokens), rows(tokens), whole(2, wide), whole(2, wide), rows(grad_qkv), whole(3, wide), rows(grad_dense),
                   rows(grad_up), whole(1, all_units), rows(grad_down), whole(1, wide)],
        name="finish",
    )(lengths, tokens, cotangent, reduced_out, reduced_hat, grad_down, grad_up, grad_qkv, grad_dense, out_row, small)

def gather_plain(dp_size, sp_size, qkv_weight, out_weight, up_weight, down_weight):
    head_width = D // sp_size
    qkv_rows = qkv_weight.shape[0]
    qkv_slab = lax.all_to_all(
        qkv_weight.reshape(qkv_rows, 3, sp_size, head_width),
        "sp",
        split_axis=2,
        concat_axis=0,
        tiled=True,
    )
    qkv_own = lax.all_gather(
        qkv_slab.reshape(qkv_rows * sp_size, 3 * head_width), "dp", axis=0, tiled=True
    )
    up_own = lax.all_gather(up_weight, "dp", axis=0, tiled=True)
    down_own = lax.all_gather(down_weight, "dp", axis=0, tiled=True)
    out_blocks = lax.all_gather(out_weight, "dp", axis=0, tiled=True)
    out_own = lax.all_to_all(
        out_blocks.reshape(sp_size, dp_size // sp_size, qkv_rows, D),
        "sp",
        split_axis=0,
        concat_axis=2,
        tiled=True,
    ).reshape(head_width, D)
    return qkv_own, out_own, up_own, down_own


def reduce_plain(
    dp_size, sp_size, rows, hidden, grad_out, grad_pre, mlp_in, attn_in, grad_proj, context
):
    def scatter(left, right):
        return lax.psum_scatter(
            contract_rows(left, right).astype(jnp.bfloat16), "dp", scatter_dimension=0, tiled=True
        )

    grad_dense = lax.all_to_all(
        contract_rows(context, grad_out)
        .astype(jnp.bfloat16)
        .reshape(dp_size // sp_size, sp_size, rows, D),
        "sp",
        split_axis=1,
        concat_axis=0,
        tiled=True,
    ).reshape(dp_size * rows, D)
    grad_dense = lax.psum_scatter(grad_dense, "dp", scatter_dimension=0, tiled=True)
    grad_qkv = lax.all_to_all(
        scatter(attn_in, grad_proj).reshape(sp_size, rows, 3, 1, D // sp_size),
        "sp",
        split_axis=0,
        concat_axis=3,
        tiled=True,
    ).reshape(rows, 3 * D)
    return scatter(hidden, grad_out), scatter(grad_pre, mlp_in), grad_qkv, grad_dense


def body(
    tokens,
    lengths,
    cotangent,
    ln_gains,
    ln_shifts,
    qkv_weight,
    qkv_bias,
    out_weight,
    up_weight,
    up_bias,
    down_weight,
    out_bias,
):
    dp_size = lax.axis_size("dp")
    sp_size = lax.axis_size("sp")
    shard = lax.axis_index("sp")
    own_rows = tokens.shape[0]
    seq_rows = own_rows * sp_size
    head_width = D // sp_size
    length = lengths[0]
    low = jnp.bfloat16
    full = jnp.float32

    qkv_rows = qkv_weight.shape[0]
    units = up_weight.shape[0]
    square = dp_size == 8 and sp_size == 4
    unit_bias = (
        lax.dynamic_index_in_dim(
            up_bias.reshape(dp_size, sp_size, units), shard, 1, keepdims=False
        )
        .reshape(dp_size * units)
        .astype(full)
    )
    bias_own = (
        lax.dynamic_index_in_dim(
            qkv_bias.reshape(3, sp_size, head_width), shard, 1, keepdims=False
        )
        .reshape(1, 3 * head_width)
        .astype(full)
    )
    positions = jnp.arange(seq_rows, dtype=jnp.int32)
    gains = ln_gains.astype(full)
    shifts = ln_shifts.astype(full)
    row_valid = positions < length
    if not square:
        cos_rows, sin_rows = rotary_rows(seq_rows)
        seq_tokens = lax.all_gather(tokens, "sp", axis=0, tiled=True)
        qkv_own, out_own, up_own, down_own = gather_plain(
            dp_size, sp_size, qkv_weight, out_weight, up_weight, down_weight
        )
        seq_cotangent = lax.all_gather(cotangent, "sp", axis=0, tiled=True)
    if square:
        (
            qkv_own,
            out_own,
            up_own,
            down_own,
            seq_tokens,
            seq_cotangent,
            attn_in,
            mlp_in,
            hidden,
            pre_act,
            partial_out,
            part_hop,
            near_pre,
            cos_rows,
            sin_rows,
            means,
            inverses,
            unit_sums,
            queries,
            key_rows,
            values,
            context,
        ) = front(
            sp_size,
            dp_size,
            lengths,
            qkv_weight,
            out_weight,
            up_weight,
            down_weight,
            tokens,
            cotangent,
            ln_gains,
            ln_shifts,
            bias_own,
            unit_bias[None],
        )
        grad_down, slab_sum, grad_pre, grad_hat, hat_hop, _, grad_out, reduced_out, small = middle(
            sp_size,
            dp_size,
            lengths,
            seq_cotangent,
            out_own,
            queries,
            key_rows,
            values,
            pre_act,
            hidden,
            down_own,
            up_own,
            qkv_own,
            seq_tokens,
            partial_out,
            part_hop,
            near_pre,
            attn_in,
            unit_sums,
            ln_gains,
            cos_rows,
            sin_rows,
            means,
            inverses,
        )
        grad_up, grad_qkv, grad_dense, reduced_hat, small = reduce_gradients(
            sp_size,
            qkv_rows,
            grad_out,
            grad_pre,
            mlp_in,
            context,
            grad_hat,
            hat_hop,
            slab_sum,
            small,
        )
        (
            output,
            input_grad,
            gain_total,
            shift_total,
            grad_qkv,
            qkv_bias_total,
            grad_dense,
            grad_up,
            unit_total,
            grad_down,
            out_bias_total,
        ) = finish(
            lengths,
            tokens,
            cotangent,
            reduced_out,
            reduced_hat,
            grad_down,
            grad_up,
            grad_qkv,
            grad_dense,
            out_bias,
            small,
            up_bias.shape[0],
        )
        unit_total = unit_total.reshape(-1)
        out_bias_total = out_bias_total.reshape(-1)
    else:
        inputs = seq_tokens.astype(full)
        centre = jnp.mean(inputs, axis=-1, keepdims=True)
        centered = inputs - centre
        inverse = lax.rsqrt(jnp.mean(centered * centered, axis=-1, keepdims=True) + eps)
        normed = centered * inverse
        attn_in = (normed * gains[0] + shifts[0]).astype(low)
        mlp_in = (normed * gains[1] + shifts[1]).astype(low)
        projected = jnp.dot(attn_in, qkv_own, preferred_element_type=full)
        queries, key_rows, values, context = attend_fwd(
            projected, bias_own, cos_rows, sin_rows, lengths
        )
        pre_act = contract_cols(mlp_in, up_own) + unit_bias
        hidden = gelu_value(pre_act).astype(low)
        partial_out = (
            jnp.dot(hidden, down_own, preferred_element_type=full)
            + jnp.dot(context, out_own, preferred_element_type=full)
        ).astype(low)
        reduced_out = lax.psum_scatter(
            partial_out, "sp", scatter_dimension=0, tiled=True
        )
        grad_out = jnp.where(row_valid[:, None], seq_cotangent, jnp.zeros_like(seq_cotangent))
        grad_hidden = contract_cols(grad_out, down_own)
        grad_pre = (grad_hidden * gelu_slope(pre_act)).astype(low)
        grad_mlp_in = jnp.dot(grad_pre, up_own, preferred_element_type=full)

        grad_context = contract_cols(grad_out, out_own).astype(low)
        grad_proj, grad_proj_sum = attend_bwd(
            queries, key_rows, values, grad_context, cos_rows, sin_rows, lengths
        )
        grad_attn_in = contract_cols(grad_proj, qkv_own)
        grad_hat = grad_attn_in * gains[0] + grad_mlp_in * gains[1]
        reduced_hat = lax.psum_scatter(
            grad_hat.astype(low), "sp", scatter_dimension=0, tiled=True
        )
        spread_units = lax.dynamic_update_index_in_dim(
            jnp.zeros((dp_size, sp_size, units), full),
            jnp.sum(grad_pre, axis=0, dtype=full).reshape(dp_size, units),
            shard,
            1,
        ).reshape(-1)
        spread_bias = lax.dynamic_update_index_in_dim(
            jnp.zeros((3, sp_size, head_width), full),
            grad_proj_sum.reshape(3, head_width),
            shard,
            1,
        ).reshape(3, D)
        gain_grad = jnp.stack(
            [jnp.sum(grad_attn_in * normed, axis=0), jnp.sum(grad_mlp_in * normed, axis=0)]
        )
        shift_grad = jnp.stack([jnp.sum(grad_attn_in, axis=0), jnp.sum(grad_mlp_in, axis=0)])
        own_valid = shard * own_rows + jnp.arange(own_rows, dtype=jnp.int32) < length
        own_cotangent = jnp.where(own_valid[:, None], cotangent.astype(full), 0.0)
        out_bias_part = jnp.sum(own_cotangent, axis=0)
        grad_down, grad_up, grad_qkv, grad_dense = reduce_plain(
            dp_size,
            sp_size,
            qkv_rows,
            hidden,
            grad_out,
            grad_pre,
            mlp_in,
            attn_in,
            grad_proj,
            context,
        )
        gain_total, shift_total, qkv_bias_total, unit_total, out_bias_total = lax.psum(
            (gain_grad, shift_grad, spread_bias, spread_units, out_bias_part), ("dp", "sp")
        )


        output = (
            tokens.astype(full) + reduced_out.astype(full) + out_bias.astype(full)
        ).astype(low)

        reduced_hat = reduced_hat.astype(full)
        own_centered = tokens.astype(full) - jnp.mean(tokens.astype(full), axis=-1, keepdims=True)
        own_inverse = lax.rsqrt(jnp.mean(own_centered * own_centered, axis=-1, keepdims=True) + eps)
        own_normed = own_centered * own_inverse
        grad_input = own_inverse * (
            reduced_hat
            - jnp.mean(reduced_hat, axis=-1, keepdims=True)
            - own_normed * jnp.mean(reduced_hat * own_normed, axis=-1, keepdims=True)
        )
        input_grad = (own_cotangent + grad_input).astype(low)
        grad_qkv, grad_dense = grad_qkv.astype(full), grad_dense.astype(full)
        grad_up, grad_down = grad_up.astype(full), grad_down.astype(full)

    return (
        output,
        input_grad,
        gain_total,
        shift_total,
        grad_qkv,
        qkv_bias_total,
        grad_dense,
        grad_up,
        unit_total,
        grad_down,
        out_bias_total,
    )


def solution(mesh):
    return jax.shard_map(
        body,
        mesh=mesh,
        in_specs=(
            P(("dp", "sp"), None),
            P("dp"),
            P(("dp", "sp"), None),
            P(),
            P(),
            P(("dp", "sp"), None),
            P(),
            P(("dp", "sp"), None),
            P(("dp", "sp"), None),
            P(),
            P(("dp", "sp"), None),
            P(),
        ),
        out_specs=(
            P(("dp", "sp"), None),
            P(("dp", "sp"), None),
            P(),
            P(),
            P(("dp", "sp"), None),
            P(),
            P(("dp", "sp"), None),
            P(("dp", "sp"), None),
            P(),
            P(("dp", "sp"), None),
            P(),
        ),
        check_vma=False,
    )
```

```python
import functools

import jax
import jax.numpy as jnp
from jax import lax
from jax.experimental import pallas as pl
from jax.experimental.pallas import tpu as pltpu
from jax.sharding import PartitionSpec as P

D = 2048
HEADS = 8
HEAD = 256
ROT = 64


eps = 1e-05
base_freq = 10000.0
root_half = 0.7071067811865476
inv_root_two_pi = 0.3989422804014327


def contract_rows(left, right):
    return lax.dot_general(
        left, right, (((0,), (0,)), ((), ())), preferred_element_type=jnp.float32
    )


def contract_cols(left, right):
    return lax.dot_general(
        left, right, (((1,), (1,)), ((), ())), preferred_element_type=jnp.float32
    )


def gelu_value(pre_act):
    return 0.5 * pre_act * (1.0 + lax.erf(pre_act * root_half))


def gelu_slope(pre_act):
    return 0.5 * (1.0 + lax.erf(pre_act * root_half)) + pre_act * inv_root_two_pi * jnp.exp(
        -0.5 * pre_act * pre_act
    )


BAND=256
def turn(x, cos_t, sin_t):
    first = x[:, :128]
    lane = lax.broadcasted_iota(jnp.int32, first.shape, 1)
    partner = jnp.where(lane < ROT // 2, pltpu.roll(first, 128 - ROT // 2, 1), pltpu.roll(first, ROT // 2, 1))
    return jnp.concatenate([first * cos_t + partner * sin_t, x[:, 128:]], axis=1)

def weights_of(q, k, start, length, scale):
    rows, cols = q.shape[0], k.shape[0]
    s = lax.dot_general(q, k, (((1,), (1,)), ((), ())), preferred_element_type=jnp.float32) * scale
    key = lax.broadcasted_iota(jnp.int32, (rows, cols), 1)
    query = start + lax.broadcasted_iota(jnp.int32, (rows, cols), 0)
    s = jnp.where((key <= query) & (key < length), s, -1e30)
    e = jnp.exp(s - jnp.max(s, axis=-1, keepdims=True))
    return e / jnp.sum(e, axis=-1, keepdims=True)

def fwd_kernel(scale, len_ref, pq, pk, pv, bq, bk, bv, cos_ref, sin_ref, q_ref, k_ref, v_ref, ctx_ref):
    length = len_ref[0]
    seq = pq.shape[0]
    cos_t, sin_t = cos_ref[...], sin_ref[...]
    q_ref[...] = turn(pq[...] + bq[...], cos_t, sin_t).astype(jnp.bfloat16)
    k_ref[...] = turn(pk[...] + bk[...], cos_t, sin_t).astype(jnp.bfloat16)
    v_ref[...] = (pv[...] + bv[...]).astype(jnp.bfloat16)
    for start in range(0, seq, BAND):
        end = start + BAND
        p = weights_of(q_ref[start:end, :], k_ref[:end, :], start, length, scale)
        ctx_ref[start:end, :] = jnp.dot(p.astype(jnp.bfloat16), v_ref[:end, :], preferred_element_type=jnp.float32).astype(jnp.bfloat16)

def attend_fwd(projected, bias, cos_t, sin_t, lengths):
    seq, width = projected.shape
    heads = width // 3 // HEAD
    col = lambda g: pl.BlockSpec((seq, HEAD), lambda h, *_, g=g: (0, g * heads + h))
    bcol = lambda g: pl.BlockSpec((1, HEAD), lambda h, *_, g=g: (0, g * heads + h))
    tab = pl.BlockSpec((seq, 128), lambda h, *_: (0, 0))
    out = pl.BlockSpec((seq, HEAD), lambda h, *_: (0, h))
    return pl.pallas_call(
        functools.partial(fwd_kernel, HEAD ** -0.5),
        grid_spec=pltpu.PrefetchScalarGridSpec(num_scalar_prefetch=1, grid=(heads,),
            in_specs=[col(0), col(1), col(2), bcol(0), bcol(1), bcol(2), tab, tab], out_specs=[out] * 4),
        out_shape=[jax.ShapeDtypeStruct((seq, heads * HEAD), jnp.bfloat16)] * 4,
        name="attend_fwd",
        cost_estimate=pl.CostEstimate(flops=heads * seq * seq * HEAD * 4, bytes_accessed=seq * width * 8, transcendentals=heads * seq * seq),
    )(lengths, projected, projected, projected, bias, bias, bias, cos_t, sin_t)

def bwd_kernel(scale, heads, len_ref, q_ref, k_ref, v_ref, g_ref, cos_ref, sin_ref, gp_ref, sum_ref, dk, dv, dq):
    length = len_ref[0]
    h = pl.program_id(0)
    seq = q_ref.shape[0]
    dk[...] = jnp.zeros_like(dk)
    dv[...] = jnp.zeros_like(dv)
    for start in range(0, seq, BAND):
        end = start + BAND
        q, g = q_ref[start:end, :], g_ref[start:end, :]
        k, v = k_ref[:end, :], v_ref[:end, :]
        p = weights_of(q, k, start, length, scale)
        gp = lax.dot_general(g, v, (((1,), (1,)), ((), ())), preferred_element_type=jnp.float32)
        ds = (p * (gp - jnp.sum(p * gp, axis=-1, keepdims=True))).astype(jnp.bfloat16)
        dq[start:end, :] = jnp.dot(ds, k, preferred_element_type=jnp.float32) * scale
        dk[:end, :] += lax.dot_general(ds, q, (((0,), (0,)), ((), ())), preferred_element_type=jnp.float32)
        dv[:end, :] += lax.dot_general(p.astype(jnp.bfloat16), g, (((0,), (0,)), ((), ())), preferred_element_type=jnp.float32)
    cos_t, sin_t = cos_ref[...], sin_ref[...]
    def back(x):
        return turn(x.astype(jnp.bfloat16).astype(jnp.float32), cos_t, -sin_t).astype(jnp.bfloat16)
    for g, piece in enumerate((back(dq[...]), back(dk[...] * scale), dv[...].astype(jnp.bfloat16))):
        at = pl.ds(pl.multiple_of((g * heads + h) * HEAD, HEAD), HEAD)
        gp_ref[:, at] = piece
        sum_ref[:, at] = jnp.sum(piece.astype(jnp.float32), axis=0, keepdims=True)

def attend_bwd(q, k, v, gctx, cos_t, sin_t, lengths):
    seq, width = q.shape
    heads = width // HEAD
    col = pl.BlockSpec((seq, HEAD), lambda h, *_: (0, h))
    tab = pl.BlockSpec((seq, 128), lambda h, *_: (0, 0))
    return pl.pallas_call(
        functools.partial(bwd_kernel, HEAD ** -0.5, heads),
        grid_spec=pltpu.PrefetchScalarGridSpec(num_scalar_prefetch=1, grid=(heads,),
            in_specs=[col] * 4 + [tab, tab],
            out_specs=[pl.BlockSpec((seq, 3 * width), lambda h, *_: (0, 0)), pl.BlockSpec((1, 3 * width), lambda h, *_: (0, 0))],
            scratch_shapes=[pltpu.VMEM((seq, HEAD), jnp.float32)] * 3),
        out_shape=[jax.ShapeDtypeStruct((seq, 3 * width), jnp.bfloat16), jax.ShapeDtypeStruct((1, 3 * width), jnp.float32)],
        name="attend_bwd",
        cost_estimate=pl.CostEstimate(flops=heads * seq * seq * HEAD * 10, bytes_accessed=seq * width * 20, transcendentals=heads * seq * seq),
    )(lengths, q, k, v, gctx, cos_t, sin_t)

def rotary_rows(seq):
    half = ROT // 2
    freq = 10000.0 ** (-jnp.arange(half, dtype=jnp.float32) * (2.0 / ROT))
    ang = jnp.arange(seq, dtype=jnp.int32).astype(jnp.float32)[:, None] * freq[None, :]
    c, s = jnp.cos(ang), jnp.sin(ang)
    rest = 128 - ROT
    return (jnp.concatenate([c, c, jnp.ones((seq, rest), jnp.float32)], 1), jnp.concatenate([-s, s, jnp.zeros((seq, rest), jnp.float32)], 1))

MESH = pl.DeviceIdType.MESH

def square_partners(dp):
    core, x, y = dp % 2, (dp // 2) % 2, dp // 4
    across_x, across_y = dp + 2 - 4 * x, dp + 4 - 8 * y
    first = across_x * (1 - core) + across_y * core
    second = across_y * (1 - core) + across_x * core
    return first, second, across_x + across_y - dp, 1 - 2 * core

class Hops:
    def __init__(self, count, dp, sp, source, result, send, recv):
        self.count, self.dp, self.sp, self.source, self.result = count, dp, sp, source, result
        self.send, self.recv, self.rows = send, recv, source.shape[0]

    def place(self, owner):
        return pl.ds(pl.multiple_of(owner * self.rows, self.rows), self.rows)

    def copy(self, way, step, owner, own):
        to = lax.rem(self.sp + (1 if way == 0 else self.count - 1), self.count)
        at = self.result.at[self.place(owner)]
        return pltpu.make_async_remote_copy(
            src_ref=self.source if own else at, dst_ref=at, send_sem=self.send.at[way, step],
            recv_sem=self.recv.at[way, step], device_id=(self.dp, to), device_id_type=MESH)

    def sends(self, way, step):
        if way == 0:
            return (self.sp >= step) & (self.sp < self.count - 1)
        return (self.sp < self.count - step) & (self.sp > 0)

    def receives(self, way, step):
        return self.sp >= step + 1 if way == 0 else self.sp < self.count - step - 1

    def owner(self, way, step):
        return self.sp - step if way == 0 else self.sp + step

    def start(self, way, step):
        @pl.when(self.sends(way, step))
        def _():
            self.copy(way, step, self.owner(way, step), step == 0).start()

    def begin(self):
        for way in (0, 1):
            self.start(way, 0)

    def relay(self, step):
        for way in (0, 1):
            @pl.when(self.receives(way, step - 1) & self.sends(way, step))
            def _():
                self.copy(way, step - 1, self.owner(way, step), False).wait_recv()
                self.copy(way, step, self.owner(way, step), False).start()

    def settle(self, step):
        for way in (0, 1):
            @pl.when(self.receives(way, step - 1) & jnp.logical_not(self.sends(way, step)))
            def _():
                self.copy(way, step - 1, self.owner(way, step), False).wait_recv()

    def finish(self):
        for step in range(self.count - 1):
            for way in (0, 1):
                @pl.when(self.sends(way, step))
                def _():
                    self.copy(way, step, self.owner(way, step), step == 0).wait_send()


NEAR = 2


def front_kernel(sp_size, len_ref, qkv_ref, out_ref, up_ref, down_ref, tok_ref, cot_ref, freq_ref, gain_ref, shift_ref,
                 qkv_bias_ref, unit_bias_ref,
                 qkv_all, out_all, up_all, down_all, tok_all, cot_all, attn_out, mlp_out, hidden_out, pre_out, part_out, part_in, gpre_out,
                 cos_ref, sin_ref, mean_ref, inv_ref, unit_ref, q_ref, k_ref, v_ref, ctx_ref,
                 tok, attn, mlp, qkv_w, up_w, hidden, pre, cot, gpre,
                 send_sem, recv_sem, slab_send, slab_recv, keep_sem, turn_send, turn_recv, tok_send, tok_recv, cot_send, cot_recv,
                 load_sem, store_sem, pre_sem, part_sem, hop_send, hop_recv, slope_sem, gpre_sem):
    full, low = jnp.float32, jnp.bfloat16
    dp, sp = lax.axis_index("dp"), lax.axis_index("sp")
    first, second, diagonal, flip = square_partners(dp)
    sibling = dp + flip
    per = 2
    pair, lane = dp // per, dp % per
    rows = qkv_ref.shape[0]
    seq, wide = tok.shape
    own_rows = tok_ref.shape[0]
    head_width = wide // sp_size
    units = down_ref.shape[0]
    slab = rows * sp_size
    width = q_ref.shape[1]
    turn_dp = sp * per + lane
    scale = HEAD ** -0.5
    band = 256

    barrier = pltpu.get_barrier_semaphore()
    for other in (first, second, sibling):
        pl.semaphore_signal(barrier, inc=1, device_id=(other, sp), device_id_type=MESH)
    for step in range(1, sp_size):
        pl.semaphore_signal(barrier, inc=1, device_id=(dp, lax.rem(sp + step, sp_size)), device_id_type=MESH)

    @pl.when(pair != sp)
    def _():
        pl.semaphore_signal(barrier, inc=1, device_id=(turn_dp, pair), device_id_type=MESH)

    pl.semaphore_wait(barrier, 2 + sp_size + jnp.where(pair != sp, 1, 0))

    def remote_copy(source, target, send, recv, device):
        return pltpu.make_async_remote_copy(
            src_ref=source, dst_ref=target, send_sem=send, recv_sem=recv, device_id=device, device_id_type=MESH)

    def slab_at(owner):
        return pl.ds(pl.multiple_of((dp * sp_size + owner) * rows, rows), rows)

    def slab_columns(part, there):
        return pl.ds(pl.multiple_of(part * wide + there * head_width, head_width), head_width)

    def slab_copy(step, part, there, origin):
        return remote_copy(
            qkv_ref.at[:, slab_columns(part, there)],
            qkv_all.at[slab_at(origin), pl.ds(part * head_width, head_width)],
            slab_send.at[step - 1, part], slab_recv.at[step - 1, part], (dp, there))

    def plain(height):
        return lambda owner: pl.ds(pl.multiple_of(owner * height, height), height)

    def turned(owner):
        return pl.ds(pl.multiple_of((owner % per) * slab + (owner // per) * rows, rows), rows)

    def turn_copy(landing):
        return remote_copy(out_ref, out_all.at[turned(landing)], turn_send, turn_recv, (turn_dp, pair))

    arrays = ((up_ref, up_all, plain(units)), (None, qkv_all, plain(slab)), (None, out_all, turned), (down_ref, down_all, plain(units)))
    UP, QKV, OUT, DOWN = 0, 1, 2, 3

    def copy(index, message, block, target):
        source, result, place = arrays[index]
        at = result.at[place(block)]
        return remote_copy(at if source is None or message > 2 else source, at,
                           send_sem.at[index, message], recv_sem.at[index, message], (target, sp))

    sends = ((dp, first), (dp, second), (dp, sibling), (first, second), (first, sibling), (second, sibling), (diagonal, sibling))
    arrivals = (first, second, sibling, diagonal, second + flip, first + flip, diagonal + flip)

    def start(index, message):
        copy(index, message, *sends[message]).start()

    def arrived(index, message):
        copy(index, message, arrivals[message], sibling).wait_recv()

    def own(index):
        for message in (0, 1, 2):
            start(index, message)

    def onward(index):
        arrived(index, 0)
        start(index, 3)
        start(index, 4)
        arrived(index, 1)
        start(index, 5)

    def corner(index):
        arrived(index, 3)
        start(index, 6)

    def complete(index):
        for message in (2, 4, 5, 6):
            arrived(index, message)

    def load(source, target, which):
        c = pltpu.make_async_copy(source, target, load_sem.at[which])
        c.start()
        return c

    for step in range(1, sp_size):
        for part in range(3):
            slab_copy(step, part, lax.rem(sp + step, sp_size), sp).start()

    @pl.when(pair != sp)
    def _():
        turn_copy(turn_dp).start()

    own(UP)
    tokens = Hops(sp_size, dp, sp, tok_ref, tok_all, tok_send, tok_recv)
    cotangents = Hops(sp_size, dp, sp, cot_ref, cot_all, cot_send, cot_recv)
    tokens.begin()
    keeps = []

    def keep(source, target):
        c = pltpu.make_async_copy(source, target, keep_sem.at[len(keeps)])
        c.start()
        keeps.append(c)

    for part in range(3):
        keep(qkv_ref.at[:, slab_columns(part, sp)], qkv_all.at[slab_at(sp), pl.ds(part * head_width, head_width)])
    keep(up_ref, up_all.at[plain(units)(dp)])
    keep(down_ref, down_all.at[plain(units)(dp)])
    keep(tok_ref, tok_all.at[tokens.place(sp)])
    keep(cot_ref, cot_all.at[cotangents.place(sp)])

    def normalize(source, source_start, target_start):
        def chunk(i, carry):
            at = pl.ds(pl.multiple_of(target_start + i * 32, 32), 32)
            values = source[pl.ds(pl.multiple_of(source_start + i * 32, 32), 32), :].astype(full)
            mean = jnp.mean(values, axis=-1, keepdims=True)
            centered = values - mean
            inverse = lax.rsqrt(jnp.mean(centered * centered, axis=-1, keepdims=True) + eps)
            normed = centered * inverse
            mean_ref[at, :] = jnp.broadcast_to(mean, (32, 128))
            inv_ref[at, :] = jnp.broadcast_to(inverse, (32, 128))
            attn[at, :] = (normed * gain_ref[0:1, :].astype(full) + shift_ref[0:1, :].astype(full)).astype(low)
            mlp[at, :] = (normed * gain_ref[1:2, :].astype(full) + shift_ref[1:2, :].astype(full)).astype(low)
            return carry
        lax.fori_loop(0, own_rows // 32, chunk, 0)

    def absorb(step):
        for way in (0, 1):
            @pl.when(tokens.receives(way, step - 1))
            def _():
                at = tokens.place(tokens.owner(way, step))
                c = load(tok_all.at[at], tok.at[at], way)
                c.wait()
                begin = tokens.owner(way, step) * own_rows
                normalize(tok, begin, begin)

    def table(i, carry):
        at = pl.ds(pl.multiple_of(i * 64, 64), 64)
        lanes = lax.broadcasted_iota(jnp.int32, (64, 128), 1)
        position = i * 64 + lax.broadcasted_iota(jnp.int32, (64, 128), 0)
        angle = position.astype(full) * freq_ref[...]
        cos_ref[at, :] = jnp.where(lanes < ROT, jnp.cos(angle), 1.0)
        sine = jnp.sin(angle)
        sin_ref[at, :] = jnp.where(lanes < ROT, jnp.where(lanes < ROT // 2, -sine, sine), 0.0)
        return carry

    normalize(tok_ref, 0, sp * own_rows)
    lax.fori_loop(0, seq // 64, table, 0)
    for step in range(1, sp_size):
        for part in range(3):
            slab_copy(step, part, sp, lax.rem(sp + sp_size - step, sp_size)).wait_recv()
    for c in keeps[:3]:
        c.wait()
    own(QKV)

    @pl.when(pair == sp)
    def _():
        c = pltpu.make_async_copy(out_ref, out_all.at[turned(dp)], keep_sem.at[7])
        c.start()
        c.wait()

    @pl.when(pair != sp)
    def _():
        turn_copy(dp).wait_recv()

    own(OUT)
    onward(UP)
    tokens.relay(1)
    onward(QKV)
    onward(OUT)
    own(DOWN)
    tokens.settle(1)
    absorb(1)
    tokens.relay(2)
    cotangents.begin()
    corner(UP)
    complete(UP)
    for c in keeps[3:]:
        c.wait()
    up_load = load(up_all, up_w, 2)
    tokens.settle(2)
    absorb(2)
    corner(QKV)
    corner(OUT)
    complete(QKV)
    qkv_load = load(qkv_all, qkv_w, 3)
    complete(OUT)
    onward(DOWN)
    tokens.settle(3)
    absorb(3)
    stores = [pltpu.make_async_copy(attn, attn_out, store_sem.at[0]), pltpu.make_async_copy(mlp, mlp_out, store_sem.at[1])]
    for c in stores:
        c.start()
    qkv_load.wait()

    def head(h, carry):
        lanes = pl.ds(pl.multiple_of(h * HEAD, HEAD), HEAD)

        def project(r, carry):
            at = pl.ds(pl.multiple_of(r * band, band), band)
            cos_t, sin_t = cos_ref[at, :], sin_ref[at, :]
            for part, target in enumerate((q_ref, k_ref, v_ref)):
                cols = pl.ds(pl.multiple_of(part * width + h * HEAD, HEAD), HEAD)
                bias_cols = pl.ds(pl.multiple_of(sp * width + h * HEAD, HEAD), HEAD)
                value = jnp.dot(attn[at, :], qkv_w[:, cols], preferred_element_type=full)
                value = value + qkv_bias_ref[part:part + 1, bias_cols].astype(full)
                if part < 2:
                    value = turn(value, cos_t, sin_t)
                target[at, lanes] = value.astype(low)
            return carry
        lax.fori_loop(0, seq // band, project, 0)
        for begin in range(0, seq, band):
            end = begin + band
            p = weights_of(q_ref[begin:end, lanes], k_ref[:end, lanes], begin, len_ref[0], scale)
            ctx_ref[begin:end, lanes] = jnp.dot(p.astype(low), v_ref[:end, lanes], preferred_element_type=full).astype(low)
        return carry

    lax.fori_loop(0, width // HEAD, head, 0)
    corner(DOWN)
    cotangents.relay(1)
    up_load.wait()

    def pre_store(block, slot):
        return pltpu.make_async_copy(pre.at[slot], pre_out.at[:, pl.ds(pl.multiple_of(block * units, units), units)],
                                     pre_sem.at[slot])

    def unit_block(block, carry):
        slot = lax.rem(block, 2)

        @pl.when(block >= 2)
        def _():
            pre_store(block - 2, slot).wait()

        of = pl.ds(pl.multiple_of(block * units, units), units)
        bias_of = pl.ds(pl.multiple_of((block * sp_size + sp) * units, units), units)

        def row_band(r, carry):
            at = pl.ds(pl.multiple_of(r * band, band), band)
            value = lax.dot_general(mlp[at, :], up_w[of, :], (((1,), (1,)), ((), ())), preferred_element_type=full)
            value = value + unit_bias_ref[:, bias_of].astype(full)
            pre[slot, at, :] = value
            hidden[at, of] = gelu_value(value).astype(low)
            return carry
        lax.fori_loop(0, seq // band, row_band, 0)
        pre_store(block, slot).start()
        return carry

    blocks = up_w.shape[0] // units
    lax.fori_loop(0, blocks // 2, unit_block, 0)
    complete(DOWN)
    half = up_w.shape[0] // 2
    stores[0].wait()
    late = [load(down_all.at[pl.ds(0, half)], tok, 0), load(down_all.at[pl.ds(half, half)], attn, 1)]
    lax.fori_loop(blocks // 2, blocks, unit_block, 0)
    out_rows = out_all.shape[0]
    late.append(load(out_all, up_w.at[pl.ds(0, out_rows)], 2))
    cotangents.relay(2)
    for block in (blocks - 2, blocks - 1):
        pre_store(block, block % 2).wait()
    stores[1].wait()
    hidden_store = pltpu.make_async_copy(hidden, hidden_out, store_sem.at[0])
    hidden_store.start()
    for c in late:
        c.wait()

    bands = seq // band
    upper = 2 * sp // sp_size

    def band_rows(r):
        return pl.ds(pl.multiple_of(((1 - upper) * (bands - 1 - r) + upper * r) * band, band), band)

    def part_store(r):
        return pltpu.make_async_copy(mlp.at[band_rows(r)], part_out.at[band_rows(r)], part_sem.at[r])

    def part_hop(way):
        to = lax.rem(sp + (1 if way == 0 else sp_size - 1), sp_size)
        return remote_copy(mlp.at[band_rows(0)], part_in.at[way], hop_send.at[way], hop_recv.at[way], (dp, to))

    def along(way):
        return sp if way == 0 else sp_size - 1 - sp

    def out_band(r, carry):
        at = band_rows(r)

        def out_columns(c, carry):
            to = pl.ds(pl.multiple_of(c * band, band), band)
            total = jnp.dot(hidden[at, :half], tok[:, to], preferred_element_type=full)
            total = total + jnp.dot(hidden[at, half:], attn[:, to], preferred_element_type=full)
            total = total + jnp.dot(ctx_ref[at, :], up_w[:out_rows, to], preferred_element_type=full)
            mlp[at, to] = total.astype(low)
            return carry
        lax.fori_loop(0, wide // band, out_columns, 0)
        part_store(r).start()
        return carry
    out_band(0, 0)
    for way in (0, 1):
        @pl.when(along(way) == 0)
        def _():
            part_hop(way).start()
    lax.fori_loop(1, bands, out_band, 0)

    for step in (1, 2):
        cotangents.settle(step)
    unit_ref[...] = jnp.zeros_like(unit_ref)
    early = NEAR

    def near_rows(n):
        return pl.ds(pl.multiple_of((upper * (bands - NEAR) + n) * band, band), band)

    def slope_room(block):
        return pre.at[block // 4, pl.ds(pl.multiple_of(lax.rem(block, 4) * band, band), band)]

    def slope_load(n, block):
        return pltpu.make_async_copy(
            pre_out.at[near_rows(n), pl.ds(pl.multiple_of(block * units, units), units)], slope_room(block), slope_sem.at[block])

    def cot_load(n):
        return pltpu.make_async_copy(cot_all.at[near_rows(n)], cot.at[lax.rem(n, 2)], gpre_sem.at[2 + lax.rem(n, 2)])

    def gpre_store(n):
        return pltpu.make_async_copy(gpre.at[lax.rem(n, 2)], gpre_out.at[near_rows(n)], gpre_sem.at[lax.rem(n, 2)])

    def first_loads(block, carry):
        slope_load(0, block).start()
        return carry
    lax.fori_loop(0, blocks, first_loads, 0)
    cot_load(0).start()

    def near_band(n, carry):
        slot = lax.rem(n, 2)
        cot_load(n).wait()

        @pl.when(n + 1 < early)
        def _():
            cot_load(n + 1).start()

        def mask(i, carry):
            at = pl.ds(pl.multiple_of(i * 32, 32), 32)
            row = (upper * (bands - NEAR) + n) * band + i * 32 + lax.broadcasted_iota(jnp.int32, (32, wide), 0)
            cot[slot, at, :] = jnp.where(row < len_ref[0], cot[slot, at, :].astype(full), 0.0).astype(low)
            return carry
        lax.fori_loop(0, band // 32, mask, 0)

        @pl.when(n >= 2)
        def _():
            gpre_store(n - 2).wait()

        for side, room in enumerate((tok, attn)):
            def unit_part(k, carry):
                block = side * (blocks // 2) + k
                slope_load(n, block).wait()
                of = pl.ds(pl.multiple_of(block * units, units), units)
                value = lax.dot_general(cot[slot], room[pl.ds(pl.multiple_of(k * units, units), units), :],
                                        (((1,), (1,)), ((), ())), preferred_element_type=full)
                value = (value * gelu_slope(slope_room(block)[...])).astype(low)
                gpre[slot, :, of] = value
                unit_ref[:, of] += jnp.sum(value.astype(full), axis=0, keepdims=True)

                @pl.when(n + 1 < early)
                def _():
                    slope_load(n + 1, block).start()
                return carry
            lax.fori_loop(0, blocks // 2, unit_part, 0)
        gpre_store(n).start()
        return carry
    lax.fori_loop(0, early, near_band, 0)
    for n in range(max(early - 2, 0), early):
        gpre_store(n).wait()
    for r in range(seq // band):
        part_store(r).wait()
    hidden_store.wait()
    for index in range(4):
        for message in range(7):
            copy(index, message, *sends[message]).wait_send()
    for step in range(1, sp_size):
        for part in range(3):
            slab_copy(step, part, lax.rem(sp + step, sp_size), sp).wait_send()

    @pl.when(pair != sp)
    def _():
        turn_copy(turn_dp).wait_send()

    tokens.finish()
    cotangents.settle(3)
    cotangents.finish()
    for way in (0, 1):
        @pl.when(along(way) == 0)
        def _():
            part_hop(way).wait_send()

        @pl.when(along(way) == 1)
        def _():
            part_hop(way).wait_recv()


def front(sp_size, dp_size, lengths, qkv_weight, out_weight, up_weight, down_weight, tokens, cotangent, gains, shifts, qkv_bias,
          unit_bias):
    rows, wide = out_weight.shape
    units = up_weight.shape[0]
    seq = tokens.shape[0] * sp_size
    width = wide // sp_size
    all_units = units * dp_size
    full, low = jnp.float32, jnp.bfloat16
    half = ROT // 2
    freq = base_freq ** (-jnp.arange(half, dtype=full) * (2.0 / ROT))
    freq = jnp.concatenate([freq, freq, jnp.zeros((128 - ROT,), full)])[None]
    hbm = pl.BlockSpec(memory_space=pltpu.HBM)
    vmem = pl.BlockSpec(memory_space=pltpu.VMEM)
    dma = pltpu.SemaphoreType.DMA
    shape = jax.ShapeDtypeStruct
    qkv_shape = (rows * sp_size * dp_size, 3 * width)
    return pl.pallas_call(
        functools.partial(front_kernel, sp_size),
        out_shape=[shape(qkv_shape, low), shape((rows * dp_size, wide), low), shape((all_units, wide), low),
                   shape((all_units, wide), low), shape((seq, wide), low), shape((seq, wide), low),
                   shape((seq, wide), low), shape((seq, wide), low), shape((seq, all_units), low), shape((seq, all_units), full),
                   shape((seq, wide), low), shape((2, seq // sp_size, wide), low), shape((seq, all_units), low)]
        + [shape((seq, 128), full)] * 4 + [shape((1, all_units), full)] + [shape((seq, width), low)] * 4,
        in_specs=[pl.BlockSpec(memory_space=pltpu.SMEM)] + [vmem] * 11,
        out_specs=[hbm] * 13 + [vmem] * 9,
        scratch_shapes=[pltpu.VMEM((seq, wide), low)] * 3 + [
            pltpu.VMEM(qkv_shape, low), pltpu.VMEM((all_units, wide), low),
            pltpu.VMEM((seq, all_units), low), pltpu.VMEM((2, seq, units), full),
            pltpu.VMEM((2, 256, wide), low), pltpu.VMEM((2, 256, all_units), low),
            dma((4, 7)), dma((4, 7)), dma((sp_size - 1, 3)), dma((sp_size - 1, 3)), dma((8,)), dma, dma,
            dma((2, sp_size)), dma((2, sp_size)), dma((2, sp_size)), dma((2, sp_size)),
            dma((4,)), dma((2,)), dma((2,)), dma((seq // 256,)), dma((2,)), dma((2,)), dma((all_units // units,)), dma((4,))],
        compiler_params=pltpu.CompilerParams(collective_id=0, has_side_effects=True, vmem_limit_bytes=62 << 20),
        cost_estimate=pl.CostEstimate(flops=26 * 10 ** 9, bytes_accessed=300 * 1000 * 1000, transcendentals=0),
        name="front",
    )(lengths, qkv_weight, out_weight, up_weight, down_weight, tokens, cotangent, freq, gains, shifts, qkv_bias, unit_bias)

CHUNK = 512


def add_into(target, *others):
    step_rows = 32

    def step(i, carry):
        at = pl.ds(pl.multiple_of(i * step_rows, step_rows), step_rows)
        total = target[at, :].astype(jnp.float32)
        for other in others:
            total = total + other[at, :].astype(jnp.float32)
        target[at, :] = total.astype(jnp.bfloat16)
        return carry

    lax.fori_loop(0, target.shape[0] // step_rows, step, 0)


class Square:
    def __init__(self, sp_size, lent, sib_send, sib_recv, one_send, one_recv, two_send, two_recv):
        self.dp, self.sp, self.sp_size = lax.axis_index("dp"), lax.axis_index("sp"), sp_size
        self.core, self.chip = self.dp % 2, self.dp // 2
        self.x, self.y = self.chip % 2, self.chip // 2
        self.sibling = self.dp + 1 - 2 * self.core
        self.across_x, self.across_y = self.dp + 2 - 4 * self.x, self.dp + 4 - 8 * self.y
        self.first = self.across_y * (1 - self.core) + self.across_x * self.core
        self.second = self.across_x * (1 - self.core) + self.across_y * self.core
        self.second_mask = 1 + self.core
        self.lent = lent
        self.sib_send, self.sib_recv, self.one_send, self.one_recv, self.two_send, self.two_recv = (
            sib_send, sib_recv, one_send, one_recv, two_send, two_recv)

    def chip_of(self, mask):
        return lax.rem(self.x + lax.rem(mask, 2), 2) + 2 * lax.rem(self.y + mask // 2, 2)

    def greet(self, barrier):
        for other in (self.first, self.second, self.sibling):
            pl.semaphore_signal(barrier, inc=1, device_id=(other, self.sp), device_id_type=MESH)
        for step in range(1, self.sp_size):
            pl.semaphore_signal(
                barrier, inc=1, device_id=(self.dp, lax.rem(self.sp + step, self.sp_size)), device_id_type=MESH)


def remote(source, target, send, recv, device):
    return pltpu.make_async_remote_copy(
        src_ref=source, dst_ref=target, send_sem=send, recv_sem=recv, device_id=device, device_id_type=MESH)


class Wide:
    def __init__(self, place, index, left, right, width, sums, sib, one, two):
        self.place, self.index, self.left, self.right, self.width = place, index, left, right, width
        self.sums, self.sib, self.one, self.two = sums, sib, one, two
        self.units = sums.shape[1]

    def product(self, block, store):
        at = pl.ds(pl.multiple_of(block * self.units, self.units), self.units)

        def columns(part, carry):
            to = pl.ds(pl.multiple_of(part * CHUNK, CHUNK), CHUNK)
            store(to, lax.dot_general(
                self.left[:, at], self.right[:, to], (((0,), (0,)), ((), ())),
                preferred_element_type=jnp.float32))
            return carry
        lax.fori_loop(0, self.width // CHUNK, columns, 0)

    def sib_copy(self, slot):
        p = self.place
        return remote(p.lent.at[slot, :, :self.width], self.sib.at[p.chip_of(3 - slot), :, :self.width],
                      p.sib_send.at[self.index, slot], p.sib_recv.at[self.index, slot], (p.sibling, p.sp))

    def for_sibling(self, previous):
        p = self.place

        def step(slot, carry):
            if previous is not None:
                previous.sib_copy(slot).wait_send()

            def store(to, total):
                p.lent[slot, :, to] = total.astype(jnp.bfloat16)
            self.product(p.chip_of(3 - slot) * 2 + 1 - p.core, store)
            self.sib_copy(slot).start()
            return carry
        lax.fori_loop(0, 4, step, 0)

    def own(self, mask, slot):
        at = self.place.chip_of(mask)
        self.sib_copy(slot).wait_recv()

        def store(to, total):
            self.sums[mask, :, to] = (total + self.sib[at, :, to].astype(jnp.float32)).astype(jnp.bfloat16)
        self.product(at * 2 + self.place.core, store)

    def for_self(self):
        core = self.place.core

        def leave(slot, carry):
            mask = 3 - slot * (1 + core)
            self.own(mask, 3 - mask)
            self.first_copy(slot).start()
            return carry
        lax.fori_loop(0, 2, leave, 0)

        def stay(slot, carry):
            mask = self.place.second_mask * (1 - slot)
            self.own(mask, 3 - mask)
            return carry
        lax.fori_loop(0, 2, stay, 0)

    def block(self, mask):
        return self.sums.at[mask, :, :self.width]

    def from_first(self, slot):
        return self.one.at[slot, :, :self.width]

    def from_second(self):
        return self.two.at[:, :self.width]

    def first_copy(self, slot):
        p = self.place
        return remote(self.block(3 - slot * (1 + p.core)), self.from_first(slot), p.one_send.at[self.index, slot],
                      p.one_recv.at[self.index, slot], (p.first, p.sp))

    def second_copy(self):
        p = self.place
        return remote(self.block(p.second_mask), self.from_second(), p.two_send.at[self.index],
                      p.two_recv.at[self.index], (p.second, p.sp))

    def onward(self):
        self.first_copy(0).wait_recv()
        add_into(self.block(self.place.second_mask), self.from_first(0))
        self.second_copy().start()

    def finish(self):
        self.first_copy(1).wait_recv()
        self.second_copy().wait_recv()
        add_into(self.block(0), self.from_first(1), self.from_second())

    def drain(self):
        for slot in (0, 1):
            self.first_copy(slot).wait_send()
        self.second_copy().wait_send()


class Dense(Wide):
    def __init__(self, place, index, left, right, width, sums, sib, one, two, part):
        self.place, self.index, self.left, self.right, self.width = place, index, left, right, width
        self.sums, self.sib, self.one, self.two, self.part = sums, sib, one, two, part
        self.units, self.rows = sums.shape[0], one.shape[1]

    def sib_copy(self, slot):
        p = self.place
        return remote(self.part, self.sib, p.sib_send.at[self.index, 0], p.sib_recv.at[self.index, 0], (p.sibling, p.sp))

    def for_sibling(self, previous):
        def store(to, total):
            self.part[:, to] = total.astype(jnp.bfloat16)
        self.product(1 - self.place.core, store)
        self.sib_copy(0).start()

    def for_self(self):
        self.sib_copy(0).wait_recv()

        def store(to, total):
            self.sums[:, to] = (total + self.sib[:, to].astype(jnp.float32)).astype(jnp.bfloat16)
        self.product(self.place.core, store)
        for slot in (0, 1):
            self.first_copy(slot).start()

    def block(self, mask):
        return self.sums.at[pl.ds(pl.multiple_of(self.place.chip_of(mask) * self.rows, self.rows), self.rows)]


class Fold:
    def __init__(self, place, source, inbox, stage, stage_sem, send, recv, begun=1):
        self.begun = begun
        self.place, self.source, self.inbox, self.stage = place, source, inbox, stage
        self.stage_sem, self.send, self.recv = stage_sem, send, recv
        self.rows = stage.shape[0]

    def along(self, way):
        last = self.place.sp_size - 1
        return self.place.sp if way == 0 else last - self.place.sp

    def rows_of(self, way, step):
        count = self.place.sp_size
        owner = self.along(way) + count - step
        owner = owner if way == 0 else count - 1 - owner
        return self.source.at[pl.ds(pl.multiple_of(owner * self.rows, self.rows), self.rows)]

    def copy(self, way, step, own):
        p = self.place
        to = lax.rem(p.sp + (1 if way == 0 else p.sp_size - 1), p.sp_size)
        source = self.rows_of(way, step) if own else self.inbox.at[way, max(step - 2, 0)]
        return remote(source, self.inbox.at[way, step - 1], self.send.at[way, step - 1],
                      self.recv.at[way, step - 1], (p.dp, to))

    def take(self, rows):
        c = pltpu.make_async_copy(rows, self.stage, self.stage_sem)
        c.start()
        c.wait()

    def step(self, step):
        last = self.place.sp_size - 1
        for way in (0, 1):
            if step >= self.begun:
                @pl.when(self.along(way) == 0)
                def _():
                    self.copy(way, step, True).start()

            if step > 1:
                @pl.when((self.along(way) > 0) & (self.along(way) < step) & (self.along(way) < last))
                def _():
                    self.take(self.rows_of(way, step))
                    if step > self.begun:
                        self.copy(way, step - 1, False).wait_recv()
                    add_into(self.inbox.at[way, step - 2], self.stage)
                    self.copy(way, step, False).start()

    def finish(self):
        last = self.place.sp_size - 1
        self.take(self.source.at[pl.ds(pl.multiple_of(self.place.sp * self.rows, self.rows), self.rows)])
        for way in (0, 1):
            @pl.when(self.along(way) > 0)
            def _():
                self.copy(way, last, False).wait_recv()
                add_into(self.stage, self.inbox.at[way, last - 1])

    def drain(self):
        last = self.place.sp_size - 1
        for way in (0, 1):
            for step in range(1, last + 1):
                if step >= self.begun:
                    @pl.when(self.along(way) == 0)
                    def _():
                        self.copy(way, step, True).wait_send()

                if step > 1:
                    @pl.when((self.along(way) > 0) & (self.along(way) < step) & (self.along(way) < last))
                    def _():
                        self.copy(way, step, False).wait_send()


def middle_kernel(sp_size, len_ref, cot_hbm, out_hbm, q_hbm, k_hbm, v_hbm, pre_hbm, hidden_hbm, down_hbm, up_hbm, qkv_hbm,
                  tok_hbm, part_hbm, hop_hbm, near_hbm, attn_hbm, unit_ref, gain_ref, cos_ref, sin_ref, mean_s, inv_s,
                  down_out, slab_out, gpre_out, hat_out, hat_in, proj_out, gout_out, red_out, small_ref,
                  cot, left, tok, gpre, up_w, qkv_w, pre, gctx, gproj, dq, dk, dv,
                  lent, down_sum, down_sib, down_one, down_two, inbox, stage,
                  load_sem, stream_sem, store_sem, stage_sem, sib_send, sib_recv, one_send, one_recv, two_send, two_recv,
                  fold_send, fold_recv, hat_send, hat_recv, sib_free, one_free, two_free, near_sem, tok_sem):
    full, low = jnp.float32, jnp.bfloat16
    place = Square(sp_size, lent, sib_send, sib_recv, one_send, one_recv, two_send, two_recv)
    seq, wide = cot.shape
    width = gctx.shape[1]
    heads = width // HEAD
    units = down_sum.shape[1]
    blocks = up_w.shape[0] // units
    out_rows = out_hbm.shape[0]
    band = 256
    bands = seq // band
    scale = HEAD ** -0.5

    def load(source, target, which):
        c = pltpu.make_async_copy(source, target, load_sem.at[which])
        c.start()
        return c

    early = [load(cot_hbm, cot, 0), load(hidden_hbm, left, 1)]

    def down_load(block, slot):
        return pltpu.make_async_copy(
            down_hbm.at[pl.ds(pl.multiple_of(block * units, units), units)],
            up_w.at[pl.ds(pl.multiple_of(out_rows + slot * units, units), units)], stream_sem.at[0, slot])

    upper = 2 * place.sp // sp_size

    def hat_rows(r):
        return pl.ds(pl.multiple_of(((1 - upper) * (bands - 1 - r) + upper * r) * band, band), band)

    far = bands - NEAR
    near = pl.ds(pl.multiple_of(upper * far * band, band), NEAR * band)
    far_rows = pl.ds(pl.multiple_of((1 - upper) * NEAR * band, band), far * band)
    near_load = pltpu.make_async_copy(near_hbm.at[near], gpre.at[near], near_sem)

    def pre_load(block, slot):
        return pltpu.make_async_copy(
            pre_hbm.at[far_rows, pl.ds(pl.multiple_of(block * units, units), units)], pre.at[slot], stream_sem.at[1, slot])

    hops = []
    for way in (0, 1):
        hops.append(load(hop_hbm.at[way], inbox.at[way, 0], 6 + way))

    barrier = pltpu.get_barrier_semaphore()
    place.greet(barrier)
    pl.semaphore_wait(barrier, 2 + sp_size)
    fold = Fold(place, part_hbm, inbox, stage, stage_sem, fold_send, fold_recv, begun=2)
    for way in (0, 1):
        hops[way].wait()
    fold.step(2)
    early.append(load(out_hbm, up_w.at[pl.ds(0, out_rows)], 2))
    for i, source in enumerate((q_hbm, k_hbm, v_hbm)):
        early.append(load(source, qkv_w.at[pl.ds(0, seq), pl.ds(i * width, width)], 3 + i))
    for slot in (0, 1):
        down_load(slot, slot).start()
        pre_load(slot, slot).start()
    small_ref[...] = jnp.zeros_like(small_ref)
    gain_row, shift_row, bias_row, unit_row = 0, 2, 4, 7
    per_row = wide // (sp_size * units)
    last_row = unit_row + blocks // per_row

    early[0].wait()

    def mask_rows(i, carry):
        at = pl.ds(pl.multiple_of(i * 32, 32), 32)
        row = i * 32 + lax.broadcasted_iota(jnp.int32, (32, wide), 0)
        cot[at, :] = jnp.where(row < len_ref[0], cot[at, :].astype(full), 0.0).astype(low)
        return carry
    lax.fori_loop(0, seq // 32, mask_rows, 0)
    stores = [pltpu.make_async_copy(cot, gout_out, store_sem.at[0])]
    stores[0].start()

    def own_rows(i, carry):
        at = pl.ds(pl.multiple_of(place.sp * (seq // sp_size) + i * 32, 32), 32)
        return carry + jnp.sum(cot[at, :].astype(full), axis=0, keepdims=True)
    small_ref[last_row:last_row + 1, :] = lax.fori_loop(0, seq // sp_size // 32, own_rows, jnp.zeros((1, wide), full))

    down = Wide(place, 0, left, cot, wide, down_sum, down_sib, down_one, down_two)
    early[1].wait()
    down.for_sibling(None)
    down.for_self()
    early[2].wait()

    def context_band(r, carry):
        at = pl.ds(pl.multiple_of(r * band, band), band)
        gctx[at, :] = lax.dot_general(
            cot[at, :], up_w[:out_rows, :], (((1,), (1,)), ((), ())), preferred_element_type=full).astype(low)
        return carry
    lax.fori_loop(0, bands, context_band, 0)
    attn_load = load(attn_hbm, left, 1)
    near_load.start()
    late_rows = pl.ds(out_rows + 2 * units, up_w.shape[0] - out_rows - 2 * units)
    up_load = load(up_hbm.at[late_rows], up_w.at[late_rows], 8)
    pl.semaphore_signal(sib_free, inc=1, device_id=(place.sibling, place.sp), device_id_type=MESH)
    for c in early[3:]:
        c.wait()

    def head(h, carry):
        lanes = pl.ds(pl.multiple_of(h * HEAD, HEAD), HEAD)
        k_lanes = pl.ds(pl.multiple_of(width + h * HEAD, HEAD), HEAD)
        v_lanes = pl.ds(pl.multiple_of(2 * width + h * HEAD, HEAD), HEAD)
        dk[...] = jnp.zeros_like(dk)
        dv[...] = jnp.zeros_like(dv)
        for begin in range(0, seq, band):
            end = begin + band
            q, g = qkv_w[begin:end, lanes], gctx[begin:end, lanes]
            k, v = qkv_w[:end, k_lanes], qkv_w[:end, v_lanes]
            p = weights_of(q, k, begin, len_ref[0], scale)
            gp = lax.dot_general(g, v, (((1,), (1,)), ((), ())), preferred_element_type=full)
            ds = (p * (gp - jnp.sum(p * gp, axis=-1, keepdims=True))).astype(low)
            dq[begin:end, :] = jnp.dot(ds, k, preferred_element_type=full) * scale
            dk[:end, :] += lax.dot_general(ds, q, (((0,), (0,)), ((), ())), preferred_element_type=full)
            dv[:end, :] += lax.dot_general(p.astype(low), g, (((0,), (0,)), ((), ())), preferred_element_type=full)

        def back(r, sums):
            at = pl.ds(pl.multiple_of(r * band, band), band)
            cos_t, sin_t = cos_ref[at, :], -sin_ref[at, :]
            pieces = (turn(dq[at, :].astype(low).astype(full), cos_t, sin_t).astype(low),
                      turn((dk[at, :] * scale).astype(low).astype(full), cos_t, sin_t).astype(low),
                      dv[at, :].astype(low))
            out = []
            for part, (piece, total) in enumerate(zip(pieces, sums)):
                gproj[at, pl.ds(pl.multiple_of(part * width + h * HEAD, HEAD), HEAD)] = piece
                out.append(total + jnp.sum(piece.astype(full), axis=0, keepdims=True))
            return tuple(out)
        sums = lax.fori_loop(0, bands, back, (jnp.zeros((1, HEAD), full),) * 3)
        for part, total in enumerate(sums):
            small_ref[bias_row + part:bias_row + part + 1,
                      pl.ds(pl.multiple_of(place.sp * width + h * HEAD, HEAD), HEAD)] = total
        return carry
    lax.fori_loop(0, heads, head, 0)
    stores.append(pltpu.make_async_copy(gproj, proj_out, store_sem.at[1]))
    stores[1].start()
    qkv_load = load(qkv_hbm, qkv_w, 3)

    def unit_block(block, carry):
        slot = lax.rem(block, 2)
        down_load(block, slot).wait()
        pre_load(block, slot).wait()
        of = pl.ds(pl.multiple_of(block * units, units), units)
        room = pl.ds(pl.multiple_of(out_rows + slot * units, units), units)

        def far_band(r, total):
            at = pl.ds(pl.multiple_of(((1 - upper) * NEAR + r) * band, band), band)
            value = lax.dot_general(cot[at, :], up_w[room, :], (((1,), (1,)), ((), ())), preferred_element_type=full)
            value = (value * gelu_slope(pre[slot, pl.ds(pl.multiple_of(r * band, band), band), :])).astype(low)
            gpre[at, of] = value
            return total + jnp.sum(value.astype(full), axis=0, keepdims=True)
        small_ref[pl.ds(unit_row + block // per_row, 1),
                  pl.ds(pl.multiple_of((lax.rem(block, per_row) * sp_size + place.sp) * units, units), units)] = (
            lax.fori_loop(0, far, far_band, unit_ref[:, of]))

        @pl.when(block + 2 < blocks)
        def _():
            down_load(block + 2, slot).start()
            pre_load(block + 2, slot).start()
        return carry

    down.onward()
    fold.step(3)
    lax.fori_loop(0, blocks, unit_block, 0)
    used = out_rows + 2 * units
    up_loads = [load(up_hbm.at[pl.ds(0, used)], up_w.at[pl.ds(0, used)], 0), up_load]

    def tok_load(r):
        return pltpu.make_async_copy(tok_hbm.at[hat_rows(r)], tok.at[r % 2], tok_sem.at[r % 2])
    tok_load(0).start()
    tok_load(1).start()
    near_load.wait()
    gpre_store = pltpu.make_async_copy(gpre, gpre_out, store_sem.at[2])
    gpre_store.start()
    stores[0].wait()
    def hat_store(r):
        return pltpu.make_async_copy(cot.at[hat_rows(r)], hat_out.at[hat_rows(r)], store_sem.at[3 + r])

    def hat_hop(way):
        to = lax.rem(place.sp + (1 if way == 0 else sp_size - 1), sp_size)
        return remote(cot.at[hat_rows(0)], hat_in.at[way], hat_send.at[way], hat_recv.at[way], (place.dp, to))

    def hat_band(r):
        at = hat_rows(r)
        tok_load(r).wait()

        def columns(c, carry):
            to = pl.ds(pl.multiple_of(c * band, band), band)
            from_mlp = jnp.dot(gpre[at, :], up_w[:, to], preferred_element_type=full)
            from_attn = lax.dot_general(gproj[at, :], qkv_w[to, :], (((1,), (1,)), ((), ())), preferred_element_type=full)
            normed = (tok[r % 2, :, to].astype(full) - mean_s[at, 0:1]) * inv_s[at, 0:1]
            small_ref[gain_row:gain_row + 1, to] += jnp.sum(from_attn * normed, axis=0, keepdims=True)
            small_ref[gain_row + 1:gain_row + 2, to] += jnp.sum(from_mlp * normed, axis=0, keepdims=True)
            small_ref[shift_row:shift_row + 1, to] += jnp.sum(from_attn, axis=0, keepdims=True)
            small_ref[shift_row + 1:shift_row + 2, to] += jnp.sum(from_mlp, axis=0, keepdims=True)
            cot[at, to] = (from_attn * gain_ref[0:1, to].astype(full) + from_mlp * gain_ref[1:2, to].astype(full)).astype(low)
            return carry
        lax.fori_loop(0, wide // band, columns, 0)
        hat_store(r).start()
        if r + 2 < bands:
            tok_load(r + 2).start()

    qkv = Wide(place, 1, left, gproj, 3 * width, down_sum, down_sib, down_one, down_two)
    attn_load.wait()
    pl.semaphore_wait(sib_free, 1)
    qkv.for_sibling(down)
    qkv_load.wait()
    for c in up_loads:
        c.wait()
    hat_band(0)
    for way in (0, 1):
        @pl.when(fold.along(way) == 0)
        def _():
            hat_hop(way).start()
    down.finish()
    stores.append(pltpu.make_async_copy(down.block(0), down_out, store_sem.at[3 + bands]))
    stores[2].start()
    pl.semaphore_signal(one_free, inc=1, device_id=(place.first, place.sp), device_id_type=MESH)
    pl.semaphore_signal(two_free, inc=1, device_id=(place.second, place.sp), device_id_type=MESH)
    down.drain()
    stores[2].wait()
    pl.semaphore_wait(one_free, 1)
    qkv.for_self()
    hat_band(1)
    pl.semaphore_wait(two_free, 1)
    qkv.onward()
    for r in range(2, bands):
        hat_band(r)
    fold.finish()
    stores.append(pltpu.make_async_copy(stage, red_out, store_sem.at[4 + bands]))
    stores[-1].start()
    qkv.finish()
    stores.append(pltpu.make_async_copy(qkv.block(0), slab_out, store_sem.at[5 + bands]))
    stores[-1].start()
    for r in range(bands):
        hat_store(r).wait()
    for which in (1, 3, 4):
        stores[which].wait()
    gpre_store.wait()
    for slot in range(4):
        qkv.sib_copy(slot).wait_send()
    qkv.drain()
    fold.drain()
    for way in (0, 1):
        @pl.when(fold.along(way) == 0)
        def _():
            hat_hop(way).wait_send()

        @pl.when(fold.along(way) == 1)
        def _():
            hat_hop(way).wait_recv()


def middle(sp_size, dp_size, lengths, cotangent, out_own, queries, key_rows, values, pre_act, hidden, down_own, up_own, qkv_own,
           tokens, partial_out, part_hop, near_pre, attn_in, unit_sums, gains, cos_t, sin_t, means, inverses):
    seq, wide = tokens.shape
    width = queries.shape[1]
    units = up_own.shape[0] // dp_size
    own = seq // sp_size
    full, low = jnp.float32, jnp.bfloat16
    hbm = pl.BlockSpec(memory_space=pltpu.HBM)
    vmem = pl.BlockSpec(memory_space=pltpu.VMEM)
    dma = pltpu.SemaphoreType.DMA
    shape = jax.ShapeDtypeStruct

    def v(*dims, kind=low):
        return pltpu.VMEM(dims, kind)
    bands = seq // 256
    return pl.pallas_call(
        functools.partial(middle_kernel, sp_size),
        out_shape=[shape((units, wide), low), shape((units, 3 * width), low), shape(hidden.shape, low), shape((seq, wide), low),
                   shape((2, own, wide), low),
                   shape((seq, 3 * width), low),
                   shape((seq, wide), low), shape((own, wide), low), shape((16, wide), full)],
        in_specs=[pl.BlockSpec(memory_space=pltpu.SMEM)] + [hbm] * 15 + [vmem] * 6,
        out_specs=[hbm] * 8 + [vmem],
        scratch_shapes=[
            v(seq, wide), v(seq, wide), v(2, 256, wide), v(*hidden.shape), v(*up_own.shape), v(*qkv_own.shape),
            v(2, (seq // 256 - NEAR) * 256, units, kind=full),
            v(seq, width), v(seq, 3 * width), v(seq, HEAD, kind=full), v(seq, HEAD, kind=full), v(seq, HEAD, kind=full),
            v(4, units, wide), v(4, units, wide), v(4, units, wide), v(2, units, wide), v(units, wide),
            v(2, sp_size - 1, own, wide), v(own, wide),
            dma((9,)), dma((2, 2)), dma((7 + bands,)), dma, dma((2, 4)), dma((2, 4)), dma((2, 2)), dma((2, 2)), dma((2,)), dma((2,)),
            dma((2, sp_size - 1)), dma((2, sp_size - 1)), dma((2,)), dma((2,)),
            pltpu.SemaphoreType.REGULAR, pltpu.SemaphoreType.REGULAR, pltpu.SemaphoreType.REGULAR, dma, dma((2,))],
        compiler_params=pltpu.CompilerParams(collective_id=3, has_side_effects=True, vmem_limit_bytes=67043328),
        cost_estimate=pl.CostEstimate(flops=40 * 10 ** 9, bytes_accessed=90 * 1000 * 1000, transcendentals=0),
        name="middle",
    )(lengths, cotangent, out_own, queries, key_rows, values, pre_act, hidden, down_own, up_own, qkv_own, tokens, partial_out,
      part_hop, near_pre, attn_in, unit_sums, gains, cos_t, sin_t, means, inverses)


def back_kernel(sp_size, cot_hbm, pre_hbm, mlp_hbm, ctx_hbm, hat_hbm, hop_hbm, slab_hbm, small_ref,
                up_out, qkv_out, dense_out, red_out, small_out,
                left, right, cot, ctx, lent,
                up_sum, dense_sum, up_sib, dense_sib, up_one, dense_one, up_two, dense_two,
                dense_part, slab, small_acc, small_in, small_z, small_fin, inbox, stage,
                load_sem, store_sem, stage_sem, sib_send, sib_recv, one_send, one_recv, two_send, two_recv,
                slab_send, slab_recv, turn_send, turn_recv, small_send, small_recv, z_send, z_recv,
                fold_send, fold_recv, plane_send, plane_recv):
    place = Square(sp_size, lent, sib_send, sib_recv, one_send, one_recv, two_send, two_recv)
    dp, sp = place.dp, place.sp
    per = 2
    pair, lane = dp // per, dp % per
    turn_dp = sp * per + lane
    slab_width = slab.shape[1]
    head_width = slab_width // 3
    rows = dense_one.shape[1]
    wide = left.shape[1]

    def load(source, target, which):
        c = pltpu.make_async_copy(source, target, load_sem.at[which])
        c.start()
        return c

    slab_load = load(slab_hbm, slab, 0)
    hops = [load(hop_hbm.at[way], inbox.at[way, 0], 1 + way) for way in (0, 1)]
    loads = [load(ctx_hbm, ctx, 3), load(cot_hbm, cot, 4)]

    barrier = pltpu.get_barrier_semaphore()
    for step in range(1, 8):
        pl.semaphore_signal(barrier, inc=1, device_id=(lax.rem(dp + step, 8), sp), device_id_type=MESH)
    for step in range(1, sp_size):
        pl.semaphore_signal(barrier, inc=1, device_id=(dp, lax.rem(sp + step, sp_size)), device_id_type=MESH)

    @pl.when(pair != sp)
    def _():
        pl.semaphore_signal(barrier, inc=1, device_id=(turn_dp, pair), device_id_type=MESH)

    pl.semaphore_wait(barrier, 6 + sp_size + jnp.where(pair != sp, 1, 0))
    fold = Fold(place, hat_hbm, inbox, stage, stage_sem, fold_send, fold_recv, begun=2)

    def small_copy(stage_of):
        partner = (place.sibling, place.across_x, place.across_y)[stage_of]
        return remote(small_ref if stage_of == 0 else small_acc.at[stage_of - 1], small_in.at[stage_of],
                      small_send.at[stage_of], small_recv.at[stage_of], (partner, sp))

    def small_step(stage_of):
        small_copy(stage_of).wait_recv()
        before = small_ref[...] if stage_of == 0 else small_acc[stage_of - 1]
        small_acc[stage_of] = before + small_in[stage_of]

    share = small_ref.shape[1] // 8

    def columns_of(owner):
        return pl.ds(pl.multiple_of(owner * share, share), share)

    def z_copy(step):
        return remote(small_acc.at[2, :, columns_of(dp)], small_z.at[sp], z_send.at[step - 1], z_recv.at[step - 1],
                      (dp, lax.rem(sp + step, sp_size)))

    def z_arrival(step):
        origin = lax.rem(sp + sp_size - step, sp_size)
        return remote(small_acc.at[2, :, columns_of(dp)], small_z.at[origin], z_send.at[step - 1], z_recv.at[step - 1],
                      (dp, origin))

    def plane_copy(step, owner, target):
        at = small_fin.at[:, columns_of(owner)]
        return remote(at, at, plane_send.at[step - 1], plane_recv.at[step - 1], (target, sp))

    def turn_copy():
        return remote(dense.block(0), dense_out, turn_send, turn_recv, (turn_dp, pair))

    def slab_rows(owner):
        return pl.ds(pl.multiple_of(owner * rows, rows), rows)

    def slab_columns(part, owner):
        return pl.ds(pl.multiple_of(part * wide + owner * head_width, head_width), head_width)

    def slab_copy(step, part, origin, there):
        return remote(slab.at[slab_rows(there), pl.ds(part * head_width, head_width)],
                      qkv_out.at[:, slab_columns(part, origin)],
                      slab_send.at[step - 1, part], slab_recv.at[step - 1, part], (dp, there))

    stores = []

    def store(source, target):
        c = pltpu.make_async_copy(source, target, store_sem.at[len(stores)])
        c.start()
        stores.append(c)

    small_copy(0).start()
    dense = Dense(place, 0, ctx, cot, wide, dense_sum, dense_sib, dense_one, dense_two, dense_part)
    up = Wide(place, 1, left, right, wide, up_sum, up_sib, up_one, up_two)
    for way in (0, 1):
        hops[way].wait()
    fold.step(2)
    slab_load.wait()
    for step in range(1, sp_size):
        for part in range(3):
            slab_copy(step, part, sp, lax.rem(sp + step, sp_size)).start()
    for part in range(3):
        store(slab.at[slab_rows(sp), pl.ds(part * head_width, head_width)], qkv_out.at[:, slab_columns(part, sp)])
    loads += [load(pre_hbm, left, 5), load(mlp_hbm, right, 6)]
    small_step(0)
    small_copy(1).start()
    loads[0].wait()
    loads[1].wait()
    dense.for_sibling(None)
    dense.for_self()
    loads[2].wait()
    loads[3].wait()
    up.for_sibling(None)
    small_step(1)
    small_copy(2).start()
    dense.onward()
    up.for_self()
    small_step(2)
    for step in range(1, sp_size):
        z_copy(step).start()
    small_z[sp] = small_acc[2, :, columns_of(dp)]
    dense.finish()

    @pl.when(pair != sp)
    def _():
        turn_copy().start()

    @pl.when(pair == sp)
    def _():
        c = pltpu.make_async_copy(dense.block(0), dense_out, store_sem.at[5])
        c.start()
        c.wait()

    fold.step(3)
    up.onward()
    for step in range(1, sp_size):
        z_arrival(step).wait_recv()
    total = small_z[0]
    for origin in range(1, sp_size):
        total = total + small_z[origin]
    small_fin[:, columns_of(dp)] = total
    for step in range(1, 8):
        plane_copy(step, dp, lax.rem(dp + step, 8)).start()
    up.finish()
    store(up.block(0), up_out)
    fold.finish()
    store(stage, red_out)
    for slot in range(4):
        up.sib_copy(slot).wait_send()
    dense.sib_copy(0).wait_send()
    for array in (dense, up):
        array.drain()
    for stage_of in range(3):
        small_copy(stage_of).wait_send()
    fold.drain()
    for step in range(1, sp_size):
        z_copy(step).wait_send()
        for part in range(3):
            slab_copy(step, part, lax.rem(sp + sp_size - step, sp_size), sp).wait_recv()
            slab_copy(step, part, sp, lax.rem(sp + step, sp_size)).wait_send()

    @pl.when(pair != sp)
    def _():
        turn_copy().wait_recv()
        turn_copy().wait_send()

    for step in range(1, 8):
        origin = lax.rem(dp + 8 - step, 8)
        plane_copy(step, origin, origin).wait_recv()
        plane_copy(step, dp, origin).wait_send()
    small_out[...] = small_fin[...]
    for c in stores:
        c.wait()


def reduce_gradients(sp_size, rows, grad_out, grad_pre, mlp_in, context, grad_hat, hat_hop, slab_sum, small):
    seq, wide = mlp_in.shape
    slab, slab_width = slab_sum.shape
    units = slab
    own = seq // sp_size
    full, low = jnp.float32, jnp.bfloat16
    hbm = pl.BlockSpec(memory_space=pltpu.HBM)
    vmem = pl.BlockSpec(memory_space=pltpu.VMEM)
    dma = pltpu.SemaphoreType.DMA
    shape = jax.ShapeDtypeStruct

    def v(*dims, kind=low):
        return pltpu.VMEM(dims, kind)
    scratch = [
        v(seq, wide), v(seq, wide), v(seq, wide), v(seq, context.shape[1]), v(4, units, wide),
        v(4, units, wide), v(slab, wide), v(4, units, wide), v(slab, wide),
        v(2, units, wide), v(2, rows, wide), v(units, wide), v(rows, wide),
        v(slab, wide), v(slab, slab_width),
        v(3, *small.shape, kind=full), v(3, *small.shape, kind=full), v(sp_size, small.shape[0], small.shape[1] // 8, kind=full), v(*small.shape, kind=full),
        v(2, sp_size - 1, own, wide), v(own, wide),
        dma((7,)), dma((6,)), dma, dma((2, 4)), dma((2, 4)), dma((2, 2)), dma((2, 2)), dma((2,)), dma((2,)),
        dma((sp_size - 1, 3)), dma((sp_size - 1, 3)), dma, dma, dma((3,)), dma((3,)),
        dma((sp_size - 1,)), dma((sp_size - 1,)), dma((2, sp_size - 1)), dma((2, sp_size - 1)), dma((7,)), dma((7,)),
    ]
    return pl.pallas_call(
        functools.partial(back_kernel, sp_size),
        out_shape=[shape((units, wide), low), shape((rows, 3 * wide), low), shape((rows, wide), low), shape((own, wide), low),
                   shape(small.shape, full)],
        in_specs=[hbm] * 7 + [vmem], out_specs=[hbm] * 4 + [vmem],
        scratch_shapes=scratch,
        compiler_params=pltpu.CompilerParams(collective_id=1, has_side_effects=True, vmem_limit_bytes=62 << 20),
        cost_estimate=pl.CostEstimate(flops=9 * 10 ** 9, bytes_accessed=200 * 1000 * 1000, transcendentals=0),
        name="reduce_gradients",
    )(grad_out, grad_pre, mlp_in, context, grad_hat, hat_hop, slab_sum, small)

def finish_kernel(len_ref, tok_ref, cot_ref, sum_ref, hat_ref, down_ref, up_ref, qkv_ref, dense_ref, bias_ref, small_ref,
                  out_ref, input_ref, gain_out, shift_out, qkv_out, qkv_bias_out, dense_out, up_out, unit_out, down_out, bias_out):
    full = jnp.float32
    part = pl.program_id(0)
    rows, wide = tok_ref.shape
    tokens = tok_ref[...].astype(full)
    out_ref[...] = (tokens + sum_ref[...].astype(full) + bias_ref[...].astype(full)).astype(out_ref.dtype)
    centered = tokens - jnp.mean(tokens, axis=-1, keepdims=True)
    inverse = lax.rsqrt(jnp.mean(centered * centered, axis=-1, keepdims=True) + eps)
    normed = centered * inverse
    hat = hat_ref[...].astype(full)
    grad = inverse * (
        hat - jnp.mean(hat, axis=-1, keepdims=True) - normed * jnp.mean(hat * normed, axis=-1, keepdims=True))
    position = (lax.axis_index("sp") * pl.num_programs(0) + part) * rows + lax.broadcasted_iota(jnp.int32, (rows, wide), 0)
    own = jnp.where(position < len_ref[0], cot_ref[...].astype(full), 0.0)
    input_ref[...] = (own + grad).astype(input_ref.dtype)
    down_out[...] = down_ref[...].astype(full)
    up_out[...] = up_ref[...].astype(full)
    qkv_out[...] = qkv_ref[...].astype(full)
    dense_out[...] = dense_ref[...].astype(full)

    @pl.when(part == 0)
    def _():
        gain_out[...] = small_ref[0:2, :]
        shift_out[...] = small_ref[2:4, :]
        qkv_bias_out[...] = small_ref[4:7, :]
        unit_rows = unit_out.shape[1] // wide
        for row in range(unit_rows):
            unit_out[:, row * wide:(row + 1) * wide] = small_ref[7 + row:8 + row, :]
        bias_out[...] = small_ref[7 + unit_rows:8 + unit_rows, :]


def finish(lengths, tokens, cotangent, reduced_out, reduced_hat, grad_down, grad_up, grad_qkv, grad_dense, out_bias, small, all_units):
    own, wide = tokens.shape
    steps = 4
    full = jnp.float32
    shape = jax.ShapeDtypeStruct

    def rows(x):
        shared = 1 if x.shape[0] // steps >= 16 else 2
        return pl.BlockSpec((x.shape[0] * shared // steps, x.shape[1]), lambda i: (i // shared, 0))

    def whole(*dims):
        return pl.BlockSpec(dims, lambda i: (0, 0))
    out_row = out_bias[None]
    return pl.pallas_call(
        finish_kernel,
        grid=(steps,),
        out_shape=[shape(tokens.shape, tokens.dtype), shape(tokens.shape, tokens.dtype), shape((2, wide), full),
                   shape((2, wide), full), shape(grad_qkv.shape, full), shape((3, wide), full), shape(grad_dense.shape, full),
                   shape(grad_up.shape, full), shape((1, all_units), full), shape(grad_down.shape, full), shape((1, wide), full)],
        in_specs=[pl.BlockSpec(memory_space=pltpu.SMEM)]
        + [rows(x) for x in (tokens, cotangent, reduced_out, reduced_hat, grad_down, grad_up, grad_qkv, grad_dense)]
        + [whole(1, wide), whole(*small.shape)],
        out_specs=[rows(tokens), rows(tokens), whole(2, wide), whole(2, wide), rows(grad_qkv), whole(3, wide), rows(grad_dense),
                   rows(grad_up), whole(1, all_units), rows(grad_down), whole(1, wide)],
        name="finish",
    )(lengths, tokens, cotangent, reduced_out, reduced_hat, grad_down, grad_up, grad_qkv, grad_dense, out_row, small)

def gather_plain(dp_size, sp_size, qkv_weight, out_weight, up_weight, down_weight):
    head_width = D // sp_size
    qkv_rows = qkv_weight.shape[0]
    qkv_slab = lax.all_to_all(
        qkv_weight.reshape(qkv_rows, 3, sp_size, head_width),
        "sp",
        split_axis=2,
        concat_axis=0,
        tiled=True,
    )
    qkv_own = lax.all_gather(
        qkv_slab.reshape(qkv_rows * sp_size, 3 * head_width), "dp", axis=0, tiled=True
    )
    up_own = lax.all_gather(up_weight, "dp", axis=0, tiled=True)
    down_own = lax.all_gather(down_weight, "dp", axis=0, tiled=True)
    out_blocks = lax.all_gather(out_weight, "dp", axis=0, tiled=True)
    out_own = lax.all_to_all(
        out_blocks.reshape(sp_size, dp_size // sp_size, qkv_rows, D),
        "sp",
        split_axis=0,
        concat_axis=2,
        tiled=True,
    ).reshape(head_width, D)
    return qkv_own, out_own, up_own, down_own


def reduce_plain(
    dp_size, sp_size, rows, hidden, grad_out, grad_pre, mlp_in, attn_in, grad_proj, context
):
    def scatter(left, right):
        return lax.psum_scatter(
            contract_rows(left, right).astype(jnp.bfloat16), "dp", scatter_dimension=0, tiled=True
        )

    grad_dense = lax.all_to_all(
        contract_rows(context, grad_out)
        .astype(jnp.bfloat16)
        .reshape(dp_size // sp_size, sp_size, rows, D),
        "sp",
        split_axis=1,
        concat_axis=0,
        tiled=True,
    ).reshape(dp_size * rows, D)
    grad_dense = lax.psum_scatter(grad_dense, "dp", scatter_dimension=0, tiled=True)
    grad_qkv = lax.all_to_all(
        scatter(attn_in, grad_proj).reshape(sp_size, rows, 3, 1, D // sp_size),
        "sp",
        split_axis=0,
        concat_axis=3,
        tiled=True,
    ).reshape(rows, 3 * D)
    return scatter(hidden, grad_out), scatter(grad_pre, mlp_in), grad_qkv, grad_dense


def body(
    tokens,
    lengths,
    cotangent,
    ln_gains,
    ln_shifts,
    qkv_weight,
    qkv_bias,
    out_weight,
    up_weight,
    up_bias,
    down_weight,
    out_bias,
):
    dp_size = lax.axis_size("dp")
    sp_size = lax.axis_size("sp")
    shard = lax.axis_index("sp")
    own_rows = tokens.shape[0]
    seq_rows = own_rows * sp_size
    head_width = D // sp_size
    length = lengths[0]
    low = jnp.bfloat16
    full = jnp.float32

    qkv_rows = qkv_weight.shape[0]
    units = up_weight.shape[0]
    square = dp_size == 8 and sp_size == 4
    positions = jnp.arange(seq_rows, dtype=jnp.int32)
    gains = ln_gains.astype(full)
    shifts = ln_shifts.astype(full)
    row_valid = positions < length
    if not square:
        unit_bias = (
            lax.dynamic_index_in_dim(
                up_bias.reshape(dp_size, sp_size, units), shard, 1, keepdims=False
            )
            .reshape(dp_size * units)
            .astype(full)
        )
        bias_own = (
            lax.dynamic_index_in_dim(
                qkv_bias.reshape(3, sp_size, head_width), shard, 1, keepdims=False
            )
            .reshape(1, 3 * head_width)
            .astype(full)
        )
        cos_rows, sin_rows = rotary_rows(seq_rows)
        seq_tokens = lax.all_gather(tokens, "sp", axis=0, tiled=True)
        qkv_own, out_own, up_own, down_own = gather_plain(
            dp_size, sp_size, qkv_weight, out_weight, up_weight, down_weight
        )
        seq_cotangent = lax.all_gather(cotangent, "sp", axis=0, tiled=True)
    if square:
        (
            qkv_own,
            out_own,
            up_own,
            down_own,
            seq_tokens,
            seq_cotangent,
            attn_in,
            mlp_in,
            hidden,
            pre_act,
            partial_out,
            part_hop,
            near_pre,
            cos_rows,
            sin_rows,
            means,
            inverses,
            unit_sums,
            queries,
            key_rows,
            values,
            context,
        ) = front(
            sp_size,
            dp_size,
            lengths,
            qkv_weight,
            out_weight,
            up_weight,
            down_weight,
            tokens,
            cotangent,
            ln_gains,
            ln_shifts,
            qkv_bias,
            up_bias[None],
        )
        grad_down, slab_sum, grad_pre, grad_hat, hat_hop, _, grad_out, reduced_out, small = middle(
            sp_size,
            dp_size,
            lengths,
            seq_cotangent,
            out_own,
            queries,
            key_rows,
            values,
            pre_act,
            hidden,
            down_own,
            up_own,
            qkv_own,
            seq_tokens,
            partial_out,
            part_hop,
            near_pre,
            attn_in,
            unit_sums,
            ln_gains,
            cos_rows,
            sin_rows,
            means,
            inverses,
        )
        grad_up, grad_qkv, grad_dense, reduced_hat, small = reduce_gradients(
            sp_size,
            qkv_rows,
            grad_out,
            grad_pre,
            mlp_in,
            context,
            grad_hat,
            hat_hop,
            slab_sum,
            small,
        )
        (
            output,
            input_grad,
            gain_total,
            shift_total,
            grad_qkv,
            qkv_bias_total,
            grad_dense,
            grad_up,
            unit_total,
            grad_down,
            out_bias_total,
        ) = finish(
            lengths,
            tokens,
            cotangent,
            reduced_out,
            reduced_hat,
            grad_down,
            grad_up,
            grad_qkv,
            grad_dense,
            out_bias,
            small,
            up_bias.shape[0],
        )
        unit_total = unit_total.reshape(-1)
        out_bias_total = out_bias_total.reshape(-1)
    else:
        inputs = seq_tokens.astype(full)
        centre = jnp.mean(inputs, axis=-1, keepdims=True)
        centered = inputs - centre
        inverse = lax.rsqrt(jnp.mean(centered * centered, axis=-1, keepdims=True) + eps)
        normed = centered * inverse
        attn_in = (normed * gains[0] + shifts[0]).astype(low)
        mlp_in = (normed * gains[1] + shifts[1]).astype(low)
        projected = jnp.dot(attn_in, qkv_own, preferred_element_type=full)
        queries, key_rows, values, context = attend_fwd(
            projected, bias_own, cos_rows, sin_rows, lengths
        )
        pre_act = contract_cols(mlp_in, up_own) + unit_bias
        hidden = gelu_value(pre_act).astype(low)
        partial_out = (
            jnp.dot(hidden, down_own, preferred_element_type=full)
            + jnp.dot(context, out_own, preferred_element_type=full)
        ).astype(low)
        reduced_out = lax.psum_scatter(
            partial_out, "sp", scatter_dimension=0, tiled=True
        )
        grad_out = jnp.where(row_valid[:, None], seq_cotangent, jnp.zeros_like(seq_cotangent))
        grad_hidden = contract_cols(grad_out, down_own)
        grad_pre = (grad_hidden * gelu_slope(pre_act)).astype(low)
        grad_mlp_in = jnp.dot(grad_pre, up_own, preferred_element_type=full)

        grad_context = contract_cols(grad_out, out_own).astype(low)
        grad_proj, grad_proj_sum = attend_bwd(
            queries, key_rows, values, grad_context, cos_rows, sin_rows, lengths
        )
        grad_attn_in = contract_cols(grad_proj, qkv_own)
        grad_hat = grad_attn_in * gains[0] + grad_mlp_in * gains[1]
        reduced_hat = lax.psum_scatter(
            grad_hat.astype(low), "sp", scatter_dimension=0, tiled=True
        )
        spread_units = lax.dynamic_update_index_in_dim(
            jnp.zeros((dp_size, sp_size, units), full),
            jnp.sum(grad_pre, axis=0, dtype=full).reshape(dp_size, units),
            shard,
            1,
        ).reshape(-1)
        spread_bias = lax.dynamic_update_index_in_dim(
            jnp.zeros((3, sp_size, head_width), full),
            grad_proj_sum.reshape(3, head_width),
            shard,
            1,
        ).reshape(3, D)
        gain_grad = jnp.stack(
            [jnp.sum(grad_attn_in * normed, axis=0), jnp.sum(grad_mlp_in * normed, axis=0)]
        )
        shift_grad = jnp.stack([jnp.sum(grad_attn_in, axis=0), jnp.sum(grad_mlp_in, axis=0)])
        own_valid = shard * own_rows + jnp.arange(own_rows, dtype=jnp.int32) < length
        own_cotangent = jnp.where(own_valid[:, None], cotangent.astype(full), 0.0)
        out_bias_part = jnp.sum(own_cotangent, axis=0)
        grad_down, grad_up, grad_qkv, grad_dense = reduce_plain(
            dp_size,
            sp_size,
            qkv_rows,
            hidden,
            grad_out,
            grad_pre,
            mlp_in,
            attn_in,
            grad_proj,
            context,
        )
        gain_total, shift_total, qkv_bias_total, unit_total, out_bias_total = lax.psum(
            (gain_grad, shift_grad, spread_bias, spread_units, out_bias_part), ("dp", "sp")
        )


        output = (
            tokens.astype(full) + reduced_out.astype(full) + out_bias.astype(full)
        ).astype(low)

        reduced_hat = reduced_hat.astype(full)
        own_centered = tokens.astype(full) - jnp.mean(tokens.astype(full), axis=-1, keepdims=True)
        own_inverse = lax.rsqrt(jnp.mean(own_centered * own_centered, axis=-1, keepdims=True) + eps)
        own_normed = own_centered * own_inverse
        grad_input = own_inverse * (
            reduced_hat
            - jnp.mean(reduced_hat, axis=-1, keepdims=True)
            - own_normed * jnp.mean(reduced_hat * own_normed, axis=-1, keepdims=True)
        )
        input_grad = (own_cotangent + grad_input).astype(low)
        grad_qkv, grad_dense = grad_qkv.astype(full), grad_dense.astype(full)
        grad_up, grad_down = grad_up.astype(full), grad_down.astype(full)

    return (
        output,
        input_grad,
        gain_total,
        shift_total,
        grad_qkv,
        qkv_bias_total,
        grad_dense,
        grad_up,
        unit_total,
        grad_down,
        out_bias_total,
    )


def solution(mesh):
    return jax.shard_map(
        body,
        mesh=mesh,
        in_specs=(
            P(("dp", "sp"), None),
            P("dp"),
            P(("dp", "sp"), None),
            P(),
            P(),
            P(("dp", "sp"), None),
            P(),
            P(("dp", "sp"), None),
            P(("dp", "sp"), None),
            P(),
            P(("dp", "sp"), None),
            P(),
        ),
        out_specs=(
            P(("dp", "sp"), None),
            P(("dp", "sp"), None),
            P(),
            P(),
            P(("dp", "sp"), None),
            P(),
            P(("dp", "sp"), None),
            P(("dp", "sp"), None),
            P(),
            P(("dp", "sp"), None),
            P(),
        ),
        check_vma=False,
    )
```

```python
import functools

import jax
import jax.numpy as jnp
from jax import lax
from jax.experimental import pallas as pl
from jax.experimental.pallas import tpu as pltpu
from jax.sharding import PartitionSpec as P

D = 2048
HEADS = 8
HEAD = 256
ROT = 64


eps = 1e-05
base_freq = 10000.0
root_half = 0.7071067811865476
inv_root_two_pi = 0.3989422804014327


def contract_rows(left, right):
    return lax.dot_general(
        left, right, (((0,), (0,)), ((), ())), preferred_element_type=jnp.float32
    )


def contract_cols(left, right):
    return lax.dot_general(
        left, right, (((1,), (1,)), ((), ())), preferred_element_type=jnp.float32
    )


def gelu_value(pre_act):
    return 0.5 * pre_act * (1.0 + lax.erf(pre_act * root_half))


def gelu_slope(pre_act):
    return 0.5 * (1.0 + lax.erf(pre_act * root_half)) + pre_act * inv_root_two_pi * jnp.exp(
        -0.5 * pre_act * pre_act
    )


BAND=256
def turn(x, cos_t, sin_t):
    first = x[:, :128]
    lane = lax.broadcasted_iota(jnp.int32, first.shape, 1)
    partner = jnp.where(lane < ROT // 2, pltpu.roll(first, 128 - ROT // 2, 1), pltpu.roll(first, ROT // 2, 1))
    return jnp.concatenate([first * cos_t + partner * sin_t, x[:, 128:]], axis=1)

def weights_of(q, k, start, length, scale):
    rows, cols = q.shape[0], k.shape[0]
    s = lax.dot_general(q, k, (((1,), (1,)), ((), ())), preferred_element_type=jnp.float32) * scale
    key = lax.broadcasted_iota(jnp.int32, (rows, cols), 1)
    query = start + lax.broadcasted_iota(jnp.int32, (rows, cols), 0)
    s = jnp.where((key <= query) & (key < length), s, -1e30)
    e = jnp.exp(s - jnp.max(s, axis=-1, keepdims=True))
    return e / jnp.sum(e, axis=-1, keepdims=True)

def fwd_kernel(scale, len_ref, pq, pk, pv, bq, bk, bv, cos_ref, sin_ref, q_ref, k_ref, v_ref, ctx_ref):
    length = len_ref[0]
    seq = pq.shape[0]
    cos_t, sin_t = cos_ref[...], sin_ref[...]
    q_ref[...] = turn(pq[...] + bq[...], cos_t, sin_t).astype(jnp.bfloat16)
    k_ref[...] = turn(pk[...] + bk[...], cos_t, sin_t).astype(jnp.bfloat16)
    v_ref[...] = (pv[...] + bv[...]).astype(jnp.bfloat16)
    for start in range(0, seq, BAND):
        end = start + BAND
        p = weights_of(q_ref[start:end, :], k_ref[:end, :], start, length, scale)
        ctx_ref[start:end, :] = jnp.dot(p.astype(jnp.bfloat16), v_ref[:end, :], preferred_element_type=jnp.float32).astype(jnp.bfloat16)

def attend_fwd(projected, bias, cos_t, sin_t, lengths):
    seq, width = projected.shape
    heads = width // 3 // HEAD
    col = lambda g: pl.BlockSpec((seq, HEAD), lambda h, *_, g=g: (0, g * heads + h))
    bcol = lambda g: pl.BlockSpec((1, HEAD), lambda h, *_, g=g: (0, g * heads + h))
    tab = pl.BlockSpec((seq, 128), lambda h, *_: (0, 0))
    out = pl.BlockSpec((seq, HEAD), lambda h, *_: (0, h))
    return pl.pallas_call(
        functools.partial(fwd_kernel, HEAD ** -0.5),
        grid_spec=pltpu.PrefetchScalarGridSpec(num_scalar_prefetch=1, grid=(heads,),
            in_specs=[col(0), col(1), col(2), bcol(0), bcol(1), bcol(2), tab, tab], out_specs=[out] * 4),
        out_shape=[jax.ShapeDtypeStruct((seq, heads * HEAD), jnp.bfloat16)] * 4,
        name="attend_fwd",
        cost_estimate=pl.CostEstimate(flops=heads * seq * seq * HEAD * 4, bytes_accessed=seq * width * 8, transcendentals=heads * seq * seq),
    )(lengths, projected, projected, projected, bias, bias, bias, cos_t, sin_t)

def bwd_kernel(scale, heads, len_ref, q_ref, k_ref, v_ref, g_ref, cos_ref, sin_ref, gp_ref, sum_ref, dk, dv, dq):
    length = len_ref[0]
    h = pl.program_id(0)
    seq = q_ref.shape[0]
    dk[...] = jnp.zeros_like(dk)
    dv[...] = jnp.zeros_like(dv)
    for start in range(0, seq, BAND):
        end = start + BAND
        q, g = q_ref[start:end, :], g_ref[start:end, :]
        k, v = k_ref[:end, :], v_ref[:end, :]
        p = weights_of(q, k, start, length, scale)
        gp = lax.dot_general(g, v, (((1,), (1,)), ((), ())), preferred_element_type=jnp.float32)
        ds = (p * (gp - jnp.sum(p * gp, axis=-1, keepdims=True))).astype(jnp.bfloat16)
        dq[start:end, :] = jnp.dot(ds, k, preferred_element_type=jnp.float32) * scale
        dk[:end, :] += lax.dot_general(ds, q, (((0,), (0,)), ((), ())), preferred_element_type=jnp.float32)
        dv[:end, :] += lax.dot_general(p.astype(jnp.bfloat16), g, (((0,), (0,)), ((), ())), preferred_element_type=jnp.float32)
    cos_t, sin_t = cos_ref[...], sin_ref[...]
    def back(x):
        return turn(x.astype(jnp.bfloat16).astype(jnp.float32), cos_t, -sin_t).astype(jnp.bfloat16)
    for g, piece in enumerate((back(dq[...]), back(dk[...] * scale), dv[...].astype(jnp.bfloat16))):
        at = pl.ds(pl.multiple_of((g * heads + h) * HEAD, HEAD), HEAD)
        gp_ref[:, at] = piece
        sum_ref[:, at] = jnp.sum(piece.astype(jnp.float32), axis=0, keepdims=True)

def attend_bwd(q, k, v, gctx, cos_t, sin_t, lengths):
    seq, width = q.shape
    heads = width // HEAD
    col = pl.BlockSpec((seq, HEAD), lambda h, *_: (0, h))
    tab = pl.BlockSpec((seq, 128), lambda h, *_: (0, 0))
    return pl.pallas_call(
        functools.partial(bwd_kernel, HEAD ** -0.5, heads),
        grid_spec=pltpu.PrefetchScalarGridSpec(num_scalar_prefetch=1, grid=(heads,),
            in_specs=[col] * 4 + [tab, tab],
            out_specs=[pl.BlockSpec((seq, 3 * width), lambda h, *_: (0, 0)), pl.BlockSpec((1, 3 * width), lambda h, *_: (0, 0))],
            scratch_shapes=[pltpu.VMEM((seq, HEAD), jnp.float32)] * 3),
        out_shape=[jax.ShapeDtypeStruct((seq, 3 * width), jnp.bfloat16), jax.ShapeDtypeStruct((1, 3 * width), jnp.float32)],
        name="attend_bwd",
        cost_estimate=pl.CostEstimate(flops=heads * seq * seq * HEAD * 10, bytes_accessed=seq * width * 20, transcendentals=heads * seq * seq),
    )(lengths, q, k, v, gctx, cos_t, sin_t)

def rotary_rows(seq):
    half = ROT // 2
    freq = 10000.0 ** (-jnp.arange(half, dtype=jnp.float32) * (2.0 / ROT))
    ang = jnp.arange(seq, dtype=jnp.int32).astype(jnp.float32)[:, None] * freq[None, :]
    c, s = jnp.cos(ang), jnp.sin(ang)
    rest = 128 - ROT
    return (jnp.concatenate([c, c, jnp.ones((seq, rest), jnp.float32)], 1), jnp.concatenate([-s, s, jnp.zeros((seq, rest), jnp.float32)], 1))

MESH = pl.DeviceIdType.MESH

def square_partners(dp):
    core, x, y = dp % 2, (dp // 2) % 2, dp // 4
    across_x, across_y = dp + 2 - 4 * x, dp + 4 - 8 * y
    first = across_x * (1 - core) + across_y * core
    second = across_y * (1 - core) + across_x * core
    return first, second, across_x + across_y - dp, 1 - 2 * core

class Hops:
    def __init__(self, count, dp, sp, source, result, send, recv):
        self.count, self.dp, self.sp, self.source, self.result = count, dp, sp, source, result
        self.send, self.recv, self.rows = send, recv, source.shape[0]

    def place(self, owner):
        return pl.ds(pl.multiple_of(owner * self.rows, self.rows), self.rows)

    def copy(self, way, step, owner, own):
        to = lax.rem(self.sp + (1 if way == 0 else self.count - 1), self.count)
        at = self.result.at[self.place(owner)]
        return pltpu.make_async_remote_copy(
            src_ref=self.source if own else at, dst_ref=at, send_sem=self.send.at[way, step],
            recv_sem=self.recv.at[way, step], device_id=(self.dp, to), device_id_type=MESH)

    def sends(self, way, step):
        if way == 0:
            return (self.sp >= step) & (self.sp < self.count - 1)
        return (self.sp < self.count - step) & (self.sp > 0)

    def receives(self, way, step):
        return self.sp >= step + 1 if way == 0 else self.sp < self.count - step - 1

    def owner(self, way, step):
        return self.sp - step if way == 0 else self.sp + step

    def start(self, way, step):
        @pl.when(self.sends(way, step))
        def _():
            self.copy(way, step, self.owner(way, step), step == 0).start()

    def begin(self):
        for way in (0, 1):
            self.start(way, 0)

    def relay(self, step):
        for way in (0, 1):
            @pl.when(self.receives(way, step - 1) & self.sends(way, step))
            def _():
                self.copy(way, step - 1, self.owner(way, step), False).wait_recv()
                self.copy(way, step, self.owner(way, step), False).start()

    def settle(self, step):
        for way in (0, 1):
            @pl.when(self.receives(way, step - 1) & jnp.logical_not(self.sends(way, step)))
            def _():
                self.copy(way, step - 1, self.owner(way, step), False).wait_recv()

    def finish(self):
        for step in range(self.count - 1):
            for way in (0, 1):
                @pl.when(self.sends(way, step))
                def _():
                    self.copy(way, step, self.owner(way, step), step == 0).wait_send()


NEAR = 2


def front_kernel(sp_size, len_ref, qkv_ref, out_ref, up_ref, down_ref, tok_ref, cot_ref, freq_ref, gain_ref, shift_ref,
                 qkv_bias_ref, unit_bias_ref,
                 qkv_all, out_all, up_all, down_all, tok_all, cot_all, attn_out, mlp_out, hidden_out, pre_out, part_out, part_in, gpre_out,
                 cos_ref, sin_ref, mean_ref, inv_ref, unit_ref, q_ref, k_ref, v_ref, ctx_ref,
                 tok, attn, mlp, qkv_w, up_w, hidden, pre, cot, gpre,
                 send_sem, recv_sem, slab_send, slab_recv, keep_sem, turn_send, turn_recv, tok_send, tok_recv, cot_send, cot_recv,
                 load_sem, store_sem, pre_sem, part_sem, hop_send, hop_recv, slope_sem, gpre_sem):
    full, low = jnp.float32, jnp.bfloat16
    dp, sp = lax.axis_index("dp"), lax.axis_index("sp")
    first, second, diagonal, flip = square_partners(dp)
    sibling = dp + flip
    per = 2
    pair, lane = dp // per, dp % per
    rows = qkv_ref.shape[0]
    seq, wide = tok.shape
    own_rows = tok_ref.shape[0]
    head_width = wide // sp_size
    units = down_ref.shape[0]
    slab = rows * sp_size
    width = q_ref.shape[1]
    turn_dp = sp * per + lane
    scale = HEAD ** -0.5
    band = 256

    barrier = pltpu.get_barrier_semaphore()
    for other in (first, second, sibling):
        pl.semaphore_signal(barrier, inc=1, device_id=(other, sp), device_id_type=MESH)
    for step in range(1, sp_size):
        pl.semaphore_signal(barrier, inc=1, device_id=(dp, lax.rem(sp + step, sp_size)), device_id_type=MESH)

    @pl.when(pair != sp)
    def _():
        pl.semaphore_signal(barrier, inc=1, device_id=(turn_dp, pair), device_id_type=MESH)

    pl.semaphore_wait(barrier, 2 + sp_size + jnp.where(pair != sp, 1, 0))

    def remote_copy(source, target, send, recv, device):
        return pltpu.make_async_remote_copy(
            src_ref=source, dst_ref=target, send_sem=send, recv_sem=recv, device_id=device, device_id_type=MESH)

    def slab_at(owner):
        return pl.ds(pl.multiple_of((dp * sp_size + owner) * rows, rows), rows)

    def slab_columns(part, there):
        return pl.ds(pl.multiple_of(part * wide + there * head_width, head_width), head_width)

    def slab_copy(step, part, there, origin):
        return remote_copy(
            qkv_ref.at[:, slab_columns(part, there)],
            qkv_all.at[slab_at(origin), pl.ds(part * head_width, head_width)],
            slab_send.at[step - 1, part], slab_recv.at[step - 1, part], (dp, there))

    def plain(height):
        return lambda owner: pl.ds(pl.multiple_of(owner * height, height), height)

    def turned(owner):
        return pl.ds(pl.multiple_of((owner % per) * slab + (owner // per) * rows, rows), rows)

    def turn_copy(landing):
        return remote_copy(out_ref, out_all.at[turned(landing)], turn_send, turn_recv, (turn_dp, pair))

    arrays = ((up_ref, up_all, plain(units)), (None, qkv_all, plain(slab)), (None, out_all, turned), (down_ref, down_all, plain(units)))
    UP, QKV, OUT, DOWN = 0, 1, 2, 3

    def copy(index, message, block, target):
        source, result, place = arrays[index]
        at = result.at[place(block)]
        return remote_copy(at if source is None or message > 2 else source, at,
                           send_sem.at[index, message], recv_sem.at[index, message], (target, sp))

    sends = ((dp, first), (dp, second), (dp, sibling), (first, second), (first, sibling), (second, sibling), (diagonal, sibling))
    arrivals = (first, second, sibling, diagonal, second + flip, first + flip, diagonal + flip)

    def start(index, message):
        copy(index, message, *sends[message]).start()

    def arrived(index, message):
        copy(index, message, arrivals[message], sibling).wait_recv()

    def own(index):
        for message in (0, 1, 2):
            start(index, message)

    def onward(index):
        arrived(index, 0)
        start(index, 3)
        start(index, 4)
        arrived(index, 1)
        start(index, 5)

    def corner(index):
        arrived(index, 3)
        start(index, 6)

    def complete(index):
        for message in (2, 4, 5, 6):
            arrived(index, message)

    def load(source, target, which):
        c = pltpu.make_async_copy(source, target, load_sem.at[which])
        c.start()
        return c

    for step in range(1, sp_size):
        for part in range(3):
            slab_copy(step, part, lax.rem(sp + step, sp_size), sp).start()

    @pl.when(pair != sp)
    def _():
        turn_copy(turn_dp).start()

    own(UP)
    tokens = Hops(sp_size, dp, sp, tok_ref, tok_all, tok_send, tok_recv)
    cotangents = Hops(sp_size, dp, sp, cot_ref, cot_all, cot_send, cot_recv)
    tokens.begin()
    keeps = []

    def keep(source, target):
        c = pltpu.make_async_copy(source, target, keep_sem.at[len(keeps)])
        c.start()
        keeps.append(c)

    for part in range(3):
        keep(qkv_ref.at[:, slab_columns(part, sp)], qkv_all.at[slab_at(sp), pl.ds(part * head_width, head_width)])
    keep(up_ref, up_all.at[plain(units)(dp)])
    keep(down_ref, down_all.at[plain(units)(dp)])
    keep(tok_ref, tok_all.at[tokens.place(sp)])
    keep(cot_ref, cot_all.at[cotangents.place(sp)])

    def normalize(source, source_start, target_start):
        def chunk(i, carry):
            at = pl.ds(pl.multiple_of(target_start + i * 32, 32), 32)
            values = source[pl.ds(pl.multiple_of(source_start + i * 32, 32), 32), :].astype(full)
            mean = jnp.mean(values, axis=-1, keepdims=True)
            centered = values - mean
            inverse = lax.rsqrt(jnp.mean(centered * centered, axis=-1, keepdims=True) + eps)
            normed = centered * inverse
            mean_ref[at, :] = jnp.broadcast_to(mean, (32, 128))
            inv_ref[at, :] = jnp.broadcast_to(inverse, (32, 128))
            attn[at, :] = (normed * gain_ref[0:1, :].astype(full) + shift_ref[0:1, :].astype(full)).astype(low)
            mlp[at, :] = (normed * gain_ref[1:2, :].astype(full) + shift_ref[1:2, :].astype(full)).astype(low)
            return carry
        lax.fori_loop(0, own_rows // 32, chunk, 0)

    def absorb(step):
        for way in (0, 1):
            @pl.when(tokens.receives(way, step - 1))
            def _():
                at = tokens.place(tokens.owner(way, step))
                c = load(tok_all.at[at], tok.at[at], way)
                c.wait()
                begin = tokens.owner(way, step) * own_rows
                normalize(tok, begin, begin)

    def table(i, carry):
        at = pl.ds(pl.multiple_of(i * 64, 64), 64)
        lanes = lax.broadcasted_iota(jnp.int32, (64, 128), 1)
        position = i * 64 + lax.broadcasted_iota(jnp.int32, (64, 128), 0)
        angle = position.astype(full) * freq_ref[...]
        cos_ref[at, :] = jnp.where(lanes < ROT, jnp.cos(angle), 1.0)
        sine = jnp.sin(angle)
        sin_ref[at, :] = jnp.where(lanes < ROT, jnp.where(lanes < ROT // 2, -sine, sine), 0.0)
        return carry

    normalize(tok_ref, 0, sp * own_rows)
    lax.fori_loop(0, seq // 64, table, 0)
    for step in range(1, sp_size):
        for part in range(3):
            slab_copy(step, part, sp, lax.rem(sp + sp_size - step, sp_size)).wait_recv()
    for c in keeps[:3]:
        c.wait()
    own(QKV)

    @pl.when(pair == sp)
    def _():
        c = pltpu.make_async_copy(out_ref, out_all.at[turned(dp)], keep_sem.at[7])
        c.start()
        c.wait()

    @pl.when(pair != sp)
    def _():
        turn_copy(dp).wait_recv()

    own(OUT)
    onward(UP)
    tokens.relay(1)
    onward(QKV)
    onward(OUT)
    own(DOWN)
    tokens.settle(1)
    absorb(1)
    tokens.relay(2)
    cotangents.begin()
    corner(UP)
    complete(UP)
    for c in keeps[3:]:
        c.wait()
    up_load = load(up_all, up_w, 2)
    tokens.settle(2)
    absorb(2)
    corner(QKV)
    corner(OUT)
    complete(QKV)
    qkv_load = load(qkv_all, qkv_w, 3)
    complete(OUT)
    onward(DOWN)
    tokens.settle(3)
    absorb(3)
    stores = [pltpu.make_async_copy(attn, attn_out, store_sem.at[0]), pltpu.make_async_copy(mlp, mlp_out, store_sem.at[1])]
    for c in stores:
        c.start()
    qkv_load.wait()

    def head(h, carry):
        lanes = pl.ds(pl.multiple_of(h * HEAD, HEAD), HEAD)

        def project(r, carry):
            at = pl.ds(pl.multiple_of(r * band, band), band)
            cos_t, sin_t = cos_ref[at, :], sin_ref[at, :]
            for part, target in enumerate((q_ref, k_ref, v_ref)):
                cols = pl.ds(pl.multiple_of(part * width + h * HEAD, HEAD), HEAD)
                bias_cols = pl.ds(pl.multiple_of(sp * width + h * HEAD, HEAD), HEAD)
                value = jnp.dot(attn[at, :], qkv_w[:, cols], preferred_element_type=full)
                value = value + qkv_bias_ref[part:part + 1, bias_cols].astype(full)
                if part < 2:
                    value = turn(value, cos_t, sin_t)
                target[at, lanes] = value.astype(low)
            return carry
        lax.fori_loop(0, seq // band, project, 0)
        for begin in range(0, seq, band):
            end = begin + band
            p = weights_of(q_ref[begin:end, lanes], k_ref[:end, lanes], begin, len_ref[0], scale)
            ctx_ref[begin:end, lanes] = jnp.dot(p.astype(low), v_ref[:end, lanes], preferred_element_type=full).astype(low)
        return carry

    lax.fori_loop(0, width // HEAD, head, 0)
    corner(DOWN)
    cotangents.relay(1)
    up_load.wait()

    def pre_store(block, slot):
        return pltpu.make_async_copy(pre.at[slot], pre_out.at[:, pl.ds(pl.multiple_of(block * units, units), units)],
                                     pre_sem.at[slot])

    def unit_block(block, carry):
        slot = lax.rem(block, 2)

        @pl.when(block >= 2)
        def _():
            pre_store(block - 2, slot).wait()

        of = pl.ds(pl.multiple_of(block * units, units), units)
        bias_of = pl.ds(pl.multiple_of((block * sp_size + sp) * units, units), units)

        def row_band(r, carry):
            at = pl.ds(pl.multiple_of(r * band, band), band)
            value = lax.dot_general(mlp[at, :], up_w[of, :], (((1,), (1,)), ((), ())), preferred_element_type=full)
            value = value + unit_bias_ref[:, bias_of].astype(full)
            pre[slot, at, :] = value
            hidden[at, of] = gelu_value(value).astype(low)
            return carry
        lax.fori_loop(0, seq // band, row_band, 0)
        pre_store(block, slot).start()
        return carry

    blocks = up_w.shape[0] // units
    lax.fori_loop(0, blocks // 2, unit_block, 0)
    complete(DOWN)
    half = up_w.shape[0] // 2
    stores[0].wait()
    late = [load(down_all.at[pl.ds(0, half)], tok, 0), load(down_all.at[pl.ds(half, half)], attn, 1)]
    lax.fori_loop(blocks // 2, blocks, unit_block, 0)
    out_rows = out_all.shape[0]
    late.append(load(out_all, up_w.at[pl.ds(0, out_rows)], 2))
    cotangents.relay(2)
    for block in (blocks - 2, blocks - 1):
        pre_store(block, block % 2).wait()
    stores[1].wait()
    hidden_store = pltpu.make_async_copy(hidden, hidden_out, store_sem.at[0])
    hidden_store.start()
    for c in late:
        c.wait()

    bands = seq // band
    upper = 2 * sp // sp_size

    def band_rows(r):
        return pl.ds(pl.multiple_of(((1 - upper) * (bands - 1 - r) + upper * r) * band, band), band)

    def part_store(r):
        return pltpu.make_async_copy(mlp.at[band_rows(r)], part_out.at[band_rows(r)], part_sem.at[r])

    def part_hop(way):
        to = lax.rem(sp + (1 if way == 0 else sp_size - 1), sp_size)
        return remote_copy(mlp.at[band_rows(0)], part_in.at[way], hop_send.at[way], hop_recv.at[way], (dp, to))

    def along(way):
        return sp if way == 0 else sp_size - 1 - sp

    def out_band(r, carry):
        at = band_rows(r)

        def out_columns(c, carry):
            to = pl.ds(pl.multiple_of(c * band, band), band)
            total = jnp.dot(hidden[at, :half], tok[:, to], preferred_element_type=full)
            total = total + jnp.dot(hidden[at, half:], attn[:, to], preferred_element_type=full)
            total = total + jnp.dot(ctx_ref[at, :], up_w[:out_rows, to], preferred_element_type=full)
            mlp[at, to] = total.astype(low)
            return carry
        lax.fori_loop(0, wide // band, out_columns, 0)
        part_store(r).start()
        return carry
    out_band(0, 0)
    for way in (0, 1):
        @pl.when(along(way) == 0)
        def _():
            part_hop(way).start()
    lax.fori_loop(1, bands, out_band, 0)

    for step in (1, 2):
        cotangents.settle(step)
    unit_ref[...] = jnp.zeros_like(unit_ref)
    early = NEAR

    def near_rows(n):
        return pl.ds(pl.multiple_of((upper * (bands - NEAR) + n) * band, band), band)

    def slope_room(block):
        return pre.at[block // 4, pl.ds(pl.multiple_of(lax.rem(block, 4) * band, band), band)]

    def slope_load(n, block):
        return pltpu.make_async_copy(
            pre_out.at[near_rows(n), pl.ds(pl.multiple_of(block * units, units), units)], slope_room(block), slope_sem.at[block])

    def cot_load(n):
        return pltpu.make_async_copy(cot_all.at[near_rows(n)], cot.at[lax.rem(n, 2)], gpre_sem.at[2 + lax.rem(n, 2)])

    def gpre_store(n):
        return pltpu.make_async_copy(gpre.at[lax.rem(n, 2)], gpre_out.at[near_rows(n)], gpre_sem.at[lax.rem(n, 2)])

    def first_loads(block, carry):
        slope_load(0, block).start()
        return carry
    lax.fori_loop(0, blocks, first_loads, 0)
    cot_load(0).start()

    def near_band(n, carry):
        slot = lax.rem(n, 2)
        cot_load(n).wait()

        @pl.when(n + 1 < early)
        def _():
            cot_load(n + 1).start()

        def mask(i, carry):
            at = pl.ds(pl.multiple_of(i * 32, 32), 32)
            row = (upper * (bands - NEAR) + n) * band + i * 32 + lax.broadcasted_iota(jnp.int32, (32, wide), 0)
            cot[slot, at, :] = jnp.where(row < len_ref[0], cot[slot, at, :].astype(full), 0.0).astype(low)
            return carry
        lax.fori_loop(0, band // 32, mask, 0)

        @pl.when(n >= 2)
        def _():
            gpre_store(n - 2).wait()

        for side, room in enumerate((tok, attn)):
            def unit_part(k, carry):
                block = side * (blocks // 2) + k
                slope_load(n, block).wait()
                of = pl.ds(pl.multiple_of(block * units, units), units)
                value = lax.dot_general(cot[slot], room[pl.ds(pl.multiple_of(k * units, units), units), :],
                                        (((1,), (1,)), ((), ())), preferred_element_type=full)
                value = (value * gelu_slope(slope_room(block)[...])).astype(low)
                gpre[slot, :, of] = value
                unit_ref[:, of] += jnp.sum(value.astype(full), axis=0, keepdims=True)

                @pl.when(n + 1 < early)
                def _():
                    slope_load(n + 1, block).start()
                return carry
            lax.fori_loop(0, blocks // 2, unit_part, 0)
        gpre_store(n).start()
        return carry
    lax.fori_loop(0, early, near_band, 0)
    for n in range(max(early - 2, 0), early):
        gpre_store(n).wait()
    for r in range(seq // band):
        part_store(r).wait()
    hidden_store.wait()
    for index in range(4):
        for message in range(7):
            copy(index, message, *sends[message]).wait_send()
    for step in range(1, sp_size):
        for part in range(3):
            slab_copy(step, part, lax.rem(sp + step, sp_size), sp).wait_send()

    @pl.when(pair != sp)
    def _():
        turn_copy(turn_dp).wait_send()

    tokens.finish()
    cotangents.settle(3)
    cotangents.finish()
    for way in (0, 1):
        @pl.when(along(way) == 0)
        def _():
            part_hop(way).wait_send()

        @pl.when(along(way) == 1)
        def _():
            part_hop(way).wait_recv()


def front(sp_size, dp_size, lengths, qkv_weight, out_weight, up_weight, down_weight, tokens, cotangent, gains, shifts, qkv_bias,
          unit_bias):
    rows, wide = out_weight.shape
    units = up_weight.shape[0]
    seq = tokens.shape[0] * sp_size
    width = wide // sp_size
    all_units = units * dp_size
    full, low = jnp.float32, jnp.bfloat16
    half = ROT // 2
    freq = base_freq ** (-jnp.arange(half, dtype=full) * (2.0 / ROT))
    freq = jnp.concatenate([freq, freq, jnp.zeros((128 - ROT,), full)])[None]
    hbm = pl.BlockSpec(memory_space=pltpu.HBM)
    vmem = pl.BlockSpec(memory_space=pltpu.VMEM)
    dma = pltpu.SemaphoreType.DMA
    shape = jax.ShapeDtypeStruct
    qkv_shape = (rows * sp_size * dp_size, 3 * width)
    return pl.pallas_call(
        functools.partial(front_kernel, sp_size),
        out_shape=[shape(qkv_shape, low), shape((rows * dp_size, wide), low), shape((all_units, wide), low),
                   shape((all_units, wide), low), shape((seq, wide), low), shape((seq, wide), low),
                   shape((seq, wide), low), shape((seq, wide), low), shape((seq, all_units), low), shape((seq, all_units), full),
                   shape((seq, wide), low), shape((2, seq // sp_size, wide), low), shape((seq, all_units), low)]
        + [shape((seq, 128), full)] * 4 + [shape((1, all_units), full)] + [shape((seq, width), low)] * 4,
        in_specs=[pl.BlockSpec(memory_space=pltpu.SMEM)] + [vmem] * 11,
        out_specs=[hbm] * 13 + [vmem] * 9,
        scratch_shapes=[pltpu.VMEM((seq, wide), low)] * 3 + [
            pltpu.VMEM(qkv_shape, low), pltpu.VMEM((all_units, wide), low),
            pltpu.VMEM((seq, all_units), low), pltpu.VMEM((2, seq, units), full),
            pltpu.VMEM((2, 256, wide), low), pltpu.VMEM((2, 256, all_units), low),
            dma((4, 7)), dma((4, 7)), dma((sp_size - 1, 3)), dma((sp_size - 1, 3)), dma((8,)), dma, dma,
            dma((2, sp_size)), dma((2, sp_size)), dma((2, sp_size)), dma((2, sp_size)),
            dma((4,)), dma((2,)), dma((2,)), dma((seq // 256,)), dma((2,)), dma((2,)), dma((all_units // units,)), dma((4,))],
        compiler_params=pltpu.CompilerParams(collective_id=0, has_side_effects=True, vmem_limit_bytes=62 << 20),
        cost_estimate=pl.CostEstimate(flops=26 * 10 ** 9, bytes_accessed=300 * 1000 * 1000, transcendentals=0),
        name="front",
    )(lengths, qkv_weight, out_weight, up_weight, down_weight, tokens, cotangent, freq, gains, shifts, qkv_bias, unit_bias)

CHUNK = 512


def add_into(target, *others):
    step_rows = 32

    def step(i, carry):
        at = pl.ds(pl.multiple_of(i * step_rows, step_rows), step_rows)
        total = target[at, :].astype(jnp.float32)
        for other in others:
            total = total + other[at, :].astype(jnp.float32)
        target[at, :] = total.astype(jnp.bfloat16)
        return carry

    lax.fori_loop(0, target.shape[0] // step_rows, step, 0)


class Square:
    def __init__(self, sp_size, lent, sib_send, sib_recv, one_send, one_recv, two_send, two_recv):
        self.dp, self.sp, self.sp_size = lax.axis_index("dp"), lax.axis_index("sp"), sp_size
        self.core, self.chip = self.dp % 2, self.dp // 2
        self.x, self.y = self.chip % 2, self.chip // 2
        self.sibling = self.dp + 1 - 2 * self.core
        self.across_x, self.across_y = self.dp + 2 - 4 * self.x, self.dp + 4 - 8 * self.y
        self.first = self.across_y * (1 - self.core) + self.across_x * self.core
        self.second = self.across_x * (1 - self.core) + self.across_y * self.core
        self.second_mask = 1 + self.core
        self.lent = lent
        self.sib_send, self.sib_recv, self.one_send, self.one_recv, self.two_send, self.two_recv = (
            sib_send, sib_recv, one_send, one_recv, two_send, two_recv)

    def chip_of(self, mask):
        return lax.rem(self.x + lax.rem(mask, 2), 2) + 2 * lax.rem(self.y + mask // 2, 2)

    def greet(self, barrier):
        for other in (self.first, self.second, self.sibling):
            pl.semaphore_signal(barrier, inc=1, device_id=(other, self.sp), device_id_type=MESH)
        for step in range(1, self.sp_size):
            pl.semaphore_signal(
                barrier, inc=1, device_id=(self.dp, lax.rem(self.sp + step, self.sp_size)), device_id_type=MESH)


def remote(source, target, send, recv, device):
    return pltpu.make_async_remote_copy(
        src_ref=source, dst_ref=target, send_sem=send, recv_sem=recv, device_id=device, device_id_type=MESH)


class Wide:
    def __init__(self, place, index, left, right, width, sums, sib, one, two):
        self.place, self.index, self.left, self.right, self.width = place, index, left, right, width
        self.sums, self.sib, self.one, self.two = sums, sib, one, two
        self.units = sums.shape[1]

    def product(self, block, store):
        at = pl.ds(pl.multiple_of(block * self.units, self.units), self.units)

        def columns(part, carry):
            to = pl.ds(pl.multiple_of(part * CHUNK, CHUNK), CHUNK)
            store(to, lax.dot_general(
                self.left[:, at], self.right[:, to], (((0,), (0,)), ((), ())),
                preferred_element_type=jnp.float32))
            return carry
        lax.fori_loop(0, self.width // CHUNK, columns, 0)

    def sib_copy(self, slot):
        p = self.place
        return remote(p.lent.at[slot, :, :self.width], self.sib.at[p.chip_of(3 - slot), :, :self.width],
                      p.sib_send.at[self.index, slot], p.sib_recv.at[self.index, slot], (p.sibling, p.sp))

    def for_sibling(self, previous):
        p = self.place

        def step(slot, carry):
            if previous is not None:
                previous.sib_copy(slot).wait_send()

            def store(to, total):
                p.lent[slot, :, to] = total.astype(jnp.bfloat16)
            self.product(p.chip_of(3 - slot) * 2 + 1 - p.core, store)
            self.sib_copy(slot).start()
            return carry
        lax.fori_loop(0, 4, step, 0)

    def own(self, mask, slot):
        at = self.place.chip_of(mask)
        self.sib_copy(slot).wait_recv()

        def store(to, total):
            self.sums[mask, :, to] = (total + self.sib[at, :, to].astype(jnp.float32)).astype(jnp.bfloat16)
        self.product(at * 2 + self.place.core, store)

    def for_self(self):
        core = self.place.core

        def leave(slot, carry):
            mask = 3 - slot * (1 + core)
            self.own(mask, 3 - mask)
            self.first_copy(slot).start()
            return carry
        lax.fori_loop(0, 2, leave, 0)

        def stay(slot, carry):
            mask = self.place.second_mask * (1 - slot)
            self.own(mask, 3 - mask)
            return carry
        lax.fori_loop(0, 2, stay, 0)

    def block(self, mask):
        return self.sums.at[mask, :, :self.width]

    def from_first(self, slot):
        return self.one.at[slot, :, :self.width]

    def from_second(self):
        return self.two.at[:, :self.width]

    def first_copy(self, slot):
        p = self.place
        return remote(self.block(3 - slot * (1 + p.core)), self.from_first(slot), p.one_send.at[self.index, slot],
                      p.one_recv.at[self.index, slot], (p.first, p.sp))

    def second_copy(self):
        p = self.place
        return remote(self.block(p.second_mask), self.from_second(), p.two_send.at[self.index],
                      p.two_recv.at[self.index], (p.second, p.sp))

    def onward(self):
        self.first_copy(0).wait_recv()
        add_into(self.block(self.place.second_mask), self.from_first(0))
        self.second_copy().start()

    def finish(self):
        self.first_copy(1).wait_recv()
        self.second_copy().wait_recv()
        add_into(self.block(0), self.from_first(1), self.from_second())

    def drain(self):
        for slot in (0, 1):
            self.first_copy(slot).wait_send()
        self.second_copy().wait_send()


class Dense(Wide):
    def __init__(self, place, index, left, right, width, sums, sib, one, two, part):
        self.place, self.index, self.left, self.right, self.width = place, index, left, right, width
        self.sums, self.sib, self.one, self.two, self.part = sums, sib, one, two, part
        self.units, self.rows = sums.shape[0], one.shape[1]

    def sib_copy(self, slot):
        p = self.place
        return remote(self.part, self.sib, p.sib_send.at[self.index, 0], p.sib_recv.at[self.index, 0], (p.sibling, p.sp))

    def for_sibling(self, previous):
        def store(to, total):
            self.part[:, to] = total.astype(jnp.bfloat16)
        self.product(1 - self.place.core, store)
        self.sib_copy(0).start()

    def for_self(self):
        self.sib_copy(0).wait_recv()

        def store(to, total):
            self.sums[:, to] = (total + self.sib[:, to].astype(jnp.float32)).astype(jnp.bfloat16)
        self.product(self.place.core, store)
        for slot in (0, 1):
            self.first_copy(slot).start()

    def block(self, mask):
        return self.sums.at[pl.ds(pl.multiple_of(self.place.chip_of(mask) * self.rows, self.rows), self.rows)]


class Fold:
    def __init__(self, place, source, inbox, stage, stage_sem, send, recv, begun=1):
        self.begun = begun
        self.place, self.source, self.inbox, self.stage = place, source, inbox, stage
        self.stage_sem, self.send, self.recv = stage_sem, send, recv
        self.rows = stage.shape[0]

    def along(self, way):
        last = self.place.sp_size - 1
        return self.place.sp if way == 0 else last - self.place.sp

    def rows_of(self, way, step):
        count = self.place.sp_size
        owner = self.along(way) + count - step
        owner = owner if way == 0 else count - 1 - owner
        return self.source.at[pl.ds(pl.multiple_of(owner * self.rows, self.rows), self.rows)]

    def copy(self, way, step, own):
        p = self.place
        to = lax.rem(p.sp + (1 if way == 0 else p.sp_size - 1), p.sp_size)
        source = self.rows_of(way, step) if own else self.inbox.at[way, max(step - 2, 0)]
        return remote(source, self.inbox.at[way, step - 1], self.send.at[way, step - 1],
                      self.recv.at[way, step - 1], (p.dp, to))

    def take(self, rows):
        c = pltpu.make_async_copy(rows, self.stage, self.stage_sem)
        c.start()
        c.wait()

    def step(self, step):
        last = self.place.sp_size - 1
        for way in (0, 1):
            if step >= self.begun:
                @pl.when(self.along(way) == 0)
                def _():
                    self.copy(way, step, True).start()

            if step > 1:
                @pl.when((self.along(way) > 0) & (self.along(way) < step) & (self.along(way) < last))
                def _():
                    self.take(self.rows_of(way, step))
                    if step > self.begun:
                        self.copy(way, step - 1, False).wait_recv()
                    add_into(self.inbox.at[way, step - 2], self.stage)
                    self.copy(way, step, False).start()

    def finish(self):
        last = self.place.sp_size - 1
        self.take(self.source.at[pl.ds(pl.multiple_of(self.place.sp * self.rows, self.rows), self.rows)])
        for way in (0, 1):
            @pl.when(self.along(way) > 0)
            def _():
                self.copy(way, last, False).wait_recv()
                add_into(self.stage, self.inbox.at[way, last - 1])

    def drain(self):
        last = self.place.sp_size - 1
        for way in (0, 1):
            for step in range(1, last + 1):
                if step >= self.begun:
                    @pl.when(self.along(way) == 0)
                    def _():
                        self.copy(way, step, True).wait_send()

                if step > 1:
                    @pl.when((self.along(way) > 0) & (self.along(way) < step) & (self.along(way) < last))
                    def _():
                        self.copy(way, step, False).wait_send()


def middle_kernel(sp_size, len_ref, cot_hbm, out_hbm, q_hbm, k_hbm, v_hbm, pre_hbm, hidden_hbm, down_hbm, up_hbm, qkv_hbm,
                  tok_hbm, part_hbm, hop_hbm, near_hbm, attn_hbm, unit_ref, gain_ref, cos_ref, sin_ref, mean_s, inv_s,
                  down_out, slab_out, gpre_out, hat_out, hat_in, proj_out, gout_out, red_out, small_ref,
                  cot, left, tok, gpre, up_w, qkv_w, pre, gctx, gproj, dq, dk, dv,
                  lent, down_sum, down_sib, down_one, down_two, inbox, stage,
                  load_sem, stream_sem, store_sem, stage_sem, sib_send, sib_recv, one_send, one_recv, two_send, two_recv,
                  fold_send, fold_recv, hat_send, hat_recv, sib_free, one_free, two_free, near_sem, tok_sem):
    full, low = jnp.float32, jnp.bfloat16
    place = Square(sp_size, lent, sib_send, sib_recv, one_send, one_recv, two_send, two_recv)
    seq, wide = cot.shape
    width = gctx.shape[1]
    heads = width // HEAD
    units = down_sum.shape[1]
    blocks = up_w.shape[0] // units
    out_rows = out_hbm.shape[0]
    band = 256
    bands = seq // band
    scale = HEAD ** -0.5

    def load(source, target, which):
        c = pltpu.make_async_copy(source, target, load_sem.at[which])
        c.start()
        return c

    early = [load(cot_hbm, cot, 0), load(hidden_hbm, left, 1)]

    def down_load(block, slot):
        return pltpu.make_async_copy(
            down_hbm.at[pl.ds(pl.multiple_of(block * units, units), units)],
            up_w.at[pl.ds(pl.multiple_of(out_rows + slot * units, units), units)], stream_sem.at[0, slot])

    upper = 2 * place.sp // sp_size

    def hat_rows(r):
        return pl.ds(pl.multiple_of(((1 - upper) * (bands - 1 - r) + upper * r) * band, band), band)

    far = bands - NEAR
    near = pl.ds(pl.multiple_of(upper * far * band, band), NEAR * band)
    far_rows = pl.ds(pl.multiple_of((1 - upper) * NEAR * band, band), far * band)
    near_load = pltpu.make_async_copy(near_hbm.at[near], gpre.at[near], near_sem)

    def pre_load(block, slot):
        return pltpu.make_async_copy(
            pre_hbm.at[far_rows, pl.ds(pl.multiple_of(block * units, units), units)], pre.at[slot], stream_sem.at[1, slot])

    hops = []
    for way in (0, 1):
        hops.append(load(hop_hbm.at[way], inbox.at[way, 0], 6 + way))

    barrier = pltpu.get_barrier_semaphore()
    place.greet(barrier)
    pl.semaphore_wait(barrier, 2 + sp_size)
    fold = Fold(place, part_hbm, inbox, stage, stage_sem, fold_send, fold_recv, begun=2)
    for way in (0, 1):
        hops[way].wait()
    fold.step(2)
    early.append(load(out_hbm, up_w.at[pl.ds(0, out_rows)], 2))
    for i, source in enumerate((q_hbm, k_hbm, v_hbm)):
        early.append(load(source, qkv_w.at[pl.ds(0, seq), pl.ds(i * width, width)], 3 + i))
    for slot in (0, 1):
        down_load(slot, slot).start()
        pre_load(slot, slot).start()
    small_ref[...] = jnp.zeros_like(small_ref)
    gain_row, shift_row, bias_row, unit_row = 0, 2, 4, 7
    per_row = wide // (sp_size * units)
    last_row = unit_row + blocks // per_row

    early[0].wait()

    def mask_rows(i, carry):
        at = pl.ds(pl.multiple_of(i * 32, 32), 32)
        row = i * 32 + lax.broadcasted_iota(jnp.int32, (32, wide), 0)
        cot[at, :] = jnp.where(row < len_ref[0], cot[at, :].astype(full), 0.0).astype(low)
        return carry
    lax.fori_loop(0, seq // 32, mask_rows, 0)
    stores = [pltpu.make_async_copy(cot, gout_out, store_sem.at[0])]
    stores[0].start()

    def own_rows(i, carry):
        at = pl.ds(pl.multiple_of(place.sp * (seq // sp_size) + i * 32, 32), 32)
        return carry + jnp.sum(cot[at, :].astype(full), axis=0, keepdims=True)
    small_ref[last_row:last_row + 1, :] = lax.fori_loop(0, seq // sp_size // 32, own_rows, jnp.zeros((1, wide), full))

    down = Wide(place, 0, left, cot, wide, down_sum, down_sib, down_one, down_two)
    early[1].wait()
    down.for_sibling(None)
    down.for_self()
    early[2].wait()

    def context_band(r, carry):
        at = pl.ds(pl.multiple_of(r * band, band), band)
        gctx[at, :] = lax.dot_general(
            cot[at, :], up_w[:out_rows, :], (((1,), (1,)), ((), ())), preferred_element_type=full).astype(low)
        return carry
    lax.fori_loop(0, bands, context_band, 0)
    attn_load = load(attn_hbm, left, 1)
    near_load.start()
    late_rows = pl.ds(out_rows + 2 * units, up_w.shape[0] - out_rows - 2 * units)
    up_load = load(up_hbm.at[late_rows], up_w.at[late_rows], 8)
    pl.semaphore_signal(sib_free, inc=1, device_id=(place.sibling, place.sp), device_id_type=MESH)
    for c in early[3:]:
        c.wait()

    def head(h, carry):
        lanes = pl.ds(pl.multiple_of(h * HEAD, HEAD), HEAD)
        k_lanes = pl.ds(pl.multiple_of(width + h * HEAD, HEAD), HEAD)
        v_lanes = pl.ds(pl.multiple_of(2 * width + h * HEAD, HEAD), HEAD)
        dk[...] = jnp.zeros_like(dk)
        dv[...] = jnp.zeros_like(dv)
        for begin in range(0, seq, band):
            end = begin + band
            q, g = qkv_w[begin:end, lanes], gctx[begin:end, lanes]
            k, v = qkv_w[:end, k_lanes], qkv_w[:end, v_lanes]
            p = weights_of(q, k, begin, len_ref[0], scale)
            gp = lax.dot_general(g, v, (((1,), (1,)), ((), ())), preferred_element_type=full)
            ds = (p * (gp - jnp.sum(p * gp, axis=-1, keepdims=True))).astype(low)
            dq[begin:end, :] = jnp.dot(ds, k, preferred_element_type=full) * scale
            dk[:end, :] += lax.dot_general(ds, q, (((0,), (0,)), ((), ())), preferred_element_type=full)
            dv[:end, :] += lax.dot_general(p.astype(low), g, (((0,), (0,)), ((), ())), preferred_element_type=full)

        def back(r, sums):
            at = pl.ds(pl.multiple_of(r * band, band), band)
            cos_t, sin_t = cos_ref[at, :], -sin_ref[at, :]
            pieces = (turn(dq[at, :].astype(low).astype(full), cos_t, sin_t).astype(low),
                      turn((dk[at, :] * scale).astype(low).astype(full), cos_t, sin_t).astype(low),
                      dv[at, :].astype(low))
            out = []
            for part, (piece, total) in enumerate(zip(pieces, sums)):
                gproj[at, pl.ds(pl.multiple_of(part * width + h * HEAD, HEAD), HEAD)] = piece
                out.append(total + jnp.sum(piece.astype(full), axis=0, keepdims=True))
            return tuple(out)
        sums = lax.fori_loop(0, bands, back, (jnp.zeros((1, HEAD), full),) * 3)
        for part, total in enumerate(sums):
            small_ref[bias_row + part:bias_row + part + 1,
                      pl.ds(pl.multiple_of(place.sp * width + h * HEAD, HEAD), HEAD)] = total
        return carry
    lax.fori_loop(0, heads, head, 0)
    stores.append(pltpu.make_async_copy(gproj, proj_out, store_sem.at[1]))
    stores[1].start()
    qkv_load = load(qkv_hbm, qkv_w, 3)

    def unit_block(block, carry):
        slot = lax.rem(block, 2)
        down_load(block, slot).wait()
        pre_load(block, slot).wait()
        of = pl.ds(pl.multiple_of(block * units, units), units)
        room = pl.ds(pl.multiple_of(out_rows + slot * units, units), units)

        def far_band(r, total):
            at = pl.ds(pl.multiple_of(((1 - upper) * NEAR + r) * band, band), band)
            value = lax.dot_general(cot[at, :], up_w[room, :], (((1,), (1,)), ((), ())), preferred_element_type=full)
            value = (value * gelu_slope(pre[slot, pl.ds(pl.multiple_of(r * band, band), band), :])).astype(low)
            gpre[at, of] = value
            return total + jnp.sum(value.astype(full), axis=0, keepdims=True)
        small_ref[pl.ds(unit_row + block // per_row, 1),
                  pl.ds(pl.multiple_of((lax.rem(block, per_row) * sp_size + place.sp) * units, units), units)] = (
            lax.fori_loop(0, far, far_band, unit_ref[:, of]))

        @pl.when(block + 2 < blocks)
        def _():
            down_load(block + 2, slot).start()
            pre_load(block + 2, slot).start()
        return carry

    down.onward()
    fold.step(3)
    lax.fori_loop(0, blocks, unit_block, 0)
    used = out_rows + 2 * units
    up_loads = [load(up_hbm.at[pl.ds(0, used)], up_w.at[pl.ds(0, used)], 0), up_load]

    def tok_load(r):
        return pltpu.make_async_copy(tok_hbm.at[hat_rows(r)], tok.at[r % 2], tok_sem.at[r % 2])
    tok_load(0).start()
    tok_load(1).start()
    near_load.wait()
    gpre_store = pltpu.make_async_copy(gpre, gpre_out, store_sem.at[2])
    gpre_store.start()
    stores[0].wait()
    def hat_store(r):
        return pltpu.make_async_copy(cot.at[hat_rows(r)], hat_out.at[hat_rows(r)], store_sem.at[3 + r])

    def hat_hop(way):
        to = lax.rem(place.sp + (1 if way == 0 else sp_size - 1), sp_size)
        return remote(cot.at[hat_rows(0)], hat_in.at[way], hat_send.at[way], hat_recv.at[way], (place.dp, to))

    def hat_band(r):
        at = hat_rows(r)
        tok_load(r).wait()

        def columns(c, carry):
            to = pl.ds(pl.multiple_of(c * band, band), band)
            from_mlp = jnp.dot(gpre[at, :], up_w[:, to], preferred_element_type=full)
            from_attn = lax.dot_general(gproj[at, :], qkv_w[to, :], (((1,), (1,)), ((), ())), preferred_element_type=full)
            normed = (tok[r % 2, :, to].astype(full) - mean_s[at, 0:1]) * inv_s[at, 0:1]
            small_ref[gain_row:gain_row + 1, to] += jnp.sum(from_attn * normed, axis=0, keepdims=True)
            small_ref[gain_row + 1:gain_row + 2, to] += jnp.sum(from_mlp * normed, axis=0, keepdims=True)
            small_ref[shift_row:shift_row + 1, to] += jnp.sum(from_attn, axis=0, keepdims=True)
            small_ref[shift_row + 1:shift_row + 2, to] += jnp.sum(from_mlp, axis=0, keepdims=True)
            cot[at, to] = (from_attn * gain_ref[0:1, to].astype(full) + from_mlp * gain_ref[1:2, to].astype(full)).astype(low)
            return carry
        lax.fori_loop(0, wide // band, columns, 0)
        hat_store(r).start()
        if r + 2 < bands:
            tok_load(r + 2).start()

    qkv = Wide(place, 1, left, gproj, 3 * width, down_sum, down_sib, down_one, down_two)
    attn_load.wait()
    pl.semaphore_wait(sib_free, 1)
    qkv.for_sibling(down)
    qkv_load.wait()
    for c in up_loads:
        c.wait()
    hat_band(0)
    for way in (0, 1):
        @pl.when(fold.along(way) == 0)
        def _():
            hat_hop(way).start()
    down.finish()
    stores.append(pltpu.make_async_copy(down.block(0), down_out, store_sem.at[3 + bands]))
    stores[2].start()
    pl.semaphore_signal(one_free, inc=1, device_id=(place.first, place.sp), device_id_type=MESH)
    pl.semaphore_signal(two_free, inc=1, device_id=(place.second, place.sp), device_id_type=MESH)
    down.drain()
    stores[2].wait()
    pl.semaphore_wait(one_free, 1)
    qkv.for_self()
    hat_band(1)
    pl.semaphore_wait(two_free, 1)
    qkv.onward()
    for r in range(2, bands):
        hat_band(r)
    fold.finish()
    stores.append(pltpu.make_async_copy(stage, red_out, store_sem.at[4 + bands]))
    stores[-1].start()
    qkv.finish()
    stores.append(pltpu.make_async_copy(qkv.block(0), slab_out, store_sem.at[5 + bands]))
    stores[-1].start()
    for r in range(bands):
        hat_store(r).wait()
    for which in (1, 3, 4):
        stores[which].wait()
    gpre_store.wait()
    for slot in range(4):
        qkv.sib_copy(slot).wait_send()
    qkv.drain()
    fold.drain()
    for way in (0, 1):
        @pl.when(fold.along(way) == 0)
        def _():
            hat_hop(way).wait_send()

        @pl.when(fold.along(way) == 1)
        def _():
            hat_hop(way).wait_recv()


def middle(sp_size, dp_size, lengths, cotangent, out_own, queries, key_rows, values, pre_act, hidden, down_own, up_own, qkv_own,
           tokens, partial_out, part_hop, near_pre, attn_in, unit_sums, gains, cos_t, sin_t, means, inverses):
    seq, wide = tokens.shape
    width = queries.shape[1]
    units = up_own.shape[0] // dp_size
    own = seq // sp_size
    full, low = jnp.float32, jnp.bfloat16
    hbm = pl.BlockSpec(memory_space=pltpu.HBM)
    vmem = pl.BlockSpec(memory_space=pltpu.VMEM)
    dma = pltpu.SemaphoreType.DMA
    shape = jax.ShapeDtypeStruct

    def v(*dims, kind=low):
        return pltpu.VMEM(dims, kind)
    bands = seq // 256
    return pl.pallas_call(
        functools.partial(middle_kernel, sp_size),
        out_shape=[shape((units, wide), low), shape((units, 3 * width), low), shape(hidden.shape, low), shape((seq, wide), low),
                   shape((2, own, wide), low),
                   shape((seq, 3 * width), low),
                   shape((seq, wide), low), shape((own, wide), low), shape((16, wide), full)],
        in_specs=[pl.BlockSpec(memory_space=pltpu.SMEM)] + [hbm] * 15 + [vmem] * 6,
        out_specs=[hbm] * 8 + [vmem],
        scratch_shapes=[
            v(seq, wide), v(seq, wide), v(2, 256, wide), v(*hidden.shape), v(*up_own.shape), v(*qkv_own.shape),
            v(2, (seq // 256 - NEAR) * 256, units, kind=full),
            v(seq, width), v(seq, 3 * width), v(seq, HEAD, kind=full), v(seq, HEAD, kind=full), v(seq, HEAD, kind=full),
            v(4, units, wide), v(4, units, wide), v(4, units, wide), v(2, units, wide), v(units, wide),
            v(2, sp_size - 1, own, wide), v(own, wide),
            dma((9,)), dma((2, 2)), dma((7 + bands,)), dma, dma((2, 4)), dma((2, 4)), dma((2, 2)), dma((2, 2)), dma((2,)), dma((2,)),
            dma((2, sp_size - 1)), dma((2, sp_size - 1)), dma((2,)), dma((2,)),
            pltpu.SemaphoreType.REGULAR, pltpu.SemaphoreType.REGULAR, pltpu.SemaphoreType.REGULAR, dma, dma((2,))],
        compiler_params=pltpu.CompilerParams(collective_id=3, has_side_effects=True, vmem_limit_bytes=67043328),
        cost_estimate=pl.CostEstimate(flops=40 * 10 ** 9, bytes_accessed=90 * 1000 * 1000, transcendentals=0),
        name="middle",
    )(lengths, cotangent, out_own, queries, key_rows, values, pre_act, hidden, down_own, up_own, qkv_own, tokens, partial_out,
      part_hop, near_pre, attn_in, unit_sums, gains, cos_t, sin_t, means, inverses)


def back_kernel(sp_size, cot_hbm, pre_hbm, mlp_hbm, ctx_hbm, hat_hbm, hop_hbm, slab_hbm, small_ref,
                up_out, qkv_out, dense_out, red_out, small_out,
                left, right, cot, ctx, lent,
                up_sum, dense_sum, up_sib, dense_sib, up_one, dense_one, up_two, dense_two,
                dense_part, slab, small_acc, small_in, small_z, small_fin, inbox, stage,
                load_sem, store_sem, stage_sem, sib_send, sib_recv, one_send, one_recv, two_send, two_recv,
                slab_send, slab_recv, turn_send, turn_recv, small_send, small_recv, z_send, z_recv,
                fold_send, fold_recv, plane_send, plane_recv):
    place = Square(sp_size, lent, sib_send, sib_recv, one_send, one_recv, two_send, two_recv)
    dp, sp = place.dp, place.sp
    per = 2
    pair, lane = dp // per, dp % per
    turn_dp = sp * per + lane
    slab_width = slab.shape[1]
    head_width = slab_width // 3
    rows = dense_one.shape[1]
    wide = left.shape[1]

    def load(source, target, which):
        c = pltpu.make_async_copy(source, target, load_sem.at[which])
        c.start()
        return c

    slab_load = load(slab_hbm, slab, 0)
    hops = [load(hop_hbm.at[way], inbox.at[way, 0], 1 + way) for way in (0, 1)]
    loads = [load(ctx_hbm, ctx, 3), load(cot_hbm, cot, 4)]

    barrier = pltpu.get_barrier_semaphore()
    for step in range(1, 8):
        pl.semaphore_signal(barrier, inc=1, device_id=(lax.rem(dp + step, 8), sp), device_id_type=MESH)
    for step in range(1, sp_size):
        pl.semaphore_signal(barrier, inc=1, device_id=(dp, lax.rem(sp + step, sp_size)), device_id_type=MESH)

    @pl.when(pair != sp)
    def _():
        pl.semaphore_signal(barrier, inc=1, device_id=(turn_dp, pair), device_id_type=MESH)

    pl.semaphore_wait(barrier, 6 + sp_size + jnp.where(pair != sp, 1, 0))
    fold = Fold(place, hat_hbm, inbox, stage, stage_sem, fold_send, fold_recv, begun=2)

    def small_copy(stage_of):
        partner = (place.sibling, place.across_x, place.across_y)[stage_of]
        return remote(small_ref if stage_of == 0 else small_acc.at[stage_of - 1], small_in.at[stage_of],
                      small_send.at[stage_of], small_recv.at[stage_of], (partner, sp))

    def small_step(stage_of):
        small_copy(stage_of).wait_recv()
        before = small_ref[...] if stage_of == 0 else small_acc[stage_of - 1]
        small_acc[stage_of] = before + small_in[stage_of]

    share = small_ref.shape[1] // 8

    def columns_of(owner):
        return pl.ds(pl.multiple_of(owner * share, share), share)

    def z_copy(step):
        return remote(small_acc.at[2, :, columns_of(dp)], small_z.at[sp], z_send.at[step - 1], z_recv.at[step - 1],
                      (dp, lax.rem(sp + step, sp_size)))

    def z_arrival(step):
        origin = lax.rem(sp + sp_size - step, sp_size)
        return remote(small_acc.at[2, :, columns_of(dp)], small_z.at[origin], z_send.at[step - 1], z_recv.at[step - 1],
                      (dp, origin))

    def plane_copy(step, owner, target):
        at = small_fin.at[:, columns_of(owner)]
        return remote(at, at, plane_send.at[step - 1], plane_recv.at[step - 1], (target, sp))

    def turn_copy():
        return remote(dense.block(0), dense_out, turn_send, turn_recv, (turn_dp, pair))

    def slab_rows(owner):
        return pl.ds(pl.multiple_of(owner * rows, rows), rows)

    def slab_columns(part, owner):
        return pl.ds(pl.multiple_of(part * wide + owner * head_width, head_width), head_width)

    def slab_copy(step, part, origin, there):
        return remote(slab.at[slab_rows(there), pl.ds(part * head_width, head_width)],
                      qkv_out.at[:, slab_columns(part, origin)],
                      slab_send.at[step - 1, part], slab_recv.at[step - 1, part], (dp, there))

    stores = []

    def store(source, target):
        c = pltpu.make_async_copy(source, target, store_sem.at[len(stores)])
        c.start()
        stores.append(c)

    small_copy(0).start()
    dense = Dense(place, 0, ctx, cot, wide, dense_sum, dense_sib, dense_one, dense_two, dense_part)
    up = Wide(place, 1, left, right, wide, up_sum, up_sib, up_one, up_two)
    for way in (0, 1):
        hops[way].wait()
    fold.step(2)
    slab_load.wait()
    for step in range(1, sp_size):
        for part in range(3):
            slab_copy(step, part, sp, lax.rem(sp + step, sp_size)).start()
    for part in range(3):
        store(slab.at[slab_rows(sp), pl.ds(part * head_width, head_width)], qkv_out.at[:, slab_columns(part, sp)])
    loads += [load(pre_hbm, left, 5), load(mlp_hbm, right, 6)]
    small_step(0)
    small_copy(1).start()
    loads[0].wait()
    loads[1].wait()
    dense.for_sibling(None)
    dense.for_self()
    loads[2].wait()
    loads[3].wait()
    up.for_sibling(None)
    small_step(1)
    small_copy(2).start()
    dense.onward()
    up.for_self()
    small_step(2)
    for step in range(1, sp_size):
        z_copy(step).start()
    small_z[sp] = small_acc[2, :, columns_of(dp)]
    dense.finish()

    @pl.when(pair != sp)
    def _():
        turn_copy().start()

    @pl.when(pair == sp)
    def _():
        c = pltpu.make_async_copy(dense.block(0), dense_out, store_sem.at[5])
        c.start()
        c.wait()

    fold.step(3)
    up.onward()
    for step in range(1, sp_size):
        z_arrival(step).wait_recv()
    total = small_z[0]
    for origin in range(1, sp_size):
        total = total + small_z[origin]
    small_fin[:, columns_of(dp)] = total
    for step in range(1, 8):
        plane_copy(step, dp, lax.rem(dp + step, 8)).start()
    up.finish()
    store(up.block(0), up_out)
    fold.finish()
    store(stage, red_out)
    for slot in range(4):
        up.sib_copy(slot).wait_send()
    dense.sib_copy(0).wait_send()
    for array in (dense, up):
        array.drain()
    for stage_of in range(3):
        small_copy(stage_of).wait_send()
    fold.drain()
    for step in range(1, sp_size):
        z_copy(step).wait_send()
        for part in range(3):
            slab_copy(step, part, lax.rem(sp + sp_size - step, sp_size), sp).wait_recv()
            slab_copy(step, part, sp, lax.rem(sp + step, sp_size)).wait_send()

    @pl.when(pair != sp)
    def _():
        turn_copy().wait_recv()
        turn_copy().wait_send()

    for step in range(1, 8):
        origin = lax.rem(dp + 8 - step, 8)
        plane_copy(step, origin, origin).wait_recv()
        plane_copy(step, dp, origin).wait_send()
    small_out[...] = small_fin[...]
    for c in stores:
        c.wait()


def reduce_gradients(sp_size, rows, grad_out, grad_pre, mlp_in, context, grad_hat, hat_hop, slab_sum, small):
    seq, wide = mlp_in.shape
    slab, slab_width = slab_sum.shape
    units = slab
    own = seq // sp_size
    full, low = jnp.float32, jnp.bfloat16
    hbm = pl.BlockSpec(memory_space=pltpu.HBM)
    vmem = pl.BlockSpec(memory_space=pltpu.VMEM)
    dma = pltpu.SemaphoreType.DMA
    shape = jax.ShapeDtypeStruct

    def v(*dims, kind=low):
        return pltpu.VMEM(dims, kind)
    scratch = [
        v(seq, wide), v(seq, wide), v(seq, wide), v(seq, context.shape[1]), v(4, units, wide),
        v(4, units, wide), v(slab, wide), v(4, units, wide), v(slab, wide),
        v(2, units, wide), v(2, rows, wide), v(units, wide), v(rows, wide),
        v(slab, wide), v(slab, slab_width),
        v(3, *small.shape, kind=full), v(3, *small.shape, kind=full), v(sp_size, small.shape[0], small.shape[1] // 8, kind=full), v(*small.shape, kind=full),
        v(2, sp_size - 1, own, wide), v(own, wide),
        dma((7,)), dma((6,)), dma, dma((2, 4)), dma((2, 4)), dma((2, 2)), dma((2, 2)), dma((2,)), dma((2,)),
        dma((sp_size - 1, 3)), dma((sp_size - 1, 3)), dma, dma, dma((3,)), dma((3,)),
        dma((sp_size - 1,)), dma((sp_size - 1,)), dma((2, sp_size - 1)), dma((2, sp_size - 1)), dma((7,)), dma((7,)),
    ]
    return pl.pallas_call(
        functools.partial(back_kernel, sp_size),
        out_shape=[shape((units, wide), low), shape((rows, 3 * wide), low), shape((rows, wide), low), shape((own, wide), low),
                   shape(small.shape, full)],
        in_specs=[hbm] * 7 + [vmem], out_specs=[hbm] * 4 + [vmem],
        scratch_shapes=scratch,
        compiler_params=pltpu.CompilerParams(collective_id=1, has_side_effects=True, vmem_limit_bytes=62 << 20),
        cost_estimate=pl.CostEstimate(flops=9 * 10 ** 9, bytes_accessed=200 * 1000 * 1000, transcendentals=0),
        name="reduce_gradients",
    )(grad_out, grad_pre, mlp_in, context, grad_hat, hat_hop, slab_sum, small)

def finish_kernel(len_ref, tok_ref, cot_ref, sum_ref, hat_ref, down_ref, up_ref, qkv_ref, dense_ref, bias_ref, small_ref,
                  out_ref, input_ref, gain_out, shift_out, qkv_out, qkv_bias_out, dense_out, up_out, unit_out, down_out, bias_out):
    full = jnp.float32
    part = pl.program_id(0)
    rows, wide = tok_ref.shape
    tokens = tok_ref[...].astype(full)
    out_ref[...] = (tokens + sum_ref[...].astype(full) + bias_ref[...].astype(full)).astype(out_ref.dtype)
    centered = tokens - jnp.mean(tokens, axis=-1, keepdims=True)
    inverse = lax.rsqrt(jnp.mean(centered * centered, axis=-1, keepdims=True) + eps)
    normed = centered * inverse
    hat = hat_ref[...].astype(full)
    grad = inverse * (
        hat - jnp.mean(hat, axis=-1, keepdims=True) - normed * jnp.mean(hat * normed, axis=-1, keepdims=True))
    position = (lax.axis_index("sp") * pl.num_programs(0) + part) * rows + lax.broadcasted_iota(jnp.int32, (rows, wide), 0)
    own = jnp.where(position < len_ref[0], cot_ref[...].astype(full), 0.0)
    input_ref[...] = (own + grad).astype(input_ref.dtype)
    down_out[...] = down_ref[...].astype(full)
    up_out[...] = up_ref[...].astype(full)
    qkv_out[...] = qkv_ref[...].astype(full)
    dense_out[...] = dense_ref[...].astype(full)

    @pl.when(part == 0)
    def _():
        gain_out[...] = small_ref[0:2, :]
        shift_out[...] = small_ref[2:4, :]
        qkv_bias_out[...] = small_ref[4:7, :]
        unit_rows = unit_out.shape[1] // wide
        for row in range(unit_rows):
            unit_out[:, row * wide:(row + 1) * wide] = small_ref[7 + row:8 + row, :]
        bias_out[...] = small_ref[7 + unit_rows:8 + unit_rows, :]


def finish(lengths, tokens, cotangent, reduced_out, reduced_hat, grad_down, grad_up, grad_qkv, grad_dense, out_bias, small, all_units):
    own, wide = tokens.shape
    steps = 2
    full = jnp.float32
    shape = jax.ShapeDtypeStruct

    def rows(x):
        shared = 1 if x.shape[0] // steps >= 16 else 2
        return pl.BlockSpec((x.shape[0] * shared // steps, x.shape[1]), lambda i: (i // shared, 0))

    def whole(*dims):
        return pl.BlockSpec(dims, lambda i: (0, 0))
    out_row = out_bias[None]
    return pl.pallas_call(
        finish_kernel,
        grid=(steps,),
        out_shape=[shape(tokens.shape, tokens.dtype), shape(tokens.shape, tokens.dtype), shape((2, wide), full),
                   shape((2, wide), full), shape(grad_qkv.shape, full), shape((3, wide), full), shape(grad_dense.shape, full),
                   shape(grad_up.shape, full), shape((1, all_units), full), shape(grad_down.shape, full), shape((1, wide), full)],
        in_specs=[pl.BlockSpec(memory_space=pltpu.SMEM)]
        + [rows(x) for x in (tokens, cotangent, reduced_out, reduced_hat, grad_down, grad_up, grad_qkv, grad_dense)]
        + [whole(1, wide), whole(*small.shape)],
        out_specs=[rows(tokens), rows(tokens), whole(2, wide), whole(2, wide), rows(grad_qkv), whole(3, wide), rows(grad_dense),
                   rows(grad_up), whole(1, all_units), rows(grad_down), whole(1, wide)],
        name="finish",
    )(lengths, tokens, cotangent, reduced_out, reduced_hat, grad_down, grad_up, grad_qkv, grad_dense, out_row, small)

def gather_plain(dp_size, sp_size, qkv_weight, out_weight, up_weight, down_weight):
    head_width = D // sp_size
    qkv_rows = qkv_weight.shape[0]
    qkv_slab = lax.all_to_all(
        qkv_weight.reshape(qkv_rows, 3, sp_size, head_width),
        "sp",
        split_axis=2,
        concat_axis=0,
        tiled=True,
    )
    qkv_own = lax.all_gather(
        qkv_slab.reshape(qkv_rows * sp_size, 3 * head_width), "dp", axis=0, tiled=True
    )
    up_own = lax.all_gather(up_weight, "dp", axis=0, tiled=True)
    down_own = lax.all_gather(down_weight, "dp", axis=0, tiled=True)
    out_blocks = lax.all_gather(out_weight, "dp", axis=0, tiled=True)
    out_own = lax.all_to_all(
        out_blocks.reshape(sp_size, dp_size // sp_size, qkv_rows, D),
        "sp",
        split_axis=0,
        concat_axis=2,
        tiled=True,
    ).reshape(head_width, D)
    return qkv_own, out_own, up_own, down_own


def reduce_plain(
    dp_size, sp_size, rows, hidden, grad_out, grad_pre, mlp_in, attn_in, grad_proj, context
):
    def scatter(left, right):
        return lax.psum_scatter(
            contract_rows(left, right).astype(jnp.bfloat16), "dp", scatter_dimension=0, tiled=True
        )

    grad_dense = lax.all_to_all(
        contract_rows(context, grad_out)
        .astype(jnp.bfloat16)
        .reshape(dp_size // sp_size, sp_size, rows, D),
        "sp",
        split_axis=1,
        concat_axis=0,
        tiled=True,
    ).reshape(dp_size * rows, D)
    grad_dense = lax.psum_scatter(grad_dense, "dp", scatter_dimension=0, tiled=True)
    grad_qkv = lax.all_to_all(
        scatter(attn_in, grad_proj).reshape(sp_size, rows, 3, 1, D // sp_size),
        "sp",
        split_axis=0,
        concat_axis=3,
        tiled=True,
    ).reshape(rows, 3 * D)
    return scatter(hidden, grad_out), scatter(grad_pre, mlp_in), grad_qkv, grad_dense


def body(
    tokens,
    lengths,
    cotangent,
    ln_gains,
    ln_shifts,
    qkv_weight,
    qkv_bias,
    out_weight,
    up_weight,
    up_bias,
    down_weight,
    out_bias,
):
    dp_size = lax.axis_size("dp")
    sp_size = lax.axis_size("sp")
    shard = lax.axis_index("sp")
    own_rows = tokens.shape[0]
    seq_rows = own_rows * sp_size
    head_width = D // sp_size
    length = lengths[0]
    low = jnp.bfloat16
    full = jnp.float32

    qkv_rows = qkv_weight.shape[0]
    units = up_weight.shape[0]
    square = dp_size == 8 and sp_size == 4
    positions = jnp.arange(seq_rows, dtype=jnp.int32)
    gains = ln_gains.astype(full)
    shifts = ln_shifts.astype(full)
    row_valid = positions < length
    if not square:
        unit_bias = (
            lax.dynamic_index_in_dim(
                up_bias.reshape(dp_size, sp_size, units), shard, 1, keepdims=False
            )
            .reshape(dp_size * units)
            .astype(full)
        )
        bias_own = (
            lax.dynamic_index_in_dim(
                qkv_bias.reshape(3, sp_size, head_width), shard, 1, keepdims=False
            )
            .reshape(1, 3 * head_width)
            .astype(full)
        )
        cos_rows, sin_rows = rotary_rows(seq_rows)
        seq_tokens = lax.all_gather(tokens, "sp", axis=0, tiled=True)
        qkv_own, out_own, up_own, down_own = gather_plain(
            dp_size, sp_size, qkv_weight, out_weight, up_weight, down_weight
        )
        seq_cotangent = lax.all_gather(cotangent, "sp", axis=0, tiled=True)
    if square:
        (
            qkv_own,
            out_own,
            up_own,
            down_own,
            seq_tokens,
            seq_cotangent,
            attn_in,
            mlp_in,
            hidden,
            pre_act,
            partial_out,
            part_hop,
            near_pre,
            cos_rows,
            sin_rows,
            means,
            inverses,
            unit_sums,
            queries,
            key_rows,
            values,
            context,
        ) = front(
            sp_size,
            dp_size,
            lengths,
            qkv_weight,
            out_weight,
            up_weight,
            down_weight,
            tokens,
            cotangent,
            ln_gains,
            ln_shifts,
            qkv_bias,
            up_bias[None],
        )
        grad_down, slab_sum, grad_pre, grad_hat, hat_hop, _, grad_out, reduced_out, small = middle(
            sp_size,
            dp_size,
            lengths,
            seq_cotangent,
            out_own,
            queries,
            key_rows,
            values,
            pre_act,
            hidden,
            down_own,
            up_own,
            qkv_own,
            seq_tokens,
            partial_out,
            part_hop,
            near_pre,
            attn_in,
            unit_sums,
            ln_gains,
            cos_rows,
            sin_rows,
            means,
            inverses,
        )
        grad_up, grad_qkv, grad_dense, reduced_hat, small = reduce_gradients(
            sp_size,
            qkv_rows,
            grad_out,
            grad_pre,
            mlp_in,
            context,
            grad_hat,
            hat_hop,
            slab_sum,
            small,
        )
        (
            output,
            input_grad,
            gain_total,
            shift_total,
            grad_qkv,
            qkv_bias_total,
            grad_dense,
            grad_up,
            unit_total,
            grad_down,
            out_bias_total,
        ) = finish(
            lengths,
            tokens,
            cotangent,
            reduced_out,
            reduced_hat,
            grad_down,
            grad_up,
            grad_qkv,
            grad_dense,
            out_bias,
            small,
            up_bias.shape[0],
        )
        unit_total = unit_total.reshape(-1)
        out_bias_total = out_bias_total.reshape(-1)
    else:
        inputs = seq_tokens.astype(full)
        centre = jnp.mean(inputs, axis=-1, keepdims=True)
        centered = inputs - centre
        inverse = lax.rsqrt(jnp.mean(centered * centered, axis=-1, keepdims=True) + eps)
        normed = centered * inverse
        attn_in = (normed * gains[0] + shifts[0]).astype(low)
        mlp_in = (normed * gains[1] + shifts[1]).astype(low)
        projected = jnp.dot(attn_in, qkv_own, preferred_element_type=full)
        queries, key_rows, values, context = attend_fwd(
            projected, bias_own, cos_rows, sin_rows, lengths
        )
        pre_act = contract_cols(mlp_in, up_own) + unit_bias
        hidden = gelu_value(pre_act).astype(low)
        partial_out = (
            jnp.dot(hidden, down_own, preferred_element_type=full)
            + jnp.dot(context, out_own, preferred_element_type=full)
        ).astype(low)
        reduced_out = lax.psum_scatter(
            partial_out, "sp", scatter_dimension=0, tiled=True
        )
        grad_out = jnp.where(row_valid[:, None], seq_cotangent, jnp.zeros_like(seq_cotangent))
        grad_hidden = contract_cols(grad_out, down_own)
        grad_pre = (grad_hidden * gelu_slope(pre_act)).astype(low)
        grad_mlp_in = jnp.dot(grad_pre, up_own, preferred_element_type=full)

        grad_context = contract_cols(grad_out, out_own).astype(low)
        grad_proj, grad_proj_sum = attend_bwd(
            queries, key_rows, values, grad_context, cos_rows, sin_rows, lengths
        )
        grad_attn_in = contract_cols(grad_proj, qkv_own)
        grad_hat = grad_attn_in * gains[0] + grad_mlp_in * gains[1]
        reduced_hat = lax.psum_scatter(
            grad_hat.astype(low), "sp", scatter_dimension=0, tiled=True
        )
        spread_units = lax.dynamic_update_index_in_dim(
            jnp.zeros((dp_size, sp_size, units), full),
            jnp.sum(grad_pre, axis=0, dtype=full).reshape(dp_size, units),
            shard,
            1,
        ).reshape(-1)
        spread_bias = lax.dynamic_update_index_in_dim(
            jnp.zeros((3, sp_size, head_width), full),
            grad_proj_sum.reshape(3, head_width),
            shard,
            1,
        ).reshape(3, D)
        gain_grad = jnp.stack(
            [jnp.sum(grad_attn_in * normed, axis=0), jnp.sum(grad_mlp_in * normed, axis=0)]
        )
        shift_grad = jnp.stack([jnp.sum(grad_attn_in, axis=0), jnp.sum(grad_mlp_in, axis=0)])
        own_valid = shard * own_rows + jnp.arange(own_rows, dtype=jnp.int32) < length
        own_cotangent = jnp.where(own_valid[:, None], cotangent.astype(full), 0.0)
        out_bias_part = jnp.sum(own_cotangent, axis=0)
        grad_down, grad_up, grad_qkv, grad_dense = reduce_plain(
            dp_size,
            sp_size,
            qkv_rows,
            hidden,
            grad_out,
            grad_pre,
            mlp_in,
            attn_in,
            grad_proj,
            context,
        )
        gain_total, shift_total, qkv_bias_total, unit_total, out_bias_total = lax.psum(
            (gain_grad, shift_grad, spread_bias, spread_units, out_bias_part), ("dp", "sp")
        )


        output = (
            tokens.astype(full) + reduced_out.astype(full) + out_bias.astype(full)
        ).astype(low)

        reduced_hat = reduced_hat.astype(full)
        own_centered = tokens.astype(full) - jnp.mean(tokens.astype(full), axis=-1, keepdims=True)
        own_inverse = lax.rsqrt(jnp.mean(own_centered * own_centered, axis=-1, keepdims=True) + eps)
        own_normed = own_centered * own_inverse
        grad_input = own_inverse * (
            reduced_hat
            - jnp.mean(reduced_hat, axis=-1, keepdims=True)
            - own_normed * jnp.mean(reduced_hat * own_normed, axis=-1, keepdims=True)
        )
        input_grad = (own_cotangent + grad_input).astype(low)
        grad_qkv, grad_dense = grad_qkv.astype(full), grad_dense.astype(full)
        grad_up, grad_down = grad_up.astype(full), grad_down.astype(full)

    return (
        output,
        input_grad,
        gain_total,
        shift_total,
        grad_qkv,
        qkv_bias_total,
        grad_dense,
        grad_up,
        unit_total,
        grad_down,
        out_bias_total,
    )


def solution(mesh):
    return jax.shard_map(
        body,
        mesh=mesh,
        in_specs=(
            P(("dp", "sp"), None),
            P("dp"),
            P(("dp", "sp"), None),
            P(),
            P(),
            P(("dp", "sp"), None),
            P(),
            P(("dp", "sp"), None),
            P(("dp", "sp"), None),
            P(),
            P(("dp", "sp"), None),
            P(),
        ),
        out_specs=(
            P(("dp", "sp"), None),
            P(("dp", "sp"), None),
            P(),
            P(),
            P(("dp", "sp"), None),
            P(),
            P(("dp", "sp"), None),
            P(("dp", "sp"), None),
            P(),
            P(("dp", "sp"), None),
            P(),
        ),
        check_vma=False,
    )
```
